32 devices in a mesh: seq: 4 (over y, x), batch: 8 (over z, core).
Axes of the slice: x: 2, y: 2, z: 4, core: 2. Of those that a mesh axis runs over, the one named last changes fastest.
Arguments:
- tokens: bfloat16 [8, 1024, 768], P('batch', 'seq'), may hold values from -6 to 6
- cotangent: bfloat16 [8, 1024, 768], P('batch', 'seq'), may hold values from -6 to 6
- segments: int32 [8, 1024], P('batch', 'seq'), may hold values from 0 to 2, never falling along the last dimension, each value on 1 to 512 neighbouring positions
- in_weight: bfloat16 [768, 3352], P(('seq', 'batch')), may hold values from -0.21875 to 0.21875
- out_weight: bfloat16 [1536, 768], P(('seq', 'batch')), may hold values from -0.15625 to 0.15625
- gain_in: float32 [768], replicated, may hold values from 0.5 to 1.5
- conv_weight: float32 [4, 1792], replicated, may hold values from -3 to 3
- conv_bias: float32 [1792], replicated, may hold values from -3 to 3
- dt_bias: float32 [24], replicated, may hold values from -5 to -3
- a_log: float32 [24], replicated, may hold values from -5.5 to 1
- d_skip: float32 [24], replicated, may hold values from 0.5 to 1.5
- gain_out: float32 [1536], replicated, may hold values from 0.5 to 1.5
Outputs:
- result: bfloat16 [8, 1024, 768], P('batch', 'seq')
- grad_tokens: bfloat16 [8, 1024, 768], P('batch', 'seq')
- grad_in_weight: float32 [768, 3352], P(('seq', 'batch'))
- grad_out_weight: float32 [1536, 768], P(('seq', 'batch'))
- grad_gain_in: float32 [768], replicated
- grad_conv_weight: float32 [4, 1792], replicated
- grad_conv_bias: float32 [1792], replicated
- grad_dt_bias: float32 [24], replicated
- grad_a_log: float32 [24], replicated
- grad_d_skip: float32 [24], replicated
- grad_gain_out: float32 [1536], replicated
The draws below stay inside these ranges and needn't reach their ends.
Inputs may be any that keep to these rules, and one draw needn't show every extreme that they name: `segments`: within each sequence the numbers start at 0 and never fall; the tokens of one number form one document of 1 to 512 tokens, and one document in each sequence has exactly 512.
All inputs are finite; a program needn't handle non-finite values.
Results may differ from the reference program's by a relative error of at most 0.0064.
Values may be sent and summed in bfloat16 or wider, within the bound.
No kernel may reach another device: no remote copies, remote signals or barrier semaphores. Data moves between devices by JAX's collectives and lax.ppermute only.
A program may use at most 128 MiB of HBM per device.

```python
import math
import jax
import jax.numpy as jnp
import numpy as np
from jax import lax

D = 768
HEADS = 24
HEADDIM = 64
STATE = 128
KERNEL = 4
GROUP = 128
INNER = 1536
CONV = 1792
PROJ = 3352
LENGTH = 1024
SEQS = 8
DOCS = 3
DOC_MOST = 512


def levels(key, extent, shards, smallest, top_value):
    def one(axis_at, shards_of):
        heights = jax.random.uniform(jax.random.fold_in(jax.random.fold_in(key, 6), axis_at), (shards_of,), jnp.float32, smallest / len(shards), top_value / len(shards))
        return jnp.repeat(jnp.exp(heights), extent[axis_at] // shards_of).reshape((-1,) + (1,) * (len(extent) - axis_at - 1))

    level = one(*shards[0])
    for cut in shards[1:]:
        level = level * one(*cut)
    return level


def length_profile(number_of, total, most, lean):
    weights = [(1 << 20) // math.isqrt(rank ** lean) + 1 for rank in range(2, number_of + 1)]
    rest, counts = total - most - (number_of - 1), [1] * (number_of - 1)
    while rest > 0:
        free = [i for i in range(number_of - 1) if counts[i] < most]
        whole, remaining = sum([weights[i] for i in free]), rest
        for i in free:
            addition = min(most - counts[i], max(1, remaining * weights[i] // whole), rest)
            counts[i] = counts[i] + addition
            rest = rest - addition
    return np.array([most] + counts)


def uneven_parts(own_key, count, total, most, slope):
    if count == 2:
        one = jax.random.randint(own_key, (), max(1, total - most), min(most, total - 1) + 1)
        return jnp.stack([one, total - one])
    sizes = jnp.asarray(length_profile(count, total, most, slope), jnp.int32)
    pairs = (count - 1) // 2
    source_of, sink = sizes[1:1 + 2 * pairs:2], sizes[2:2 + 2 * pairs:2]
    slack = jnp.minimum(source_of - 1, most - sink)
    shifted = jax.random.randint(jax.random.fold_in(own_key, 1), (pairs,), 0, 1 << 20) % (slack + 1)
    sizes = sizes.at[1:1 + 2 * pairs:2].set(source_of - shifted).at[2:2 + 2 * pairs:2].set(sink + shifted)
    return sizes[jax.random.permutation(jax.random.fold_in(own_key, 2), count)]


def normal_values(key, shape, scale, bound, pieces=(), kind=jnp.bfloat16):
    values = jax.random.normal(key, shape, jnp.float32) * scale
    if len(pieces) > 0:
        values = levels(key, shape, pieces, -0.22, 0.18) * values
    return jnp.clip(values, min=-bound, max=bound).astype(kind)


def setup_inputs(seed: int = 0) -> dict:
    arg_keys = jax.random.split(jax.random.key(seed), 13)
    tokens = normal_values(arg_keys[0], (SEQS, LENGTH, D), 1.0, 6.0, ((0, 8), (1, 4)))
    cotangent = normal_values(arg_keys[1], (SEQS, LENGTH, D), 1.0, 6.0, ((0, 8), (1, 4)))
    segments = jax.vmap(lambda own: jnp.searchsorted(jnp.cumsum(uneven_parts(own, DOCS, LENGTH, DOC_MOST, 0)), jnp.arange(LENGTH), side="right"))(jax.random.split(arg_keys[2], SEQS)).reshape((SEQS, LENGTH)).astype(jnp.int32)
    in_weight = normal_values(arg_keys[3], (D, PROJ), D ** -0.5, 0.21875, ((0, 32),))
    out_weight = normal_values(arg_keys[4], (INNER, D), INNER ** -0.5, 0.15625, ((0, 32),))
    gain_in = jnp.clip(1.0 + 0.1 * jax.random.normal(arg_keys[5], (D,), jnp.float32), 0.5, 1.5)
    conv_weight = normal_values(arg_keys[6], (KERNEL, CONV), KERNEL ** -0.5, 3.0, (), jnp.float32)
    conv_bias = normal_values(arg_keys[7], (CONV,), 0.5, 3.0, (), jnp.float32)
    dt_bias = jnp.clip(jax.random.uniform(arg_keys[8], (HEADS,), jnp.float32, -5.0, -3.0), -5.0, -3.0)
    a_log = jnp.clip(jax.random.uniform(arg_keys[9], (HEADS,), jnp.float32, -5.5, 1.0), -5.5, 1.0)
    d_skip = jnp.clip(jax.random.uniform(arg_keys[10], (HEADS,), jnp.float32, 0.5, 1.5), 0.5, 1.5)
    gain_out = jnp.clip(1.0 + 0.1 * jax.random.normal(arg_keys[11], (INNER,), jnp.float32), 0.5, 1.5)
    return {"tokens": tokens, "cotangent": cotangent, "segments": segments, "in_weight": in_weight, "out_weight": out_weight, "gain_in": gain_in, "conv_weight": conv_weight, "conv_bias": conv_bias, "dt_bias": dt_bias, "a_log": a_log, "d_skip": d_skip, "gain_out": gain_out}


highest = lax.Precision.HIGHEST
norm_eps = 1e-05

@jax.custom_vjp
def low(v):
    return lax.optimization_barrier(v.astype(jnp.bfloat16)).astype(jnp.float32)

@jax.custom_vjp
def low_back(v):
    return v

def low_keep(v):
    return (low(v), None)

def low_pass(kept, grad):
    return (grad,)

def back_keep(v):
    return (v, None)

def back_low(kept, grad):
    return (low(grad),)
low.defvjp(low_keep, low_pass)
low_back.defvjp(back_keep, back_low)

def rms_scale(values, gain):
    mean_square = lax.optimization_barrier(jnp.mean(values * values, axis=-1, keepdims=True))
    return values * lax.rsqrt(mean_square + norm_eps) * gain

def causal_conv(extended, ext_segs, conv_weight, conv_bias, row_count):
    target = ext_segs[KERNEL - 1:]
    total = jnp.zeros((row_count, conv_weight.shape[1]), jnp.float32) + conv_bias[None, :]
    for offset in range(KERNEL):
        window = extended[offset:offset + row_count]
        same_doc = (ext_segs[offset:offset + row_count] == target).astype(jnp.float32)
        total = total + conv_weight[offset][None, :] * window * same_doc[:, None]
    return jax.nn.silu(total)

def prepare(xbc, dt_raw, edge_rows, ext_segs, conv_weight, conv_bias, dt_bias, a_log):
    row_count = xbc.shape[0]
    extended = jnp.concatenate([edge_rows, xbc], axis=0)
    mixed = causal_conv(extended, ext_segs, conv_weight, conv_bias, row_count)
    values = mixed[:, :INNER].reshape(row_count, HEADS, HEADDIM)
    key_vecs = mixed[:, INNER:INNER + STATE]
    queries = mixed[:, INNER + STATE:]
    step_sizes = jax.nn.softplus(dt_raw + dt_bias[None, :])
    log_decay = -step_sizes * jnp.exp(a_log)[None, :]
    return (values, key_vecs, queries, step_sizes, log_decay)

def group_block(carried, block_in):
    state_in, last_seg = carried
    values, key_vecs, queries, step_sizes, log_decay, seg_ids = block_in
    length_here = seg_ids.shape[0]
    cumulative = jnp.cumsum(log_decay, axis=0)
    positions = jnp.arange(length_here)
    allowed = (seg_ids[:, None] == seg_ids[None, :]) & (positions[:, None] >= positions[None, :])
    gap_logs = cumulative[:, None, :] - cumulative[None, :, :]
    decay_mask = jnp.where(allowed[:, :, None], jnp.exp(jnp.minimum(gap_logs, 0.0)), 0.0)
    scores = jnp.dot(queries, key_vecs.T, precision=highest)
    weights = decay_mask * scores[:, :, None] * step_sizes[None, :, :]
    inside = jnp.einsum('tsh,shp->thp', weights, values, precision=highest)
    keep_factor = jnp.where((seg_ids == last_seg)[:, None], jnp.exp(cumulative), 0.0)
    carried_out = jnp.einsum('tn,hpn->thp', queries, state_in, precision=highest) * keep_factor[:, :, None]
    to_end = jnp.where((seg_ids == seg_ids[-1])[:, None], jnp.exp(cumulative[-1][None, :] - cumulative), 0.0) * step_sizes
    fresh_state = jnp.einsum('sh,shp,sn->hpn', to_end, values, key_vecs, precision=highest)
    new_state = state_in * keep_factor[-1][:, None, None] + fresh_state
    return ((new_state, seg_ids[-1]), inside + carried_out)

def grouped_ssd(values, key_vecs, queries, step_sizes, log_decay, seg_ids, d_skip, state_in, last_seg):
    row_count = seg_ids.shape[0]
    block_count = row_count // GROUP

    def blocked(member):
        return member.reshape((block_count, GROUP) + member.shape[1:])
    inputs = (blocked(values), blocked(key_vecs), blocked(queries), blocked(step_sizes), blocked(log_decay), blocked(seg_ids))
    (final_state, last_out), outputs = lax.scan(jax.checkpoint(group_block), (state_in, last_seg), inputs)
    outputs = outputs.reshape(row_count, HEADS, HEADDIM) + d_skip[None, :, None] * values
    return (outputs, final_state)

def gated_norm(mixed_out, gate_z, gain_out):
    return rms_scale(mixed_out * jax.nn.silu(gate_z), gain_out)

def layer(params, tokens_f, seg_ids):
    in_weight, out_weight, gain_in, conv_weight, conv_bias, dt_bias, a_log, d_skip, gain_out = params
    length_here = tokens_f.shape[0]
    normed = low(rms_scale(tokens_f, gain_in))
    projected = low_back(jnp.dot(normed, in_weight, precision=highest))
    gate_z = projected[:, :INNER]
    xbc = projected[:, INNER:INNER + CONV]
    dt_raw = projected[:, INNER + CONV:]
    zero_rows = jnp.zeros((KERNEL - 1, CONV), jnp.float32)
    ext_segs = jnp.concatenate([jnp.zeros((KERNEL - 1,), jnp.int32), seg_ids.astype(jnp.int32)])
    values, key_vecs, queries, step_sizes, log_decay = prepare(xbc, dt_raw, zero_rows, ext_segs, conv_weight, conv_bias, dt_bias, a_log)
    zero_state = jnp.zeros((HEADS, HEADDIM, STATE), jnp.float32)
    mixed_out, final_state = grouped_ssd(values, key_vecs, queries, step_sizes, log_decay, seg_ids, d_skip, zero_state, seg_ids[0])
    gated = low(gated_norm(mixed_out.reshape(length_here, INNER), gate_z, gain_out))
    return tokens_f + jnp.dot(gated, out_weight, precision=highest)

def reference(tokens, cotangent, segments, in_weight, out_weight, gain_in, conv_weight, conv_bias, dt_bias, a_log, d_skip, gain_out):
    params = (in_weight.astype(jnp.float32), out_weight.astype(jnp.float32), gain_in, conv_weight, conv_bias, dt_bias, a_log, d_skip, gain_out)
    zero_grads = jax.tree.map(jnp.zeros_like, params)

    def one_sequence(totals, member):
        tokens_f, cot_f, seg_ids = member

        def forward(params_in, tokens_in):
            return layer(params_in, tokens_in, seg_ids)
        output_seq, pullback = jax.vjp(forward, params, tokens_f)
        grad_params, grad_seq = pullback(cot_f)
        totals = jax.tree.map(lambda total_one, grad_one: total_one + grad_one, totals, grad_params)
        return (totals, (output_seq.astype(jnp.bfloat16), grad_seq.astype(jnp.bfloat16)))
    totals, (outputs, grad_all) = lax.scan(one_sequence, zero_grads, (tokens.astype(jnp.float32), cotangent.astype(jnp.float32), segments))
    return (outputs, grad_all, totals[0], totals[1], totals[2], totals[3], totals[4], totals[5], totals[6], totals[7], totals[8])
```

```python
import functools

import jax
import jax.numpy as jnp
from jax import lax
from jax.experimental import pallas as pl
from jax.experimental.pallas import tpu as pltpu
from jax.sharding import PartitionSpec as P

HEADS = 24
HEADDIM = 64
STATE = 128
KERNEL = 4
GROUP = 128
INNER = 1536
CONV = 1792
WIDTH = 768
LANES = 128
LEAD = 8


highest = lax.Precision.HIGHEST
norm_eps = 1e-05
f32 = jnp.float32
bf16 = jnp.bfloat16
contract_last = (((1,), (1,)), ((), ()))
contract_first = (((0,), (0,)), ((), ()))


def mm(a, b):
    return jnp.dot(a.astype(bf16), b.astype(bf16), preferred_element_type=f32)


def mm_nt(a, b):
    return lax.dot_general(
        a.astype(bf16), b.astype(bf16), contract_last, preferred_element_type=f32
    )


def mm_tn(a, b):
    return lax.dot_general(
        a.astype(bf16), b.astype(bf16), contract_first, preferred_element_type=f32
    )


def mm_exact(a, b):
    return jnp.dot(a, b, precision=highest, preferred_element_type=f32)


def iota(shape, dim):
    return lax.broadcasted_iota(jnp.int32, shape, dim)


def aligned(value, unit):
    return pl.multiple_of(value, unit)


def wide(columns, count):
    rows = columns.shape[0]
    low = iota((rows, LANES), 1) < HEADDIM
    parts = []
    for pair in range(count // 2):
        left = jnp.broadcast_to(columns[:, 2 * pair : 2 * pair + 1], (rows, LANES))
        right = jnp.broadcast_to(columns[:, 2 * pair + 1 : 2 * pair + 2], (rows, LANES))
        parts.append(jnp.where(low, left, right))
    return jnp.concatenate(parts, axis=1)


def softplus(value):
    return jnp.maximum(value, 0.0) + jnp.log1p(jnp.exp(-jnp.abs(value)))


def sigmoid(value):
    return 1.0 / (1.0 + jnp.exp(-value))


class Plan:
    def __init__(self, mesh_seq, mesh_batch, rows, in_rows, out_rows):
        self.seq = mesh_seq
        self.batch = mesh_batch
        self.line = mesh_batch // 2
        self.rows = rows
        self.total = rows * mesh_seq
        self.blocks = self.total // GROUP
        self.heads = HEADS // mesh_seq
        self.chan = self.heads * HEADDIM
        self.mixed = self.chan + 2 * STATE
        self.cols = self.mixed + LANES
        self.in_rows = in_rows
        self.out_rows = out_rows


def place():
    s = lax.axis_index("seq")
    b = lax.axis_index("batch")
    return s, lax.shift_right_logical(b, 1), lax.bitwise_and(b, 1)


def in_place(plan, ids, line_xor, core_xor, seq_xor):
    s, z, c = ids
    owner = (s ^ seq_xor) * plan.batch + (z ^ line_xor) * 2 + (c ^ core_xor)
    return aligned(owner * plan.in_rows, 8)


def block_values(plan, b, x_ref, segc_ref, segr_ref, dt_ref, convw, convb, heads_ref):
    base = aligned(b * GROUP, GROUP)
    win = x_ref[pl.ds(base, GROUP + LEAD), :]
    segw = segc_ref[pl.ds(base, GROUP + LEAD), :]
    seg = segw[LEAD:]
    prev = segw[LEAD - 1 : LEAD]
    repeat = plan.mixed // LANES
    pre = jnp.broadcast_to(convb, (GROUP, plan.mixed))
    shifts = []
    for k in range(KERNEL):
        start = LEAD - KERNEL + 1 + k
        part = win[start : start + GROUP]
        if k < KERNEL - 1:
            same = (segw[start : start + GROUP] == seg).astype(f32)
            part = part * jnp.concatenate([same] * repeat, axis=1)
        shifts.append(part)
        pre = pre + convw[k : k + 1] * part
    sig = sigmoid(pre)
    mixed = pre * sig
    values = mixed[:, : plan.chan]
    keys = mixed[:, plan.chan : plan.chan + STATE]
    queries = mixed[:, plan.chan + STATE :]
    dt_in = dt_ref[pl.ds(base, GROUP), :] + heads_ref[0:1, :LANES]
    steps = softplus(dt_in)
    decay = -steps * jnp.exp(heads_ref[1:2, :LANES])
    row = iota((GROUP, GROUP), 0)
    col = iota((GROUP, GROUP), 1)
    tri = (row >= col).astype(f32)
    cum = mm_exact(tri, decay)
    cum_t = cum.T
    steps_t = steps.T
    segr = segr_ref[pl.ds(b, 1), :]
    allowed = (seg == segr) & (row >= col)
    scores = mm_nt(queries, keys)
    keep = jnp.where(seg == prev, jnp.exp(cum), 0.0)
    last = cum[GROUP - 1 :]
    to_last = jnp.where(seg == seg[GROUP - 1 :], jnp.exp(last - cum), 0.0)
    return dict(
        base=base, seg=seg, shifts=shifts, pre=pre, sig=sig, values=values, keys=keys,
        queries=queries, dt_in=dt_in, steps=steps, decay=decay, tri=tri, cum=cum, cum_t=cum_t,
        steps_t=steps_t, allowed=allowed, scores=scores, keep=keep, to_last=to_last,
    )


def head_decay(v, h):
    gap = v["cum"][:, h : h + 1] - v["cum_t"][h : h + 1, :]
    return jnp.where(v["allowed"], jnp.exp(jnp.minimum(gap, 0.0)), 0.0)


def split_pair(pair):
    low = iota(pair.shape, 1) < HEADDIM
    return jnp.concatenate([jnp.where(low, pair, 0.0), jnp.where(low, 0.0, pair)], axis=0)


def fill_segments(plan, s, pieces, segc_ref, segr_ref):
    per = plan.rows // GROUP
    segc_ref[...] = jnp.zeros_like(segc_ref)
    segr_ref[...] = jnp.zeros_like(segr_ref)
    for m in range(plan.seq):
        line = pieces[m][plan.in_rows : plan.in_rows + 1, : plan.rows].astype(f32)
        for j in range(per):
            b = (s ^ m) * per + j
            segr_ref[pl.ds(b, 1), :] = line[:, j * GROUP : (j + 1) * GROUP]
    every = segr_ref[...]
    turned = jnp.concatenate(
        [every, jnp.zeros((LANES - every.shape[0], GROUP), f32)], axis=0
    ).T
    for b in range(plan.blocks):
        segc_ref[LEAD + b * GROUP : LEAD + (b + 1) * GROUP, :] = jnp.broadcast_to(
            turned[:, b : b + 1], (GROUP, LANES)
        )


def forward_kernel(plan, *refs):
    n = plan.seq
    toks, refs = refs[:n], refs[n:]
    pieces, refs = refs[:n], refs[n:]
    weights, refs = refs[: 2 * plan.line], refs[2 * plan.line :]
    gain_ref, convw_ref, convb_ref, heads_ref = refs[:4]
    normed_ref, w_ref, x_ref, dt_ref, y_ref, states_ref, segc_ref, segr_ref = refs[4:12]
    wf_ref, state_ref = refs[12:]
    ids = place()
    s = ids[0]
    fill_segments(plan, s, pieces, segc_ref, segr_ref)
    for core_xor in range(2):
        for line_xor in range(plan.line):
            piece = weights[core_xor * plan.line + line_xor]
            for m in range(n):
                dest = pl.ds(in_place(plan, ids, line_xor, core_xor, m), plan.in_rows)
                wf_ref[dest, :] = piece[m * plan.in_rows : (m + 1) * plan.in_rows, :].astype(f32)
    w_ref[...] = wf_ref[...].astype(bf16)
    x_ref[0:LEAD, :] = jnp.zeros((LEAD, plan.mixed), f32)
    for m in range(n):
        tok = toks[m][...].astype(f32)
        scale = lax.rsqrt(jnp.mean(tok * tok, axis=1, keepdims=True) + norm_eps)
        low = (tok * scale * gain_ref[...]).astype(bf16)
        start = (s ^ m) * plan.rows
        normed_ref[pl.ds(aligned(start, plan.rows), plan.rows), :] = low
        out = jnp.dot(low, w_ref[...], preferred_element_type=f32)
        x_ref[pl.ds(aligned(start + LEAD, 8), plan.rows), :] = out[:, : plan.mixed]
        dt_ref[pl.ds(aligned(start, plan.rows), plan.rows), :] = out[:, plan.mixed :]
    state_ref[...] = jnp.zeros_like(state_ref)
    convw = convw_ref[...]
    convb = convb_ref[...]

    def step(b, carry):
        v = block_values(plan, b, x_ref, segc_ref, segr_ref, dt_ref, convw, convb, heads_ref)
        state = state_ref[...]
        states_ref[b] = state
        parts = []
        for pair in range(plan.heads // 2):
            lanes = slice(pair * LANES, (pair + 1) * LANES)
            weights_pair = []
            for h in (2 * pair, 2 * pair + 1):
                decay = head_decay(v, h)
                weights_pair.append(decay * v["scores"] * v["steps_t"][h : h + 1, :])
            parts.append(
                mm(jnp.concatenate(weights_pair, axis=1), split_pair(v["values"][:, lanes]))
            )
        inside = jnp.concatenate(parts, axis=1)
        keep = wide(v["keep"], plan.heads)
        carried = mm(v["queries"], state) * keep
        y_ref[pl.ds(v["base"], GROUP), :] = inside + carried + heads_ref[2:3, :] * v["values"]
        to_end = wide(v["to_last"] * v["steps"], plan.heads)
        state_ref[...] = state * keep[GROUP - 1 :] + mm_tn(v["keys"], v["values"] * to_end)
        return carry

    lax.fori_loop(0, plan.blocks, step, 0)


def gate_kernel(plan, *refs):
    n = plan.seq
    normed_ref, y_ref = refs[:2]
    weights = refs[2 : 2 + 2 * plan.line]
    cots = refs[2 + 2 * plan.line : 2 + 2 * plan.line + n]
    gain_ref = refs[2 + 2 * plan.line + n]
    outs = refs[3 + 2 * plan.line + n :]
    wz_ref, z_ref, du_ref, stats_ref = outs[:4]
    parts = outs[4 : 4 + n]
    wf_ref, wo_ref = outs[4 + n :]
    ids = place()
    s, z, c = ids
    half = plan.in_rows * n // 2
    for core_xor in range(2):
        for line_xor in range(plan.line):
            piece = weights[core_xor * plan.line + line_xor]
            for m in range(n):
                dest = pl.ds(in_place(plan, ids, line_xor, core_xor, m), plan.in_rows)
                top = (m // 2) * plan.in_rows
                left = (m % 2) * plan.chan
                wf_ref[dest, :] = piece[
                    top : top + plan.in_rows, left : left + plan.chan
                ].astype(f32)
            start = ((z ^ line_xor) * 2 + (c ^ core_xor)) * plan.out_rows
            wo_ref[pl.ds(aligned(start, 16), plan.out_rows), :] = piece[
                half : half + plan.out_rows, :
            ]
    wz_ref[...] = wf_ref[...].astype(bf16)
    gain = gain_ref[...]
    lane = iota((plan.rows, LANES), 1)
    square = jnp.zeros((GROUP, LANES), f32)
    lane = iota((GROUP, LANES), 1)
    per = plan.rows // GROUP
    for m in range(n):
        start = aligned((s ^ m) * plan.rows, plan.rows)
        gate = jnp.dot(
            normed_ref[pl.ds(start, plan.rows), :], wz_ref[...], preferred_element_type=f32
        )
        z_ref[pl.ds(start, plan.rows), :] = gate
        gated = y_ref[pl.ds(start, plan.rows), :] * gate * sigmoid(gate)
        scaled = gated * gain
        parts[m][...] = mm(scaled, wo_ref[...]).astype(parts[m].dtype)
        du = mm_nt(cots[m][...], wo_ref[...])
        du_ref[pl.ds(start, plan.rows), :] = du
        norm = jnp.sum(gated * gated, axis=1, keepdims=True)
        dots = jnp.sum(du * scaled, axis=1, keepdims=True)
        for j in range(per):
            b = (s ^ m) * per + j
            rows = slice(j * GROUP, (j + 1) * GROUP)
            square = square + jnp.where(lane == b, norm[rows], 0.0)
            square = square + jnp.where(lane == b + plan.blocks, dots[rows], 0.0)
    stats_ref[...] = square.T[: 2 * plan.blocks]


def emit_rows(plan, ids, source_ref, put):
    for core_xor in range(2):
        for line_xor in range(plan.line):
            for m in range(plan.seq):
                rows = source_ref[
                    pl.ds(in_place(plan, ids, line_xor, core_xor, m), plan.in_rows), :
                ]
                put(core_xor, line_xor, m, rows)


def regate_kernel(plan, *refs):
    n = plan.seq
    stats = refs[:n]
    normed_ref, y_ref, z_ref, du_ref = refs[n : n + 4]
    cots = refs[n + 4 : 2 * n + 4]
    gain_ref = refs[2 * n + 4]
    dy_ref, dz_ref, scale_ref, gain_out_ref, keep_ref, send_ref = refs[2 * n + 5 : 2 * n + 11]
    gated_ref, gz_ref, go_ref = refs[2 * n + 11 :]
    ids = place()
    s, z, c = ids
    total = stats[0][...]
    for m in range(1, n):
        total = total + stats[m][...]
    turned = jnp.concatenate(
        [total, jnp.zeros((LANES - total.shape[0], GROUP), f32)], axis=0
    ).T
    gain = gain_ref[...]
    sums = jnp.zeros((1, plan.chan), f32)
    for b in range(plan.blocks):
        rows = slice(b * GROUP, (b + 1) * GROUP)
        r = lax.rsqrt(turned[:, b : b + 1] / INNER + norm_eps)
        dot = turned[:, plan.blocks + b : plan.blocks + b + 1] / INNER
        scale_ref[rows, :] = jnp.broadcast_to(r, (GROUP, LANES))
        gate = z_ref[rows, :]
        sig = sigmoid(gate)
        silu = gate * sig
        y = y_ref[rows, :]
        gated = y * silu
        du = du_ref[rows, :]
        normal = gated * r
        grad_pre = r * (du * gain) - normal * (r * r * dot)
        dy_ref[rows, :] = grad_pre * silu
        dz_ref[rows, :] = (grad_pre * y * sig * (1.0 + gate * (1.0 - sig))).astype(bf16)
        gated_ref[rows, :] = (normal * gain).astype(bf16)
        sums = sums + jnp.sum(du * normal, axis=0, keepdims=True)
    gain_out_ref[...] = sums
    gz_ref[...] = mm_tn(normed_ref[...], dz_ref[...])
    out = None
    for m in range(n):
        start = aligned((s ^ m) * plan.rows, plan.rows)
        one = mm_tn(gated_ref[pl.ds(start, plan.rows), :], cots[m][...])
        out = one if out is None else out + one
    go_ref[...] = out
    half = plan.in_rows * n // 2
    both = (keep_ref, send_ref)

    def put(core_xor, line_xor, m, rows):
        top = (m // 2) * plan.in_rows
        left = (m % 2) * plan.chan
        both[core_xor][line_xor, top : top + plan.in_rows, left : left + plan.chan] = rows.astype(
            bf16
        )

    emit_rows(plan, ids, gz_ref, put)
    for core_xor in range(2):
        for line_xor in range(plan.line):
            start = ((z ^ line_xor) * 2 + (c ^ core_xor)) * plan.out_rows
            both[core_xor][line_xor, half : half + plan.out_rows, :] = go_ref[
                pl.ds(aligned(start, 16), plan.out_rows), :
            ].astype(bf16)


def backward_kernel(plan, *refs):
    n = plan.seq
    toks = refs[:n]
    normed_ref, w_ref, wz_ref, x_ref, dt_ref, states_ref, segc_ref, segr_ref = refs[n : n + 8]
    dy_ref, dz_ref, gain_out_ref, convw_ref, convb_ref, heads_ref = refs[n + 8 : n + 14]
    outs = refs[n + 14 :]
    grads, outs = outs[:n], outs[n:]
    keep_ref, send_ref, small_ref = outs[:3]
    gp_ref, gw_ref, gn_ref, adj_ref, edge_ref, acc_ref, head_ref = outs[3:]
    ids = place()
    s = ids[0]
    convw = convw_ref[...]
    convb = convb_ref[...]
    adj_ref[...] = jnp.zeros_like(adj_ref)
    edge_ref[...] = jnp.zeros_like(edge_ref)
    acc_ref[...] = jnp.zeros_like(acc_ref)
    head_ref[...] = jnp.zeros_like(head_ref)
    repeat = plan.mixed // LANES
    pick = (iota((plan.chan, LANES), 0) // HEADDIM == iota((plan.chan, LANES), 1)).astype(f32)
    lane = iota((GROUP, LANES), 1)

    def step(turn, carry):
        b = plan.blocks - 1 - turn
        v = block_values(plan, b, x_ref, segc_ref, segr_ref, dt_ref, convw, convb, heads_ref)
        base = v["base"]
        state = states_ref[b]
        adj = adj_ref[...]
        dy = dy_ref[pl.ds(base, GROUP), :]
        values = v["values"]
        keep = wide(v["keep"], plan.heads)
        to_end = wide(v["to_last"] * v["steps"], plan.heads)
        kept = dy * keep
        dq = mm_nt(kept, state)
        cross = kept * mm(v["queries"], state)
        fed = mm(v["keys"], adj)
        dk = mm_nt(values * to_end, adj)
        adj_ref[...] = adj * keep[GROUP - 1 :] + mm_tn(v["queries"], kept)
        ended = jnp.sum(state * adj, axis=0, keepdims=True)
        pushed = fed * values
        skipped = jnp.sum(dy * values, axis=0, keepdims=True)
        few = jnp.concatenate([ended, skipped, jnp.zeros((6, plan.chan), f32)], axis=0)
        sums = mm_exact(jnp.concatenate([cross, pushed, few], axis=0), pick)
        cross_h = sums[:GROUP]
        pushed_h = sums[GROUP : 2 * GROUP]
        ended_h = sums[2 * GROUP : 2 * GROUP + 1]
        skipped_h = sums[2 * GROUP + 1 : 2 * GROUP + 2]
        grad_steps = pushed_h * v["to_last"]
        pulled = grad_steps * v["steps"]
        dcum = cross_h - pulled
        at_end = jnp.sum(pulled, axis=0, keepdims=True) + v["keep"][GROUP - 1 :] * ended_h
        dscores = jnp.zeros((GROUP, GROUP), f32)
        columns = []
        dvs = []
        for pair in range(plan.heads // 2):
            lanes = slice(pair * LANES, (pair + 1) * LANES)
            dy_pair = split_pair(dy[:, lanes])
            products = mm_nt(dy_pair, values[:, lanes])
            stacked = []
            for j, h in enumerate((2 * pair, 2 * pair + 1)):
                decay = head_decay(v, h)
                steps_row = v["steps_t"][h : h + 1, :]
                weighted = decay * products[j * GROUP : (j + 1) * GROUP]
                direct = weighted * v["scores"]
                dscores = dscores + weighted * steps_row
                rowsum = jnp.sum(direct * steps_row, axis=1, keepdims=True)
                dcum = dcum + jnp.where(lane == h, rowsum, 0.0)
                columns.append(jnp.sum(direct, axis=0, keepdims=True))
                stacked.append(decay * v["scores"] * steps_row)
            dvs.append(mm_tn(jnp.concatenate(stacked, axis=0), dy_pair))
        dv = jnp.concatenate(dvs, axis=1) + fed * to_end + heads_ref[2:3, :] * dy
        columns.append(jnp.zeros((LANES - plan.heads, GROUP), f32))
        down = jnp.concatenate(columns, axis=0).T
        grad_steps = grad_steps + down
        dcum = dcum - down * v["steps"]
        row = iota((GROUP, LANES), 0)
        dcum = dcum + jnp.where(row == GROUP - 1, at_end, 0.0)
        dk = dk + mm_tn(dscores, v["queries"])
        dq = dq + mm(dscores, v["keys"])
        ddecay = lax.dot_general(
            v["tri"], dcum, contract_first, precision=highest, preferred_element_type=f32
        )
        grad_steps = grad_steps - ddecay * jnp.exp(heads_ref[1:2, :LANES])
        grad_dt = grad_steps * sigmoid(v["dt_in"])
        head_ref[0:1, :] += jnp.sum(grad_dt, axis=0, keepdims=True)
        head_ref[1:2, :] += jnp.sum(ddecay * v["decay"], axis=0, keepdims=True)
        head_ref[2:3, :] += skipped_h
        dmixed = jnp.concatenate([dv, dk, dq], axis=1)
        pre, sig = v["pre"], v["sig"]
        dpre = dmixed * (sig * (1.0 + pre * (1.0 - sig)))
        acc_ref[4:5, :] += jnp.sum(dpre, axis=0, keepdims=True)
        longer = jnp.concatenate([dpre, edge_ref[...]], axis=0)
        edge_ref[...] = dpre[:LEAD]
        segn = segc_ref[pl.ds(aligned(base + LEAD, 8), GROUP + LEAD), :]
        dx = jnp.zeros((GROUP, plan.mixed), f32)
        for k in range(KERNEL):
            acc_ref[k : k + 1, :] += jnp.sum(dpre * v["shifts"][k], axis=0, keepdims=True)
            ahead = KERNEL - 1 - k
            part = longer[ahead : ahead + GROUP]
            if ahead:
                same = (segn[ahead : ahead + GROUP] == v["seg"]).astype(f32)
                part = part * jnp.concatenate([same] * repeat, axis=1)
            dx = dx + convw[k : k + 1] * part
        live = jnp.where(lane < plan.heads, grad_dt, 0.0)
        gp_ref[pl.ds(base, GROUP), :] = jnp.concatenate([dx, live], axis=1).astype(bf16)
        return carry

    lax.fori_loop(0, plan.blocks, step, 0)
    gn_ref[...] = mm_nt(gp_ref[...], w_ref[...]) + mm_nt(dz_ref[...], wz_ref[...])
    gain_in = jnp.zeros((1, WIDTH), f32)
    for m in range(n):
        tok = toks[m][...].astype(f32)
        scale = lax.rsqrt(jnp.mean(tok * tok, axis=1, keepdims=True) + norm_eps)
        part = gn_ref[pl.ds(aligned((s ^ m) * plan.rows, plan.rows), plan.rows), :]
        gain_in = gain_in + jnp.sum(part * (tok * scale), axis=0, keepdims=True)
        grads[m][...] = part.astype(grads[m].dtype)
    gw_ref[...] = mm_tn(normed_ref[...], gp_ref[...])
    both = (keep_ref, send_ref)

    def put(core_xor, line_xor, m, rows):
        top = m * plan.in_rows
        both[core_xor][line_xor, top : top + plan.in_rows, :] = rows.astype(bf16)

    emit_rows(plan, ids, gw_ref, put)
    small_ref[...] = jnp.zeros_like(small_ref)
    small_ref[0:1, :WIDTH] = gain_in
    small_ref[1:6, : plan.mixed] = acc_ref[0:5, :]
    small_ref[6:7, : plan.chan] = gain_out_ref[...]
    for j in range(3):
        small_ref[7:8, j * LANES : (j + 1) * LANES] = head_ref[j : j + 1, :]


def add_split_kernel(count, keep_ref, got_ref, *outs):
    for m in range(count):
        outs[m][...] = (keep_ref[m].astype(f32) + got_ref[m].astype(f32)).astype(bf16)


def gate_sum_kernel(plan, *refs):
    parts, outs = refs[: plan.line], refs[plan.line :]
    total = parts[0][...].astype(f32)
    for part in parts[1:]:
        total = total + part[...].astype(f32)
    half = plan.in_rows * plan.seq // 2
    for m in range(plan.seq):
        top = (m // 2) * plan.in_rows
        left = (m % 2) * plan.chan
        outs[m][...] = total[top : top + plan.in_rows, left : left + plan.chan].astype(bf16)
    outs[plan.seq][...] = total[half : half + plan.out_rows]


def row_sum_kernel(plan, *refs):
    parts, outs = refs[: plan.line], refs[plan.line :]
    for m in range(plan.seq):
        rows = slice(m * plan.in_rows, (m + 1) * plan.in_rows)
        total = parts[0][rows, :].astype(f32)
        for part in parts[1:]:
            total = total + part[rows, :].astype(f32)
        outs[m][...] = total.astype(bf16)


def columns_kernel(plan, *refs):
    n = plan.seq
    gates, mains = refs[:n], refs[n : 2 * n]
    out_ref, gate_ref, main_ref = refs[2 * n :]
    s = lax.axis_index("seq")
    for m in range(n):
        gate_ref[m] = gates[m][...].astype(f32)
        main_ref[m] = mains[m][...].astype(f32)
    shared = jnp.zeros((plan.in_rows, 2 * STATE), f32)
    lane = iota((plan.in_rows, LANES), 1)
    dts = jnp.zeros((plan.in_rows, LANES), f32)
    for g in range(n):
        out_ref[:, g * plan.chan : (g + 1) * plan.chan] = gate_ref[s ^ g]
        main = main_ref[s ^ g]
        out_ref[:, INNER + g * plan.chan : INNER + (g + 1) * plan.chan] = main[:, : plan.chan]
        shared = shared + main[:, plan.chan : plan.mixed]
        one = main[:, plan.mixed :]
        moved = one if g == 0 else pltpu.roll(one, g * plan.heads, 1)
        dts = jnp.where(lane // plan.heads == g, moved, dts)
    out_ref[:, 2 * INNER : INNER + CONV] = shared
    out_ref[:, INNER + CONV :] = dts[:, :HEADS]


def small_kernel(plan, *refs):
    n = plan.seq
    parts = refs[:n]
    gain_in_ref, convw_ref, convb_ref, dtb_ref, alog_ref, skip_ref, gain_out_ref, all_ref = refs[n:]
    s = lax.axis_index("seq")
    for m in range(n):
        all_ref[m] = parts[m][...]
    gain_in = jnp.zeros((1, WIDTH), f32)
    shared = jnp.zeros((5, 2 * STATE), f32)
    lane = iota((1, LANES), 1)
    heads = [jnp.zeros((1, LANES), f32) for _ in range(3)]
    for g in range(n):
        part = all_ref[s ^ g]
        gain_in = gain_in + part[0:1, :WIDTH]
        cols = slice(g * plan.chan, (g + 1) * plan.chan)
        convw_ref[:, cols] = part[1:5, : plan.chan]
        convb_ref[:, cols] = part[5:6, : plan.chan]
        gain_out_ref[:, cols] = part[6:7, : plan.chan]
        shared = shared + part[1:6, plan.chan : plan.mixed]
        for j in range(3):
            one = part[7:8, j * LANES : (j + 1) * LANES]
            moved = one if g == 0 else pltpu.roll(one, g * plan.heads, 1)
            heads[j] = jnp.where(lane // plan.heads == g, moved, heads[j])
    gain_in_ref[...] = gain_in
    convw_ref[:, INNER:] = shared[:4]
    convb_ref[:, INNER:] = shared[4:]
    dtb_ref[...] = heads[0][:, :HEADS]
    alog_ref[...] = heads[1][:, :HEADS]
    skip_ref[...] = heads[2][:, :HEADS]


def result_kernel(plan, tok_ref, scale_ref, *refs):
    parts, out_ref = refs[: plan.seq], refs[plan.seq]
    s = lax.axis_index("seq")
    total = parts[0][...].astype(f32)
    for part in parts[1:]:
        total = total + part[...].astype(f32)
    r = scale_ref[pl.ds(aligned(s * plan.rows, plan.rows), plan.rows), :]
    r = jnp.concatenate([r] * (WIDTH // LANES), axis=1)
    out_ref[...] = (tok_ref[...].astype(f32) + total * r).astype(bf16)


def token_kernel(plan, tok_ref, cot_ref, gain_ref, *refs):
    parts, out_ref = refs[: plan.seq], refs[plan.seq]
    total = parts[0][...].astype(f32)
    for part in parts[1:]:
        total = total + part[...].astype(f32)
    tok = tok_ref[...].astype(f32)
    q = lax.rsqrt(jnp.mean(tok * tok, axis=1, keepdims=True) + norm_eps)
    w = total * gain_ref[...]
    mean = jnp.mean(w * tok, axis=1, keepdims=True)
    grad = cot_ref[...].astype(f32) + q * w - tok * (q * q * q * mean)
    out_ref[...] = grad.astype(bf16)


def call(body, plan, outs, scratch, *args, flops=0, name=None):
    shapes = [jax.ShapeDtypeStruct(shape, kind) for shape, kind in outs]
    size = sum(a.size * a.dtype.itemsize for a in args)
    size += sum(a.size * a.dtype.itemsize for a in shapes)
    return pl.pallas_call(
        functools.partial(body, plan),
        out_shape=shapes,
        in_specs=[pl.BlockSpec(memory_space=pltpu.VMEM)] * len(args),
        out_specs=[pl.BlockSpec(memory_space=pltpu.VMEM)] * len(shapes),
        scratch_shapes=[pltpu.VMEM(shape, kind) for shape, kind in scratch],
        compiler_params=pltpu.CompilerParams(vmem_limit_bytes=VMEM_LIMIT),
        cost_estimate=pl.CostEstimate(flops=flops, bytes_accessed=size, transcendentals=0),
        name=name,
    )(*args)


VMEM_LIMIT = 48 * 1024 * 1024


def swap(value, axis, by):
    size = lax.axis_size(axis)
    return lax.ppermute(value, axis, [(i, i ^ by) for i in range(size)])


def after(value, *others):
    return lax.optimization_barrier((value, *others))[0]


def head_parallel(
    tokens, cotangent, segments, in_weight, out_weight, gain_in, conv_weight, conv_bias,
    dt_bias, a_log, d_skip, gain_out,
):
    rows = tokens.shape[1]
    plan = Plan(
        lax.axis_size("seq"), lax.axis_size("batch"), rows, in_weight.shape[0], out_weight.shape[0]
    )
    n, line, chan, heads = plan.seq, plan.line, plan.chan, plan.heads
    s = lax.axis_index("seq")
    tok, cot = tokens[0], cotangent[0]

    seg_row = jnp.pad(segments.astype(bf16), ((0, 7), (0, plan.cols + chan - rows)))
    blocks = []
    for g in range(n):
        main = [
            in_weight[:, INNER + g * chan : INNER + (g + 1) * chan],
            in_weight[:, 2 * INNER : INNER + CONV],
            jnp.pad(
                in_weight[:, INNER + CONV + g * heads : INNER + CONV + (g + 1) * heads],
                ((0, 0), (0, LANES - heads)),
            ),
            in_weight[:, g * chan : (g + 1) * chan],
        ]
        blocks.append(jnp.concatenate([jnp.concatenate(main, axis=1), seg_row], axis=0))
    blocks = jnp.stack(blocks)
    own = [lax.dynamic_index_in_dim(blocks, s ^ m, 0, False) for m in range(n)]
    pieces = [own[0]] + [swap(own[m], "seq", m) for m in range(1, n)]
    toks = [tok] + [swap(tok, "seq", m) for m in range(1, n)]

    r = plan.in_rows
    main_shard = jnp.concatenate([p[:r, : plan.cols] for p in pieces], axis=0)
    gate_cols = [p[:r, plan.cols :] for p in pieces]
    gate_shard = jnp.concatenate(
        [jnp.concatenate(gate_cols[i : i + 2], axis=1) for i in range(0, n, 2)] + [out_weight],
        axis=0,
    )

    def spread(shard):
        mine = [shard] + [swap(shard, "batch", 2 * m) for m in range(1, line)]
        return mine + [swap(one, "batch", 1) for one in mine]

    main_parts = spread(main_shard)
    later = after(gate_shard, *main_parts[:line])
    gate_parts = spread(later)
    cot_later = after(cot, *toks)
    cots = [cot] + [swap(cot_later, "seq", m) for m in range(1, n)]

    def own_cols(value):
        group = lax.dynamic_slice_in_dim(value, s * chan, chan, value.ndim - 1)
        return jnp.concatenate([group, value[..., INNER:]], axis=-1)

    convw = own_cols(conv_weight)
    convb = own_cols(conv_bias)[None]
    own_gain = lax.dynamic_slice_in_dim(gain_out, s * chan, chan, 0)[None]

    def own_heads(value):
        return lax.dynamic_slice_in_dim(value, s * heads, heads, 0)

    def padded(value):
        return jnp.pad(value, (0, chan - value.shape[0]))[None]

    per_head = jnp.concatenate(
        [
            padded(own_heads(dt_bias)),
            padded(own_heads(a_log)),
            jnp.repeat(own_heads(d_skip), HEADDIM)[None],
            jnp.zeros((5, chan), f32),
        ],
        axis=0,
    )
    gain_row = gain_in[None]
    total = plan.total
    seg_rows = -(-plan.blocks // 8) * 8
    normed, w_main, x, dt_raw, y, states, segc, segr = call(
        forward_kernel, plan,
        [
            ((total, WIDTH), bf16), ((WIDTH, plan.cols), bf16),
            ((total + LEAD, plan.mixed), f32), ((total, LANES), f32), ((total, chan), f32),
            ((plan.blocks, STATE, chan), f32), ((total + 2 * LEAD, LANES), f32),
            ((seg_rows, GROUP), f32),
        ],
        [((WIDTH, plan.cols), f32), ((STATE, chan), f32)],
        *toks, *pieces, *main_parts, gain_row, convw, convb, per_head,
        flops=2 * total * WIDTH * plan.cols, name="ssd_forward",
    )
    piece_shape = (rows, WIDTH)
    w_gate, z, du, stats, *outs = call(
        gate_kernel, plan,
        [
            ((WIDTH, chan), bf16), ((total, chan), f32), ((total, chan), f32),
            ((2 * plan.blocks, GROUP), f32),
        ] + [(piece_shape, bf16)] * n,
        [((WIDTH, chan), f32), ((chan, WIDTH), bf16)],
        normed, y, *gate_parts, *cots, own_gain,
        flops=6 * total * WIDTH * chan, name="gate_forward",
    )
    all_stats = [stats] + [swap(stats, "seq", m) for m in range(1, n)]
    dy, dz, scale, gain_out_grad, keep, send = call(
        regate_kernel, plan,
        [
            ((total, chan), f32), ((total, chan), bf16), ((total, LANES), f32), ((1, chan), f32),
            ((line, n * r // 2 + plan.out_rows, WIDTH), bf16),
            ((line, n * r // 2 + plan.out_rows, WIDTH), bf16),
        ],
        [((total, chan), bf16), ((WIDTH, chan), f32), ((chan, WIDTH), f32)],
        *all_stats, normed, y, z, du, *cots, own_gain,
        flops=4 * total * WIDTH * chan, name="gate_backward",
    )

    def reduce_line(keep, send, width):
        got = swap(send, "batch", 1)
        rows_here = keep.shape[1]
        parts = call(
            lambda count, *refs: add_split_kernel(count, *refs), line,
            [((rows_here, width), bf16)] * line, [], keep, got, name="core_sum",
        )
        return [parts[0]] + [swap(parts[m], "batch", 2 * m) for m in range(1, line)]

    out_late = [after(o, dy) for o in outs[1:]]
    out_parts = [outs[0]] + [swap(out_late[m - 1], "seq", m) for m in range(1, n)]
    gate_lines = reduce_line(keep, send, WIDTH)
    *gate_grads, shard_out = call(
        gate_sum_kernel, plan,
        [((r, chan), bf16)] * n + [((plan.out_rows, WIDTH), f32)], [], *gate_lines,
        name="gate_sum",
    )
    gate_grads = [gate_grads[0]] + [swap(gate_grads[m], "seq", m) for m in range(1, n)]
    (result,) = call(
        result_kernel, plan, [(piece_shape, bf16)], [], tok, scale, *out_parts, name="result"
    )

    *grads, keep, send, small = call(
        backward_kernel, plan,
        [(piece_shape, bf16)] * n
        + [((line, n * r, plan.cols), bf16)] * 2
        + [((8, max(WIDTH, plan.mixed)), f32)],
        [
            ((total, plan.cols), bf16), ((WIDTH, plan.cols), f32), ((total, WIDTH), f32),
            ((STATE, chan), f32), ((LEAD, plan.mixed), f32), ((8, plan.mixed), f32),
            ((8, LANES), f32),
        ],
        *toks, normed, w_main, w_gate, x, dt_raw, states, segc, segr, dy, dz, gain_out_grad,
        convw, convb, per_head,
        flops=2 * total * WIDTH * (2 * plan.cols + chan), name="ssd_backward",
    )
    main_lines = reduce_line(keep, send, plan.cols)
    grad_parts = [grads[0]] + [swap(grads[m], "seq", m) for m in range(1, n)]
    small = small + swap(small, "batch", 1)
    small = sum([swap(small, "batch", 2 * m) for m in range(1, line)], small)
    small_parts = [small] + [swap(small, "seq", m) for m in range(1, n)]
    main_grads = call(
        row_sum_kernel, plan, [((r, plan.cols), bf16)] * n, [], *main_lines, name="main_sum"
    )
    main_grads = [main_grads[0]] + [swap(main_grads[m], "seq", m) for m in range(1, n)]
    (grad_tokens,) = call(
        token_kernel, plan, [(piece_shape, bf16)], [], tok, cot, gain_row, *grad_parts,
        name="token_grad",
    )
    (shard_in,) = call(
        columns_kernel, plan, [((r, in_weight.shape[1]), f32)],
        [((n, r, chan), f32), ((n, r, plan.cols), f32)], *gate_grads, *main_grads, name="columns",
    )
    smalls = call(
        small_kernel, plan,
        [
            ((1, WIDTH), f32), ((KERNEL, CONV), f32), ((1, CONV), f32), ((1, HEADS), f32),
            ((1, HEADS), f32), ((1, HEADS), f32), ((1, INNER), f32),
        ],
        [((n,) + small.shape, f32)], *small_parts, name="small_grads",
    )
    return (
        result[None], grad_tokens[None], shard_in, shard_out, smalls[0][0], smalls[1],
        smalls[2][0], smalls[3][0], smalls[4][0], smalls[5][0], smalls[6][0],
    )


def shifted(value, axis, by):
    size = lax.axis_size(axis)
    pairs = [(i, i + by) for i in range(size) if 0 <= i + by < size]
    return lax.ppermute(value, axis, pairs)


def prefix(value, axis, join, neutral):
    place = lax.axis_index(axis)
    gathered = jax.tree.map(
        lambda a, kind: lax.all_gather(a.astype(kind), axis), value, (jnp.bfloat16, jnp.bfloat16)
    )
    state = jax.tree.map(lambda a, e: jnp.zeros_like(a) + jnp.asarray(e, a.dtype), value, neutral)

    def one(turn, state):
        return join(
            state,
            jax.tree.map(
                lambda a, own: lax.dynamic_index_in_dim(a, turn, 0, False).astype(own.dtype),
                gathered,
                value,
            ),
        )

    return lax.fori_loop(0, place, one, state)


def prefix_2(value, axis, join, neutral):
    count = lax.axis_size(axis)
    place = lax.axis_index(axis)
    ahead = count - 1 - place
    gathered = jax.tree.map(
        lambda a, kind: lax.all_gather(a.astype(kind), axis),
        value,
        jax.tree.map(lambda a: jnp.bfloat16 if a.dtype == jnp.float32 else a.dtype, value),
    )
    state = jax.tree.map(lambda a, e: jnp.zeros_like(a) + jnp.asarray(e, a.dtype), value, neutral)

    def one(turn, state):
        source = count - 1 - turn
        return join(
            state,
            jax.tree.map(
                lambda a, own: lax.dynamic_index_in_dim(a, source, 0, False).astype(own.dtype),
                gathered,
                value,
            ),
        )

    return lax.fori_loop(0, ahead, one, state)


def rms_scale(values, gain):
    mean_square = jnp.mean(values * values, axis=-1, keepdims=True)
    return values * lax.rsqrt(mean_square + norm_eps) * gain


def causal_conv(extended, ext_segs, conv_weight, conv_bias, row_count):
    target = ext_segs[KERNEL - 1 :]
    total = jnp.zeros((row_count, conv_weight.shape[1]), jnp.float32) + conv_bias[None, :]
    for offset in range(KERNEL):
        window = extended[offset : offset + row_count]
        same_doc = (ext_segs[offset : offset + row_count] == target).astype(jnp.float32)
        total = total + conv_weight[offset][None, :] * window * same_doc[:, None]
    return jax.nn.silu(total)


def prepare(xbc, dt_raw, edge_rows, ext_segs, conv_weight, conv_bias, dt_bias, a_log):
    row_count = xbc.shape[0]
    extended = jnp.concatenate([edge_rows, xbc], axis=0)
    mixed = causal_conv(extended, ext_segs, conv_weight, conv_bias, row_count)
    values = mixed[:, :INNER].reshape(row_count, HEADS, HEADDIM)
    key_vecs = mixed[:, INNER : INNER + STATE]
    queries = mixed[:, INNER + STATE :]
    step_sizes = jax.nn.softplus(dt_raw + dt_bias[None, :])
    log_decay = -step_sizes * jnp.exp(a_log)[None, :]
    return (values, key_vecs, queries, step_sizes, log_decay)


def group_block(carried, block_in):
    state_in, last_seg = carried
    values, key_vecs, queries, step_sizes, log_decay, seg_ids = block_in
    length_here = seg_ids.shape[0]
    cumulative = jnp.cumsum(log_decay, axis=0)
    positions = jnp.arange(length_here)
    allowed = (seg_ids[:, None] == seg_ids[None, :]) & (positions[:, None] >= positions[None, :])
    gap_logs = cumulative[:, None, :] - cumulative[None, :, :]
    decay_mask = jnp.where(allowed[:, :, None], jnp.exp(jnp.minimum(gap_logs, 0.0)), 0.0)
    scores = jnp.dot(queries, key_vecs.T, precision=highest)
    weights = decay_mask * scores[:, :, None] * step_sizes[None, :, :]
    inside = jnp.einsum("tsh,shp->thp", weights, values, precision=highest)
    keep_factor = jnp.where((seg_ids == last_seg)[:, None], jnp.exp(cumulative), 0.0)
    carried_out = (
        jnp.einsum("tn,hpn->thp", queries, state_in, precision=highest) * keep_factor[:, :, None]
    )
    to_end = (
        jnp.where(
            (seg_ids == seg_ids[-1])[:, None], jnp.exp(cumulative[-1][None, :] - cumulative), 0.0
        )
        * step_sizes
    )
    fresh_state = jnp.einsum("sh,shp,sn->hpn", to_end, values, key_vecs, precision=highest)
    new_state = state_in * keep_factor[-1][:, None, None] + fresh_state
    return ((new_state, seg_ids[-1]), inside + carried_out)


def grouped_ssd(
    values, key_vecs, queries, step_sizes, log_decay, seg_ids, d_skip, state_in, last_seg
):
    row_count = seg_ids.shape[0]
    block_count = row_count // GROUP

    def blocked(member):
        return member.reshape((block_count, GROUP) + member.shape[1:])

    inputs = (
        blocked(values),
        blocked(key_vecs),
        blocked(queries),
        blocked(step_sizes),
        blocked(log_decay),
        blocked(seg_ids),
    )
    (final_state, last_out), outputs = lax.scan(
        jax.checkpoint(group_block), (state_in, last_seg), inputs
    )
    outputs = outputs.reshape(row_count, HEADS, HEADDIM) + d_skip[None, :, None] * values
    return (outputs, final_state)


def gated_norm(mixed_out, gate_z, gain_out):
    return rms_scale(mixed_out * jax.nn.silu(gate_z), gain_out)


def chain_combine(earlier, later):
    decay_early, state_early = earlier
    decay_late, state_late = later
    return (decay_early * decay_late, decay_late[:, None, None] * state_early + state_late)


def cross_term(queries, log_decay, state_in, seg_ids, prev_seg):
    cumulative = jnp.cumsum(log_decay, axis=0)
    keep_factor = jnp.where((seg_ids == prev_seg)[:, None], jnp.exp(cumulative), 0.0)
    return jnp.einsum("tn,hpn->thp", queries, state_in, precision=highest) * keep_factor[:, :, None]


def device_decay(log_decay, seg_ids, prev_seg):
    total_log = jnp.sum(log_decay, axis=0)
    return jnp.where(seg_ids[-1] == prev_seg, jnp.exp(total_log), 0.0)


def on_device(
    tokens,
    cotangent,
    segments,
    in_weight,
    out_weight,
    gain_in,
    conv_weight,
    conv_bias,
    dt_bias,
    a_log,
    d_skip,
    gain_out,
):
    tokens_f = tokens[0].astype(jnp.float32)
    cot_low = cotangent[0]
    seg_ids = segments[0]
    row_count = seg_ids.shape[0]
    full_in, full_out = (
        lax.all_gather(in_weight, ("seq", "batch"), axis=0, tiled=True),
        lax.all_gather(out_weight, ("seq", "batch"), axis=0, tiled=True),
    )
    normed, norm_pull = jax.vjp(rms_scale, tokens_f, gain_in)
    normed_low = normed.astype(jnp.bfloat16)
    projected = jnp.dot(normed_low, full_in, preferred_element_type=jnp.float32)
    gate_z = projected[:, :INNER]
    xbc = projected[:, INNER : INNER + CONV]
    dt_raw = projected[:, INNER + CONV :]
    tail_start = row_count - KERNEL + 1
    edge_rows, edge_segs = shifted(
        (xbc[tail_start:], seg_ids[tail_start:].astype(jnp.float32)), "seq", 1
    )
    prev_segs = edge_segs.astype(jnp.int32)
    prev_seg = prev_segs[KERNEL - 2]
    ext_segs = jnp.concatenate([prev_segs, seg_ids])

    def prepare_local(xbc_in, dt_in, edge_in, weight_in, bias_in, shift_in, alog_in):
        return prepare(xbc_in, dt_in, edge_in, ext_segs, weight_in, bias_in, shift_in, alog_in)

    prepared, prepare_pull = jax.vjp(
        prepare_local, xbc, dt_raw, edge_rows, conv_weight, conv_bias, dt_bias, a_log
    )
    values, key_vecs, queries, step_sizes, log_decay = prepared
    zeros_state = jnp.zeros((HEADS, HEADDIM, STATE), jnp.float32)

    def local_ssd(values_in, keys_in, queries_in, sizes_in, logs_in, skip_in):
        return grouped_ssd(
            values_in,
            keys_in,
            queries_in,
            sizes_in,
            logs_in,
            seg_ids,
            skip_in,
            zeros_state,
            seg_ids[0],
        )

    (local_out, local_state), ssd_pull = jax.vjp(
        local_ssd, values, key_vecs, queries, step_sizes, log_decay, d_skip
    )

    def decay_local(logs_in):
        return device_decay(logs_in, seg_ids, prev_seg)

    decay_here, decay_pull = jax.vjp(decay_local, log_decay)
    identity = (jnp.ones((HEADS,), jnp.float32), zeros_state)
    decay_prefix, state_in = prefix((decay_here, local_state), "seq", chain_combine, identity)

    def cross_local(queries_in, logs_in, state_arg):
        return cross_term(queries_in, logs_in, state_arg, seg_ids, prev_seg)

    cross_out, cross_pull = jax.vjp(cross_local, queries, log_decay, state_in)
    mixed_out = (local_out + cross_out).reshape(row_count, INNER)
    gated, gated_pull = jax.vjp(gated_norm, mixed_out, gate_z, gain_out)
    gated_low = gated.astype(jnp.bfloat16)
    result = tokens_f + jnp.dot(gated_low, full_out, preferred_element_type=jnp.float32)
    back_in, back_out = (
        lax.all_gather(in_weight, ("seq", "batch"), axis=0, tiled=True),
        lax.all_gather(out_weight, ("seq", "batch"), axis=0, tiled=True),
    )
    contract_last = (((1,), (1,)), ((), ()))
    contract_first = (((0,), (0,)), ((), ()))
    grad_gated = lax.dot_general(
        cot_low, back_out, contract_last, preferred_element_type=jnp.float32
    )
    grad_mixed, grad_gate, grad_gain_out = gated_pull(grad_gated)
    grad_mixed = grad_mixed.reshape(row_count, HEADS, HEADDIM)
    grad_q_cross, grad_log_cross, grad_state_in = cross_pull(grad_mixed)
    decay_after, grad_exit = prefix_2((decay_here, grad_state_in), "seq", chain_combine, identity)
    grad_decay = jnp.sum(grad_exit * state_in, axis=(1, 2))
    grad_log_dev = decay_pull(grad_decay)[0]
    grad_values, grad_keys, grad_q_local, grad_sizes, grad_log_local, grad_skip = ssd_pull(
        (grad_mixed, grad_exit)
    )
    prep_grads = prepare_pull(
        (
            grad_values,
            grad_keys,
            grad_q_local + grad_q_cross,
            grad_sizes,
            grad_log_local + grad_log_cross + grad_log_dev,
        )
    )
    grad_xbc, grad_dt, grad_edge, grad_conv_w, grad_conv_b, grad_dt_bias, grad_a_log = prep_grads
    grad_next = shifted(grad_edge, "seq", -1)
    grad_xbc = grad_xbc.at[tail_start:].add(grad_next)
    grad_proj = jnp.concatenate([grad_gate, grad_xbc, grad_dt], axis=1).astype(jnp.bfloat16)
    grad_normed = lax.dot_general(
        grad_proj, back_in, contract_last, preferred_element_type=jnp.float32
    )
    grad_tokens_norm, grad_gain_in = norm_pull(grad_normed)
    grad_tokens = (cot_low.astype(jnp.float32) + grad_tokens_norm).astype(jnp.bfloat16)
    grad_in_w = lax.dot_general(
        normed_low, grad_proj, contract_first, preferred_element_type=jnp.float32
    )
    grad_out_w = lax.dot_general(
        gated_low, cot_low, contract_first, preferred_element_type=jnp.float32
    )
    shard_in, shard_out = (
        lax.psum_scatter(grad_in_w, ("seq", "batch"), scatter_dimension=0, tiled=True),
        lax.psum_scatter(grad_out_w, ("seq", "batch"), scatter_dimension=0, tiled=True),
    )
    summed = lax.psum(
        (
            grad_gain_in,
            grad_conv_w,
            grad_conv_b,
            grad_dt_bias,
            grad_a_log,
            grad_skip,
            grad_gain_out,
        ),
        ("seq", "batch"),
    )
    return (
        result.astype(jnp.bfloat16)[None],
        grad_tokens[None],
        shard_in,
        shard_out,
        summed[0],
        summed[1],
        summed[2],
        summed[3],
        summed[4],
        summed[5],
        summed[6],
    )


def solution(mesh):
    in_specs = (
        P("batch", "seq", None),
        P("batch", "seq", None),
        P("batch", "seq"),
        P(("seq", "batch"), None),
        P(("seq", "batch"), None),
        P(),
        P(),
        P(),
        P(),
        P(),
        P(),
        P(),
    )
    out_specs = (
        P("batch", "seq", None),
        P("batch", "seq", None),
        P(("seq", "batch"), None),
        P(("seq", "batch"), None),
        P(),
        P(),
        P(),
        P(),
        P(),
        P(),
        P(),
    )
    count = mesh.shape["seq"]
    even = HEADS % (2 * count) == 0 and count & (count - 1) == 0
    return jax.shard_map(
        head_parallel if even else on_device, mesh=mesh, in_specs=in_specs, out_specs=out_specs, check_vma=False
    )
```

```python
import functools

import jax
import jax.numpy as jnp
from jax import lax
from jax.experimental import pallas as pl
from jax.experimental.pallas import tpu as pltpu
from jax.sharding import PartitionSpec as P

HEADS = 24
HEADDIM = 64
STATE = 128
KERNEL = 4
GROUP = 128
INNER = 1536
CONV = 1792
WIDTH = 768
LANES = 128
LEAD = 8


highest = lax.Precision.HIGHEST
norm_eps = 1e-05
f32 = jnp.float32
bf16 = jnp.bfloat16
contract_last = (((1,), (1,)), ((), ()))
contract_first = (((0,), (0,)), ((), ()))


def mm(a, b):
    return jnp.dot(a.astype(bf16), b.astype(bf16), preferred_element_type=f32)


def mm_nt(a, b):
    return lax.dot_general(
        a.astype(bf16), b.astype(bf16), contract_last, preferred_element_type=f32
    )


def mm_tn(a, b):
    return lax.dot_general(
        a.astype(bf16), b.astype(bf16), contract_first, preferred_element_type=f32
    )


def mm_exact(a, b):
    return jnp.dot(a, b, precision=highest, preferred_element_type=f32)


def iota(shape, dim):
    return lax.broadcasted_iota(jnp.int32, shape, dim)


def aligned(value, unit):
    return pl.multiple_of(value, unit)


def wide(columns, count):
    rows = columns.shape[0]
    low = iota((rows, LANES), 1) < HEADDIM
    parts = []
    for pair in range(count // 2):
        left = jnp.broadcast_to(columns[:, 2 * pair : 2 * pair + 1], (rows, LANES))
        right = jnp.broadcast_to(columns[:, 2 * pair + 1 : 2 * pair + 2], (rows, LANES))
        parts.append(jnp.where(low, left, right))
    return jnp.concatenate(parts, axis=1)


def softplus(value):
    return jnp.maximum(value, 0.0) + jnp.log1p(jnp.exp(-jnp.abs(value)))


def sigmoid(value):
    return 1.0 / (1.0 + jnp.exp(-value))


class Plan:
    def __init__(self, mesh_seq, mesh_batch, rows, in_rows, out_rows):
        self.seq = mesh_seq
        self.batch = mesh_batch
        self.line = mesh_batch // 2
        self.rows = rows
        self.total = rows * mesh_seq
        self.blocks = self.total // GROUP
        self.heads = HEADS // mesh_seq
        self.chan = self.heads * HEADDIM
        self.mixed = self.chan + 2 * STATE
        self.cols = self.mixed + LANES
        self.in_rows = in_rows
        self.out_rows = out_rows


def place():
    s = lax.axis_index("seq")
    b = lax.axis_index("batch")
    return s, lax.shift_right_logical(b, 1), lax.bitwise_and(b, 1)


def in_place(plan, ids, line_xor, core_xor, seq_xor):
    s, z, c = ids
    owner = (s ^ seq_xor) * plan.batch + (z ^ line_xor) * 2 + (c ^ core_xor)
    return aligned(owner * plan.in_rows, 8)


def block_values(plan, b, x_ref, segc_ref, segr_ref, dt_ref, convw, convb, heads_ref):
    base = aligned(b * GROUP, GROUP)
    win = x_ref[pl.ds(base, GROUP + LEAD), :]
    segw = segc_ref[pl.ds(base, GROUP + LEAD), :]
    seg = segw[LEAD:]
    prev = segw[LEAD - 1 : LEAD]
    repeat = plan.mixed // LANES
    pre = jnp.broadcast_to(convb, (GROUP, plan.mixed))
    shifts = []
    for k in range(KERNEL):
        start = LEAD - KERNEL + 1 + k
        part = win[start : start + GROUP]
        if k < KERNEL - 1:
            same = (segw[start : start + GROUP] == seg).astype(f32)
            part = part * jnp.concatenate([same] * repeat, axis=1)
        shifts.append(part)
        pre = pre + convw[k : k + 1] * part
    sig = sigmoid(pre)
    mixed = pre * sig
    values = mixed[:, : plan.chan]
    keys = mixed[:, plan.chan : plan.chan + STATE]
    queries = mixed[:, plan.chan + STATE :]
    dt_in = dt_ref[pl.ds(base, GROUP), :] + heads_ref[0:1, :LANES]
    steps = softplus(dt_in)
    decay = -steps * jnp.exp(heads_ref[1:2, :LANES])
    row = iota((GROUP, GROUP), 0)
    col = iota((GROUP, GROUP), 1)
    tri = (row >= col).astype(f32)
    cum = mm_exact(tri, decay)
    cum_t = cum.T
    steps_t = steps.T
    segr = segr_ref[pl.ds(b, 1), :]
    allowed = (seg == segr) & (row >= col)
    scores = mm_nt(queries, keys)
    keep = jnp.where(seg == prev, jnp.exp(cum), 0.0)
    last = cum[GROUP - 1 :]
    to_last = jnp.where(seg == seg[GROUP - 1 :], jnp.exp(last - cum), 0.0)
    return dict(
        base=base, seg=seg, shifts=shifts, pre=pre, sig=sig, values=values, keys=keys,
        queries=queries, dt_in=dt_in, steps=steps, decay=decay, tri=tri, cum=cum, cum_t=cum_t,
        steps_t=steps_t, allowed=allowed, scores=scores, keep=keep, to_last=to_last,
    )


def head_decay(v, h):
    gap = v["cum"][:, h : h + 1] - v["cum_t"][h : h + 1, :]
    return jnp.where(v["allowed"], jnp.exp(jnp.minimum(gap, 0.0)), 0.0)


def split_pair(pair):
    low = iota(pair.shape, 1) < HEADDIM
    return jnp.concatenate([jnp.where(low, pair, 0.0), jnp.where(low, 0.0, pair)], axis=0)


def fetch(pairs, sems):
    copies = [
        pltpu.make_async_copy(src, dst, sems.at[i]) for i, (src, dst) in enumerate(pairs)
    ]
    for copy in copies:
        copy.start()
    for copy in copies:
        copy.wait()


def pack_kernel(plan, w_any, seg_any, *outs):
    n, heads, chan = plan.seq, plan.heads, plan.chan
    blocks, outs = outs[:n], outs[n:]
    w_ref, seg_ref, sems, all_ref = outs
    fetch([(w_any, w_ref), (seg_any, seg_ref)], sems)
    s = lax.axis_index("seq")
    lane = iota((plan.in_rows, LANES), 1)
    tail = w_ref[:, INNER + CONV :].astype(f32)
    tail = jnp.concatenate(
        [tail, jnp.zeros((plan.in_rows, LANES - HEADS), f32)], axis=1
    )
    for g in range(n):
        moved = tail if g == 0 else pltpu.roll(tail, LANES - g * heads, 1)
        all_ref[g] = jnp.concatenate(
            [
                w_ref[:, INNER + g * chan : INNER + (g + 1) * chan],
                w_ref[:, 2 * INNER : INNER + CONV],
                jnp.where(lane < heads, moved, 0.0).astype(bf16),
                w_ref[:, g * chan : (g + 1) * chan],
            ],
            axis=1,
        )
    seg = jnp.broadcast_to(seg_ref[...].astype(f32), (8, plan.rows)).astype(bf16)
    for m in range(n):
        blocks[m][0 : plan.in_rows, :] = all_ref[s ^ m]
        blocks[m][plan.in_rows : plan.in_rows + 8, :] = jnp.zeros((8, plan.cols + chan), bf16)
        blocks[m][plan.in_rows : plan.in_rows + 8, : plan.rows] = seg


def own_params_kernel(
    plan, convw_ref, convb_ref, dtb_ref, alog_ref, skip_ref, gain_ref, conv_ref, heads_ref,
    own_gain_ref,
):
    n, heads, chan = plan.seq, plan.heads, plan.chan
    s = lax.axis_index("seq")
    own = pl.ds(aligned(s * chan, LANES), chan)
    conv_ref[...] = jnp.zeros_like(conv_ref)
    conv_ref[0:KERNEL, :chan] = convw_ref[:, own]
    conv_ref[0:KERNEL, chan:] = convw_ref[:, INNER:]
    conv_ref[KERNEL : KERNEL + 1, :chan] = convb_ref[:, own]
    conv_ref[KERNEL : KERNEL + 1, chan:] = convb_ref[:, INNER:]
    own_gain_ref[...] = gain_ref[:, own]
    one_lane = iota((1, LANES), 1)

    def own_heads(ref):
        row = jnp.concatenate([ref[...], jnp.zeros((1, LANES - HEADS), f32)], axis=1)
        found = row
        for g in range(1, n):
            found = jnp.where(s == g, pltpu.roll(row, LANES - g * heads, 1), found)
        return jnp.where(one_lane < heads, found, 0.0)

    heads_ref[...] = jnp.zeros_like(heads_ref)
    heads_ref[0:1, :LANES] = own_heads(dtb_ref)
    heads_ref[1:2, :LANES] = own_heads(alog_ref)
    heads_ref[2:3, :] = wide(own_heads(skip_ref), heads)


def regroup_kernel(plan, *refs):
    n, r = plan.seq, plan.in_rows
    pieces, out_w_ref = refs[:n], refs[n]
    main_ref, gate_ref = refs[n + 1 :]
    half = r * n // 2
    for m in range(n):
        main_ref[m * r : (m + 1) * r, :] = pieces[m][0:r, : plan.cols]
        top, left = (m // 2) * r, (m % 2) * plan.chan
        gate_ref[top : top + r, left : left + plan.chan] = pieces[m][0:r, plan.cols :]
    gate_ref[half : half + plan.out_rows, :] = out_w_ref[...]


def fill_segments(plan, s, pieces, segc_ref, segr_ref):
    per = plan.rows // GROUP
    segc_ref[...] = jnp.zeros_like(segc_ref)
    segr_ref[...] = jnp.zeros_like(segr_ref)
    for m in range(plan.seq):
        line = pieces[m][plan.in_rows : plan.in_rows + 1, : plan.rows].astype(f32)
        for j in range(per):
            b = (s ^ m) * per + j
            segr_ref[pl.ds(b, 1), :] = line[:, j * GROUP : (j + 1) * GROUP]
    every = segr_ref[...]
    turned = jnp.concatenate(
        [every, jnp.zeros((LANES - every.shape[0], GROUP), f32)], axis=0
    ).T
    for b in range(plan.blocks):
        segc_ref[LEAD + b * GROUP : LEAD + (b + 1) * GROUP, :] = jnp.broadcast_to(
            turned[:, b : b + 1], (GROUP, LANES)
        )


def project_kernel(plan, *refs):
    n = plan.seq
    toks, refs = refs[:n], refs[n:]
    pieces, refs = refs[:n], refs[n:]
    weights, refs = refs[: 2 * plan.line], refs[2 * plan.line :]
    gain_ref = refs[0]
    normed_ref, w_ref, x_ref, dt_ref, segc_ref, segr_ref, wf_ref = refs[1:]
    ids = place()
    s = ids[0]
    fill_segments(plan, s, pieces, segc_ref, segr_ref)
    for core_xor in range(2):
        for line_xor in range(plan.line):
            piece = weights[core_xor * plan.line + line_xor]
            for m in range(n):
                dest = pl.ds(in_place(plan, ids, line_xor, core_xor, m), plan.in_rows)
                wf_ref[dest, :] = piece[m * plan.in_rows : (m + 1) * plan.in_rows, :].astype(f32)
    w_ref[...] = wf_ref[...].astype(bf16)
    x_ref[0:LEAD, :] = jnp.zeros((LEAD, plan.mixed), f32)
    for m in range(n):
        tok = toks[m][...].astype(f32)
        scale = lax.rsqrt(jnp.mean(tok * tok, axis=1, keepdims=True) + norm_eps)
        low = (tok * scale * gain_ref[...]).astype(bf16)
        start = (s ^ m) * plan.rows
        normed_ref[pl.ds(aligned(start, plan.rows), plan.rows), :] = low
        out = jnp.dot(low, w_ref[...], preferred_element_type=f32)
        x_ref[pl.ds(aligned(start + LEAD, 8), plan.rows), :] = out[:, : plan.mixed]
        dt_ref[pl.ds(aligned(start, plan.rows), plan.rows), :] = out[:, plan.mixed :]


def scan_kernel(plan, first, last, *refs):
    x_ref, dt_ref, segc_ref, segr_ref, conv_ref, heads_ref = refs[:6]
    refs = refs[6:]
    if first:
        early_y_ref, early_states_ref, early_ref = refs[:3]
        refs = refs[3:]
    y_ref, states_ref, state_ref = refs
    if first:
        y_ref[: first * GROUP, :] = early_y_ref[...]
        states_ref[:first] = early_states_ref[...]
        state_ref[...] = early_ref[...]
    else:
        state_ref[...] = jnp.zeros_like(state_ref)
    convw = conv_ref[0:KERNEL, :]
    convb = conv_ref[KERNEL : KERNEL + 1, :]

    def step(b, carry):
        v = block_values(plan, b, x_ref, segc_ref, segr_ref, dt_ref, convw, convb, heads_ref)
        state = state_ref[...]
        states_ref[b] = state
        parts = []
        for pair in range(plan.heads // 2):
            lanes = slice(pair * LANES, (pair + 1) * LANES)
            weights_pair = []
            for h in (2 * pair, 2 * pair + 1):
                decay = head_decay(v, h)
                weights_pair.append(decay * v["scores"] * v["steps_t"][h : h + 1, :])
            parts.append(
                mm(jnp.concatenate(weights_pair, axis=1), split_pair(v["values"][:, lanes]))
            )
        inside = jnp.concatenate(parts, axis=1)
        keep = wide(v["keep"], plan.heads)
        carried = mm(v["queries"], state) * keep
        y_ref[pl.ds(v["base"], GROUP), :] = inside + carried + heads_ref[2:3, :] * v["values"]
        to_end = wide(v["to_last"] * v["steps"], plan.heads)
        state_ref[...] = state * keep[GROUP - 1 :] + mm_tn(v["keys"], v["values"] * to_end)
        return carry

    lax.fori_loop(first, last, step, 0)


def gate_kernel(plan, *refs):
    n = plan.seq
    normed_ref, y_ref = refs[:2]
    weights = refs[2 : 2 + 2 * plan.line]
    cots = refs[2 + 2 * plan.line : 2 + 2 * plan.line + n]
    gain_ref = refs[2 + 2 * plan.line + n]
    outs = refs[3 + 2 * plan.line + n :]
    wz_ref, z_ref, du_ref, stats_ref = outs[:4]
    parts = outs[4 : 4 + n]
    wf_ref, wo_ref = outs[4 + n :]
    ids = place()
    s, z, c = ids
    half = plan.in_rows * n // 2
    for core_xor in range(2):
        for line_xor in range(plan.line):
            piece = weights[core_xor * plan.line + line_xor]
            for m in range(n):
                dest = pl.ds(in_place(plan, ids, line_xor, core_xor, m), plan.in_rows)
                top = (m // 2) * plan.in_rows
                left = (m % 2) * plan.chan
                wf_ref[dest, :] = piece[
                    top : top + plan.in_rows, left : left + plan.chan
                ].astype(f32)
            start = ((z ^ line_xor) * 2 + (c ^ core_xor)) * plan.out_rows
            wo_ref[pl.ds(aligned(start, 16), plan.out_rows), :] = piece[
                half : half + plan.out_rows, :
            ]
    wz_ref[...] = wf_ref[...].astype(bf16)
    gain = gain_ref[...]
    lane = iota((plan.rows, LANES), 1)
    square = jnp.zeros((GROUP, LANES), f32)
    lane = iota((GROUP, LANES), 1)
    per = plan.rows // GROUP
    for m in range(n):
        start = aligned((s ^ m) * plan.rows, plan.rows)
        gate = jnp.dot(
            normed_ref[pl.ds(start, plan.rows), :], wz_ref[...], preferred_element_type=f32
        )
        z_ref[pl.ds(start, plan.rows), :] = gate
        gated = y_ref[pl.ds(start, plan.rows), :] * gate * sigmoid(gate)
        scaled = gated * gain
        parts[m][...] = mm(scaled, wo_ref[...]).astype(parts[m].dtype)
        du = mm_nt(cots[m][...], wo_ref[...])
        du_ref[pl.ds(start, plan.rows), :] = du
        norm = jnp.sum(gated * gated, axis=1, keepdims=True)
        dots = jnp.sum(du * scaled, axis=1, keepdims=True)
        for j in range(per):
            b = (s ^ m) * per + j
            rows = slice(j * GROUP, (j + 1) * GROUP)
            square = square + jnp.where(lane == b, norm[rows], 0.0)
            square = square + jnp.where(lane == b + plan.blocks, dots[rows], 0.0)
    stats_ref[...] = square.T[: 2 * plan.blocks]


def emit_rows(plan, ids, source_ref, put):
    for core_xor in range(2):
        for line_xor in range(plan.line):
            for m in range(plan.seq):
                rows = source_ref[
                    pl.ds(in_place(plan, ids, line_xor, core_xor, m), plan.in_rows), :
                ]
                put(core_xor, line_xor, m, rows)


def row_products(w_ref, grad_ref):
    lane = iota((LANES, LANES), 1)
    square = jnp.zeros((LANES, LANES), f32)
    for i in range(w_ref.shape[0] // LANES):
        rows = slice(i * LANES, (i + 1) * LANES)
        product = w_ref[rows, :].astype(f32) * grad_ref[rows, :]
        square = square + jnp.where(lane == i, jnp.sum(product, axis=1, keepdims=True), 0.0)
    return square.T[:8]


def regate_kernel(plan, *refs):
    n = plan.seq
    stats = refs[:n]
    normed_ref, y_ref, z_ref, du_ref, wz_ref = refs[n : n + 5]
    cots = refs[n + 5 : 2 * n + 5]
    gain_ref = refs[2 * n + 5]
    dy_ref, dz_ref, scale_ref, gain_out_ref, share_ref, keep_ref, send_ref = refs[
        2 * n + 6 : 2 * n + 13
    ]
    gated_ref, gz_ref, go_ref = refs[2 * n + 13 :]
    ids = place()
    s, z, c = ids
    total = stats[0][...]
    for m in range(1, n):
        total = total + stats[m][...]
    turned = jnp.concatenate(
        [total, jnp.zeros((LANES - total.shape[0], GROUP), f32)], axis=0
    ).T
    gain = gain_ref[...]
    sums = jnp.zeros((1, plan.chan), f32)
    for b in range(plan.blocks):
        rows = slice(b * GROUP, (b + 1) * GROUP)
        r = lax.rsqrt(turned[:, b : b + 1] / INNER + norm_eps)
        dot = turned[:, plan.blocks + b : plan.blocks + b + 1] / INNER
        scale_ref[rows, :] = jnp.broadcast_to(r, (GROUP, LANES))
        gate = z_ref[rows, :]
        sig = sigmoid(gate)
        silu = gate * sig
        y = y_ref[rows, :]
        gated = y * silu
        du = du_ref[rows, :]
        normal = gated * r
        grad_pre = r * (du * gain) - normal * (r * r * dot)
        dy_ref[rows, :] = grad_pre * silu
        dz_ref[rows, :] = (grad_pre * y * sig * (1.0 + gate * (1.0 - sig))).astype(bf16)
        gated_ref[rows, :] = (normal * gain).astype(bf16)
        sums = sums + jnp.sum(du * normal, axis=0, keepdims=True)
    gain_out_ref[...] = sums
    gz_ref[...] = mm_tn(normed_ref[...], dz_ref[...])
    share_ref[...] = row_products(wz_ref, gz_ref)
    out = None
    for m in range(n):
        start = aligned((s ^ m) * plan.rows, plan.rows)
        one = mm_tn(gated_ref[pl.ds(start, plan.rows), :], cots[m][...])
        out = one if out is None else out + one
    go_ref[...] = out
    half = plan.in_rows * n // 2
    both = (keep_ref, send_ref)

    def put(core_xor, line_xor, m, rows):
        top = (m // 2) * plan.in_rows
        left = (m % 2) * plan.chan
        both[core_xor][line_xor, top : top + plan.in_rows, left : left + plan.chan] = rows.astype(
            bf16
        )

    emit_rows(plan, ids, gz_ref, put)
    for core_xor in range(2):
        for line_xor in range(plan.line):
            start = ((z ^ line_xor) * 2 + (c ^ core_xor)) * plan.out_rows
            both[core_xor][line_xor, half : half + plan.out_rows, :] = go_ref[
                pl.ds(aligned(start, 16), plan.out_rows), :
            ].astype(bf16)


def scan_back_kernel(plan, first, last, *refs):
    x_ref, dt_ref, states_ref, segc_ref, segr_ref, dy_ref, conv_ref, heads_ref = refs[:8]
    refs = refs[8:]
    later = last < plan.blocks
    if later:
        before, refs = refs[:5], refs[5:]
    gp_ref, adj_ref, edge_ref, acc_ref, head_ref = refs
    low = first * GROUP
    if later:
        gp_ref[(last - first) * GROUP :, :] = before[0][...]
        adj_ref[...] = before[1][...]
        edge_ref[...] = before[2][...]
        acc_ref[...] = before[3][...]
        head_ref[...] = before[4][...]
    else:
        adj_ref[...] = jnp.zeros_like(adj_ref)
        edge_ref[...] = jnp.zeros_like(edge_ref)
        acc_ref[...] = jnp.zeros_like(acc_ref)
        head_ref[...] = jnp.zeros_like(head_ref)
    convw = conv_ref[0:KERNEL, :]
    convb = conv_ref[KERNEL : KERNEL + 1, :]
    repeat = plan.mixed // LANES
    pick = (iota((plan.chan, LANES), 0) // HEADDIM == iota((plan.chan, LANES), 1)).astype(f32)
    lane = iota((GROUP, LANES), 1)

    def step(turn, carry):
        b = last - 1 - turn
        v = block_values(plan, b, x_ref, segc_ref, segr_ref, dt_ref, convw, convb, heads_ref)
        base = v["base"]
        state = states_ref[b]
        adj = adj_ref[...]
        dy = dy_ref[pl.ds(base, GROUP), :]
        values = v["values"]
        keep = wide(v["keep"], plan.heads)
        to_end = wide(v["to_last"] * v["steps"], plan.heads)
        kept = dy * keep
        dq = mm_nt(kept, state)
        cross = kept * mm(v["queries"], state)
        fed = mm(v["keys"], adj)
        dk = mm_nt(values * to_end, adj)
        adj_ref[...] = adj * keep[GROUP - 1 :] + mm_tn(v["queries"], kept)
        ended = jnp.sum(state * adj, axis=0, keepdims=True)
        pushed = fed * values
        skipped = jnp.sum(dy * values, axis=0, keepdims=True)
        few = jnp.concatenate([ended, skipped, jnp.zeros((6, plan.chan), f32)], axis=0)
        sums = mm_exact(jnp.concatenate([cross, pushed, few], axis=0), pick)
        cross_h = sums[:GROUP]
        pushed_h = sums[GROUP : 2 * GROUP]
        ended_h = sums[2 * GROUP : 2 * GROUP + 1]
        skipped_h = sums[2 * GROUP + 1 : 2 * GROUP + 2]
        grad_steps = pushed_h * v["to_last"]
        pulled = grad_steps * v["steps"]
        dcum = cross_h - pulled
        at_end = jnp.sum(pulled, axis=0, keepdims=True) + v["keep"][GROUP - 1 :] * ended_h
        dscores = jnp.zeros((GROUP, GROUP), f32)
        columns = []
        dvs = []
        for pair in range(plan.heads // 2):
            lanes = slice(pair * LANES, (pair + 1) * LANES)
            dy_pair = split_pair(dy[:, lanes])
            products = mm_nt(dy_pair, values[:, lanes])
            stacked = []
            for j, h in enumerate((2 * pair, 2 * pair + 1)):
                decay = head_decay(v, h)
                steps_row = v["steps_t"][h : h + 1, :]
                weighted = decay * products[j * GROUP : (j + 1) * GROUP]
                direct = weighted * v["scores"]
                dscores = dscores + weighted * steps_row
                rowsum = jnp.sum(direct * steps_row, axis=1, keepdims=True)
                dcum = dcum + jnp.where(lane == h, rowsum, 0.0)
                columns.append(jnp.sum(direct, axis=0, keepdims=True))
                stacked.append(decay * v["scores"] * steps_row)
            dvs.append(mm_tn(jnp.concatenate(stacked, axis=0), dy_pair))
        dv = jnp.concatenate(dvs, axis=1) + fed * to_end + heads_ref[2:3, :] * dy
        columns.append(jnp.zeros((LANES - plan.heads, GROUP), f32))
        down = jnp.concatenate(columns, axis=0).T
        grad_steps = grad_steps + down
        dcum = dcum - down * v["steps"]
        row = iota((GROUP, LANES), 0)
        dcum = dcum + jnp.where(row == GROUP - 1, at_end, 0.0)
        dk = dk + mm_tn(dscores, v["queries"])
        dq = dq + mm(dscores, v["keys"])
        ddecay = lax.dot_general(
            v["tri"], dcum, contract_first, precision=highest, preferred_element_type=f32
        )
        grad_steps = grad_steps - ddecay * jnp.exp(heads_ref[1:2, :LANES])
        grad_dt = grad_steps * sigmoid(v["dt_in"])
        head_ref[0:1, :] += jnp.sum(grad_dt, axis=0, keepdims=True)
        head_ref[1:2, :] += jnp.sum(ddecay * v["decay"], axis=0, keepdims=True)
        head_ref[2:3, :] += skipped_h
        dmixed = jnp.concatenate([dv, dk, dq], axis=1)
        pre, sig = v["pre"], v["sig"]
        dpre = dmixed * (sig * (1.0 + pre * (1.0 - sig)))
        acc_ref[4:5, :] += jnp.sum(dpre, axis=0, keepdims=True)
        longer = jnp.concatenate([dpre, edge_ref[...]], axis=0)
        edge_ref[...] = dpre[:LEAD]
        segn = segc_ref[pl.ds(aligned(base + LEAD, 8), GROUP + LEAD), :]
        dx = jnp.zeros((GROUP, plan.mixed), f32)
        for k in range(KERNEL):
            acc_ref[k : k + 1, :] += jnp.sum(dpre * v["shifts"][k], axis=0, keepdims=True)
            ahead = KERNEL - 1 - k
            part = longer[ahead : ahead + GROUP]
            if ahead:
                same = (segn[ahead : ahead + GROUP] == v["seg"]).astype(f32)
                part = part * jnp.concatenate([same] * repeat, axis=1)
            dx = dx + convw[k : k + 1] * part
        live = jnp.where(lane < plan.heads, grad_dt, 0.0)
        gp_ref[pl.ds(aligned(base - low, GROUP), GROUP), :] = jnp.concatenate([dx, live], axis=1).astype(bf16)
        return carry

    lax.fori_loop(0, last - first, step, 0)


def main_grads_kernel(
    plan, normed_ref, gp_ref, w_ref, gain_ref, share_ref, gain_out_ref, acc_ref, head_ref,
    keep_ref, send_ref, gw_ref, small_ref,
):
    ids = place()
    gw_ref[...] = mm_tn(normed_ref[...], gp_ref[...])
    both = (keep_ref, send_ref)

    def put(core_xor, line_xor, m, rows):
        top = m * plan.in_rows
        both[core_xor][line_xor, top : top + plan.in_rows, :] = rows.astype(bf16)

    emit_rows(plan, ids, gw_ref, put)
    share = share_ref[...] + row_products(w_ref, gw_ref)
    small_ref[...] = jnp.zeros_like(small_ref)
    for i in range(WIDTH // LANES):
        lanes = slice(i * LANES, (i + 1) * LANES)
        small_ref[0:1, lanes] = share[i : i + 1] / gain_ref[:, lanes]
    small_ref[1:6, : plan.mixed] = acc_ref[0:5, :]
    small_ref[6:7, : plan.chan] = gain_out_ref[...]
    for j in range(3):
        small_ref[7:8, j * LANES : (j + 1) * LANES] = head_ref[j : j + 1, :]
    high, low = two_parts(small_ref[...])
    last = plan.seq * plan.in_rows
    for ref in both:
        for line_xor in range(plan.line):
            ref[line_xor, last : last + 8, :] = high
            ref[line_xor, last + 8 : last + 16, :] = low


def normed_grads_kernel(plan, gp_ref, w_ref, dz_ref, wz_ref, *grads):
    s = lax.axis_index("seq")
    for m in range(plan.seq):
        rows = pl.ds(aligned((s ^ m) * plan.rows, plan.rows), plan.rows)
        part = mm_nt(gp_ref[rows, :], w_ref[...]) + mm_nt(dz_ref[rows, :], wz_ref[...])
        grads[m][...] = part.astype(grads[m].dtype)


def two_parts(value):
    high = value.astype(bf16)
    return high, (value - high.astype(f32)).astype(bf16)


def joined(ref, top):
    return ref[top : top + 8, :].astype(f32) + ref[top + 8 : top + 16, :].astype(f32)


def main_split_kernel(plan, keep_ref, got_ref, *outs):
    last = plan.seq * plan.in_rows
    small = joined(keep_ref.at[0], last) + joined(got_ref.at[0], last)
    high, low = two_parts(small)
    for m in range(plan.line):
        total = keep_ref[m, :last, :].astype(f32) + got_ref[m, :last, :].astype(f32)
        outs[m][:last, :] = total.astype(bf16)
        outs[m][last : last + 8, :] = high
        outs[m][last + 8 :, :] = low


def gate_split_kernel(plan, keep_ref, got_ref, *outs):
    for m in range(plan.line):
        outs[m][...] = (keep_ref[m].astype(f32) + got_ref[m].astype(f32)).astype(bf16)


def gate_sum_kernel(plan, *refs):
    parts, outs = refs[: plan.line], refs[plan.line :]
    total = parts[0][...].astype(f32)
    for part in parts[1:]:
        total = total + part[...].astype(f32)
    half = plan.in_rows * plan.seq // 2
    for m in range(plan.seq):
        top = (m // 2) * plan.in_rows
        left = (m % 2) * plan.chan
        outs[m][...] = total[top : top + plan.in_rows, left : left + plan.chan].astype(bf16)
    outs[plan.seq][...] = total[half : half + plan.out_rows]


def row_sum_kernel(plan, *refs):
    parts, outs = refs[: plan.line], refs[plan.line :]
    last = plan.seq * plan.in_rows
    small = joined(parts[0], last)
    for part in parts[1:]:
        small = small + joined(part, last)
    high, low = two_parts(small)
    for m in range(plan.seq):
        rows = slice(m * plan.in_rows, (m + 1) * plan.in_rows)
        total = parts[0][rows, :].astype(f32)
        for part in parts[1:]:
            total = total + part[rows, :].astype(f32)
        outs[m][: plan.in_rows, :] = total.astype(bf16)
        outs[m][plan.in_rows : plan.in_rows + 8, :] = high
        outs[m][plan.in_rows + 8 :, :] = low


def columns_kernel(plan, *refs):
    n = plan.seq
    gates, mains = refs[:n], refs[n : 2 * n]
    out_ref, gate_ref, main_ref = refs[2 * n :]
    s = lax.axis_index("seq")
    for m in range(n):
        gate_ref[m] = gates[m][...].astype(f32)
        main_ref[m] = mains[m][: plan.in_rows, :].astype(f32)
    shared = jnp.zeros((plan.in_rows, 2 * STATE), f32)
    lane = iota((plan.in_rows, LANES), 1)
    dts = jnp.zeros((plan.in_rows, LANES), f32)
    for g in range(n):
        out_ref[:, g * plan.chan : (g + 1) * plan.chan] = gate_ref[s ^ g]
        main = main_ref[s ^ g]
        out_ref[:, INNER + g * plan.chan : INNER + (g + 1) * plan.chan] = main[:, : plan.chan]
        shared = shared + main[:, plan.chan : plan.mixed]
        one = main[:, plan.mixed :]
        moved = one if g == 0 else pltpu.roll(one, g * plan.heads, 1)
        dts = jnp.where(lane // plan.heads == g, moved, dts)
    out_ref[:, 2 * INNER : INNER + CONV] = shared
    out_ref[:, INNER + CONV :] = dts[:, :HEADS]


def small_kernel(plan, *refs):
    n = plan.seq
    parts = refs[:n]
    gain_in_ref, convw_ref, convb_ref, dtb_ref, alog_ref, skip_ref, gain_out_ref, all_ref = refs[n:]
    s = lax.axis_index("seq")
    for m in range(n):
        all_ref[m] = joined(parts[m], plan.in_rows)
    gain_in = jnp.zeros((1, WIDTH), f32)
    shared = jnp.zeros((5, 2 * STATE), f32)
    lane = iota((1, LANES), 1)
    heads = [jnp.zeros((1, LANES), f32) for _ in range(3)]
    for g in range(n):
        part = all_ref[s ^ g]
        gain_in = gain_in + part[0:1, :WIDTH]
        cols = slice(g * plan.chan, (g + 1) * plan.chan)
        convw_ref[:, cols] = part[1:5, : plan.chan]
        convb_ref[:, cols] = part[5:6, : plan.chan]
        gain_out_ref[:, cols] = part[6:7, : plan.chan]
        shared = shared + part[1:6, plan.chan : plan.mixed]
        for j in range(3):
            one = part[7:8, j * LANES : (j + 1) * LANES]
            moved = one if g == 0 else pltpu.roll(one, g * plan.heads, 1)
            heads[j] = jnp.where(lane // plan.heads == g, moved, heads[j])
    gain_in_ref[...] = gain_in
    convw_ref[:, INNER:] = shared[:4]
    convb_ref[:, INNER:] = shared[4:]
    dtb_ref[...] = heads[0][:, :HEADS]
    alog_ref[...] = heads[1][:, :HEADS]
    skip_ref[...] = heads[2][:, :HEADS]


def result_kernel(plan, tok_ref, scale_ref, *refs):
    parts, out_ref = refs[: plan.seq], refs[plan.seq]
    s = lax.axis_index("seq")
    total = parts[0][...].astype(f32)
    for part in parts[1:]:
        total = total + part[...].astype(f32)
    r = scale_ref[pl.ds(aligned(s * plan.rows, plan.rows), plan.rows), :]
    r = jnp.concatenate([r] * (WIDTH // LANES), axis=1)
    out_ref[...] = (tok_ref[...].astype(f32) + total * r).astype(bf16)


def token_kernel(plan, tok_ref, cot_ref, gain_ref, *refs):
    parts, out_ref = refs[: plan.seq], refs[plan.seq]
    total = parts[0][...].astype(f32)
    for part in parts[1:]:
        total = total + part[...].astype(f32)
    tok = tok_ref[...].astype(f32)
    q = lax.rsqrt(jnp.mean(tok * tok, axis=1, keepdims=True) + norm_eps)
    w = total * gain_ref[...]
    mean = jnp.mean(w * tok, axis=1, keepdims=True)
    grad = cot_ref[...].astype(f32) + q * w - tok * (q * q * q * mean)
    out_ref[...] = grad.astype(bf16)


def call(body, plan, outs, scratch, *args, mib=4, micros=1, name=None, kept=0):
    shapes = [jax.ShapeDtypeStruct(shape, kind) for shape, kind in outs]
    size = sum(a.size * a.dtype.itemsize for a in args)
    size += sum(a.size * a.dtype.itemsize for a in shapes)
    return pl.pallas_call(
        functools.partial(body, plan),
        out_shape=shapes,
        in_specs=[pl.BlockSpec(memory_space=pl.ANY)] * kept
        + [pl.BlockSpec(memory_space=pltpu.VMEM)] * (len(args) - kept),
        out_specs=[pl.BlockSpec(memory_space=pltpu.VMEM)] * len(shapes),
        scratch_shapes=[
            pltpu.VMEM(*one) if isinstance(one, tuple) else one for one in scratch
        ],
        compiler_params=pltpu.CompilerParams(vmem_limit_bytes=mib * 2**20),
        cost_estimate=pl.CostEstimate(
            flops=micros * FLOPS_PER_MICRO, bytes_accessed=size, transcendentals=0
        ),
        name=name,
    )(*args)


FLOPS_PER_MICRO = 1_000_000_000


def swap(value, axis, by):
    size = lax.axis_size(axis)
    return lax.ppermute(value, axis, [(i, i ^ by) for i in range(size)])


def after(value, *others):
    return lax.optimization_barrier((value, *others))[0]


def head_parallel(
    tokens, cotangent, segments, in_weight, out_weight, gain_in, conv_weight, conv_bias,
    dt_bias, a_log, d_skip, gain_out,
):
    rows = tokens.shape[1]
    plan = Plan(
        lax.axis_size("seq"), lax.axis_size("batch"), rows, in_weight.shape[0], out_weight.shape[0]
    )
    n, line, chan, heads = plan.seq, plan.line, plan.chan, plan.heads
    s = lax.axis_index("seq")
    tok, cot = tokens[0], cotangent[0]

    r = plan.in_rows
    own = call(
        pack_kernel, plan, [((r + 8, plan.cols + chan), bf16)] * n,
        [
            (in_weight.shape, bf16), (segments.shape, jnp.int32), pltpu.SemaphoreType.DMA((2,)),
            ((n, r, plan.cols + chan), bf16),
        ],
        in_weight, segments, name="pack", kept=2,
    )
    pieces = [own[0]] + [swap(own[m], "seq", m) for m in range(1, n)]
    toks = [tok] + [swap(tok, "seq", m) for m in range(1, n)]
    main_shard, gate_shard = call(
        regroup_kernel, plan,
        [((n * r, plan.cols), bf16), ((n * r // 2 + plan.out_rows, WIDTH), bf16)], [],
        *pieces, out_weight, name="regroup",
    )

    def along(shard):
        return [shard] + [swap(shard, "batch", 2 * m) for m in range(1, line)]

    def both_cores(parts):
        return parts + [swap(one, "batch", 1) for one in parts]

    main_line = along(main_shard)
    main_parts = both_cores(main_line)
    gate_line = along(after(gate_shard, *main_line))
    cot_near = after(cot, *toks)
    conv, per_head, own_gain = call(
        own_params_kernel, plan,
        [((8, plan.mixed), f32), ((8, chan), f32), ((1, chan), f32)], [],
        conv_weight, conv_bias[None], dt_bias[None], a_log[None], d_skip[None], gain_out[None],
        name="own_params",
    )
    gain_row = gain_in[None]
    total = plan.total
    seg_rows = -(-plan.blocks // 8) * 8
    normed, w_main, x, dt_raw, segc, segr = call(
        project_kernel, plan,
        [
            ((total, WIDTH), bf16), ((WIDTH, plan.cols), bf16),
            ((total + LEAD, plan.mixed), f32), ((total, LANES), f32),
            ((total + 2 * LEAD, LANES), f32), ((seg_rows, GROUP), f32),
        ],
        [((WIDTH, plan.cols), f32)],
        *toks, *pieces, *main_parts, gain_row, mib=16, micros=5, name="project",
    )
    cot_far = after(cot, normed)
    cots = [cot] + [swap(cot_near if m < 3 else cot_far, "seq", m) for m in range(1, n)]
    half = plan.blocks // 2
    state_shape = (STATE, chan)
    scan_in = (x, dt_raw, segc, segr, conv, per_head)

    def scan_part(first, last, *early):
        return call(
            lambda p, *refs: scan_kernel(p, first, last, *refs), plan,
            [((last * GROUP, chan), f32), ((last,) + state_shape, f32), (state_shape, f32)], [],
            *scan_in, *early, mib=12, micros=4, name="scan_forward",
        )

    early = list(scan_part(0, half))
    gate_line = [after(one, early[2]) for one in gate_line]
    gate_parts = both_cores(gate_line)
    early[2] = after(early[2], *gate_line, *cots[1:3])
    y, states, _ = scan_part(half, plan.blocks, *early)
    piece_shape = (rows, WIDTH)
    w_gate, z, du, stats, *outs = call(
        gate_kernel, plan,
        [
            ((WIDTH, chan), bf16), ((total, chan), f32), ((total, chan), f32),
            ((2 * plan.blocks, GROUP), f32),
        ] + [(piece_shape, bf16)] * n,
        [((WIDTH, chan), f32), ((chan, WIDTH), bf16)],
        normed, y, *gate_parts, *cots, own_gain,
        mib=16, micros=6, name="gate_forward",
    )
    all_stats = [stats] + [swap(stats, "seq", m) for m in range(1, n)]
    dy, dz, scale, gain_out_grad, share, keep, send = call(
        regate_kernel, plan,
        [
            ((total, chan), f32), ((total, chan), bf16), ((total, LANES), f32), ((1, chan), f32),
            ((8, LANES), f32),
            ((line, n * r // 2 + plan.out_rows, WIDTH), bf16),
            ((line, n * r // 2 + plan.out_rows, WIDTH), bf16),
        ],
        [((total, chan), bf16), ((WIDTH, chan), f32), ((chan, WIDTH), f32)],
        *all_stats, normed, y, z, du, w_gate, *cots, own_gain,
        mib=16, micros=6, name="gate_backward",
    )

    def reduce_line(keep, send, body, name):
        got = swap(send, "batch", 1)
        parts = call(
            body, plan, [(keep.shape[1:], bf16)] * line, [], keep, got, name=name,
        )
        return parts

    def line_exchange(parts):
        return [parts[0]] + [swap(parts[m], "batch", 2 * m) for m in range(1, line)]

    gate_half = reduce_line(keep, send, gate_split_kernel, "gate_core_sum")
    gate_lines = line_exchange(gate_half)
    dy = after(dy, *gate_half)
    back_in = (x, dt_raw, states, segc, segr, dy, conv, per_head)

    def scan_back_part(first, last, *before):
        return call(
            lambda p, *refs: scan_back_kernel(p, first, last, *refs), plan,
            [
                ((total - first * GROUP, plan.cols), bf16), (state_shape, f32),
                ((LEAD, plan.mixed), f32), ((8, plan.mixed), f32), ((8, LANES), f32),
            ], [],
            *back_in, *before, mib=16, micros=10, name="scan_backward",
        )

    before = list(scan_back_part(half, plan.blocks))
    out_far = after(outs[n - 1], before[1])
    out_parts = [outs[0]] + [
        swap(outs[m] if m < 3 else out_far, "seq", m) for m in range(1, n)
    ]
    *gate_grads, shard_out = call(
        gate_sum_kernel, plan,
        [((r, chan), bf16)] * n + [((plan.out_rows, WIDTH), f32)], [], *gate_lines,
        name="gate_sum",
    )
    before[1] = after(before[1], *gate_lines, *out_parts[1:3])
    gp, _, _, acc, head_acc = scan_back_part(0, half, *before)
    gate_grads = [gate_grads[0]] + [swap(gate_grads[m], "seq", m) for m in range(1, n)]
    (result,) = call(
        result_kernel, plan, [(piece_shape, bf16)], [], tok, scale, *out_parts, name="result"
    )

    keep, send = call(
        main_grads_kernel, plan, [((line, n * r + 16, plan.cols), bf16)] * 2,
        [((WIDTH, plan.cols), f32), ((8, plan.cols), f32)],
        normed, gp, w_main, gain_row, share, gain_out_grad, acc, head_acc,
        mib=12, micros=4, name="main_grads",
    )
    grads = call(
        normed_grads_kernel, plan, [(piece_shape, bf16)] * n, [], gp, w_main, dz, w_gate,
        mib=12, micros=3, name="normed_grads",
    )
    main_lines = line_exchange(reduce_line(keep, send, main_split_kernel, "main_core_sum"))
    grads = [after(one, *out_parts) for one in grads]
    grad_parts = [grads[0]] + [swap(grads[m], "seq", m) for m in range(1, n)]
    main_grads = call(
        row_sum_kernel, plan, [((r + 16, plan.cols), bf16)] * n, [], *main_lines, name="main_sum"
    )
    main_grads = [main_grads[0]] + [swap(main_grads[m], "seq", m) for m in range(1, n)]
    (grad_tokens,) = call(
        token_kernel, plan, [(piece_shape, bf16)], [], tok, cot, gain_row, *grad_parts,
        name="token_grad",
    )
    (shard_in,) = call(
        columns_kernel, plan, [((r, in_weight.shape[1]), f32)],
        [((n, r, chan), f32), ((n, r, plan.cols), f32)], *gate_grads, *main_grads, name="columns",
    )
    smalls = call(
        small_kernel, plan,
        [
            ((1, WIDTH), f32), ((KERNEL, CONV), f32), ((1, CONV), f32), ((1, HEADS), f32),
            ((1, HEADS), f32), ((1, HEADS), f32), ((1, INNER), f32),
        ],
        [((n, 8, plan.cols), f32)], *main_grads, name="small_grads",
    )
    return (
        result[None], grad_tokens[None], shard_in, shard_out, smalls[0][0], smalls[1],
        smalls[2][0], smalls[3][0], smalls[4][0], smalls[5][0], smalls[6][0],
    )


def shifted(value, axis, by):
    size = lax.axis_size(axis)
    pairs = [(i, i + by) for i in range(size) if 0 <= i + by < size]
    return lax.ppermute(value, axis, pairs)


def prefix(value, axis, join, neutral):
    place = lax.axis_index(axis)
    gathered = jax.tree.map(
        lambda a, kind: lax.all_gather(a.astype(kind), axis), value, (jnp.bfloat16, jnp.bfloat16)
    )
    state = jax.tree.map(lambda a, e: jnp.zeros_like(a) + jnp.asarray(e, a.dtype), value, neutral)

    def one(turn, state):
        return join(
            state,
            jax.tree.map(
                lambda a, own: lax.dynamic_index_in_dim(a, turn, 0, False).astype(own.dtype),
                gathered,
                value,
            ),
        )

    return lax.fori_loop(0, place, one, state)


def prefix_2(value, axis, join, neutral):
    count = lax.axis_size(axis)
    place = lax.axis_index(axis)
    ahead = count - 1 - place
    gathered = jax.tree.map(
        lambda a, kind: lax.all_gather(a.astype(kind), axis),
        value,
        jax.tree.map(lambda a: jnp.bfloat16 if a.dtype == jnp.float32 else a.dtype, value),
    )
    state = jax.tree.map(lambda a, e: jnp.zeros_like(a) + jnp.asarray(e, a.dtype), value, neutral)

    def one(turn, state):
        source = count - 1 - turn
        return join(
            state,
            jax.tree.map(
                lambda a, own: lax.dynamic_index_in_dim(a, source, 0, False).astype(own.dtype),
                gathered,
                value,
            ),
        )

    return lax.fori_loop(0, ahead, one, state)


def rms_scale(values, gain):
    mean_square = jnp.mean(values * values, axis=-1, keepdims=True)
    return values * lax.rsqrt(mean_square + norm_eps) * gain


def causal_conv(extended, ext_segs, conv_weight, conv_bias, row_count):
    target = ext_segs[KERNEL - 1 :]
    total = jnp.zeros((row_count, conv_weight.shape[1]), jnp.float32) + conv_bias[None, :]
    for offset in range(KERNEL):
        window = extended[offset : offset + row_count]
        same_doc = (ext_segs[offset : offset + row_count] == target).astype(jnp.float32)
        total = total + conv_weight[offset][None, :] * window * same_doc[:, None]
    return jax.nn.silu(total)


def prepare(xbc, dt_raw, edge_rows, ext_segs, conv_weight, conv_bias, dt_bias, a_log):
    row_count = xbc.shape[0]
    extended = jnp.concatenate([edge_rows, xbc], axis=0)
    mixed = causal_conv(extended, ext_segs, conv_weight, conv_bias, row_count)
    values = mixed[:, :INNER].reshape(row_count, HEADS, HEADDIM)
    key_vecs = mixed[:, INNER : INNER + STATE]
    queries = mixed[:, INNER + STATE :]
    step_sizes = jax.nn.softplus(dt_raw + dt_bias[None, :])
    log_decay = -step_sizes * jnp.exp(a_log)[None, :]
    return (values, key_vecs, queries, step_sizes, log_decay)


def group_block(carried, block_in):
    state_in, last_seg = carried
    values, key_vecs, queries, step_sizes, log_decay, seg_ids = block_in
    length_here = seg_ids.shape[0]
    cumulative = jnp.cumsum(log_decay, axis=0)
    positions = jnp.arange(length_here)
    allowed = (seg_ids[:, None] == seg_ids[None, :]) & (positions[:, None] >= positions[None, :])
    gap_logs = cumulative[:, None, :] - cumulative[None, :, :]
    decay_mask = jnp.where(allowed[:, :, None], jnp.exp(jnp.minimum(gap_logs, 0.0)), 0.0)
    scores = jnp.dot(queries, key_vecs.T, precision=highest)
    weights = decay_mask * scores[:, :, None] * step_sizes[None, :, :]
    inside = jnp.einsum("tsh,shp->thp", weights, values, precision=highest)
    keep_factor = jnp.where((seg_ids == last_seg)[:, None], jnp.exp(cumulative), 0.0)
    carried_out = (
        jnp.einsum("tn,hpn->thp", queries, state_in, precision=highest) * keep_factor[:, :, None]
    )
    to_end = (
        jnp.where(
            (seg_ids == seg_ids[-1])[:, None], jnp.exp(cumulative[-1][None, :] - cumulative), 0.0
        )
        * step_sizes
    )
    fresh_state = jnp.einsum("sh,shp,sn->hpn", to_end, values, key_vecs, precision=highest)
    new_state = state_in * keep_factor[-1][:, None, None] + fresh_state
    return ((new_state, seg_ids[-1]), inside + carried_out)


def grouped_ssd(
    values, key_vecs, queries, step_sizes, log_decay, seg_ids, d_skip, state_in, last_seg
):
    row_count = seg_ids.shape[0]
    block_count = row_count // GROUP

    def blocked(member):
        return member.reshape((block_count, GROUP) + member.shape[1:])

    inputs = (
        blocked(values),
        blocked(key_vecs),
        blocked(queries),
        blocked(step_sizes),
        blocked(log_decay),
        blocked(seg_ids),
    )
    (final_state, last_out), outputs = lax.scan(
        jax.checkpoint(group_block), (state_in, last_seg), inputs
    )
    outputs = outputs.reshape(row_count, HEADS, HEADDIM) + d_skip[None, :, None] * values
    return (outputs, final_state)


def gated_norm(mixed_out, gate_z, gain_out):
    return rms_scale(mixed_out * jax.nn.silu(gate_z), gain_out)


def chain_combine(earlier, later):
    decay_early, state_early = earlier
    decay_late, state_late = later
    return (decay_early * decay_late, decay_late[:, None, None] * state_early + state_late)


def cross_term(queries, log_decay, state_in, seg_ids, prev_seg):
    cumulative = jnp.cumsum(log_decay, axis=0)
    keep_factor = jnp.where((seg_ids == prev_seg)[:, None], jnp.exp(cumulative), 0.0)
    return jnp.einsum("tn,hpn->thp", queries, state_in, precision=highest) * keep_factor[:, :, None]


def device_decay(log_decay, seg_ids, prev_seg):
    total_log = jnp.sum(log_decay, axis=0)
    return jnp.where(seg_ids[-1] == prev_seg, jnp.exp(total_log), 0.0)


def on_device(
    tokens,
    cotangent,
    segments,
    in_weight,
    out_weight,
    gain_in,
    conv_weight,
    conv_bias,
    dt_bias,
    a_log,
    d_skip,
    gain_out,
):
    tokens_f = tokens[0].astype(jnp.float32)
    cot_low = cotangent[0]
    seg_ids = segments[0]
    row_count = seg_ids.shape[0]
    full_in, full_out = (
        lax.all_gather(in_weight, ("seq", "batch"), axis=0, tiled=True),
        lax.all_gather(out_weight, ("seq", "batch"), axis=0, tiled=True),
    )
    normed, norm_pull = jax.vjp(rms_scale, tokens_f, gain_in)
    normed_low = normed.astype(jnp.bfloat16)
    projected = jnp.dot(normed_low, full_in, preferred_element_type=jnp.float32)
    gate_z = projected[:, :INNER]
    xbc = projected[:, INNER : INNER + CONV]
    dt_raw = projected[:, INNER + CONV :]
    tail_start = row_count - KERNEL + 1
    edge_rows, edge_segs = shifted(
        (xbc[tail_start:], seg_ids[tail_start:].astype(jnp.float32)), "seq", 1
    )
    prev_segs = edge_segs.astype(jnp.int32)
    prev_seg = prev_segs[KERNEL - 2]
    ext_segs = jnp.concatenate([prev_segs, seg_ids])

    def prepare_local(xbc_in, dt_in, edge_in, weight_in, bias_in, shift_in, alog_in):
        return prepare(xbc_in, dt_in, edge_in, ext_segs, weight_in, bias_in, shift_in, alog_in)

    prepared, prepare_pull = jax.vjp(
        prepare_local, xbc, dt_raw, edge_rows, conv_weight, conv_bias, dt_bias, a_log
    )
    values, key_vecs, queries, step_sizes, log_decay = prepared
    zeros_state = jnp.zeros((HEADS, HEADDIM, STATE), jnp.float32)

    def local_ssd(values_in, keys_in, queries_in, sizes_in, logs_in, skip_in):
        return grouped_ssd(
            values_in,
            keys_in,
            queries_in,
            sizes_in,
            logs_in,
            seg_ids,
            skip_in,
            zeros_state,
            seg_ids[0],
        )

    (local_out, local_state), ssd_pull = jax.vjp(
        local_ssd, values, key_vecs, queries, step_sizes, log_decay, d_skip
    )

    def decay_local(logs_in):
        return device_decay(logs_in, seg_ids, prev_seg)

    decay_here, decay_pull = jax.vjp(decay_local, log_decay)
    identity = (jnp.ones((HEADS,), jnp.float32), zeros_state)
    decay_prefix, state_in = prefix((decay_here, local_state), "seq", chain_combine, identity)

    def cross_local(queries_in, logs_in, state_arg):
        return cross_term(queries_in, logs_in, state_arg, seg_ids, prev_seg)

    cross_out, cross_pull = jax.vjp(cross_local, queries, log_decay, state_in)
    mixed_out = (local_out + cross_out).reshape(row_count, INNER)
    gated, gated_pull = jax.vjp(gated_norm, mixed_out, gate_z, gain_out)
    gated_low = gated.astype(jnp.bfloat16)
    result = tokens_f + jnp.dot(gated_low, full_out, preferred_element_type=jnp.float32)
    back_in, back_out = (
        lax.all_gather(in_weight, ("seq", "batch"), axis=0, tiled=True),
        lax.all_gather(out_weight, ("seq", "batch"), axis=0, tiled=True),
    )
    contract_last = (((1,), (1,)), ((), ()))
    contract_first = (((0,), (0,)), ((), ()))
    grad_gated = lax.dot_general(
        cot_low, back_out, contract_last, preferred_element_type=jnp.float32
    )
    grad_mixed, grad_gate, grad_gain_out = gated_pull(grad_gated)
    grad_mixed = grad_mixed.reshape(row_count, HEADS, HEADDIM)
    grad_q_cross, grad_log_cross, grad_state_in = cross_pull(grad_mixed)
    decay_after, grad_exit = prefix_2((decay_here, grad_state_in), "seq", chain_combine, identity)
    grad_decay = jnp.sum(grad_exit * state_in, axis=(1, 2))
    grad_log_dev = decay_pull(grad_decay)[0]
    grad_values, grad_keys, grad_q_local, grad_sizes, grad_log_local, grad_skip = ssd_pull(
        (grad_mixed, grad_exit)
    )
    prep_grads = prepare_pull(
        (
            grad_values,
            grad_keys,
            grad_q_local + grad_q_cross,
            grad_sizes,
            grad_log_local + grad_log_cross + grad_log_dev,
        )
    )
    grad_xbc, grad_dt, grad_edge, grad_conv_w, grad_conv_b, grad_dt_bias, grad_a_log = prep_grads
    grad_next = shifted(grad_edge, "seq", -1)
    grad_xbc = grad_xbc.at[tail_start:].add(grad_next)
    grad_proj = jnp.concatenate([grad_gate, grad_xbc, grad_dt], axis=1).astype(jnp.bfloat16)
    grad_normed = lax.dot_general(
        grad_proj, back_in, contract_last, preferred_element_type=jnp.float32
    )
    grad_tokens_norm, grad_gain_in = norm_pull(grad_normed)
    grad_tokens = (cot_low.astype(jnp.float32) + grad_tokens_norm).astype(jnp.bfloat16)
    grad_in_w = lax.dot_general(
        normed_low, grad_proj, contract_first, preferred_element_type=jnp.float32
    )
    grad_out_w = lax.dot_general(
        gated_low, cot_low, contract_first, preferred_element_type=jnp.float32
    )
    shard_in, shard_out = (
        lax.psum_scatter(grad_in_w, ("seq", "batch"), scatter_dimension=0, tiled=True),
        lax.psum_scatter(grad_out_w, ("seq", "batch"), scatter_dimension=0, tiled=True),
    )
    summed = lax.psum(
        (
            grad_gain_in,
            grad_conv_w,
            grad_conv_b,
            grad_dt_bias,
            grad_a_log,
            grad_skip,
            grad_gain_out,
        ),
        ("seq", "batch"),
    )
    return (
        result.astype(jnp.bfloat16)[None],
        grad_tokens[None],
        shard_in,
        shard_out,
        summed[0],
        summed[1],
        summed[2],
        summed[3],
        summed[4],
        summed[5],
        summed[6],
    )


def solution(mesh):
    in_specs = (
        P("batch", "seq", None),
        P("batch", "seq", None),
        P("batch", "seq"),
        P(("seq", "batch"), None),
        P(("seq", "batch"), None),
        P(),
        P(),
        P(),
        P(),
        P(),
        P(),
        P(),
    )
    out_specs = (
        P("batch", "seq", None),
        P("batch", "seq", None),
        P(("seq", "batch"), None),
        P(("seq", "batch"), None),
        P(),
        P(),
        P(),
        P(),
        P(),
        P(),
        P(),
    )
    count = mesh.shape["seq"]
    even = HEADS % (2 * count) == 0 and count & (count - 1) == 0
    return jax.shard_map(
        head_parallel if even else on_device, mesh=mesh, in_specs=in_specs, out_specs=out_specs, check_vma=False
    )
```

```python
import functools

import jax
import jax.numpy as jnp
from jax import lax
from jax.experimental import pallas as pl
from jax.experimental.pallas import tpu as pltpu
from jax.sharding import PartitionSpec as P

HEADS = 24
HEADDIM = 64
STATE = 128
KERNEL = 4
GROUP = 128
INNER = 1536
CONV = 1792
WIDTH = 768
LANES = 128
LEAD = 8


highest = lax.Precision.HIGHEST
norm_eps = 1e-05
f32 = jnp.float32
bf16 = jnp.bfloat16
contract_last = (((1,), (1,)), ((), ()))
contract_first = (((0,), (0,)), ((), ()))


def mm(a, b):
    return jnp.dot(a.astype(bf16), b.astype(bf16), preferred_element_type=f32)


def mm_nt(a, b):
    return lax.dot_general(
        a.astype(bf16), b.astype(bf16), contract_last, preferred_element_type=f32
    )


def mm_tn(a, b):
    return lax.dot_general(
        a.astype(bf16), b.astype(bf16), contract_first, preferred_element_type=f32
    )


def two_parts(value):
    high = value.astype(bf16)
    return high, (value - high.astype(f32)).astype(bf16)


def mask_mm(mask, value):
    width = value.shape[1]
    out = mm(mask, jnp.concatenate(two_parts(value), axis=1))
    return out[:, :width] + out[:, width:]


def iota(shape, dim):
    return lax.broadcasted_iota(jnp.int32, shape, dim)


def aligned(value, unit):
    return pl.multiple_of(value, unit)


def wide(columns, chan):
    half = LANES // 2
    high, low = two_parts(columns)
    low = pltpu.roll(low.astype(f32), half, 1)
    both = jnp.where(iota(columns.shape, 1) < half, high.astype(f32), low)
    spread = iota((LANES, chan), 1) // HEADDIM == lax.rem(iota((LANES, chan), 0), half)
    return mm(both, spread.astype(f32))


def softplus(value):
    return jnp.maximum(value, 0.0) + jnp.log1p(jnp.exp(-jnp.abs(value)))


def sigmoid(value):
    return 0.5 + 0.5 * jnp.tanh(0.5 * value)


class Plan:
    def __init__(self, mesh_seq, mesh_batch, rows, in_rows, out_rows):
        self.seq = mesh_seq
        self.batch = mesh_batch
        self.line = mesh_batch // 2
        self.rows = rows
        self.total = rows * mesh_seq
        self.blocks = self.total // GROUP
        self.heads = HEADS // mesh_seq
        self.chan = self.heads * HEADDIM
        self.mixed = self.chan + 2 * STATE
        self.cols = self.mixed + LANES
        self.in_rows = in_rows
        self.out_rows = out_rows


def place():
    s = lax.axis_index("seq")
    b = lax.axis_index("batch")
    return s, lax.shift_right_logical(b, 1), lax.bitwise_and(b, 1)


def in_place(plan, ids, line_xor, core_xor, seq_xor):
    s, z, c = ids
    owner = (s ^ seq_xor) * plan.batch + (z ^ line_xor) * 2 + (c ^ core_xor)
    return aligned(owner * plan.in_rows, 8)


def block_values(plan, b, x_ref, segc_ref, segr_ref, dt_ref, convw, convb, heads_ref):
    base = aligned(b * GROUP, GROUP)
    win = x_ref[pl.ds(base, GROUP + LEAD), :]
    segw = segc_ref[pl.ds(base, GROUP + LEAD), :]
    seg = segw[LEAD:]
    prev = segw[LEAD - 1 : LEAD]
    repeat = plan.mixed // LANES
    pre = jnp.broadcast_to(convb, (GROUP, plan.mixed))
    shifts = []
    for k in range(KERNEL):
        start = LEAD - KERNEL + 1 + k
        part = win[start : start + GROUP]
        if k < KERNEL - 1:
            same = (segw[start : start + GROUP] == seg).astype(f32)
            part = part * jnp.concatenate([same] * repeat, axis=1)
        shifts.append(part)
        pre = pre + convw[k : k + 1] * part
    sig = sigmoid(pre)
    mixed = pre * sig
    values = mixed[:, : plan.chan]
    keys = mixed[:, plan.chan : plan.chan + STATE]
    queries = mixed[:, plan.chan + STATE :]
    dt_in = dt_ref[pl.ds(base, GROUP), :] + heads_ref[0:1, :LANES]
    steps = softplus(dt_in)
    decay = -steps * jnp.exp(heads_ref[1:2, :LANES])
    row = iota((GROUP, GROUP), 0)
    col = iota((GROUP, GROUP), 1)
    tri = (row >= col).astype(f32)
    cum = mask_mm(tri, decay)
    half = LANES // 2
    turned = jnp.where(col < half, cum, pltpu.roll(steps, half, 1)).T
    cum_t = turned[:half]
    steps_t = turned[half:]
    segr = segr_ref[pl.ds(b, 1), :]
    allowed = (seg == segr) & (row >= col)
    scores = mm_nt(queries, keys)
    keep = jnp.where(seg == prev, jnp.exp(cum), 0.0)
    last = cum[GROUP - 1 :]
    to_last = jnp.where(seg == seg[GROUP - 1 :], jnp.exp(last - cum), 0.0)
    return dict(
        base=base, seg=seg, shifts=shifts, pre=pre, sig=sig, values=values, keys=keys,
        queries=queries, dt_in=dt_in, steps=steps, decay=decay, tri=tri, cum=cum, cum_t=cum_t,
        steps_t=steps_t, allowed=allowed, scores=scores, keep=keep, to_last=to_last,
    )


def head_decay(v, h):
    gap = v["cum"][:, h : h + 1] - v["cum_t"][h : h + 1, :]
    return jnp.where(v["allowed"], jnp.exp(jnp.minimum(gap, 0.0)), 0.0)


def split_pair(pair):
    low = iota(pair.shape, 1) < HEADDIM
    return jnp.concatenate([jnp.where(low, pair, 0.0), jnp.where(low, 0.0, pair)], axis=0)


def fetch(pairs, sems):
    copies = [
        pltpu.make_async_copy(src, dst, sems.at[i]) for i, (src, dst) in enumerate(pairs)
    ]
    for copy in copies:
        copy.start()
    for copy in copies:
        copy.wait()


def pack_kernel(plan, w_any, seg_any, *outs):
    n, heads, chan = plan.seq, plan.heads, plan.chan
    blocks, outs = outs[:n], outs[n:]
    w_ref, seg_ref, sems, all_ref = outs
    fetch([(w_any, w_ref), (seg_any, seg_ref)], sems)
    s = lax.axis_index("seq")
    lane = iota((plan.in_rows, LANES), 1)
    tail = w_ref[:, INNER + CONV :].astype(f32)
    tail = jnp.concatenate(
        [tail, jnp.zeros((plan.in_rows, LANES - HEADS), f32)], axis=1
    )
    for g in range(n):
        moved = tail if g == 0 else pltpu.roll(tail, LANES - g * heads, 1)
        all_ref[g] = jnp.concatenate(
            [
                w_ref[:, INNER + g * chan : INNER + (g + 1) * chan],
                w_ref[:, 2 * INNER : INNER + CONV],
                jnp.where(lane < heads, moved, 0.0).astype(bf16),
                w_ref[:, g * chan : (g + 1) * chan],
            ],
            axis=1,
        )
    seg = jnp.broadcast_to(seg_ref[...].astype(f32), (8, plan.rows)).astype(bf16)
    for m in range(n):
        blocks[m][0 : plan.in_rows, :] = all_ref[s ^ m]
        blocks[m][plan.in_rows : plan.in_rows + 8, :] = jnp.zeros((8, plan.cols + chan), bf16)
        blocks[m][plan.in_rows : plan.in_rows + 8, : plan.rows] = seg


def own_params_kernel(
    plan, convw_ref, convb_ref, dtb_ref, alog_ref, skip_ref, gain_ref, conv_ref, heads_ref,
    own_gain_ref,
):
    n, heads, chan = plan.seq, plan.heads, plan.chan
    s = lax.axis_index("seq")
    own = pl.ds(aligned(s * chan, LANES), chan)
    conv_ref[...] = jnp.zeros_like(conv_ref)
    conv_ref[0:KERNEL, :chan] = convw_ref[:, own]
    conv_ref[0:KERNEL, chan:] = convw_ref[:, INNER:]
    conv_ref[KERNEL : KERNEL + 1, :chan] = convb_ref[:, own]
    conv_ref[KERNEL : KERNEL + 1, chan:] = convb_ref[:, INNER:]
    own_gain_ref[...] = gain_ref[:, own]
    one_lane = iota((1, LANES), 1)

    def own_heads(ref):
        row = jnp.concatenate([ref[...], jnp.zeros((1, LANES - HEADS), f32)], axis=1)
        found = row
        for g in range(1, n):
            found = jnp.where(s == g, pltpu.roll(row, LANES - g * heads, 1), found)
        return jnp.where(one_lane < heads, found, 0.0)

    heads_ref[...] = jnp.zeros_like(heads_ref)
    heads_ref[0:1, :LANES] = own_heads(dtb_ref)
    heads_ref[1:2, :LANES] = own_heads(alog_ref)
    skip = jnp.broadcast_to(own_heads(skip_ref), (8, LANES))
    heads_ref[2:3, :] = wide(skip, chan)[0:1]


def regroup_kernel(plan, *refs):
    n, r = plan.seq, plan.in_rows
    pieces, out_w_ref = refs[:n], refs[n]
    main_ref, gate_ref = refs[n + 1 :]
    half = r * n // 2
    for m in range(n):
        main_ref[m * r : (m + 1) * r, :] = pieces[m][0:r, : plan.cols]
        top, left = (m // 2) * r, (m % 2) * plan.chan
        gate_ref[top : top + r, left : left + plan.chan] = pieces[m][0:r, plan.cols :]
    gate_ref[half : half + plan.out_rows, :] = out_w_ref[...]


def fill_segments(plan, s, pieces, segc_ref, segr_ref):
    per = plan.rows // GROUP
    segc_ref[...] = jnp.zeros_like(segc_ref)
    segr_ref[...] = jnp.zeros_like(segr_ref)
    for m in range(plan.seq):
        line = pieces[m][plan.in_rows : plan.in_rows + 1, : plan.rows].astype(f32)
        for j in range(per):
            b = (s ^ m) * per + j
            segr_ref[pl.ds(b, 1), :] = line[:, j * GROUP : (j + 1) * GROUP]
    every = segr_ref[...]
    turned = jnp.concatenate(
        [every, jnp.zeros((LANES - every.shape[0], GROUP), f32)], axis=0
    ).T
    for b in range(plan.blocks):
        segc_ref[LEAD + b * GROUP : LEAD + (b + 1) * GROUP, :] = jnp.broadcast_to(
            turned[:, b : b + 1], (GROUP, LANES)
        )


def project_kernel(plan, *refs):
    n = plan.seq
    toks, refs = refs[:n], refs[n:]
    pieces, refs = refs[:n], refs[n:]
    weights, refs = refs[: 2 * plan.line], refs[2 * plan.line :]
    gain_ref = refs[0]
    normed_ref, w_ref, x_ref, dt_ref, segc_ref, segr_ref, wf_ref = refs[1:]
    ids = place()
    s = ids[0]
    fill_segments(plan, s, pieces, segc_ref, segr_ref)
    for core_xor in range(2):
        for line_xor in range(plan.line):
            piece = weights[core_xor * plan.line + line_xor]
            for m in range(n):
                dest = pl.ds(in_place(plan, ids, line_xor, core_xor, m), plan.in_rows)
                wf_ref[dest, :] = piece[m * plan.in_rows : (m + 1) * plan.in_rows, :].astype(f32)
    w_ref[...] = wf_ref[...].astype(bf16)
    x_ref[0:LEAD, :] = jnp.zeros((LEAD, plan.mixed), f32)
    for m in range(n):
        tok = toks[m][...].astype(f32)
        scale = lax.rsqrt(jnp.mean(tok * tok, axis=1, keepdims=True) + norm_eps)
        low = (tok * scale * gain_ref[...]).astype(bf16)
        start = (s ^ m) * plan.rows
        normed_ref[pl.ds(aligned(start, plan.rows), plan.rows), :] = low
        out = jnp.dot(low, w_ref[...], preferred_element_type=f32)
        x_ref[pl.ds(aligned(start + LEAD, 8), plan.rows), :] = out[:, : plan.mixed]
        dt_ref[pl.ds(aligned(start, plan.rows), plan.rows), :] = out[:, plan.mixed :]


def scan_kernel(plan, first, last, *refs):
    x_ref, dt_ref, segc_ref, segr_ref, conv_ref, heads_ref = refs[:6]
    refs = refs[6:]
    if first:
        early_y_ref, early_states_ref, early_ref = refs[:3]
        refs = refs[3:]
    y_ref, states_ref, state_ref = refs
    if first:
        y_ref[: first * GROUP, :] = early_y_ref[...]
        states_ref[:first] = early_states_ref[...]
        state_ref[...] = early_ref[...]
    else:
        state_ref[...] = jnp.zeros_like(state_ref)
    convw = conv_ref[0:KERNEL, :]
    convb = conv_ref[KERNEL : KERNEL + 1, :]

    def step(b, carry):
        v = block_values(plan, b, x_ref, segc_ref, segr_ref, dt_ref, convw, convb, heads_ref)
        state = state_ref[...]
        states_ref[b] = state
        parts = []
        for pair in range(plan.heads // 2):
            lanes = slice(pair * LANES, (pair + 1) * LANES)
            weights_pair = []
            for h in (2 * pair, 2 * pair + 1):
                decay = head_decay(v, h)
                weights_pair.append(decay * v["scores"] * v["steps_t"][h : h + 1, :])
            parts.append(
                mm(jnp.concatenate(weights_pair, axis=1), split_pair(v["values"][:, lanes]))
            )
        inside = jnp.concatenate(parts, axis=1)
        spread = wide(
            jnp.concatenate([v["keep"], v["to_last"] * v["steps"]], axis=0), plan.chan
        )
        keep, to_end = spread[:GROUP], spread[GROUP:]
        carried = mm(v["queries"], state) * keep
        y_ref[pl.ds(v["base"], GROUP), :] = inside + carried + heads_ref[2:3, :] * v["values"]
        state_ref[...] = state * keep[GROUP - 1 :] + mm_tn(v["keys"], v["values"] * to_end)
        return carry

    lax.fori_loop(first, last, step, 0, unroll=True)


def gate_kernel(plan, *refs):
    n = plan.seq
    normed_ref, y_ref = refs[:2]
    weights = refs[2 : 2 + 2 * plan.line]
    cots = refs[2 + 2 * plan.line : 2 + 2 * plan.line + n]
    gain_ref = refs[2 + 2 * plan.line + n]
    outs = refs[3 + 2 * plan.line + n :]
    wz_ref, z_ref, du_ref, stats_ref = outs[:4]
    parts = outs[4 : 4 + n]
    wf_ref, wo_ref = outs[4 + n :]
    ids = place()
    s, z, c = ids
    half = plan.in_rows * n // 2
    for core_xor in range(2):
        for line_xor in range(plan.line):
            piece = weights[core_xor * plan.line + line_xor]
            for m in range(n):
                dest = pl.ds(in_place(plan, ids, line_xor, core_xor, m), plan.in_rows)
                top = (m // 2) * plan.in_rows
                left = (m % 2) * plan.chan
                wf_ref[dest, :] = piece[
                    top : top + plan.in_rows, left : left + plan.chan
                ].astype(f32)
            start = ((z ^ line_xor) * 2 + (c ^ core_xor)) * plan.out_rows
            wo_ref[pl.ds(aligned(start, 16), plan.out_rows), :] = piece[
                half : half + plan.out_rows, :
            ]
    wz_ref[...] = wf_ref[...].astype(bf16)
    gain = gain_ref[...]
    lane = iota((plan.rows, LANES), 1)
    square = jnp.zeros((GROUP, LANES), f32)
    lane = iota((GROUP, LANES), 1)
    per = plan.rows // GROUP
    for m in range(n):
        start = aligned((s ^ m) * plan.rows, plan.rows)
        gate = jnp.dot(
            normed_ref[pl.ds(start, plan.rows), :], wz_ref[...], preferred_element_type=f32
        )
        z_ref[pl.ds(start, plan.rows), :] = gate
        gated = y_ref[pl.ds(start, plan.rows), :] * gate * sigmoid(gate)
        scaled = gated * gain
        parts[m][...] = mm(scaled, wo_ref[...]).astype(parts[m].dtype)
        du = mm_nt(cots[m][...], wo_ref[...])
        du_ref[pl.ds(start, plan.rows), :] = du
        norm = jnp.sum(gated * gated, axis=1, keepdims=True)
        dots = jnp.sum(du * scaled, axis=1, keepdims=True)
        for j in range(per):
            b = (s ^ m) * per + j
            rows = slice(j * GROUP, (j + 1) * GROUP)
            square = square + jnp.where(lane == b, norm[rows], 0.0)
            square = square + jnp.where(lane == b + plan.blocks, dots[rows], 0.0)
    stats_ref[...] = square.T[: 2 * plan.blocks]


def emit_rows(plan, ids, source_ref, put):
    for core_xor in range(2):
        for line_xor in range(plan.line):
            for m in range(plan.seq):
                rows = source_ref[
                    pl.ds(in_place(plan, ids, line_xor, core_xor, m), plan.in_rows), :
                ]
                put(core_xor, line_xor, m, rows)


def row_products(w_ref, grad_ref):
    lane = iota((LANES, LANES), 1)
    square = jnp.zeros((LANES, LANES), f32)
    for i in range(w_ref.shape[0] // LANES):
        rows = slice(i * LANES, (i + 1) * LANES)
        product = w_ref[rows, :].astype(f32) * grad_ref[rows, :]
        square = square + jnp.where(lane == i, jnp.sum(product, axis=1, keepdims=True), 0.0)
    return square.T[:8]


def regate_kernel(plan, *refs):
    n = plan.seq
    stats = refs[:n]
    normed_ref, y_ref, z_ref, du_ref, wz_ref = refs[n : n + 5]
    cots = refs[n + 5 : 2 * n + 5]
    gain_ref = refs[2 * n + 5]
    dy_ref, dz_ref, scale_ref, gain_out_ref, share_ref, keep_ref, send_ref = refs[
        2 * n + 6 : 2 * n + 13
    ]
    gated_ref, gz_ref, go_ref = refs[2 * n + 13 :]
    ids = place()
    s, z, c = ids
    total = stats[0][...]
    for m in range(1, n):
        total = total + stats[m][...]
    turned = jnp.concatenate(
        [total, jnp.zeros((LANES - total.shape[0], GROUP), f32)], axis=0
    ).T
    gain = gain_ref[...]
    sums = jnp.zeros((1, plan.chan), f32)
    for b in range(plan.blocks):
        rows = slice(b * GROUP, (b + 1) * GROUP)
        r = lax.rsqrt(turned[:, b : b + 1] / INNER + norm_eps)
        dot = turned[:, plan.blocks + b : plan.blocks + b + 1] / INNER
        scale_ref[rows, :] = jnp.broadcast_to(r, (GROUP, LANES))
        gate = z_ref[rows, :]
        sig = sigmoid(gate)
        silu = gate * sig
        y = y_ref[rows, :]
        gated = y * silu
        du = du_ref[rows, :]
        normal = gated * r
        grad_pre = r * (du * gain) - normal * (r * r * dot)
        dy_ref[rows, :] = grad_pre * silu
        dz_ref[rows, :] = (grad_pre * y * sig * (1.0 + gate * (1.0 - sig))).astype(bf16)
        gated_ref[rows, :] = (normal * gain).astype(bf16)
        sums = sums + jnp.sum(du * normal, axis=0, keepdims=True)
    gain_out_ref[...] = sums
    gz_ref[...] = mm_tn(normed_ref[...], dz_ref[...])
    share_ref[...] = row_products(wz_ref, gz_ref)
    out = None
    for m in range(n):
        start = aligned((s ^ m) * plan.rows, plan.rows)
        one = mm_tn(gated_ref[pl.ds(start, plan.rows), :], cots[m][...])
        out = one if out is None else out + one
    go_ref[...] = out
    half = plan.in_rows * n // 2
    both = (keep_ref, send_ref)

    def put(core_xor, line_xor, m, rows):
        top = (m // 2) * plan.in_rows
        left = (m % 2) * plan.chan
        both[core_xor][line_xor, top : top + plan.in_rows, left : left + plan.chan] = rows.astype(
            bf16
        )

    emit_rows(plan, ids, gz_ref, put)
    for core_xor in range(2):
        for line_xor in range(plan.line):
            start = ((z ^ line_xor) * 2 + (c ^ core_xor)) * plan.out_rows
            both[core_xor][line_xor, half : half + plan.out_rows, :] = go_ref[
                pl.ds(aligned(start, 16), plan.out_rows), :
            ].astype(bf16)


def scan_back_kernel(plan, first, last, *refs):
    x_ref, dt_ref, states_ref, segc_ref, segr_ref, dy_ref, conv_ref, heads_ref = refs[:8]
    refs = refs[8:]
    later = last < plan.blocks
    if later:
        before, refs = refs[:5], refs[5:]
    gp_ref, adj_ref, edge_ref, acc_ref, head_ref = refs
    low = first * GROUP
    if later:
        gp_ref[(last - first) * GROUP :, :] = before[0][...]
        adj_ref[...] = before[1][...]
        edge_ref[...] = before[2][...]
        acc_ref[...] = before[3][...]
        head_ref[...] = before[4][...]
    else:
        adj_ref[...] = jnp.zeros_like(adj_ref)
        edge_ref[...] = jnp.zeros_like(edge_ref)
        acc_ref[...] = jnp.zeros_like(acc_ref)
        head_ref[...] = jnp.zeros_like(head_ref)
    convw = conv_ref[0:KERNEL, :]
    convb = conv_ref[KERNEL : KERNEL + 1, :]
    repeat = plan.mixed // LANES
    pick = (iota((plan.chan, LANES), 0) // HEADDIM == iota((plan.chan, LANES), 1)).astype(f32)
    lane = iota((GROUP, LANES), 1)

    def step(turn, carry):
        b = last - 1 - turn
        v = block_values(plan, b, x_ref, segc_ref, segr_ref, dt_ref, convw, convb, heads_ref)
        base = v["base"]
        state = states_ref[b]
        adj = adj_ref[...]
        dy = dy_ref[pl.ds(base, GROUP), :]
        values = v["values"]
        spread = wide(
            jnp.concatenate([v["keep"], v["to_last"] * v["steps"]], axis=0), plan.chan
        )
        keep, to_end = spread[:GROUP], spread[GROUP:]
        kept = dy * keep
        dq = mm_nt(kept, state)
        cross = kept * mm(v["queries"], state)
        fed = mm(v["keys"], adj)
        dk = mm_nt(values * to_end, adj)
        adj_ref[...] = adj * keep[GROUP - 1 :] + mm_tn(v["queries"], kept)
        ended = jnp.sum(state * adj, axis=0, keepdims=True)
        pushed = fed * values
        skipped = jnp.sum(dy * values, axis=0, keepdims=True)
        few = jnp.concatenate([ended, skipped, jnp.zeros((6, plan.chan), f32)], axis=0)
        high = few.astype(bf16).astype(f32)
        sums = mm(jnp.concatenate([cross, pushed, high, few - high], axis=0), pick)
        cross_h = sums[:GROUP]
        pushed_h = sums[GROUP : 2 * GROUP]
        few_h = sums[2 * GROUP : 2 * GROUP + 8] + sums[2 * GROUP + 8 :]
        ended_h = few_h[0:1]
        skipped_h = few_h[1:2]
        grad_steps = pushed_h * v["to_last"]
        pulled = grad_steps * v["steps"]
        dcum = cross_h - pulled
        at_end = jnp.sum(pulled, axis=0, keepdims=True) + v["keep"][GROUP - 1 :] * ended_h
        dscores = jnp.zeros((GROUP, GROUP), f32)
        columns = []
        dvs = []
        for pair in range(plan.heads // 2):
            lanes = slice(pair * LANES, (pair + 1) * LANES)
            dy_pair = split_pair(dy[:, lanes])
            products = mm_nt(dy_pair, values[:, lanes])
            stacked = []
            for j, h in enumerate((2 * pair, 2 * pair + 1)):
                decay = head_decay(v, h)
                steps_row = v["steps_t"][h : h + 1, :]
                weighted = decay * products[j * GROUP : (j + 1) * GROUP]
                direct = weighted * v["scores"]
                dscores = dscores + weighted * steps_row
                rowsum = jnp.sum(direct * steps_row, axis=1, keepdims=True)
                dcum = dcum + jnp.where(lane == h, rowsum, 0.0)
                columns.append(jnp.sum(direct, axis=0, keepdims=True))
                stacked.append(decay * v["scores"] * steps_row)
            dvs.append(mm_tn(jnp.concatenate(stacked, axis=0), dy_pair))
        dv = jnp.concatenate(dvs, axis=1) + fed * to_end + heads_ref[2:3, :] * dy
        columns.append(jnp.zeros((LANES - plan.heads, GROUP), f32))
        down = jnp.concatenate(columns, axis=0).T
        grad_steps = grad_steps + down
        dcum = dcum - down * v["steps"]
        row = iota((GROUP, LANES), 0)
        dcum = dcum + jnp.where(row == GROUP - 1, at_end, 0.0)
        dk = dk + mm_tn(dscores, v["queries"])
        dq = dq + mm(dscores, v["keys"])
        ddecay = mask_mm(iota((GROUP, GROUP), 0) <= iota((GROUP, GROUP), 1), dcum)
        grad_steps = grad_steps - ddecay * jnp.exp(heads_ref[1:2, :LANES])
        grad_dt = grad_steps * sigmoid(v["dt_in"])
        head_ref[0:1, :] += jnp.sum(grad_dt, axis=0, keepdims=True)
        head_ref[1:2, :] += jnp.sum(ddecay * v["decay"], axis=0, keepdims=True)
        head_ref[2:3, :] += skipped_h
        dmixed = jnp.concatenate([dv, dk, dq], axis=1)
        pre, sig = v["pre"], v["sig"]
        dpre = dmixed * (sig * (1.0 + pre * (1.0 - sig)))
        acc_ref[4:5, :] += jnp.sum(dpre, axis=0, keepdims=True)
        longer = jnp.concatenate([dpre, edge_ref[...]], axis=0)
        edge_ref[...] = dpre[:LEAD]
        segn = segc_ref[pl.ds(aligned(base + LEAD, 8), GROUP + LEAD), :]
        dx = jnp.zeros((GROUP, plan.mixed), f32)
        for k in range(KERNEL):
            acc_ref[k : k + 1, :] += jnp.sum(dpre * v["shifts"][k], axis=0, keepdims=True)
            ahead = KERNEL - 1 - k
            part = longer[ahead : ahead + GROUP]
            if ahead:
                same = (segn[ahead : ahead + GROUP] == v["seg"]).astype(f32)
                part = part * jnp.concatenate([same] * repeat, axis=1)
            dx = dx + convw[k : k + 1] * part
        live = jnp.where(lane < plan.heads, grad_dt, 0.0)
        gp_ref[pl.ds(aligned(base - low, GROUP), GROUP), :] = jnp.concatenate([dx, live], axis=1).astype(bf16)
        return carry

    lax.fori_loop(0, last - first, step, 0, unroll=True)


def main_grads_kernel(
    plan, normed_ref, gp_ref, w_ref, gain_ref, share_ref, gain_out_ref, acc_ref, head_ref,
    keep_ref, send_ref, gw_ref, small_ref,
):
    ids = place()
    gw_ref[...] = mm_tn(normed_ref[...], gp_ref[...])
    both = (keep_ref, send_ref)

    def put(core_xor, line_xor, m, rows):
        top = m * plan.in_rows
        both[core_xor][line_xor, top : top + plan.in_rows, :] = rows.astype(bf16)

    emit_rows(plan, ids, gw_ref, put)
    share = share_ref[...] + row_products(w_ref, gw_ref)
    small_ref[...] = jnp.zeros_like(small_ref)
    for i in range(WIDTH // LANES):
        lanes = slice(i * LANES, (i + 1) * LANES)
        small_ref[0:1, lanes] = share[i : i + 1] / gain_ref[:, lanes]
    small_ref[1:6, : plan.mixed] = acc_ref[0:5, :]
    small_ref[6:7, : plan.chan] = gain_out_ref[...]
    for j in range(3):
        small_ref[7:8, j * LANES : (j + 1) * LANES] = head_ref[j : j + 1, :]
    high, low = two_parts(small_ref[...])
    last = plan.seq * plan.in_rows
    for ref in both:
        for line_xor in range(plan.line):
            ref[line_xor, last : last + 8, :] = high
            ref[line_xor, last + 8 : last + 16, :] = low


def normed_grads_kernel(plan, gp_ref, w_ref, dz_ref, wz_ref, *grads):
    s = lax.axis_index("seq")
    for m in range(plan.seq):
        rows = pl.ds(aligned((s ^ m) * plan.rows, plan.rows), plan.rows)
        part = mm_nt(gp_ref[rows, :], w_ref[...]) + mm_nt(dz_ref[rows, :], wz_ref[...])
        grads[m][...] = part.astype(grads[m].dtype)


def joined(ref, top):
    return ref[top : top + 8, :].astype(f32) + ref[top + 8 : top + 16, :].astype(f32)


def main_split_kernel(plan, keep_ref, got_ref, *outs):
    last = plan.seq * plan.in_rows
    small = joined(keep_ref.at[0], last) + joined(got_ref.at[0], last)
    high, low = two_parts(small)
    for m in range(plan.line):
        total = keep_ref[m, :last, :].astype(f32) + got_ref[m, :last, :].astype(f32)
        outs[m][:last, :] = total.astype(bf16)
        outs[m][last : last + 8, :] = high
        outs[m][last + 8 :, :] = low


def gate_split_kernel(plan, keep_ref, got_ref, *outs):
    for m in range(plan.line):
        outs[m][...] = (keep_ref[m].astype(f32) + got_ref[m].astype(f32)).astype(bf16)


def gate_sum_kernel(plan, *refs):
    parts, (gate_ref, out_ref) = refs[: plan.line], refs[plan.line :]
    total = parts[0][...].astype(f32)
    for part in parts[1:]:
        total = total + part[...].astype(f32)
    half = plan.in_rows * plan.seq // 2
    gate_ref[...] = total[:half].astype(bf16)
    out_ref[...] = total[half : half + plan.out_rows]


def row_sum_kernel(plan, gate_ref, *refs):
    parts, outs = refs[: plan.line], refs[plan.line :]
    r, chan = plan.in_rows, plan.chan
    last = plan.seq * r
    small = joined(parts[0], last)
    for part in parts[1:]:
        small = small + joined(part, last)
    high, low = two_parts(small)
    for m in range(plan.seq):
        rows = slice(m * r, (m + 1) * r)
        total = parts[0][rows, :].astype(f32)
        for part in parts[1:]:
            total = total + part[rows, :].astype(f32)
        outs[m][:r, :] = total.astype(bf16)
        outs[m][r : r + 8, :] = high
        outs[m][r + 8 : r + 16, :] = low
        top, left = (m // 2) * r, (m % 2) * chan
        outs[m][r + 16 :, :chan] = gate_ref[top : top + r, left : left + chan]
        outs[m][r + 16 :, chan:] = jnp.zeros((r, plan.cols - chan), bf16)


def columns_kernel(plan, *refs):
    n, r, chan, heads = plan.seq, plan.in_rows, plan.chan, plan.heads
    parts, refs = refs[:n], refs[n:]
    out_ref, gain_in_ref, convw_ref, convb_ref, dtb_ref, alog_ref, skip_ref = refs[:7]
    gain_out_ref, gate_ref, main_ref, small_ref = refs[7:]
    s = lax.axis_index("seq")
    for m in range(n):
        main_ref[m] = parts[m][:r, :].astype(f32)
        small_ref[m] = joined(parts[m], r)
        gate_ref[m] = parts[m][r + 16 :, :chan].astype(f32)
    shared = jnp.zeros((r, 2 * STATE), f32)
    lane = iota((r, LANES), 1)
    dts = jnp.zeros((r, LANES), f32)
    gain_in = jnp.zeros((1, WIDTH), f32)
    small_shared = jnp.zeros((5, 2 * STATE), f32)
    one_lane = iota((1, LANES), 1)
    rows = [jnp.zeros((1, LANES), f32) for _ in range(3)]
    for g in range(n):
        cols = slice(g * chan, (g + 1) * chan)
        out_ref[:, cols] = gate_ref[s ^ g]
        main = main_ref[s ^ g]
        out_ref[:, INNER + g * chan : INNER + (g + 1) * chan] = main[:, :chan]
        shared = shared + main[:, chan : plan.mixed]
        one = main[:, plan.mixed :]
        moved = one if g == 0 else pltpu.roll(one, g * heads, 1)
        dts = jnp.where(lane // heads == g, moved, dts)
        part = small_ref[s ^ g]
        gain_in = gain_in + part[0:1, :WIDTH]
        convw_ref[:, cols] = part[1:5, :chan]
        convb_ref[cols] = part[5, :chan]
        gain_out_ref[cols] = part[6, :chan]
        small_shared = small_shared + part[1:6, chan : plan.mixed]
        for j in range(3):
            one = part[7:8, j * LANES : (j + 1) * LANES]
            moved = one if g == 0 else pltpu.roll(one, g * heads, 1)
            rows[j] = jnp.where(one_lane // heads == g, moved, rows[j])
    out_ref[:, 2 * INNER : INNER + CONV] = shared
    out_ref[:, INNER + CONV :] = dts[:, :HEADS]
    gain_in_ref[...] = gain_in[0]
    convw_ref[:, INNER:] = small_shared[:4]
    convb_ref[INNER:] = small_shared[4]
    dtb_ref[...] = rows[0][:, :HEADS]
    alog_ref[...] = rows[1][:, :HEADS]
    skip_ref[...] = rows[2][:, :HEADS]


def result_kernel(plan, tok_ref, scale_ref, *refs):
    parts, out_ref = refs[: plan.seq], refs[plan.seq]
    s = lax.axis_index("seq")
    total = parts[0][...].astype(f32)
    for part in parts[1:]:
        total = total + part[...].astype(f32)
    r = scale_ref[pl.ds(aligned(s * plan.rows, plan.rows), plan.rows), :]
    r = jnp.concatenate([r] * (WIDTH // LANES), axis=1)
    out_ref[...] = (tok_ref[...].astype(f32) + total * r).astype(bf16)


def token_kernel(plan, tok_ref, cot_ref, gain_ref, *refs):
    parts, out_ref = refs[: plan.seq], refs[plan.seq]
    total = parts[0][...].astype(f32)
    for part in parts[1:]:
        total = total + part[...].astype(f32)
    tok = tok_ref[...].astype(f32)
    q = lax.rsqrt(jnp.mean(tok * tok, axis=1, keepdims=True) + norm_eps)
    w = total * gain_ref[...]
    mean = jnp.mean(w * tok, axis=1, keepdims=True)
    grad = cot_ref[...].astype(f32) + q * w - tok * (q * q * q * mean)
    out_ref[...] = grad.astype(bf16)


def call(body, plan, outs, scratch, *args, mib=4, micros=1, name=None, kept=0):
    shapes = [jax.ShapeDtypeStruct(shape, kind) for shape, kind in outs]
    size = sum(a.size * a.dtype.itemsize for a in args)
    size += sum(a.size * a.dtype.itemsize for a in shapes)
    return pl.pallas_call(
        functools.partial(body, plan),
        out_shape=shapes,
        in_specs=[pl.BlockSpec(memory_space=pltpu.HBM)] * kept
        + [pl.BlockSpec(memory_space=pltpu.VMEM)] * (len(args) - kept),
        out_specs=[pl.BlockSpec(memory_space=pltpu.VMEM)] * len(shapes),
        scratch_shapes=[
            pltpu.VMEM(*one) if isinstance(one, tuple) else one for one in scratch
        ],
        compiler_params=pltpu.CompilerParams(vmem_limit_bytes=mib * 2**20),
        cost_estimate=pl.CostEstimate(
            flops=micros * FLOPS_PER_MICRO, bytes_accessed=size, transcendentals=0
        ),
        name=name,
    )(*args)


FLOPS_PER_MICRO = 1_000_000_000


def swap(value, axis, by):
    size = lax.axis_size(axis)
    return lax.ppermute(value, axis, [(i, i ^ by) for i in range(size)])


def after(value, *others):
    return lax.optimization_barrier((value, *others))[0]


def head_parallel(
    tokens, cotangent, segments, in_weight, out_weight, gain_in, conv_weight, conv_bias,
    dt_bias, a_log, d_skip, gain_out,
):
    rows = tokens.shape[1]
    plan = Plan(
        lax.axis_size("seq"), lax.axis_size("batch"), rows, in_weight.shape[0], out_weight.shape[0]
    )
    n, line, chan, heads = plan.seq, plan.line, plan.chan, plan.heads
    s = lax.axis_index("seq")
    tok, cot = tokens[0], cotangent[0]

    r = plan.in_rows
    own = call(
        pack_kernel, plan, [((r + 8, plan.cols + chan), bf16)] * n,
        [
            (in_weight.shape, bf16), (segments.shape, jnp.int32), pltpu.SemaphoreType.DMA((2,)),
            ((n, r, plan.cols + chan), bf16),
        ],
        in_weight, segments, mib=60, name="pack", kept=2,
    )
    pieces = [own[0]] + [swap(own[m], "seq", m) for m in range(1, n)]
    tok_later = after(tok, *pieces)
    toks = [tok] + [swap(tok_later, "seq", m) for m in range(1, n)]
    main_shard, gate_shard = call(
        regroup_kernel, plan,
        [((n * r, plan.cols), bf16), ((n * r // 2 + plan.out_rows, WIDTH), bf16)], [],
        *pieces, out_weight, name="regroup",
    )

    def along(shard):
        return [shard] + [swap(shard, "batch", 2 * m) for m in range(1, line)]

    def both_cores(parts):
        return parts + [swap(one, "batch", 1) for one in parts]

    main_line = along(main_shard)
    main_parts = both_cores(main_line)
    gate_line = along(after(gate_shard, *main_line))
    cot_near = after(cot, *toks)
    conv, per_head, own_gain = call(
        own_params_kernel, plan,
        [((8, plan.mixed), f32), ((8, chan), f32), ((1, chan), f32)], [],
        conv_weight, conv_bias[None], dt_bias[None], a_log[None], d_skip[None], gain_out[None],
        name="own_params",
    )
    gain_row = gain_in[None]
    total = plan.total
    seg_rows = -(-plan.blocks // 8) * 8
    normed, w_main, x, dt_raw, segc, segr = call(
        project_kernel, plan,
        [
            ((total, WIDTH), bf16), ((WIDTH, plan.cols), bf16),
            ((total + LEAD, plan.mixed), f32), ((total, LANES), f32),
            ((total + 2 * LEAD, LANES), f32), ((seg_rows, GROUP), f32),
        ],
        [((WIDTH, plan.cols), f32)],
        *toks, *pieces, *main_parts, gain_row, mib=16, micros=5, name="project",
    )
    cot_far = after(cot, normed)
    cots = [cot] + [swap(cot_near if m < 3 else cot_far, "seq", m) for m in range(1, n)]
    half = plan.blocks // 2
    state_shape = (STATE, chan)
    scan_in = (x, dt_raw, segc, segr, conv, per_head)

    def scan_part(first, last, *early):
        return call(
            lambda p, *refs: scan_kernel(p, first, last, *refs), plan,
            [((last * GROUP, chan), f32), ((last,) + state_shape, f32), (state_shape, f32)], [],
            *scan_in, *early, mib=12, micros=4, name="scan_forward",
        )

    early = list(scan_part(0, half))
    gate_line = [after(one, early[2]) for one in gate_line]
    gate_parts = both_cores(gate_line)
    early[2] = after(early[2], *gate_line, *cots[1:3])
    y, states, _ = scan_part(half, plan.blocks, *early)
    piece_shape = (rows, WIDTH)
    w_gate, z, du, stats, *outs = call(
        gate_kernel, plan,
        [
            ((WIDTH, chan), bf16), ((total, chan), f32), ((total, chan), f32),
            ((2 * plan.blocks, GROUP), f32),
        ] + [(piece_shape, bf16)] * n,
        [((WIDTH, chan), f32), ((chan, WIDTH), bf16)],
        normed, y, *gate_parts, *cots, own_gain,
        mib=16, micros=6, name="gate_forward",
    )
    all_stats = [stats] + [swap(stats, "seq", m) for m in range(1, n)]
    dy, dz, scale, gain_out_grad, share, keep, send = call(
        regate_kernel, plan,
        [
            ((total, chan), f32), ((total, chan), bf16), ((total, LANES), f32), ((1, chan), f32),
            ((8, LANES), f32),
            ((line, n * r // 2 + plan.out_rows, WIDTH), bf16),
            ((line, n * r // 2 + plan.out_rows, WIDTH), bf16),
        ],
        [((total, chan), bf16), ((WIDTH, chan), f32), ((chan, WIDTH), f32)],
        *all_stats, normed, y, z, du, w_gate, *cots, own_gain,
        mib=16, micros=6, name="gate_backward",
    )

    def reduce_line(keep, send, body, name):
        got = swap(send, "batch", 1)
        parts = call(
            body, plan, [(keep.shape[1:], bf16)] * line, [], keep, got, name=name,
        )
        return list(parts)

    def line_exchange(parts):
        return [parts[0]] + [swap(parts[m], "batch", 2 * m) for m in range(1, line)]

    gate_half = reduce_line(keep, send, gate_split_kernel, "gate_core_sum")
    dy = after(dy, *gate_half)
    back_in = (x, dt_raw, states, segc, segr, dy, conv, per_head)

    def scan_back_part(first, last, *before):
        return call(
            lambda p, *refs: scan_back_kernel(p, first, last, *refs), plan,
            [
                ((total - first * GROUP, plan.cols), bf16), (state_shape, f32),
                ((LEAD, plan.mixed), f32), ((8, plan.mixed), f32), ((8, LANES), f32),
            ], [],
            *back_in, *before, mib=16, micros=10, name="scan_backward",
        )

    before = list(scan_back_part(half, plan.blocks))
    out_parts = [outs[0]] + [swap(outs[m], "seq", m) for m in range(1, n)]
    gate_half[-1] = after(gate_half[-1], before[1])
    gate_lines = line_exchange(gate_half)
    gate_rows, shard_out = call(
        gate_sum_kernel, plan,
        [((n * r // 2, WIDTH), bf16), ((plan.out_rows, WIDTH), f32)], [], *gate_lines,
        name="gate_sum",
    )
    before[1] = after(before[1], *gate_lines[:-1])
    gp, _, _, acc, head_acc = scan_back_part(0, half, *before)
    (result,) = call(
        result_kernel, plan, [(piece_shape, bf16)], [], tok, scale, *out_parts, name="result"
    )

    grads = call(
        normed_grads_kernel, plan, [(piece_shape, bf16)] * n, [], gp, w_main, dz, w_gate,
        mib=12, micros=3, name="normed_grads",
    )
    gp_late = after(gp, *out_parts, *gate_lines, *grads)
    keep, send = call(
        main_grads_kernel, plan, [((line, n * r + 16, plan.cols), bf16)] * 2,
        [((WIDTH, plan.cols), f32), ((8, plan.cols), f32)],
        normed, gp_late, w_main, gain_row, share, gain_out_grad, acc, head_acc,
        mib=12, micros=4, name="main_grads",
    )
    main_half = reduce_line(keep, send, main_split_kernel, "main_core_sum")
    main_lines = line_exchange(main_half)
    grad_parts = [grads[0]] + [swap(grads[m], "seq", m) for m in range(1, n)]
    last = call(
        row_sum_kernel, plan, [((2 * r + 16, plan.cols), bf16)] * n, [], gate_rows, *main_lines,
        name="main_sum",
    )
    last = [last[0]] + [swap(last[m], "seq", m) for m in range(1, n)]
    (grad_tokens,) = call(
        token_kernel, plan, [(piece_shape, bf16)], [], tok, cot, gain_row, *grad_parts,
        name="token_grad",
    )
    shard_in, *smalls = call(
        columns_kernel, plan,
        [
            ((r, in_weight.shape[1]), f32),
            ((WIDTH,), f32), ((KERNEL, CONV), f32), ((CONV,), f32), ((1, HEADS), f32),
            ((1, HEADS), f32), ((1, HEADS), f32), ((INNER,), f32),
        ],
        [((n, r, chan), f32), ((n, r, plan.cols), f32), ((n, 8, plan.cols), f32)],
        *last, name="columns",
    )
    return (
        result[None], grad_tokens[None], shard_in, shard_out, smalls[0], smalls[1],
        smalls[2], smalls[3][0], smalls[4][0], smalls[5][0], smalls[6],
    )


def shifted(value, axis, by):
    size = lax.axis_size(axis)
    pairs = [(i, i + by) for i in range(size) if 0 <= i + by < size]
    return lax.ppermute(value, axis, pairs)


def prefix(value, axis, join, neutral):
    place = lax.axis_index(axis)
    gathered = jax.tree.map(
        lambda a, kind: lax.all_gather(a.astype(kind), axis), value, (jnp.bfloat16, jnp.bfloat16)
    )
    state = jax.tree.map(lambda a, e: jnp.zeros_like(a) + jnp.asarray(e, a.dtype), value, neutral)

    def one(turn, state):
        return join(
            state,
            jax.tree.map(
                lambda a, own: lax.dynamic_index_in_dim(a, turn, 0, False).astype(own.dtype),
                gathered,
                value,
            ),
        )

    return lax.fori_loop(0, place, one, state)


def prefix_2(value, axis, join, neutral):
    count = lax.axis_size(axis)
    place = lax.axis_index(axis)
    ahead = count - 1 - place
    gathered = jax.tree.map(
        lambda a, kind: lax.all_gather(a.astype(kind), axis),
        value,
        jax.tree.map(lambda a: jnp.bfloat16 if a.dtype == jnp.float32 else a.dtype, value),
    )
    state = jax.tree.map(lambda a, e: jnp.zeros_like(a) + jnp.asarray(e, a.dtype), value, neutral)

    def one(turn, state):
        source = count - 1 - turn
        return join(
            state,
            jax.tree.map(
                lambda a, own: lax.dynamic_index_in_dim(a, source, 0, False).astype(own.dtype),
                gathered,
                value,
            ),
        )

    return lax.fori_loop(0, ahead, one, state)


def rms_scale(values, gain):
    mean_square = jnp.mean(values * values, axis=-1, keepdims=True)
    return values * lax.rsqrt(mean_square + norm_eps) * gain


def causal_conv(extended, ext_segs, conv_weight, conv_bias, row_count):
    target = ext_segs[KERNEL - 1 :]
    total = jnp.zeros((row_count, conv_weight.shape[1]), jnp.float32) + conv_bias[None, :]
    for offset in range(KERNEL):
        window = extended[offset : offset + row_count]
        same_doc = (ext_segs[offset : offset + row_count] == target).astype(jnp.float32)
        total = total + conv_weight[offset][None, :] * window * same_doc[:, None]
    return jax.nn.silu(total)


def prepare(xbc, dt_raw, edge_rows, ext_segs, conv_weight, conv_bias, dt_bias, a_log):
    row_count = xbc.shape[0]
    extended = jnp.concatenate([edge_rows, xbc], axis=0)
    mixed = causal_conv(extended, ext_segs, conv_weight, conv_bias, row_count)
    values = mixed[:, :INNER].reshape(row_count, HEADS, HEADDIM)
    key_vecs = mixed[:, INNER : INNER + STATE]
    queries = mixed[:, INNER + STATE :]
    step_sizes = jax.nn.softplus(dt_raw + dt_bias[None, :])
    log_decay = -step_sizes * jnp.exp(a_log)[None, :]
    return (values, key_vecs, queries, step_sizes, log_decay)


def group_block(carried, block_in):
    state_in, last_seg = carried
    values, key_vecs, queries, step_sizes, log_decay, seg_ids = block_in
    length_here = seg_ids.shape[0]
    cumulative = jnp.cumsum(log_decay, axis=0)
    positions = jnp.arange(length_here)
    allowed = (seg_ids[:, None] == seg_ids[None, :]) & (positions[:, None] >= positions[None, :])
    gap_logs = cumulative[:, None, :] - cumulative[None, :, :]
    decay_mask = jnp.where(allowed[:, :, None], jnp.exp(jnp.minimum(gap_logs, 0.0)), 0.0)
    scores = jnp.dot(queries, key_vecs.T, precision=highest)
    weights = decay_mask * scores[:, :, None] * step_sizes[None, :, :]
    inside = jnp.einsum("tsh,shp->thp", weights, values, precision=highest)
    keep_factor = jnp.where((seg_ids == last_seg)[:, None], jnp.exp(cumulative), 0.0)
    carried_out = (
        jnp.einsum("tn,hpn->thp", queries, state_in, precision=highest) * keep_factor[:, :, None]
    )
    to_end = (
        jnp.where(
            (seg_ids == seg_ids[-1])[:, None], jnp.exp(cumulative[-1][None, :] - cumulative), 0.0
        )
        * step_sizes
    )
    fresh_state = jnp.einsum("sh,shp,sn->hpn", to_end, values, key_vecs, precision=highest)
    new_state = state_in * keep_factor[-1][:, None, None] + fresh_state
    return ((new_state, seg_ids[-1]), inside + carried_out)


def grouped_ssd(
    values, key_vecs, queries, step_sizes, log_decay, seg_ids, d_skip, state_in, last_seg
):
    row_count = seg_ids.shape[0]
    block_count = row_count // GROUP

    def blocked(member):
        return member.reshape((block_count, GROUP) + member.shape[1:])

    inputs = (
        blocked(values),
        blocked(key_vecs),
        blocked(queries),
        blocked(step_sizes),
        blocked(log_decay),
        blocked(seg_ids),
    )
    (final_state, last_out), outputs = lax.scan(
        jax.checkpoint(group_block), (state_in, last_seg), inputs
    )
    outputs = outputs.reshape(row_count, HEADS, HEADDIM) + d_skip[None, :, None] * values
    return (outputs, final_state)


def gated_norm(mixed_out, gate_z, gain_out):
    return rms_scale(mixed_out * jax.nn.silu(gate_z), gain_out)


def chain_combine(earlier, later):
    decay_early, state_early = earlier
    decay_late, state_late = later
    return (decay_early * decay_late, decay_late[:, None, None] * state_early + state_late)


def cross_term(queries, log_decay, state_in, seg_ids, prev_seg):
    cumulative = jnp.cumsum(log_decay, axis=0)
    keep_factor = jnp.where((seg_ids == prev_seg)[:, None], jnp.exp(cumulative), 0.0)
    return jnp.einsum("tn,hpn->thp", queries, state_in, precision=highest) * keep_factor[:, :, None]


def device_decay(log_decay, seg_ids, prev_seg):
    total_log = jnp.sum(log_decay, axis=0)
    return jnp.where(seg_ids[-1] == prev_seg, jnp.exp(total_log), 0.0)


def on_device(
    tokens,
    cotangent,
    segments,
    in_weight,
    out_weight,
    gain_in,
    conv_weight,
    conv_bias,
    dt_bias,
    a_log,
    d_skip,
    gain_out,
):
    tokens_f = tokens[0].astype(jnp.float32)
    cot_low = cotangent[0]
    seg_ids = segments[0]
    row_count = seg_ids.shape[0]
    full_in, full_out = (
        lax.all_gather(in_weight, ("seq", "batch"), axis=0, tiled=True),
        lax.all_gather(out_weight, ("seq", "batch"), axis=0, tiled=True),
    )
    normed, norm_pull = jax.vjp(rms_scale, tokens_f, gain_in)
    normed_low = normed.astype(jnp.bfloat16)
    projected = jnp.dot(normed_low, full_in, preferred_element_type=jnp.float32)
    gate_z = projected[:, :INNER]
    xbc = projected[:, INNER : INNER + CONV]
    dt_raw = projected[:, INNER + CONV :]
    tail_start = row_count - KERNEL + 1
    edge_rows, edge_segs = shifted(
        (xbc[tail_start:], seg_ids[tail_start:].astype(jnp.float32)), "seq", 1
    )
    prev_segs = edge_segs.astype(jnp.int32)
    prev_seg = prev_segs[KERNEL - 2]
    ext_segs = jnp.concatenate([prev_segs, seg_ids])

    def prepare_local(xbc_in, dt_in, edge_in, weight_in, bias_in, shift_in, alog_in):
        return prepare(xbc_in, dt_in, edge_in, ext_segs, weight_in, bias_in, shift_in, alog_in)

    prepared, prepare_pull = jax.vjp(
        prepare_local, xbc, dt_raw, edge_rows, conv_weight, conv_bias, dt_bias, a_log
    )
    values, key_vecs, queries, step_sizes, log_decay = prepared
    zeros_state = jnp.zeros((HEADS, HEADDIM, STATE), jnp.float32)

    def local_ssd(values_in, keys_in, queries_in, sizes_in, logs_in, skip_in):
        return grouped_ssd(
            values_in,
            keys_in,
            queries_in,
            sizes_in,
            logs_in,
            seg_ids,
            skip_in,
            zeros_state,
            seg_ids[0],
        )

    (local_out, local_state), ssd_pull = jax.vjp(
        local_ssd, values, key_vecs, queries, step_sizes, log_decay, d_skip
    )

    def decay_local(logs_in):
        return device_decay(logs_in, seg_ids, prev_seg)

    decay_here, decay_pull = jax.vjp(decay_local, log_decay)
    identity = (jnp.ones((HEADS,), jnp.float32), zeros_state)
    decay_prefix, state_in = prefix((decay_here, local_state), "seq", chain_combine, identity)

    def cross_local(queries_in, logs_in, state_arg):
        return cross_term(queries_in, logs_in, state_arg, seg_ids, prev_seg)

    cross_out, cross_pull = jax.vjp(cross_local, queries, log_decay, state_in)
    mixed_out = (local_out + cross_out).reshape(row_count, INNER)
    gated, gated_pull = jax.vjp(gated_norm, mixed_out, gate_z, gain_out)
    gated_low = gated.astype(jnp.bfloat16)
    result = tokens_f + jnp.dot(gated_low, full_out, preferred_element_type=jnp.float32)
    back_in, back_out = (
        lax.all_gather(in_weight, ("seq", "batch"), axis=0, tiled=True),
        lax.all_gather(out_weight, ("seq", "batch"), axis=0, tiled=True),
    )
    contract_last = (((1,), (1,)), ((), ()))
    contract_first = (((0,), (0,)), ((), ()))
    grad_gated = lax.dot_general(
        cot_low, back_out, contract_last, preferred_element_type=jnp.float32
    )
    grad_mixed, grad_gate, grad_gain_out = gated_pull(grad_gated)
    grad_mixed = grad_mixed.reshape(row_count, HEADS, HEADDIM)
    grad_q_cross, grad_log_cross, grad_state_in = cross_pull(grad_mixed)
    decay_after, grad_exit = prefix_2((decay_here, grad_state_in), "seq", chain_combine, identity)
    grad_decay = jnp.sum(grad_exit * state_in, axis=(1, 2))
    grad_log_dev = decay_pull(grad_decay)[0]
    grad_values, grad_keys, grad_q_local, grad_sizes, grad_log_local, grad_skip = ssd_pull(
        (grad_mixed, grad_exit)
    )
    prep_grads = prepare_pull(
        (
            grad_values,
            grad_keys,
            grad_q_local + grad_q_cross,
            grad_sizes,
            grad_log_local + grad_log_cross + grad_log_dev,
        )
    )
    grad_xbc, grad_dt, grad_edge, grad_conv_w, grad_conv_b, grad_dt_bias, grad_a_log = prep_grads
    grad_next = shifted(grad_edge, "seq", -1)
    grad_xbc = grad_xbc.at[tail_start:].add(grad_next)
    grad_proj = jnp.concatenate([grad_gate, grad_xbc, grad_dt], axis=1).astype(jnp.bfloat16)
    grad_normed = lax.dot_general(
        grad_proj, back_in, contract_last, preferred_element_type=jnp.float32
    )
    grad_tokens_norm, grad_gain_in = norm_pull(grad_normed)
    grad_tokens = (cot_low.astype(jnp.float32) + grad_tokens_norm).astype(jnp.bfloat16)
    grad_in_w = lax.dot_general(
        normed_low, grad_proj, contract_first, preferred_element_type=jnp.float32
    )
    grad_out_w = lax.dot_general(
        gated_low, cot_low, contract_first, preferred_element_type=jnp.float32
    )
    shard_in, shard_out = (
        lax.psum_scatter(grad_in_w, ("seq", "batch"), scatter_dimension=0, tiled=True),
        lax.psum_scatter(grad_out_w, ("seq", "batch"), scatter_dimension=0, tiled=True),
    )
    summed = lax.psum(
        (
            grad_gain_in,
            grad_conv_w,
            grad_conv_b,
            grad_dt_bias,
            grad_a_log,
            grad_skip,
            grad_gain_out,
        ),
        ("seq", "batch"),
    )
    return (
        result.astype(jnp.bfloat16)[None],
        grad_tokens[None],
        shard_in,
        shard_out,
        summed[0],
        summed[1],
        summed[2],
        summed[3],
        summed[4],
        summed[5],
        summed[6],
    )


def solution(mesh):
    in_specs = (
        P("batch", "seq", None),
        P("batch", "seq", None),
        P("batch", "seq"),
        P(("seq", "batch"), None),
        P(("seq", "batch"), None),
        P(),
        P(),
        P(),
        P(),
        P(),
        P(),
        P(),
    )
    out_specs = (
        P("batch", "seq", None),
        P("batch", "seq", None),
        P(("seq", "batch"), None),
        P(("seq", "batch"), None),
        P(),
        P(),
        P(),
        P(),
        P(),
        P(),
        P(),
    )
    count = mesh.shape["seq"]
    even = HEADS % (2 * count) == 0 and count & (count - 1) == 0
    return jax.shard_map(
        head_parallel if even else on_device, mesh=mesh, in_specs=in_specs, out_specs=out_specs, check_vma=False
    )
```

```python
import functools

import jax
import jax.numpy as jnp
from jax import lax
from jax.experimental import pallas as pl
from jax.experimental.pallas import tpu as pltpu
from jax.sharding import PartitionSpec as P

HEADS = 24
HEADDIM = 64
STATE = 128
KERNEL = 4
GROUP = 128
INNER = 1536
CONV = 1792
WIDTH = 768
LANES = 128
LEAD = 8
TINY = 1e-37


highest = lax.Precision.HIGHEST
norm_eps = 1e-05
f32 = jnp.float32
bf16 = jnp.bfloat16
contract_last = (((1,), (1,)), ((), ()))
contract_first = (((0,), (0,)), ((), ()))


def mm(a, b):
    return jnp.dot(a.astype(bf16), b.astype(bf16), preferred_element_type=f32)


def mm_nt(a, b):
    return lax.dot_general(
        a.astype(bf16), b.astype(bf16), contract_last, preferred_element_type=f32
    )


def mm_tn(a, b):
    return lax.dot_general(
        a.astype(bf16), b.astype(bf16), contract_first, preferred_element_type=f32
    )


def two_parts(value):
    high = value.astype(bf16)
    return high, (value - high.astype(f32)).astype(bf16)


def mask_mm(mask, value):
    width = value.shape[1]
    out = mm(mask, jnp.concatenate(two_parts(value), axis=1))
    return out[:, :width] + out[:, width:]


def iota(shape, dim):
    return lax.broadcasted_iota(jnp.int32, shape, dim)


def aligned(value, unit):
    return pl.multiple_of(value, unit)


def wide(columns, chan):
    half = LANES // 2
    high, low = two_parts(columns)
    low = pltpu.roll(low.astype(f32), half, 1)
    both = jnp.where(iota(columns.shape, 1) < half, high.astype(f32), low)
    spread = iota((LANES, chan), 1) // HEADDIM == lax.rem(iota((LANES, chan), 0), half)
    return mm(both, spread.astype(f32))


def softplus(value):
    return jnp.maximum(value, 0.0) + jnp.log1p(jnp.exp(-jnp.abs(value)))


def sigmoid(value):
    return 0.5 + 0.5 * jnp.tanh(0.5 * value)


class Plan:
    def __init__(self, mesh_seq, mesh_batch, rows, in_rows, out_rows):
        self.seq = mesh_seq
        self.batch = mesh_batch
        self.line = mesh_batch // 2
        self.rows = rows
        self.total = rows * mesh_seq
        self.blocks = self.total // GROUP
        self.heads = HEADS // mesh_seq
        self.chan = self.heads * HEADDIM
        self.mixed = self.chan + 2 * STATE
        self.cols = self.mixed + LANES
        self.in_rows = in_rows
        self.out_rows = out_rows


def place():
    s = lax.axis_index("seq")
    b = lax.axis_index("batch")
    return s, lax.shift_right_logical(b, 1), lax.bitwise_and(b, 1)


def in_place(plan, ids, line_xor, core_xor, seq_xor):
    s, z, c = ids
    owner = (s ^ seq_xor) * plan.batch + (z ^ line_xor) * 2 + (c ^ core_xor)
    return aligned(owner * plan.in_rows, 8)


def exact_sigmoid(value):
    return 1.0 / (1.0 + jnp.exp(-value))


def convolved(plan, base, x_ref, segc_ref, convw, convb):
    win = x_ref[pl.ds(base, GROUP + LEAD), :]
    segw = segc_ref[pl.ds(base, GROUP + LEAD), :]
    seg = segw[LEAD:]
    pre = convb + convw[KERNEL - 1 : KERNEL] * win[LEAD:]
    for k in range(KERNEL - 1):
        start = LEAD - KERNEL + 1 + k
        same = (segw[start : start + GROUP] == seg).astype(f32)
        same = jnp.concatenate([same] * (plan.mixed // LANES), axis=1)
        pre = pre + convw[k : k + 1] * win[start : start + GROUP] * same
    sig = sigmoid(pre)
    mixed = pre * sig
    return mixed, sig + mixed * (1.0 - sig)


def decays(dt_in, heads_ref):
    steps = softplus(dt_in)
    row = iota((GROUP, GROUP), 0)
    col = iota((GROUP, GROUP), 1)
    decay = -steps * jnp.exp(heads_ref[1:2, :LANES])
    cum = mask_mm(row >= col, decay)
    half = LANES // 2
    turned = jnp.where(col < half, cum, pltpu.roll(steps, half, 1)).T
    return steps, cum, turned


def edges(segc_ref, base, cum):
    seg = segc_ref[pl.ds(aligned(base + LEAD, 8), GROUP), :]
    prev = segc_ref[pl.ds(base, LEAD), :][LEAD - 1 :]
    keep = jnp.where(seg == prev, jnp.exp(cum), 0.0)
    last = cum[GROUP - 1 :]
    to_last = jnp.where(seg == seg[GROUP - 1 :], jnp.exp(last - cum), 0.0)
    return seg, keep, to_last


def head_decay(cum, turned, h):
    return jnp.exp(jnp.minimum(cum[:, h : h + 1] - turned[h : h + 1, :], 0.0))


def split_pair(pair):
    low = iota(pair.shape, 1) < HEADDIM
    return jnp.concatenate([jnp.where(low, pair, 0.0), jnp.where(low, 0.0, pair)], axis=0)


def fetch(pairs, sems):
    copies = [
        pltpu.make_async_copy(src, dst, sems.at[i]) for i, (src, dst) in enumerate(pairs)
    ]
    for copy in copies:
        copy.start()
    for copy in copies:
        copy.wait()


def pack_kernel(plan, w_any, seg_any, *outs):
    n, heads, chan = plan.seq, plan.heads, plan.chan
    blocks, outs = outs[:n], outs[n:]
    w_ref, seg_ref, sems, all_ref = outs
    fetch([(w_any, w_ref), (seg_any, seg_ref)], sems)
    s = lax.axis_index("seq")
    lane = iota((plan.in_rows, LANES), 1)
    tail = w_ref[:, INNER + CONV :].astype(f32)
    tail = jnp.concatenate(
        [tail, jnp.zeros((plan.in_rows, LANES - HEADS), f32)], axis=1
    )
    for g in range(n):
        moved = tail if g == 0 else pltpu.roll(tail, LANES - g * heads, 1)
        all_ref[g] = jnp.concatenate(
            [
                w_ref[:, INNER + g * chan : INNER + (g + 1) * chan],
                w_ref[:, 2 * INNER : INNER + CONV],
                jnp.where(lane < heads, moved, 0.0).astype(bf16),
                w_ref[:, g * chan : (g + 1) * chan],
            ],
            axis=1,
        )
    seg = jnp.broadcast_to(seg_ref[...].astype(f32), (8, plan.rows)).astype(bf16)
    for m in range(n):
        blocks[m][0 : plan.in_rows, :] = all_ref[s ^ m]
        blocks[m][plan.in_rows : plan.in_rows + 8, :] = jnp.zeros((8, plan.cols + chan), bf16)
        blocks[m][plan.in_rows : plan.in_rows + 8, : plan.rows] = seg


def own_params_kernel(
    plan, convw_ref, convb_ref, dtb_ref, alog_ref, skip_ref, gain_ref, conv_ref, heads_ref,
    own_gain_ref,
):
    n, heads, chan = plan.seq, plan.heads, plan.chan
    s = lax.axis_index("seq")
    own = pl.ds(aligned(s * chan, LANES), chan)
    conv_ref[...] = jnp.zeros_like(conv_ref)
    conv_ref[0:KERNEL, :chan] = convw_ref[:, own]
    conv_ref[0:KERNEL, chan:] = convw_ref[:, INNER:]
    conv_ref[KERNEL : KERNEL + 1, :chan] = convb_ref[:, own]
    conv_ref[KERNEL : KERNEL + 1, chan:] = convb_ref[:, INNER:]
    own_gain_ref[...] = gain_ref[:, own]
    one_lane = iota((1, LANES), 1)

    def own_heads(ref):
        row = jnp.concatenate([ref[...], jnp.zeros((1, LANES - HEADS), f32)], axis=1)
        found = row
        for g in range(1, n):
            found = jnp.where(s == g, pltpu.roll(row, LANES - g * heads, 1), found)
        return jnp.where(one_lane < heads, found, 0.0)

    heads_ref[...] = jnp.zeros_like(heads_ref)
    heads_ref[0:1, :LANES] = own_heads(dtb_ref)
    heads_ref[1:2, :LANES] = own_heads(alog_ref)
    skip = jnp.broadcast_to(own_heads(skip_ref), (8, LANES))
    heads_ref[2:3, :] = wide(skip, chan)[0:1]


def regroup_kernel(plan, *refs):
    n, r = plan.seq, plan.in_rows
    pieces, out_w_ref = refs[:n], refs[n]
    main_ref, gate_ref = refs[n + 1 :]
    half = r * n // 2
    for m in range(n):
        main_ref[m * r : (m + 1) * r, :] = pieces[m][0:r, : plan.cols]
        top, left = (m // 2) * r, (m % 2) * plan.chan
        gate_ref[top : top + r, left : left + plan.chan] = pieces[m][0:r, plan.cols :]
    gate_ref[half : half + plan.out_rows, :] = out_w_ref[...]


def fill_segments(plan, s, pieces, segc_ref, segr_ref):
    per = plan.rows // GROUP
    segc_ref[...] = jnp.zeros_like(segc_ref)
    segr_ref[...] = jnp.zeros_like(segr_ref)
    for m in range(plan.seq):
        line = pieces[m][plan.in_rows : plan.in_rows + 1, : plan.rows].astype(f32)
        for j in range(per):
            b = (s ^ m) * per + j
            segr_ref[pl.ds(b, 1), :] = line[:, j * GROUP : (j + 1) * GROUP]
    every = segr_ref[...]
    turned = jnp.concatenate(
        [every, jnp.zeros((LANES - every.shape[0], GROUP), f32)], axis=0
    ).T
    for b in range(plan.blocks):
        segc_ref[LEAD + b * GROUP : LEAD + (b + 1) * GROUP, :] = jnp.broadcast_to(
            turned[:, b : b + 1], (GROUP, LANES)
        )


def project_kernel(plan, *refs):
    n = plan.seq
    toks, refs = refs[:n], refs[n:]
    pieces, refs = refs[:n], refs[n:]
    weights, refs = refs[: 2 * plan.line], refs[2 * plan.line :]
    gain_ref = refs[0]
    normed_ref, w_ref, x_ref, dt_ref, segc_ref, segr_ref, wf_ref = refs[1:]
    ids = place()
    s = ids[0]
    fill_segments(plan, s, pieces, segc_ref, segr_ref)
    for core_xor in range(2):
        for line_xor in range(plan.line):
            piece = weights[core_xor * plan.line + line_xor]
            for m in range(n):
                dest = pl.ds(in_place(plan, ids, line_xor, core_xor, m), plan.in_rows)
                wf_ref[dest, :] = piece[m * plan.in_rows : (m + 1) * plan.in_rows, :].astype(f32)
    w_ref[...] = wf_ref[...].astype(bf16)
    x_ref[0:LEAD, :] = jnp.zeros((LEAD, plan.mixed), f32)
    for m in range(n):
        tok = toks[m][...].astype(f32)
        scale = lax.rsqrt(jnp.mean(tok * tok, axis=1, keepdims=True) + norm_eps)
        low = (tok * scale * gain_ref[...]).astype(bf16)
        start = (s ^ m) * plan.rows
        normed_ref[pl.ds(aligned(start, plan.rows), plan.rows), :] = low
        out = jnp.dot(low, w_ref[...], preferred_element_type=f32)
        x_ref[pl.ds(aligned(start + LEAD, 8), plan.rows), :] = out[:, : plan.mixed]
        dt_ref[pl.ds(aligned(start, plan.rows), plan.rows), :] = out[:, plan.mixed :]


def scan_kernel(plan, first, last, *refs):
    x_ref, dt_ref, segc_ref, segr_ref, conv_ref, heads_ref = refs[:6]
    refs = refs[6:]
    if first:
        early_y_ref, early_ref = refs[:2]
        refs = refs[2:]
    y_ref, state_ref, states_ref, mixed_ref, slope_ref, table_ref, scores_ref = refs
    if first:
        y_ref[: first * GROUP, :] = early_y_ref[...]
        state_ref[...] = early_ref[...]
    else:
        state_ref[...] = jnp.zeros_like(state_ref)
    convw = conv_ref[0:KERNEL, :]
    convb = conv_ref[KERNEL : KERNEL + 1, :]
    chan, half = plan.chan, LANES // 2
    causal = iota((GROUP, GROUP), 0) >= iota((GROUP, GROUP), 1)

    def step(turn, carry):
        base = aligned((first + turn) * GROUP, GROUP)
        here = pl.ds(aligned(turn * GROUP, GROUP), GROUP)
        mixed, slope = convolved(plan, base, x_ref, segc_ref, convw, convb)
        mixed_ref[here, :] = mixed
        slope_ref[here, :] = slope
        values = mixed[:, :chan]
        keys = mixed[:, chan : chan + STATE]
        queries = mixed[:, chan + STATE :]
        dt_in = dt_ref[pl.ds(base, GROUP), :] + heads_ref[0:1, :LANES]
        steps, cum, turned = decays(dt_in, heads_ref)
        table_ref[0, here, :] = steps
        table_ref[1, here, :] = cum
        table_ref[2, here, :] = turned
        seg, keep, to_last = edges(segc_ref, base, cum)
        allowed = (seg == segr_ref[pl.ds(first + turn, 1), :]) & causal
        scores = jnp.where(allowed, mm_nt(queries, keys), 0.0)
        scores_ref[here, :] = scores
        state = state_ref[...]
        states_ref[turn] = state
        parts = []
        for pair in range(plan.heads // 2):
            lanes = slice(pair * LANES, (pair + 1) * LANES)
            weights_pair = []
            for h in (2 * pair, 2 * pair + 1):
                decay = head_decay(cum, turned, h)
                weights_pair.append(decay * scores * turned[half + h : half + h + 1, :])
            parts.append(mm(jnp.concatenate(weights_pair, axis=1), split_pair(values[:, lanes])))
        inside = jnp.concatenate(parts, axis=1)
        spread = wide(jnp.concatenate([keep, to_last * steps], axis=0), chan)
        keep, to_end = spread[:GROUP], spread[GROUP:]
        carried = mm(queries, state) * keep
        y_ref[pl.ds(base, GROUP), :] = inside + carried + heads_ref[2:3, :] * values
        state_ref[...] = state * keep[GROUP - 1 :] + mm_tn(keys, values * to_end)
        return carry

    lax.fori_loop(0, last - first, step, 0, unroll=True)


def gate_kernel(plan, *refs):
    n = plan.seq
    normed_ref, y_ref = refs[:2]
    weights = refs[2 : 2 + 2 * plan.line]
    cots = refs[2 + 2 * plan.line : 2 + 2 * plan.line + n]
    gain_ref = refs[2 + 2 * plan.line + n]
    outs = refs[3 + 2 * plan.line + n :]
    wz_ref, z_ref, du_ref, stats_ref = outs[:4]
    parts = outs[4 : 4 + n]
    wf_ref, wo_ref = outs[4 + n :]
    ids = place()
    s, z, c = ids
    half = plan.in_rows * n // 2
    for core_xor in range(2):
        for line_xor in range(plan.line):
            piece = weights[core_xor * plan.line + line_xor]
            for m in range(n):
                dest = pl.ds(in_place(plan, ids, line_xor, core_xor, m), plan.in_rows)
                top = (m // 2) * plan.in_rows
                left = (m % 2) * plan.chan
                wf_ref[dest, :] = piece[
                    top : top + plan.in_rows, left : left + plan.chan
                ].astype(f32)
            start = ((z ^ line_xor) * 2 + (c ^ core_xor)) * plan.out_rows
            wo_ref[pl.ds(aligned(start, 16), plan.out_rows), :] = piece[
                half : half + plan.out_rows, :
            ]
    wz_ref[...] = wf_ref[...].astype(bf16)
    gain = gain_ref[...]
    lane = iota((plan.rows, LANES), 1)
    square = jnp.zeros((GROUP, LANES), f32)
    lane = iota((GROUP, LANES), 1)
    per = plan.rows // GROUP
    for m in range(n):
        start = aligned((s ^ m) * plan.rows, plan.rows)
        gate = jnp.dot(
            normed_ref[pl.ds(start, plan.rows), :], wz_ref[...], preferred_element_type=f32
        )
        z_ref[pl.ds(start, plan.rows), :] = gate
        gated = y_ref[pl.ds(start, plan.rows), :] * gate * sigmoid(gate)
        scaled = gated * gain
        parts[m][...] = mm(scaled, wo_ref[...]).astype(parts[m].dtype)
        du = mm_nt(cots[m][...], wo_ref[...])
        du_ref[pl.ds(start, plan.rows), :] = du
        norm = jnp.sum(gated * gated, axis=1, keepdims=True)
        dots = jnp.sum(du * scaled, axis=1, keepdims=True)
        for j in range(per):
            b = (s ^ m) * per + j
            rows = slice(j * GROUP, (j + 1) * GROUP)
            square = square + jnp.where(lane == b, norm[rows], 0.0)
            square = square + jnp.where(lane == b + plan.blocks, dots[rows], 0.0)
    stats_ref[...] = square.T[: 2 * plan.blocks]


def emit_rows(plan, ids, source_ref, put):
    for core_xor in range(2):
        for line_xor in range(plan.line):
            for m in range(plan.seq):
                rows = source_ref[
                    pl.ds(in_place(plan, ids, line_xor, core_xor, m), plan.in_rows), :
                ]
                put(core_xor, line_xor, m, rows)


def row_products(w_ref, grad_ref):
    lane = iota((LANES, LANES), 1)
    square = jnp.zeros((LANES, LANES), f32)
    for i in range(w_ref.shape[0] // LANES):
        rows = slice(i * LANES, (i + 1) * LANES)
        product = w_ref[rows, :].astype(f32) * grad_ref[rows, :]
        square = square + jnp.where(lane == i, jnp.sum(product, axis=1, keepdims=True), 0.0)
    return square.T[:8]


def regate_kernel(plan, *refs):
    n = plan.seq
    stats = refs[:n]
    normed_ref, y_ref, z_ref, du_ref, wz_ref = refs[n : n + 5]
    cots = refs[n + 5 : 2 * n + 5]
    gain_ref = refs[2 * n + 5]
    dy_ref, dz_ref, scale_ref, gain_out_ref, share_ref, keep_ref, send_ref = refs[
        2 * n + 6 : 2 * n + 13
    ]
    gated_ref, gz_ref, go_ref = refs[2 * n + 13 :]
    ids = place()
    s, z, c = ids
    total = stats[0][...]
    for m in range(1, n):
        total = total + stats[m][...]
    turned = jnp.concatenate(
        [total, jnp.zeros((LANES - total.shape[0], GROUP), f32)], axis=0
    ).T
    gain = gain_ref[...]
    sums = jnp.zeros((1, plan.chan), f32)
    for b in range(plan.blocks):
        rows = slice(b * GROUP, (b + 1) * GROUP)
        r = lax.rsqrt(turned[:, b : b + 1] / INNER + norm_eps)
        dot = turned[:, plan.blocks + b : plan.blocks + b + 1] / INNER
        scale_ref[rows, :] = jnp.broadcast_to(r, (GROUP, LANES))
        gate = z_ref[rows, :]
        sig = sigmoid(gate)
        silu = gate * sig
        y = y_ref[rows, :]
        gated = y * silu
        du = du_ref[rows, :]
        normal = gated * r
        grad_pre = r * (du * gain) - normal * (r * r * dot)
        dy_ref[rows, :] = grad_pre * silu
        dz_ref[rows, :] = (grad_pre * y * sig * (1.0 + gate * (1.0 - sig))).astype(bf16)
        gated_ref[rows, :] = (normal * gain).astype(bf16)
        sums = sums + jnp.sum(du * normal, axis=0, keepdims=True)
    gain_out_ref[...] = sums
    gz_ref[...] = mm_tn(normed_ref[...], dz_ref[...])
    share_ref[...] = row_products(wz_ref, gz_ref)
    out = None
    for m in range(n):
        start = aligned((s ^ m) * plan.rows, plan.rows)
        one = mm_tn(gated_ref[pl.ds(start, plan.rows), :], cots[m][...])
        out = one if out is None else out + one
    go_ref[...] = out
    half = plan.in_rows * n // 2
    both = (keep_ref, send_ref)

    def put(core_xor, line_xor, m, rows):
        top = (m // 2) * plan.in_rows
        left = (m % 2) * plan.chan
        both[core_xor][line_xor, top : top + plan.in_rows, left : left + plan.chan] = rows.astype(
            bf16
        )

    emit_rows(plan, ids, gz_ref, put)
    for core_xor in range(2):
        for line_xor in range(plan.line):
            start = ((z ^ line_xor) * 2 + (c ^ core_xor)) * plan.out_rows
            both[core_xor][line_xor, half : half + plan.out_rows, :] = go_ref[
                pl.ds(aligned(start, 16), plan.out_rows), :
            ].astype(bf16)


def scan_back_kernel(plan, first, last, *refs):
    x_ref, dt_ref, segc_ref, segr_ref, dy_ref, conv_ref, heads_ref = refs[:7]
    states_ref, mixed_ref, slope_ref, table_ref, scores_ref = refs[7:12]
    refs = refs[12:]
    later = last < plan.blocks
    if later:
        before, refs = refs[:5], refs[5:]
    gp_ref, adj_ref, edge_ref, acc_ref, head_ref = refs
    if later:
        gp_ref[(last - first) * GROUP :, :] = before[0][...]
        adj_ref[...] = before[1][...]
        edge_ref[...] = before[2][...]
        acc_ref[...] = before[3][...]
        head_ref[...] = before[4][...]
    else:
        adj_ref[...] = jnp.zeros_like(adj_ref)
        edge_ref[...] = jnp.zeros_like(edge_ref)
        acc_ref[...] = jnp.zeros_like(acc_ref)
        head_ref[...] = jnp.zeros_like(head_ref)
    convw = conv_ref[0:KERNEL, :]
    chan, half = plan.chan, LANES // 2
    repeat = plan.mixed // LANES
    pick = (iota((chan, LANES), 0) // HEADDIM == iota((chan, LANES), 1)).astype(f32)
    row = iota((GROUP, LANES), 0)
    lane = iota((GROUP, LANES), 1)

    def step(turn, carry):
        b = last - 1 - turn
        base = aligned(b * GROUP, GROUP)
        here = pl.ds(aligned((b - first) * GROUP, GROUP), GROUP)
        values = mixed_ref[here, :chan]
        keys = mixed_ref[here, chan : chan + STATE]
        queries = mixed_ref[here, chan + STATE :]
        steps = table_ref[0, here, :]
        cum = table_ref[1, here, :]
        turned = table_ref[2, here, :]
        scores = scores_ref[here, :]
        seg, keep_h, to_last = edges(segc_ref, base, cum)
        state = states_ref[b - first]
        adj = adj_ref[...]
        dy = dy_ref[pl.ds(base, GROUP), :]
        spread = wide(jnp.concatenate([keep_h, to_last * steps], axis=0), chan)
        keep, to_end = spread[:GROUP], spread[GROUP:]
        kept = dy * keep
        dq = mm_nt(kept, state)
        cross = kept * mm(queries, state)
        fed = mm(keys, adj)
        dk = mm_nt(values * to_end, adj)
        adj_ref[...] = adj * keep[GROUP - 1 :] + mm_tn(queries, kept)
        ended = jnp.sum(state * adj, axis=0, keepdims=True)
        pushed = fed * values
        skipped = jnp.sum(dy * values, axis=0, keepdims=True)
        few = jnp.concatenate([ended, skipped, jnp.zeros((6, chan), f32)], axis=0)
        high = few.astype(bf16).astype(f32)
        sums = mm(jnp.concatenate([cross, pushed, high, few - high], axis=0), pick)
        cross_h = sums[:GROUP]
        pushed_h = sums[GROUP : 2 * GROUP]
        few_h = sums[2 * GROUP : 2 * GROUP + 8] + sums[2 * GROUP + 8 :]
        ended_h = few_h[0:1]
        skipped_h = few_h[1:2]
        grad_steps = pushed_h * to_last
        pulled = grad_steps * steps
        dcum = cross_h - pulled
        at_end = jnp.sum(pulled, axis=0, keepdims=True) + keep_h[GROUP - 1 :] * ended_h
        dscores = None
        columns = []
        dvs = []
        for pair in range(plan.heads // 2):
            lanes = slice(pair * LANES, (pair + 1) * LANES)
            dy_pair = split_pair(dy[:, lanes])
            products = mm_nt(dy_pair, values[:, lanes])
            stacked = []
            for j, h in enumerate((2 * pair, 2 * pair + 1)):
                scaled = head_decay(cum, turned, h) * turned[half + h : half + h + 1, :]
                weighted = scaled * products[j * GROUP : (j + 1) * GROUP]
                both = weighted * scores
                dscores = weighted if dscores is None else dscores + weighted
                dcum = jnp.where(lane == h, dcum + jnp.sum(both, axis=1, keepdims=True), dcum)
                columns.append(jnp.sum(both, axis=0, keepdims=True))
                stacked.append(scaled * scores)
            dvs.append(mm_tn(jnp.concatenate(stacked, axis=0), dy_pair))
        allowed = (seg == segr_ref[pl.ds(b, 1), :]) & (row >= lane)
        dscores = jnp.where(allowed, dscores, 0.0)
        dv = jnp.concatenate(dvs, axis=1) + fed * to_end + heads_ref[2:3, :] * dy
        columns.append(jnp.zeros((LANES - plan.heads, GROUP), f32))
        down = jnp.concatenate(columns, axis=0).T
        grad_steps = grad_steps + down / jnp.maximum(steps, TINY)
        dcum = dcum - down
        dcum = dcum + jnp.where(row == GROUP - 1, at_end, 0.0)
        dk = dk + mm_tn(dscores, queries)
        dq = dq + mm(dscores, keys)
        ddecay = mask_mm(row <= lane, dcum)
        rate = jnp.exp(heads_ref[1:2, :LANES])
        grad_steps = grad_steps - ddecay * rate
        dt_in = dt_ref[pl.ds(base, GROUP), :] + heads_ref[0:1, :LANES]
        grad_dt = grad_steps * exact_sigmoid(dt_in)
        head_ref[0:1, :] += jnp.sum(grad_dt, axis=0, keepdims=True)
        head_ref[1:2, :] -= jnp.sum(ddecay * steps, axis=0, keepdims=True) * rate
        head_ref[2:3, :] += skipped_h
        dpre = jnp.concatenate([dv, dk, dq], axis=1) * slope_ref[here, :]
        longer = jnp.concatenate([dpre, edge_ref[...]], axis=0)
        edge_ref[...] = dpre[:LEAD]
        segn = segc_ref[pl.ds(aligned(base + LEAD, 8), GROUP + LEAD), :]
        x = x_ref[pl.ds(aligned(base + LEAD, 8), GROUP), :]
        acc_ref[KERNEL : KERNEL + 1, :] += jnp.sum(dpre, axis=0, keepdims=True)
        acc_ref[KERNEL - 1 : KERNEL, :] += jnp.sum(dpre * x, axis=0, keepdims=True)
        dx = convw[KERNEL - 1 : KERNEL] * dpre
        for k in range(KERNEL - 1):
            ahead = KERNEL - 1 - k
            same = (segn[ahead : ahead + GROUP] == seg).astype(f32)
            part = longer[ahead : ahead + GROUP] * jnp.concatenate([same] * repeat, axis=1)
            acc_ref[k : k + 1, :] += jnp.sum(part * x, axis=0, keepdims=True)
            dx = dx + convw[k : k + 1] * part
        live = jnp.where(lane < plan.heads, grad_dt, 0.0)
        gp_ref[here, :] = jnp.concatenate([dx, live], axis=1).astype(bf16)
        return carry

    lax.fori_loop(0, last - first, step, 0, unroll=True)


def main_grads_kernel(
    plan, normed_ref, gp_ref, w_ref, gain_ref, share_ref, gain_out_ref, acc_ref, head_ref,
    keep_ref, send_ref, gw_ref, small_ref,
):
    ids = place()
    gw_ref[...] = mm_tn(normed_ref[...], gp_ref[...])
    both = (keep_ref, send_ref)

    def put(core_xor, line_xor, m, rows):
        top = m * plan.in_rows
        both[core_xor][line_xor, top : top + plan.in_rows, :] = rows.astype(bf16)

    emit_rows(plan, ids, gw_ref, put)
    share = share_ref[...] + row_products(w_ref, gw_ref)
    small_ref[...] = jnp.zeros_like(small_ref)
    for i in range(WIDTH // LANES):
        lanes = slice(i * LANES, (i + 1) * LANES)
        small_ref[0:1, lanes] = share[i : i + 1] / gain_ref[:, lanes]
    small_ref[1:6, : plan.mixed] = acc_ref[0:5, :]
    small_ref[6:7, : plan.chan] = gain_out_ref[...]
    for j in range(3):
        small_ref[7:8, j * LANES : (j + 1) * LANES] = head_ref[j : j + 1, :]
    high, low = two_parts(small_ref[...])
    last = plan.seq * plan.in_rows
    for ref in both:
        for line_xor in range(plan.line):
            ref[line_xor, last : last + 8, :] = high
            ref[line_xor, last + 8 : last + 16, :] = low


def normed_grads_kernel(plan, gp_ref, w_ref, dz_ref, wz_ref, *grads):
    s = lax.axis_index("seq")
    for m in range(plan.seq):
        rows = pl.ds(aligned((s ^ m) * plan.rows, plan.rows), plan.rows)
        part = mm_nt(gp_ref[rows, :], w_ref[...]) + mm_nt(dz_ref[rows, :], wz_ref[...])
        grads[m][...] = part.astype(grads[m].dtype)


def joined(ref, top):
    return ref[top : top + 8, :].astype(f32) + ref[top + 8 : top + 16, :].astype(f32)


def main_split_kernel(plan, keep_ref, got_ref, *outs):
    last = plan.seq * plan.in_rows
    small = joined(keep_ref.at[0], last) + joined(got_ref.at[0], last)
    high, low = two_parts(small)
    for m in range(plan.line):
        total = keep_ref[m, :last, :].astype(f32) + got_ref[m, :last, :].astype(f32)
        outs[m][:last, :] = total.astype(bf16)
        outs[m][last : last + 8, :] = high
        outs[m][last + 8 :, :] = low


def gate_split_kernel(plan, keep_ref, got_ref, *outs):
    for m in range(plan.line):
        outs[m][...] = (keep_ref[m].astype(f32) + got_ref[m].astype(f32)).astype(bf16)


def gate_sum_kernel(plan, *refs):
    parts, (gate_ref, out_ref) = refs[: plan.line], refs[plan.line :]
    total = parts[0][...].astype(f32)
    for part in parts[1:]:
        total = total + part[...].astype(f32)
    half = plan.in_rows * plan.seq // 2
    gate_ref[...] = total[:half].astype(bf16)
    out_ref[...] = total[half : half + plan.out_rows]


def row_sum_kernel(plan, gate_ref, *refs):
    parts, outs = refs[: plan.line], refs[plan.line :]
    r, chan = plan.in_rows, plan.chan
    last = plan.seq * r
    small = joined(parts[0], last)
    for part in parts[1:]:
        small = small + joined(part, last)
    high, low = two_parts(small)
    for m in range(plan.seq):
        rows = slice(m * r, (m + 1) * r)
        total = parts[0][rows, :].astype(f32)
        for part in parts[1:]:
            total = total + part[rows, :].astype(f32)
        outs[m][:r, :] = total.astype(bf16)
        outs[m][r : r + 8, :] = high
        outs[m][r + 8 : r + 16, :] = low
        top, left = (m // 2) * r, (m % 2) * chan
        outs[m][r + 16 :, :chan] = gate_ref[top : top + r, left : left + chan]
        outs[m][r + 16 :, chan:] = jnp.zeros((r, plan.cols - chan), bf16)


def columns_kernel(plan, *refs):
    n, r, chan, heads = plan.seq, plan.in_rows, plan.chan, plan.heads
    parts, refs = refs[:n], refs[n:]
    out_ref, gain_in_ref, convw_ref, convb_ref, dtb_ref, alog_ref, skip_ref = refs[:7]
    gain_out_ref, gate_ref, main_ref, small_ref = refs[7:]
    s = lax.axis_index("seq")
    for m in range(n):
        main_ref[m] = parts[m][:r, :].astype(f32)
        small_ref[m] = joined(parts[m], r)
        gate_ref[m] = parts[m][r + 16 :, :chan].astype(f32)
    shared = jnp.zeros((r, 2 * STATE), f32)
    lane = iota((r, LANES), 1)
    dts = jnp.zeros((r, LANES), f32)
    gain_in = jnp.zeros((1, WIDTH), f32)
    small_shared = jnp.zeros((5, 2 * STATE), f32)
    one_lane = iota((1, LANES), 1)
    rows = [jnp.zeros((1, LANES), f32) for _ in range(3)]
    for g in range(n):
        cols = slice(g * chan, (g + 1) * chan)
        out_ref[:, cols] = gate_ref[s ^ g]
        main = main_ref[s ^ g]
        out_ref[:, INNER + g * chan : INNER + (g + 1) * chan] = main[:, :chan]
        shared = shared + main[:, chan : plan.mixed]
        one = main[:, plan.mixed :]
        moved = one if g == 0 else pltpu.roll(one, g * heads, 1)
        dts = jnp.where(lane // heads == g, moved, dts)
        part = small_ref[s ^ g]
        gain_in = gain_in + part[0:1, :WIDTH]
        convw_ref[:, cols] = part[1:5, :chan]
        convb_ref[cols] = part[5, :chan]
        gain_out_ref[cols] = part[6, :chan]
        small_shared = small_shared + part[1:6, chan : plan.mixed]
        for j in range(3):
            one = part[7:8, j * LANES : (j + 1) * LANES]
            moved = one if g == 0 else pltpu.roll(one, g * heads, 1)
            rows[j] = jnp.where(one_lane // heads == g, moved, rows[j])
    out_ref[:, 2 * INNER : INNER + CONV] = shared
    out_ref[:, INNER + CONV :] = dts[:, :HEADS]
    gain_in_ref[...] = gain_in[0]
    convw_ref[:, INNER:] = small_shared[:4]
    convb_ref[INNER:] = small_shared[4]
    dtb_ref[...] = rows[0][:, :HEADS]
    alog_ref[...] = rows[1][:, :HEADS]
    skip_ref[...] = rows[2][:, :HEADS]


def result_kernel(plan, tok_ref, scale_ref, *refs):
    parts, out_ref = refs[: plan.seq], refs[plan.seq]
    s = lax.axis_index("seq")
    total = parts[0][...].astype(f32)
    for part in parts[1:]:
        total = total + part[...].astype(f32)
    r = scale_ref[pl.ds(aligned(s * plan.rows, plan.rows), plan.rows), :]
    r = jnp.concatenate([r] * (WIDTH // LANES), axis=1)
    out_ref[...] = (tok_ref[...].astype(f32) + total * r).astype(bf16)


def token_kernel(plan, tok_ref, cot_ref, gain_ref, *refs):
    parts, out_ref = refs[: plan.seq], refs[plan.seq]
    total = parts[0][...].astype(f32)
    for part in parts[1:]:
        total = total + part[...].astype(f32)
    tok = tok_ref[...].astype(f32)
    q = lax.rsqrt(jnp.mean(tok * tok, axis=1, keepdims=True) + norm_eps)
    w = total * gain_ref[...]
    mean = jnp.mean(w * tok, axis=1, keepdims=True)
    grad = cot_ref[...].astype(f32) + q * w - tok * (q * q * q * mean)
    out_ref[...] = grad.astype(bf16)


def call(body, plan, outs, scratch, *args, mib=4, micros=1, name=None, kept=0):
    shapes = [jax.ShapeDtypeStruct(shape, kind) for shape, kind in outs]
    size = sum(a.size * a.dtype.itemsize for a in args)
    size += sum(a.size * a.dtype.itemsize for a in shapes)
    return pl.pallas_call(
        functools.partial(body, plan),
        out_shape=shapes,
        in_specs=[pl.BlockSpec(memory_space=pltpu.HBM)] * kept
        + [pl.BlockSpec(memory_space=pltpu.VMEM)] * (len(args) - kept),
        out_specs=[pl.BlockSpec(memory_space=pltpu.VMEM)] * len(shapes),
        scratch_shapes=[
            pltpu.VMEM(*one) if isinstance(one, tuple) else one for one in scratch
        ],
        compiler_params=pltpu.CompilerParams(vmem_limit_bytes=mib * 2**20),
        cost_estimate=pl.CostEstimate(
            flops=micros * FLOPS_PER_MICRO, bytes_accessed=0, transcendentals=0
        ),
        name=name,
    )(*args)


FLOPS_PER_MICRO = 3_000_000_000
LATE = 4


def swap(value, axis, by):
    size = lax.axis_size(axis)
    return lax.ppermute(value, axis, [(i, i ^ by) for i in range(size)])


def after(value, *others):
    return lax.optimization_barrier((value, *others))[0]


def head_parallel(
    tokens, cotangent, segments, in_weight, out_weight, gain_in, conv_weight, conv_bias,
    dt_bias, a_log, d_skip, gain_out,
):
    rows = tokens.shape[1]
    plan = Plan(
        lax.axis_size("seq"), lax.axis_size("batch"), rows, in_weight.shape[0], out_weight.shape[0]
    )
    n, line, chan, heads = plan.seq, plan.line, plan.chan, plan.heads
    s = lax.axis_index("seq")
    tok, cot = tokens[0], cotangent[0]

    r = plan.in_rows
    own = call(
        pack_kernel, plan, [((r + 8, plan.cols + chan), bf16)] * n,
        [
            (in_weight.shape, bf16), (segments.shape, jnp.int32), pltpu.SemaphoreType.DMA((2,)),
            ((n, r, plan.cols + chan), bf16),
        ],
        in_weight, segments, mib=60, name="pack", kept=2,
    )
    pieces = [own[0]] + [swap(own[m], "seq", m) for m in range(1, n)]
    tok_later = after(tok, *pieces)
    toks = [tok] + [swap(tok_later, "seq", m) for m in range(1, n)]
    main_shard, gate_shard = call(
        regroup_kernel, plan,
        [((n * r, plan.cols), bf16), ((n * r // 2 + plan.out_rows, WIDTH), bf16)], [],
        *pieces, out_weight, name="regroup",
    )

    def along(shard):
        return [shard] + [swap(shard, "batch", 2 * m) for m in range(1, line)]

    def both_cores(parts):
        return parts + [swap(one, "batch", 1) for one in parts]

    main_line = along(main_shard)
    main_parts = both_cores(main_line)
    gate_line = along(after(gate_shard, *main_line))
    cot_near = after(cot, *toks)
    conv, per_head, own_gain = call(
        own_params_kernel, plan,
        [((8, plan.mixed), f32), ((8, chan), f32), ((1, chan), f32)], [],
        conv_weight, conv_bias[None], dt_bias[None], a_log[None], d_skip[None], gain_out[None],
        name="own_params",
    )
    gain_row = gain_in[None]
    total = plan.total
    seg_rows = -(-plan.blocks // 8) * 8
    normed, w_main, x, dt_raw, segc, segr = call(
        project_kernel, plan,
        [
            ((total, WIDTH), bf16), ((WIDTH, plan.cols), bf16),
            ((total + LEAD, plan.mixed), f32), ((total, LANES), f32),
            ((total + 2 * LEAD, LANES), f32), ((seg_rows, GROUP), f32),
        ],
        [((WIDTH, plan.cols), f32)],
        *toks, *pieces, *main_parts, gain_row, mib=16, micros=5, name="project",
    )
    cot_far = after(cot, normed)
    cots = [cot] + [swap(cot_near if m < 3 else cot_far, "seq", m) for m in range(1, n)]
    half = plan.blocks // 2
    state_shape = (STATE, chan)
    scan_in = (x, dt_raw, segc, segr, conv, per_head)

    def scan_part(first, last, *early):
        count, size = last - first, (last - first) * GROUP
        return list(call(
            lambda p, *refs: scan_kernel(p, first, last, *refs), plan,
            [
                ((last * GROUP, chan), f32), (state_shape, f32), ((count,) + state_shape, f32),
                ((size, plan.mixed), f32), ((size, plan.mixed), f32), ((3, size, LANES), f32),
                ((size, GROUP), f32),
            ], [],
            *scan_in, *early, mib=16, micros=4, name="scan_forward",
        ))

    early_y, early_state, *early = scan_part(0, half)
    gate_line = [after(one, early_state) for one in gate_line]
    gate_parts = both_cores(gate_line)
    early_state = after(early_state, *gate_line, *cots[1:3])
    y, _, *late = scan_part(half, plan.blocks, early_y, early_state)
    piece_shape = (rows, WIDTH)
    w_gate, z, du, stats, *outs = call(
        gate_kernel, plan,
        [
            ((WIDTH, chan), bf16), ((total, chan), f32), ((total, chan), f32),
            ((2 * plan.blocks, GROUP), f32),
        ] + [(piece_shape, bf16)] * n,
        [((WIDTH, chan), f32), ((chan, WIDTH), bf16)],
        normed, y, *gate_parts, *cots, own_gain,
        mib=16, micros=6, name="gate_forward",
    )
    all_stats = [stats] + [swap(stats, "seq", m) for m in range(1, n)]
    dy, dz, scale, gain_out_grad, share, keep, send = call(
        regate_kernel, plan,
        [
            ((total, chan), f32), ((total, chan), bf16), ((total, LANES), f32), ((1, chan), f32),
            ((8, LANES), f32),
            ((line, n * r // 2 + plan.out_rows, WIDTH), bf16),
            ((line, n * r // 2 + plan.out_rows, WIDTH), bf16),
        ],
        [((total, chan), bf16), ((WIDTH, chan), f32), ((chan, WIDTH), f32)],
        *all_stats, normed, y, z, du, w_gate, *cots, own_gain,
        mib=16, micros=6, name="gate_backward",
    )

    def reduce_line(keep, send, body, name):
        got = swap(send, "batch", 1)
        parts = call(
            body, plan, [(keep.shape[1:], bf16)] * line, [], keep, got, name=name, micros=LATE,
        )
        return list(parts)

    def line_exchange(parts):
        return [parts[0]] + [swap(parts[m], "batch", 2 * m) for m in range(1, line)]

    gate_half = reduce_line(keep, send, gate_split_kernel, "gate_core_sum")
    dy = after(dy, *gate_half)
    back_in = (x, dt_raw, segc, segr, dy, conv, per_head)

    def scan_back_part(first, last, saved, *before):
        return call(
            lambda p, *refs: scan_back_kernel(p, first, last, *refs), plan,
            [
                ((total - first * GROUP, plan.cols), bf16), (state_shape, f32),
                ((LEAD, plan.mixed), f32), ((8, plan.mixed), f32), ((8, LANES), f32),
            ], [],
            *back_in, *saved, *before, mib=16, micros=7, name="scan_backward",
        )

    before = list(scan_back_part(half, plan.blocks, late))
    out_parts = [outs[0]] + [swap(outs[m], "seq", m) for m in range(1, n)]
    gate_half[-1] = after(gate_half[-1], before[1])
    gate_lines = line_exchange(gate_half)
    gate_rows, shard_out = call(
        gate_sum_kernel, plan,
        [((n * r // 2, WIDTH), bf16), ((plan.out_rows, WIDTH), f32)], [], *gate_lines,
        name="gate_sum", micros=LATE,
    )
    before[1] = after(before[1], *gate_lines[:-1])
    gp, _, _, acc, head_acc = scan_back_part(0, half, early, *before)
    (result,) = call(
        result_kernel, plan, [(piece_shape, bf16)], [], tok, scale, *out_parts, name="result", micros=LATE
    )

    grads = call(
        normed_grads_kernel, plan, [(piece_shape, bf16)] * n, [], gp, w_main, dz, w_gate,
        mib=12, micros=3 * LATE, name="normed_grads",
    )
    gp_late = after(gp, *out_parts, *gate_lines, *grads)
    keep, send = call(
        main_grads_kernel, plan, [((line, n * r + 16, plan.cols), bf16)] * 2,
        [((WIDTH, plan.cols), f32), ((8, plan.cols), f32)],
        normed, gp_late, w_main, gain_row, share, gain_out_grad, acc, head_acc,
        mib=12, micros=4 * LATE, name="main_grads",
    )
    main_half = reduce_line(keep, send, main_split_kernel, "main_core_sum")
    main_lines = line_exchange(main_half)
    grad_parts = [grads[0]] + [swap(grads[m], "seq", m) for m in range(1, n)]
    last = call(
        row_sum_kernel, plan, [((2 * r + 16, plan.cols), bf16)] * n, [], gate_rows, *main_lines,
        name="main_sum", micros=LATE,
    )
    last = [last[0]] + [swap(last[m], "seq", m) for m in range(1, n)]
    (grad_tokens,) = call(
        token_kernel, plan, [(piece_shape, bf16)], [], tok, cot, gain_row, *grad_parts,
        name="token_grad", micros=LATE,
    )
    shard_in, *smalls = call(
        columns_kernel, plan,
        [
            ((r, in_weight.shape[1]), f32),
            ((WIDTH,), f32), ((KERNEL, CONV), f32), ((CONV,), f32), ((1, HEADS), f32),
            ((1, HEADS), f32), ((1, HEADS), f32), ((INNER,), f32),
        ],
        [((n, r, chan), f32), ((n, r, plan.cols), f32), ((n, 8, plan.cols), f32)],
        *last, name="columns", micros=LATE,
    )
    return (
        result[None], grad_tokens[None], shard_in, shard_out, smalls[0], smalls[1],
        smalls[2], smalls[3][0], smalls[4][0], smalls[5][0], smalls[6],
    )


def shifted(value, axis, by):
    size = lax.axis_size(axis)
    pairs = [(i, i + by) for i in range(size) if 0 <= i + by < size]
    return lax.ppermute(value, axis, pairs)


def prefix(value, axis, join, neutral):
    place = lax.axis_index(axis)
    gathered = jax.tree.map(
        lambda a, kind: lax.all_gather(a.astype(kind), axis), value, (jnp.bfloat16, jnp.bfloat16)
    )
    state = jax.tree.map(lambda a, e: jnp.zeros_like(a) + jnp.asarray(e, a.dtype), value, neutral)

    def one(turn, state):
        return join(
            state,
            jax.tree.map(
                lambda a, own: lax.dynamic_index_in_dim(a, turn, 0, False).astype(own.dtype),
                gathered,
                value,
            ),
        )

    return lax.fori_loop(0, place, one, state)


def prefix_2(value, axis, join, neutral):
    count = lax.axis_size(axis)
    place = lax.axis_index(axis)
    ahead = count - 1 - place
    gathered = jax.tree.map(
        lambda a, kind: lax.all_gather(a.astype(kind), axis),
        value,
        jax.tree.map(lambda a: jnp.bfloat16 if a.dtype == jnp.float32 else a.dtype, value),
    )
    state = jax.tree.map(lambda a, e: jnp.zeros_like(a) + jnp.asarray(e, a.dtype), value, neutral)

    def one(turn, state):
        source = count - 1 - turn
        return join(
            state,
            jax.tree.map(
                lambda a, own: lax.dynamic_index_in_dim(a, source, 0, False).astype(own.dtype),
                gathered,
                value,
            ),
        )

    return lax.fori_loop(0, ahead, one, state)


def rms_scale(values, gain):
    mean_square = jnp.mean(values * values, axis=-1, keepdims=True)
    return values * lax.rsqrt(mean_square + norm_eps) * gain


def causal_conv(extended, ext_segs, conv_weight, conv_bias, row_count):
    target = ext_segs[KERNEL - 1 :]
    total = jnp.zeros((row_count, conv_weight.shape[1]), jnp.float32) + conv_bias[None, :]
    for offset in range(KERNEL):
        window = extended[offset : offset + row_count]
        same_doc = (ext_segs[offset : offset + row_count] == target).astype(jnp.float32)
        total = total + conv_weight[offset][None, :] * window * same_doc[:, None]
    return jax.nn.silu(total)


def prepare(xbc, dt_raw, edge_rows, ext_segs, conv_weight, conv_bias, dt_bias, a_log):
    row_count = xbc.shape[0]
    extended = jnp.concatenate([edge_rows, xbc], axis=0)
    mixed = causal_conv(extended, ext_segs, conv_weight, conv_bias, row_count)
    values = mixed[:, :INNER].reshape(row_count, HEADS, HEADDIM)
    key_vecs = mixed[:, INNER : INNER + STATE]
    queries = mixed[:, INNER + STATE :]
    step_sizes = jax.nn.softplus(dt_raw + dt_bias[None, :])
    log_decay = -step_sizes * jnp.exp(a_log)[None, :]
    return (values, key_vecs, queries, step_sizes, log_decay)


def group_block(carried, block_in):
    state_in, last_seg = carried
    values, key_vecs, queries, step_sizes, log_decay, seg_ids = block_in
    length_here = seg_ids.shape[0]
    cumulative = jnp.cumsum(log_decay, axis=0)
    positions = jnp.arange(length_here)
    allowed = (seg_ids[:, None] == seg_ids[None, :]) & (positions[:, None] >= positions[None, :])
    gap_logs = cumulative[:, None, :] - cumulative[None, :, :]
    decay_mask = jnp.where(allowed[:, :, None], jnp.exp(jnp.minimum(gap_logs, 0.0)), 0.0)
    scores = jnp.dot(queries, key_vecs.T, precision=highest)
    weights = decay_mask * scores[:, :, None] * step_sizes[None, :, :]
    inside = jnp.einsum("tsh,shp->thp", weights, values, precision=highest)
    keep_factor = jnp.where((seg_ids == last_seg)[:, None], jnp.exp(cumulative), 0.0)
    carried_out = (
        jnp.einsum("tn,hpn->thp", queries, state_in, precision=highest) * keep_factor[:, :, None]
    )
    to_end = (
        jnp.where(
            (seg_ids == seg_ids[-1])[:, None], jnp.exp(cumulative[-1][None, :] - cumulative), 0.0
        )
        * step_sizes
    )
    fresh_state = jnp.einsum("sh,shp,sn->hpn", to_end, values, key_vecs, precision=highest)
    new_state = state_in * keep_factor[-1][:, None, None] + fresh_state
    return ((new_state, seg_ids[-1]), inside + carried_out)


def grouped_ssd(
    values, key_vecs, queries, step_sizes, log_decay, seg_ids, d_skip, state_in, last_seg
):
    row_count = seg_ids.shape[0]
    block_count = row_count // GROUP

    def blocked(member):
        return member.reshape((block_count, GROUP) + member.shape[1:])

    inputs = (
        blocked(values),
        blocked(key_vecs),
        blocked(queries),
        blocked(step_sizes),
        blocked(log_decay),
        blocked(seg_ids),
    )
    (final_state, last_out), outputs = lax.scan(
        jax.checkpoint(group_block), (state_in, last_seg), inputs
    )
    outputs = outputs.reshape(row_count, HEADS, HEADDIM) + d_skip[None, :, None] * values
    return (outputs, final_state)


def gated_norm(mixed_out, gate_z, gain_out):
    return rms_scale(mixed_out * jax.nn.silu(gate_z), gain_out)


def chain_combine(earlier, later):
    decay_early, state_early = earlier
    decay_late, state_late = later
    return (decay_early * decay_late, decay_late[:, None, None] * state_early + state_late)


def cross_term(queries, log_decay, state_in, seg_ids, prev_seg):
    cumulative = jnp.cumsum(log_decay, axis=0)
    keep_factor = jnp.where((seg_ids == prev_seg)[:, None], jnp.exp(cumulative), 0.0)
    return jnp.einsum("tn,hpn->thp", queries, state_in, precision=highest) * keep_factor[:, :, None]


def device_decay(log_decay, seg_ids, prev_seg):
    total_log = jnp.sum(log_decay, axis=0)
    return jnp.where(seg_ids[-1] == prev_seg, jnp.exp(total_log), 0.0)


def on_device(
    tokens,
    cotangent,
    segments,
    in_weight,
    out_weight,
    gain_in,
    conv_weight,
    conv_bias,
    dt_bias,
    a_log,
    d_skip,
    gain_out,
):
    tokens_f = tokens[0].astype(jnp.float32)
    cot_low = cotangent[0]
    seg_ids = segments[0]
    row_count = seg_ids.shape[0]
    full_in, full_out = (
        lax.all_gather(in_weight, ("seq", "batch"), axis=0, tiled=True),
        lax.all_gather(out_weight, ("seq", "batch"), axis=0, tiled=True),
    )
    normed, norm_pull = jax.vjp(rms_scale, tokens_f, gain_in)
    normed_low = normed.astype(jnp.bfloat16)
    projected = jnp.dot(normed_low, full_in, preferred_element_type=jnp.float32)
    gate_z = projected[:, :INNER]
    xbc = projected[:, INNER : INNER + CONV]
    dt_raw = projected[:, INNER + CONV :]
    tail_start = row_count - KERNEL + 1
    edge_rows, edge_segs = shifted(
        (xbc[tail_start:], seg_ids[tail_start:].astype(jnp.float32)), "seq", 1
    )
    prev_segs = edge_segs.astype(jnp.int32)
    prev_seg = prev_segs[KERNEL - 2]
    ext_segs = jnp.concatenate([prev_segs, seg_ids])

    def prepare_local(xbc_in, dt_in, edge_in, weight_in, bias_in, shift_in, alog_in):
        return prepare(xbc_in, dt_in, edge_in, ext_segs, weight_in, bias_in, shift_in, alog_in)

    prepared, prepare_pull = jax.vjp(
        prepare_local, xbc, dt_raw, edge_rows, conv_weight, conv_bias, dt_bias, a_log
    )
    values, key_vecs, queries, step_sizes, log_decay = prepared
    zeros_state = jnp.zeros((HEADS, HEADDIM, STATE), jnp.float32)

    def local_ssd(values_in, keys_in, queries_in, sizes_in, logs_in, skip_in):
        return grouped_ssd(
            values_in,
            keys_in,
            queries_in,
            sizes_in,
            logs_in,
            seg_ids,
            skip_in,
            zeros_state,
            seg_ids[0],
        )

    (local_out, local_state), ssd_pull = jax.vjp(
        local_ssd, values, key_vecs, queries, step_sizes, log_decay, d_skip
    )

    def decay_local(logs_in):
        return device_decay(logs_in, seg_ids, prev_seg)

    decay_here, decay_pull = jax.vjp(decay_local, log_decay)
    identity = (jnp.ones((HEADS,), jnp.float32), zeros_state)
    decay_prefix, state_in = prefix((decay_here, local_state), "seq", chain_combine, identity)

    def cross_local(queries_in, logs_in, state_arg):
        return cross_term(queries_in, logs_in, state_arg, seg_ids, prev_seg)

    cross_out, cross_pull = jax.vjp(cross_local, queries, log_decay, state_in)
    mixed_out = (local_out + cross_out).reshape(row_count, INNER)
    gated, gated_pull = jax.vjp(gated_norm, mixed_out, gate_z, gain_out)
    gated_low = gated.astype(jnp.bfloat16)
    result = tokens_f + jnp.dot(gated_low, full_out, preferred_element_type=jnp.float32)
    back_in, back_out = (
        lax.all_gather(in_weight, ("seq", "batch"), axis=0, tiled=True),
        lax.all_gather(out_weight, ("seq", "batch"), axis=0, tiled=True),
    )
    contract_last = (((1,), (1,)), ((), ()))
    contract_first = (((0,), (0,)), ((), ()))
    grad_gated = lax.dot_general(
        cot_low, back_out, contract_last, preferred_element_type=jnp.float32
    )
    grad_mixed, grad_gate, grad_gain_out = gated_pull(grad_gated)
    grad_mixed = grad_mixed.reshape(row_count, HEADS, HEADDIM)
    grad_q_cross, grad_log_cross, grad_state_in = cross_pull(grad_mixed)
    decay_after, grad_exit = prefix_2((decay_here, grad_state_in), "seq", chain_combine, identity)
    grad_decay = jnp.sum(grad_exit * state_in, axis=(1, 2))
    grad_log_dev = decay_pull(grad_decay)[0]
    grad_values, grad_keys, grad_q_local, grad_sizes, grad_log_local, grad_skip = ssd_pull(
        (grad_mixed, grad_exit)
    )
    prep_grads = prepare_pull(
        (
            grad_values,
            grad_keys,
            grad_q_local + grad_q_cross,
            grad_sizes,
            grad_log_local + grad_log_cross + grad_log_dev,
        )
    )
    grad_xbc, grad_dt, grad_edge, grad_conv_w, grad_conv_b, grad_dt_bias, grad_a_log = prep_grads
    grad_next = shifted(grad_edge, "seq", -1)
    grad_xbc = grad_xbc.at[tail_start:].add(grad_next)
    grad_proj = jnp.concatenate([grad_gate, grad_xbc, grad_dt], axis=1).astype(jnp.bfloat16)
    grad_normed = lax.dot_general(
        grad_proj, back_in, contract_last, preferred_element_type=jnp.float32
    )
    grad_tokens_norm, grad_gain_in = norm_pull(grad_normed)
    grad_tokens = (cot_low.astype(jnp.float32) + grad_tokens_norm).astype(jnp.bfloat16)
    grad_in_w = lax.dot_general(
        normed_low, grad_proj, contract_first, preferred_element_type=jnp.float32
    )
    grad_out_w = lax.dot_general(
        gated_low, cot_low, contract_first, preferred_element_type=jnp.float32
    )
    shard_in, shard_out = (
        lax.psum_scatter(grad_in_w, ("seq", "batch"), scatter_dimension=0, tiled=True),
        lax.psum_scatter(grad_out_w, ("seq", "batch"), scatter_dimension=0, tiled=True),
    )
    summed = lax.psum(
        (
            grad_gain_in,
            grad_conv_w,
            grad_conv_b,
            grad_dt_bias,
            grad_a_log,
            grad_skip,
            grad_gain_out,
        ),
        ("seq", "batch"),
    )
    return (
        result.astype(jnp.bfloat16)[None],
        grad_tokens[None],
        shard_in,
        shard_out,
        summed[0],
        summed[1],
        summed[2],
        summed[3],
        summed[4],
        summed[5],
        summed[6],
    )


def solution(mesh):
    in_specs = (
        P("batch", "seq", None),
        P("batch", "seq", None),
        P("batch", "seq"),
        P(("seq", "batch"), None),
        P(("seq", "batch"), None),
        P(),
        P(),
        P(),
        P(),
        P(),
        P(),
        P(),
    )
    out_specs = (
        P("batch", "seq", None),
        P("batch", "seq", None),
        P(("seq", "batch"), None),
        P(("seq", "batch"), None),
        P(),
        P(),
        P(),
        P(),
        P(),
        P(),
        P(),
    )
    count = mesh.shape["seq"]
    even = HEADS % (2 * count) == 0 and count & (count - 1) == 0
    return jax.shard_map(
        head_parallel if even else on_device, mesh=mesh, in_specs=in_specs, out_specs=out_specs, check_vma=False
    )
```

```python
import functools

import jax
import jax.numpy as jnp
from jax import lax
from jax.experimental import pallas as pl
from jax.experimental.pallas import tpu as pltpu
from jax.sharding import PartitionSpec as P

HEADS = 24
HEADDIM = 64
STATE = 128
KERNEL = 4
GROUP = 128
INNER = 1536
CONV = 1792
WIDTH = 768
LANES = 128
LEAD = 8
TINY = 1e-37


highest = lax.Precision.HIGHEST
norm_eps = 1e-05
f32 = jnp.float32
bf16 = jnp.bfloat16
contract_last = (((1,), (1,)), ((), ()))
contract_first = (((0,), (0,)), ((), ()))


def mm(a, b):
    return jnp.dot(a.astype(bf16), b.astype(bf16), preferred_element_type=f32)


def mm_nt(a, b):
    return lax.dot_general(
        a.astype(bf16), b.astype(bf16), contract_last, preferred_element_type=f32
    )


def mm_tn(a, b):
    return lax.dot_general(
        a.astype(bf16), b.astype(bf16), contract_first, preferred_element_type=f32
    )


def two_parts(value):
    high = value.astype(bf16)
    return high, (value - high.astype(f32)).astype(bf16)


def mask_mm(mask, value):
    width = value.shape[1]
    out = mm(mask, jnp.concatenate(two_parts(value), axis=1))
    return out[:, :width] + out[:, width:]


def iota(shape, dim):
    return lax.broadcasted_iota(jnp.int32, shape, dim)


def aligned(value, unit):
    return pl.multiple_of(value, unit)


def wide(columns, chan):
    half = LANES // 2
    high, low = two_parts(columns)
    low = pltpu.roll(low.astype(f32), half, 1)
    both = jnp.where(iota(columns.shape, 1) < half, high.astype(f32), low)
    spread = iota((LANES, chan), 1) // HEADDIM == lax.rem(iota((LANES, chan), 0), half)
    return mm(both, spread.astype(f32))


def softplus(value):
    return jnp.maximum(value, 0.0) + jnp.log1p(jnp.exp(-jnp.abs(value)))


def sigmoid(value):
    return 0.5 + 0.5 * jnp.tanh(0.5 * value)


class Plan:
    def __init__(self, mesh_seq, mesh_batch, rows, in_rows, out_rows):
        self.seq = mesh_seq
        self.batch = mesh_batch
        self.line = mesh_batch // 2
        self.rows = rows
        self.total = rows * mesh_seq
        self.blocks = self.total // GROUP
        self.heads = HEADS // mesh_seq
        self.chan = self.heads * HEADDIM
        self.mixed = self.chan + 2 * STATE
        self.cols = self.mixed + LANES
        self.in_rows = in_rows
        self.out_rows = out_rows


def place():
    s = lax.axis_index("seq")
    b = lax.axis_index("batch")
    return s, lax.shift_right_logical(b, 1), lax.bitwise_and(b, 1)


def in_place(plan, ids, line_xor, core_xor, seq_xor):
    s, z, c = ids
    owner = (s ^ seq_xor) * plan.batch + (z ^ line_xor) * 2 + (c ^ core_xor)
    return aligned(owner * plan.in_rows, 8)


def exact_sigmoid(value):
    return 1.0 / (1.0 + jnp.exp(-value))


def convolved(plan, base, x_ref, segc_ref, convw, convb):
    win = x_ref[pl.ds(base, GROUP + LEAD), :]
    segw = segc_ref[pl.ds(base, GROUP + LEAD), :]
    seg = segw[LEAD:]
    pre = convb + convw[KERNEL - 1 : KERNEL] * win[LEAD:]
    for k in range(KERNEL - 1):
        start = LEAD - KERNEL + 1 + k
        same = (segw[start : start + GROUP] == seg).astype(f32)
        same = jnp.concatenate([same] * (plan.mixed // LANES), axis=1)
        pre = pre + convw[k : k + 1] * win[start : start + GROUP] * same
    sig = sigmoid(pre)
    mixed = pre * sig
    return mixed, sig + mixed * (1.0 - sig)


def decays(dt_in, heads_ref):
    steps = softplus(dt_in)
    row = iota((GROUP, GROUP), 0)
    col = iota((GROUP, GROUP), 1)
    decay = -steps * jnp.exp(heads_ref[1:2, :LANES])
    cum = mask_mm(row >= col, decay)
    half = LANES // 2
    turned = jnp.where(col < half, cum, pltpu.roll(steps, half, 1)).T
    return steps, cum, turned


def edges(segc_ref, base, cum):
    seg = segc_ref[pl.ds(aligned(base + LEAD, 8), GROUP), :]
    prev = segc_ref[pl.ds(base, LEAD), :][LEAD - 1 :]
    keep = jnp.where(seg == prev, jnp.exp(cum), 0.0)
    last = cum[GROUP - 1 :]
    to_last = jnp.where(seg == seg[GROUP - 1 :], jnp.exp(last - cum), 0.0)
    return seg, keep, to_last


def head_decay(cum, turned, h):
    return jnp.exp(jnp.minimum(cum[:, h : h + 1] - turned[h : h + 1, :], 0.0))


def split_pair(pair):
    low = iota(pair.shape, 1) < HEADDIM
    return jnp.concatenate([jnp.where(low, pair, 0.0), jnp.where(low, 0.0, pair)], axis=0)


def fetch(pairs, sems):
    copies = [
        pltpu.make_async_copy(src, dst, sems.at[i]) for i, (src, dst) in enumerate(pairs)
    ]
    for copy in copies:
        copy.start()
    for copy in copies:
        copy.wait()


def pack_kernel(plan, w_any, seg_any, *outs):
    n, heads, chan = plan.seq, plan.heads, plan.chan
    blocks, outs = outs[:n], outs[n:]
    w_ref, seg_ref, sems, all_ref = outs
    fetch([(w_any, w_ref), (seg_any, seg_ref)], sems)
    s = lax.axis_index("seq")
    lane = iota((plan.in_rows, LANES), 1)
    tail = w_ref[:, INNER + CONV :].astype(f32)
    tail = jnp.concatenate(
        [tail, jnp.zeros((plan.in_rows, LANES - HEADS), f32)], axis=1
    )
    for g in range(n):
        moved = tail if g == 0 else pltpu.roll(tail, LANES - g * heads, 1)
        all_ref[g] = jnp.concatenate(
            [
                w_ref[:, INNER + g * chan : INNER + (g + 1) * chan],
                w_ref[:, 2 * INNER : INNER + CONV],
                jnp.where(lane < heads, moved, 0.0).astype(bf16),
                w_ref[:, g * chan : (g + 1) * chan],
            ],
            axis=1,
        )
    seg = jnp.broadcast_to(seg_ref[...].astype(f32), (8, plan.rows)).astype(bf16)
    for m in range(n):
        blocks[m][0 : plan.in_rows, :] = all_ref[s ^ m]
        blocks[m][plan.in_rows : plan.in_rows + 8, :] = jnp.zeros((8, plan.cols + chan), bf16)
        blocks[m][plan.in_rows : plan.in_rows + 8, : plan.rows] = seg


def own_params_kernel(
    plan, convw_ref, convb_ref, dtb_ref, alog_ref, skip_ref, gain_ref, conv_ref, heads_ref,
    own_gain_ref,
):
    n, heads, chan = plan.seq, plan.heads, plan.chan
    s = lax.axis_index("seq")
    own = pl.ds(aligned(s * chan, LANES), chan)
    conv_ref[...] = jnp.zeros_like(conv_ref)
    conv_ref[0:KERNEL, :chan] = convw_ref[:, own]
    conv_ref[0:KERNEL, chan:] = convw_ref[:, INNER:]
    conv_ref[KERNEL : KERNEL + 1, :chan] = convb_ref[:, own]
    conv_ref[KERNEL : KERNEL + 1, chan:] = convb_ref[:, INNER:]
    own_gain_ref[...] = gain_ref[:, own]
    one_lane = iota((1, LANES), 1)

    def own_heads(ref):
        row = jnp.concatenate([ref[...], jnp.zeros((1, LANES - HEADS), f32)], axis=1)
        found = row
        for g in range(1, n):
            found = jnp.where(s == g, pltpu.roll(row, LANES - g * heads, 1), found)
        return jnp.where(one_lane < heads, found, 0.0)

    heads_ref[...] = jnp.zeros_like(heads_ref)
    heads_ref[0:1, :LANES] = own_heads(dtb_ref)
    heads_ref[1:2, :LANES] = own_heads(alog_ref)
    skip = jnp.broadcast_to(own_heads(skip_ref), (8, LANES))
    heads_ref[2:3, :] = wide(skip, chan)[0:1]


def regroup_kernel(plan, *refs):
    n, r = plan.seq, plan.in_rows
    pieces, out_w_ref = refs[:n], refs[n]
    main_ref, gate_ref = refs[n + 1 :]
    half = r * n // 2
    for m in range(n):
        main_ref[m * r : (m + 1) * r, :] = pieces[m][0:r, : plan.cols]
        top, left = (m // 2) * r, (m % 2) * plan.chan
        gate_ref[top : top + r, left : left + plan.chan] = pieces[m][0:r, plan.cols :]
    gate_ref[half : half + plan.out_rows, :] = out_w_ref[...]


def fill_segments(plan, s, pieces, segc_ref, segr_ref):
    per = plan.rows // GROUP
    segc_ref[...] = jnp.zeros_like(segc_ref)
    segr_ref[...] = jnp.zeros_like(segr_ref)
    for m in range(plan.seq):
        line = pieces[m][plan.in_rows : plan.in_rows + 1, : plan.rows].astype(f32)
        for j in range(per):
            b = (s ^ m) * per + j
            segr_ref[pl.ds(b, 1), :] = line[:, j * GROUP : (j + 1) * GROUP]
    every = segr_ref[...]
    turned = jnp.concatenate(
        [every, jnp.zeros((LANES - every.shape[0], GROUP), f32)], axis=0
    ).T
    for b in range(plan.blocks):
        segc_ref[LEAD + b * GROUP : LEAD + (b + 1) * GROUP, :] = jnp.broadcast_to(
            turned[:, b : b + 1], (GROUP, LANES)
        )


def project_kernel(plan, *refs):
    n = plan.seq
    toks, refs = refs[:n], refs[n:]
    pieces, refs = refs[:n], refs[n:]
    weights, refs = refs[: 2 * plan.line], refs[2 * plan.line :]
    gain_ref = refs[0]
    normed_ref, w_ref, x_ref, dt_ref, segc_ref, segr_ref, wf_ref = refs[1:]
    ids = place()
    s = ids[0]
    fill_segments(plan, s, pieces, segc_ref, segr_ref)
    for core_xor in range(2):
        for line_xor in range(plan.line):
            piece = weights[core_xor * plan.line + line_xor]
            for m in range(n):
                dest = pl.ds(in_place(plan, ids, line_xor, core_xor, m), plan.in_rows)
                wf_ref[dest, :] = piece[m * plan.in_rows : (m + 1) * plan.in_rows, :].astype(f32)
    w_ref[...] = wf_ref[...].astype(bf16)
    x_ref[0:LEAD, :] = jnp.zeros((LEAD, plan.mixed), f32)
    for m in range(n):
        tok = toks[m][...].astype(f32)
        scale = lax.rsqrt(jnp.mean(tok * tok, axis=1, keepdims=True) + norm_eps)
        low = (tok * scale * gain_ref[...]).astype(bf16)
        start = (s ^ m) * plan.rows
        normed_ref[pl.ds(aligned(start, plan.rows), plan.rows), :] = low
        out = jnp.dot(low, w_ref[...], preferred_element_type=f32)
        x_ref[pl.ds(aligned(start + LEAD, 8), plan.rows), :] = out[:, : plan.mixed]
        dt_ref[pl.ds(aligned(start, plan.rows), plan.rows), :] = out[:, plan.mixed :]


def scan_kernel(plan, first, last, *refs):
    x_ref, dt_ref, segc_ref, segr_ref, conv_ref, heads_ref = refs[:6]
    refs = refs[6:]
    if first:
        early_y_ref, early_ref = refs[:2]
        refs = refs[2:]
    y_ref, state_ref, states_ref, mixed_ref, slope_ref, table_ref, scores_ref = refs
    if first:
        y_ref[: first * GROUP, :] = early_y_ref[...]
        state_ref[...] = early_ref[...]
    else:
        state_ref[...] = jnp.zeros_like(state_ref)
    convw = conv_ref[0:KERNEL, :]
    convb = conv_ref[KERNEL : KERNEL + 1, :]
    chan, half = plan.chan, LANES // 2
    causal = iota((GROUP, GROUP), 0) >= iota((GROUP, GROUP), 1)

    def step(turn, carry):
        base = aligned((first + turn) * GROUP, GROUP)
        here = pl.ds(aligned(turn * GROUP, GROUP), GROUP)
        mixed, slope = convolved(plan, base, x_ref, segc_ref, convw, convb)
        mixed_ref[here, :] = mixed
        slope_ref[here, :] = slope
        values = mixed[:, :chan]
        keys = mixed[:, chan : chan + STATE]
        queries = mixed[:, chan + STATE :]
        dt_in = dt_ref[pl.ds(base, GROUP), :] + heads_ref[0:1, :LANES]
        steps, cum, turned = decays(dt_in, heads_ref)
        table_ref[0, here, :] = steps
        table_ref[1, here, :] = cum
        table_ref[2, here, :] = turned
        seg, keep, to_last = edges(segc_ref, base, cum)
        allowed = (seg == segr_ref[pl.ds(first + turn, 1), :]) & causal
        scores = jnp.where(allowed, mm_nt(queries, keys), 0.0)
        scores_ref[here, :] = scores
        state = state_ref[...]
        states_ref[turn] = state
        parts = []
        for pair in range(plan.heads // 2):
            lanes = slice(pair * LANES, (pair + 1) * LANES)
            weights_pair = []
            for h in (2 * pair, 2 * pair + 1):
                decay = head_decay(cum, turned, h)
                weights_pair.append(decay * scores * turned[half + h : half + h + 1, :])
            parts.append(mm(jnp.concatenate(weights_pair, axis=1), split_pair(values[:, lanes])))
        inside = jnp.concatenate(parts, axis=1)
        spread = wide(jnp.concatenate([keep, to_last * steps], axis=0), chan)
        keep, to_end = spread[:GROUP], spread[GROUP:]
        carried = mm(queries, state) * keep
        y_ref[pl.ds(base, GROUP), :] = inside + carried + heads_ref[2:3, :] * values
        state_ref[...] = state * keep[GROUP - 1 :] + mm_tn(keys, values * to_end)
        return carry

    lax.fori_loop(0, last - first, step, 0, unroll=True)


def gate_kernel(plan, *refs):
    n = plan.seq
    normed_ref, y_ref = refs[:2]
    weights = refs[2 : 2 + 2 * plan.line]
    cots = refs[2 + 2 * plan.line : 2 + 2 * plan.line + n]
    gain_ref = refs[2 + 2 * plan.line + n]
    outs = refs[3 + 2 * plan.line + n :]
    wz_ref, z_ref, du_ref, stats_ref = outs[:4]
    parts = outs[4 : 4 + n]
    wf_ref, wo_ref = outs[4 + n :]
    ids = place()
    s, z, c = ids
    half = plan.in_rows * n // 2
    for core_xor in range(2):
        for line_xor in range(plan.line):
            piece = weights[core_xor * plan.line + line_xor]
            for m in range(n):
                dest = pl.ds(in_place(plan, ids, line_xor, core_xor, m), plan.in_rows)
                top = (m // 2) * plan.in_rows
                left = (m % 2) * plan.chan
                wf_ref[dest, :] = piece[
                    top : top + plan.in_rows, left : left + plan.chan
                ].astype(f32)
            start = ((z ^ line_xor) * 2 + (c ^ core_xor)) * plan.out_rows
            wo_ref[pl.ds(aligned(start, 16), plan.out_rows), :] = piece[
                half : half + plan.out_rows, :
            ]
    wz_ref[...] = wf_ref[...].astype(bf16)
    gain = gain_ref[...]
    lane = iota((plan.rows, LANES), 1)
    square = jnp.zeros((GROUP, LANES), f32)
    lane = iota((GROUP, LANES), 1)
    per = plan.rows // GROUP
    for m in range(n):
        start = aligned((s ^ m) * plan.rows, plan.rows)
        gate = jnp.dot(
            normed_ref[pl.ds(start, plan.rows), :], wz_ref[...], preferred_element_type=f32
        )
        z_ref[pl.ds(start, plan.rows), :] = gate
        gated = y_ref[pl.ds(start, plan.rows), :] * gate * sigmoid(gate)
        scaled = gated * gain
        parts[m][...] = mm(scaled, wo_ref[...]).astype(parts[m].dtype)
        du = mm_nt(cots[m][...], wo_ref[...])
        du_ref[pl.ds(start, plan.rows), :] = du
        norm = jnp.sum(gated * gated, axis=1, keepdims=True)
        dots = jnp.sum(du * scaled, axis=1, keepdims=True)
        for j in range(per):
            b = (s ^ m) * per + j
            rows = slice(j * GROUP, (j + 1) * GROUP)
            square = square + jnp.where(lane == b, norm[rows], 0.0)
            square = square + jnp.where(lane == b + plan.blocks, dots[rows], 0.0)
    stats_ref[...] = square.T[: 2 * plan.blocks]


def emit_rows(plan, ids, source_ref, put):
    for core_xor in range(2):
        for line_xor in range(plan.line):
            for m in range(plan.seq):
                rows = source_ref[
                    pl.ds(in_place(plan, ids, line_xor, core_xor, m), plan.in_rows), :
                ]
                put(core_xor, line_xor, m, rows)


def row_products(w_ref, grad_ref):
    lane = iota((LANES, LANES), 1)
    square = jnp.zeros((LANES, LANES), f32)
    for i in range(w_ref.shape[0] // LANES):
        rows = slice(i * LANES, (i + 1) * LANES)
        product = w_ref[rows, :].astype(f32) * grad_ref[rows, :]
        square = square + jnp.where(lane == i, jnp.sum(product, axis=1, keepdims=True), 0.0)
    return square.T[:8]


def regate_kernel(plan, *refs):
    n = plan.seq
    stats = refs[:n]
    normed_ref, y_ref, z_ref, du_ref, wz_ref = refs[n : n + 5]
    cots = refs[n + 5 : 2 * n + 5]
    gain_ref = refs[2 * n + 5]
    dy_ref, dz_ref, scale_ref, gain_out_ref, share_ref, keep_ref, send_ref = refs[
        2 * n + 6 : 2 * n + 13
    ]
    gated_ref, gz_ref, go_ref = refs[2 * n + 13 :]
    ids = place()
    s, z, c = ids
    total = stats[0][...]
    for m in range(1, n):
        total = total + stats[m][...]
    turned = jnp.concatenate(
        [total, jnp.zeros((LANES - total.shape[0], GROUP), f32)], axis=0
    ).T
    gain = gain_ref[...]
    sums = jnp.zeros((1, plan.chan), f32)
    for b in range(plan.blocks):
        rows = slice(b * GROUP, (b + 1) * GROUP)
        r = lax.rsqrt(turned[:, b : b + 1] / INNER + norm_eps)
        dot = turned[:, plan.blocks + b : plan.blocks + b + 1] / INNER
        scale_ref[rows, :] = jnp.broadcast_to(r, (GROUP, LANES))
        gate = z_ref[rows, :]
        sig = sigmoid(gate)
        silu = gate * sig
        y = y_ref[rows, :]
        gated = y * silu
        du = du_ref[rows, :]
        normal = gated * r
        grad_pre = r * (du * gain) - normal * (r * r * dot)
        dy_ref[rows, :] = grad_pre * silu
        dz_ref[rows, :] = (grad_pre * y * sig * (1.0 + gate * (1.0 - sig))).astype(bf16)
        gated_ref[rows, :] = (normal * gain).astype(bf16)
        sums = sums + jnp.sum(du * normal, axis=0, keepdims=True)
    gain_out_ref[...] = sums
    gz_ref[...] = mm_tn(normed_ref[...], dz_ref[...])
    share_ref[...] = row_products(wz_ref, gz_ref)
    out = None
    for m in range(n):
        start = aligned((s ^ m) * plan.rows, plan.rows)
        one = mm_tn(gated_ref[pl.ds(start, plan.rows), :], cots[m][...])
        out = one if out is None else out + one
    go_ref[...] = out
    half = plan.in_rows * n // 2
    both = (keep_ref, send_ref)

    def put(core_xor, line_xor, m, rows):
        top = (m // 2) * plan.in_rows
        left = (m % 2) * plan.chan
        both[core_xor][line_xor, top : top + plan.in_rows, left : left + plan.chan] = rows.astype(
            bf16
        )

    emit_rows(plan, ids, gz_ref, put)
    for core_xor in range(2):
        for line_xor in range(plan.line):
            start = ((z ^ line_xor) * 2 + (c ^ core_xor)) * plan.out_rows
            both[core_xor][line_xor, half : half + plan.out_rows, :] = go_ref[
                pl.ds(aligned(start, 16), plan.out_rows), :
            ].astype(bf16)


def scan_back_kernel(plan, first, last, *refs):
    x_ref, dt_ref, segc_ref, segr_ref, dy_ref, conv_ref, heads_ref = refs[:7]
    states_ref, mixed_ref, slope_ref, table_ref, scores_ref = refs[7:12]
    refs = refs[12:]
    later = last < plan.blocks
    if later:
        before, refs = refs[:5], refs[5:]
    gp_ref, adj_ref, edge_ref, acc_ref, head_ref = refs
    if later:
        gp_ref[(last - first) * GROUP :, :] = before[0][...]
        adj_ref[...] = before[1][...]
        edge_ref[...] = before[2][...]
        acc_ref[...] = before[3][...]
        head_ref[...] = before[4][...]
    else:
        adj_ref[...] = jnp.zeros_like(adj_ref)
        edge_ref[...] = jnp.zeros_like(edge_ref)
        acc_ref[...] = jnp.zeros_like(acc_ref)
        head_ref[...] = jnp.zeros_like(head_ref)
    convw = conv_ref[0:KERNEL, :]
    chan, half = plan.chan, LANES // 2
    repeat = plan.mixed // LANES
    pick = (iota((chan, LANES), 0) // HEADDIM == iota((chan, LANES), 1)).astype(f32)
    row = iota((GROUP, LANES), 0)
    lane = iota((GROUP, LANES), 1)

    def step(turn, carry):
        b = last - 1 - turn
        base = aligned(b * GROUP, GROUP)
        here = pl.ds(aligned((b - first) * GROUP, GROUP), GROUP)
        values = mixed_ref[here, :chan]
        keys = mixed_ref[here, chan : chan + STATE]
        queries = mixed_ref[here, chan + STATE :]
        steps = table_ref[0, here, :]
        cum = table_ref[1, here, :]
        turned = table_ref[2, here, :]
        scores = scores_ref[here, :]
        seg, keep_h, to_last = edges(segc_ref, base, cum)
        state = states_ref[b - first]
        adj = adj_ref[...]
        dy = dy_ref[pl.ds(base, GROUP), :]
        spread = wide(jnp.concatenate([keep_h, to_last * steps], axis=0), chan)
        keep, to_end = spread[:GROUP], spread[GROUP:]
        kept = dy * keep
        dq = mm_nt(kept, state)
        cross = kept * mm(queries, state)
        fed = mm(keys, adj)
        dk = mm_nt(values * to_end, adj)
        adj_ref[...] = adj * keep[GROUP - 1 :] + mm_tn(queries, kept)
        ended = jnp.sum(state * adj, axis=0, keepdims=True)
        pushed = fed * values
        skipped = jnp.sum(dy * values, axis=0, keepdims=True)
        few = jnp.concatenate([ended, skipped, jnp.zeros((6, chan), f32)], axis=0)
        high = few.astype(bf16).astype(f32)
        sums = mm(jnp.concatenate([cross, pushed, high, few - high], axis=0), pick)
        cross_h = sums[:GROUP]
        pushed_h = sums[GROUP : 2 * GROUP]
        few_h = sums[2 * GROUP : 2 * GROUP + 8] + sums[2 * GROUP + 8 :]
        ended_h = few_h[0:1]
        skipped_h = few_h[1:2]
        grad_steps = pushed_h * to_last
        pulled = grad_steps * steps
        dcum = cross_h - pulled
        at_end = jnp.sum(pulled, axis=0, keepdims=True) + keep_h[GROUP - 1 :] * ended_h
        dscores = None
        columns = []
        dvs = []
        for pair in range(plan.heads // 2):
            lanes = slice(pair * LANES, (pair + 1) * LANES)
            dy_pair = split_pair(dy[:, lanes])
            products = mm_nt(dy_pair, values[:, lanes])
            stacked = []
            for j, h in enumerate((2 * pair, 2 * pair + 1)):
                scaled = head_decay(cum, turned, h) * turned[half + h : half + h + 1, :]
                weighted = scaled * products[j * GROUP : (j + 1) * GROUP]
                both = weighted * scores
                dscores = weighted if dscores is None else dscores + weighted
                dcum = jnp.where(lane == h, dcum + jnp.sum(both, axis=1, keepdims=True), dcum)
                columns.append(jnp.sum(both, axis=0, keepdims=True))
                stacked.append(scaled * scores)
            dvs.append(mm_tn(jnp.concatenate(stacked, axis=0), dy_pair))
        allowed = (seg == segr_ref[pl.ds(b, 1), :]) & (row >= lane)
        dscores = jnp.where(allowed, dscores, 0.0)
        dv = jnp.concatenate(dvs, axis=1) + fed * to_end + heads_ref[2:3, :] * dy
        columns.append(jnp.zeros((LANES - plan.heads, GROUP), f32))
        down = jnp.concatenate(columns, axis=0).T
        grad_steps = grad_steps + down / jnp.maximum(steps, TINY)
        dcum = dcum - down
        dcum = dcum + jnp.where(row == GROUP - 1, at_end, 0.0)
        dk = dk + mm_tn(dscores, queries)
        dq = dq + mm(dscores, keys)
        ddecay = mask_mm(row <= lane, dcum)
        rate = jnp.exp(heads_ref[1:2, :LANES])
        grad_steps = grad_steps - ddecay * rate
        dt_in = dt_ref[pl.ds(base, GROUP), :] + heads_ref[0:1, :LANES]
        grad_dt = grad_steps * exact_sigmoid(dt_in)
        head_ref[0:1, :] += jnp.sum(grad_dt, axis=0, keepdims=True)
        head_ref[1:2, :] -= jnp.sum(ddecay * steps, axis=0, keepdims=True) * rate
        head_ref[2:3, :] += skipped_h
        dpre = jnp.concatenate([dv, dk, dq], axis=1) * slope_ref[here, :]
        longer = jnp.concatenate([dpre, edge_ref[...]], axis=0)
        edge_ref[...] = dpre[:LEAD]
        segn = segc_ref[pl.ds(aligned(base + LEAD, 8), GROUP + LEAD), :]
        x = x_ref[pl.ds(aligned(base + LEAD, 8), GROUP), :]
        acc_ref[KERNEL : KERNEL + 1, :] += jnp.sum(dpre, axis=0, keepdims=True)
        acc_ref[KERNEL - 1 : KERNEL, :] += jnp.sum(dpre * x, axis=0, keepdims=True)
        dx = convw[KERNEL - 1 : KERNEL] * dpre
        for k in range(KERNEL - 1):
            ahead = KERNEL - 1 - k
            same = (segn[ahead : ahead + GROUP] == seg).astype(f32)
            part = longer[ahead : ahead + GROUP] * jnp.concatenate([same] * repeat, axis=1)
            acc_ref[k : k + 1, :] += jnp.sum(part * x, axis=0, keepdims=True)
            dx = dx + convw[k : k + 1] * part
        live = jnp.where(lane < plan.heads, grad_dt, 0.0)
        gp_ref[here, :] = jnp.concatenate([dx, live], axis=1).astype(bf16)
        return carry

    lax.fori_loop(0, last - first, step, 0, unroll=True)


def main_grads_kernel(
    plan, normed_ref, gp_ref, w_ref, gain_ref, share_ref, gain_out_ref, acc_ref, head_ref,
    keep_ref, send_ref, gw_ref, small_ref,
):
    ids = place()
    gw_ref[...] = mm_tn(normed_ref[...], gp_ref[...])
    both = (keep_ref, send_ref)

    def put(core_xor, line_xor, m, rows):
        top = m * plan.in_rows
        both[core_xor][line_xor, top : top + plan.in_rows, :] = rows.astype(bf16)

    emit_rows(plan, ids, gw_ref, put)
    share = share_ref[...] + row_products(w_ref, gw_ref)
    small_ref[...] = jnp.zeros_like(small_ref)
    for i in range(WIDTH // LANES):
        lanes = slice(i * LANES, (i + 1) * LANES)
        small_ref[0:1, lanes] = share[i : i + 1] / gain_ref[:, lanes]
    small_ref[1:6, : plan.mixed] = acc_ref[0:5, :]
    small_ref[6:7, : plan.chan] = gain_out_ref[...]
    for j in range(3):
        small_ref[7:8, j * LANES : (j + 1) * LANES] = head_ref[j : j + 1, :]
    high, low = two_parts(small_ref[...])
    last = plan.seq * plan.in_rows
    for ref in both:
        for line_xor in range(plan.line):
            ref[line_xor, last : last + 8, :] = high
            ref[line_xor, last + 8 : last + 16, :] = low


def normed_grads_kernel(plan, gp_ref, w_ref, dz_ref, wz_ref, *grads):
    s = lax.axis_index("seq")
    for m in range(plan.seq):
        rows = pl.ds(aligned((s ^ m) * plan.rows, plan.rows), plan.rows)
        part = mm_nt(gp_ref[rows, :], w_ref[...]) + mm_nt(dz_ref[rows, :], wz_ref[...])
        grads[m][...] = part.astype(grads[m].dtype)


def joined(ref, top):
    return ref[top : top + 8, :].astype(f32) + ref[top + 8 : top + 16, :].astype(f32)


def main_split_kernel(plan, keep_ref, got_ref, *outs):
    last = plan.seq * plan.in_rows
    small = joined(keep_ref.at[0], last) + joined(got_ref.at[0], last)
    high, low = two_parts(small)
    for m in range(plan.line):
        total = keep_ref[m, :last, :].astype(f32) + got_ref[m, :last, :].astype(f32)
        outs[m][:last, :] = total.astype(bf16)
        outs[m][last : last + 8, :] = high
        outs[m][last + 8 :, :] = low


def gate_split_kernel(plan, keep_ref, got_ref, *outs):
    for m in range(plan.line):
        outs[m][...] = (keep_ref[m].astype(f32) + got_ref[m].astype(f32)).astype(bf16)


def gate_sum_kernel(plan, *refs):
    parts, (gate_ref, out_ref) = refs[: plan.line], refs[plan.line :]
    total = parts[0][...].astype(f32)
    for part in parts[1:]:
        total = total + part[...].astype(f32)
    half = plan.in_rows * plan.seq // 2
    gate_ref[...] = total[:half].astype(bf16)
    out_ref[...] = total[half : half + plan.out_rows]


def row_sum_kernel(plan, gate_ref, *refs):
    parts, outs = refs[: plan.line], refs[plan.line :]
    r, chan = plan.in_rows, plan.chan
    last = plan.seq * r
    small = joined(parts[0], last)
    for part in parts[1:]:
        small = small + joined(part, last)
    high, low = two_parts(small)
    for m in range(plan.seq):
        rows = slice(m * r, (m + 1) * r)
        total = parts[0][rows, :].astype(f32)
        for part in parts[1:]:
            total = total + part[rows, :].astype(f32)
        outs[m][:r, :] = total.astype(bf16)
        outs[m][r : r + 8, :] = high
        outs[m][r + 8 : r + 16, :] = low
        top, left = (m // 2) * r, (m % 2) * chan
        outs[m][r + 16 :, :chan] = gate_ref[top : top + r, left : left + chan]
        outs[m][r + 16 :, chan:] = jnp.zeros((r, plan.cols - chan), bf16)


def columns_kernel(plan, *refs):
    n, r, chan, heads = plan.seq, plan.in_rows, plan.chan, plan.heads
    parts, refs = refs[:n], refs[n:]
    out_ref, gain_in_ref, convw_ref, convb_ref, dtb_ref, alog_ref, skip_ref = refs[:7]
    gain_out_ref, gate_ref, main_ref, small_ref = refs[7:]
    s = lax.axis_index("seq")
    for m in range(n):
        main_ref[m] = parts[m][:r, :].astype(f32)
        small_ref[m] = joined(parts[m], r)
        gate_ref[m] = parts[m][r + 16 :, :chan].astype(f32)
    shared = jnp.zeros((r, 2 * STATE), f32)
    lane = iota((r, LANES), 1)
    dts = jnp.zeros((r, LANES), f32)
    gain_in = jnp.zeros((1, WIDTH), f32)
    small_shared = jnp.zeros((5, 2 * STATE), f32)
    one_lane = iota((1, LANES), 1)
    rows = [jnp.zeros((1, LANES), f32) for _ in range(3)]
    for g in range(n):
        cols = slice(g * chan, (g + 1) * chan)
        out_ref[:, cols] = gate_ref[s ^ g]
        main = main_ref[s ^ g]
        out_ref[:, INNER + g * chan : INNER + (g + 1) * chan] = main[:, :chan]
        shared = shared + main[:, chan : plan.mixed]
        one = main[:, plan.mixed :]
        moved = one if g == 0 else pltpu.roll(one, g * heads, 1)
        dts = jnp.where(lane // heads == g, moved, dts)
        part = small_ref[s ^ g]
        gain_in = gain_in + part[0:1, :WIDTH]
        convw_ref[:, cols] = part[1:5, :chan]
        convb_ref[cols] = part[5, :chan]
        gain_out_ref[cols] = part[6, :chan]
        small_shared = small_shared + part[1:6, chan : plan.mixed]
        for j in range(3):
            one = part[7:8, j * LANES : (j + 1) * LANES]
            moved = one if g == 0 else pltpu.roll(one, g * heads, 1)
            rows[j] = jnp.where(one_lane // heads == g, moved, rows[j])
    out_ref[:, 2 * INNER : INNER + CONV] = shared
    out_ref[:, INNER + CONV :] = dts[:, :HEADS]
    gain_in_ref[...] = gain_in[0]
    convw_ref[:, INNER:] = small_shared[:4]
    convb_ref[INNER:] = small_shared[4]
    dtb_ref[...] = rows[0][:, :HEADS]
    alog_ref[...] = rows[1][:, :HEADS]
    skip_ref[...] = rows[2][:, :HEADS]


def result_kernel(plan, tok_ref, scale_ref, *refs):
    parts, out_ref = refs[: plan.seq], refs[plan.seq]
    s = lax.axis_index("seq")
    total = parts[0][...].astype(f32)
    for part in parts[1:]:
        total = total + part[...].astype(f32)
    r = scale_ref[pl.ds(aligned(s * plan.rows, plan.rows), plan.rows), :]
    r = jnp.concatenate([r] * (WIDTH // LANES), axis=1)
    out_ref[...] = (tok_ref[...].astype(f32) + total * r).astype(bf16)


def token_kernel(plan, tok_ref, cot_ref, gain_ref, *refs):
    parts, out_ref = refs[: plan.seq], refs[plan.seq]
    total = parts[0][...].astype(f32)
    for part in parts[1:]:
        total = total + part[...].astype(f32)
    tok = tok_ref[...].astype(f32)
    q = lax.rsqrt(jnp.mean(tok * tok, axis=1, keepdims=True) + norm_eps)
    w = total * gain_ref[...]
    mean = jnp.mean(w * tok, axis=1, keepdims=True)
    grad = cot_ref[...].astype(f32) + q * w - tok * (q * q * q * mean)
    out_ref[...] = grad.astype(bf16)


def call(body, plan, outs, scratch, *args, mib=4, micros=1, name=None, kept=0):
    shapes = [jax.ShapeDtypeStruct(shape, kind) for shape, kind in outs]
    size = sum(a.size * a.dtype.itemsize for a in args)
    size += sum(a.size * a.dtype.itemsize for a in shapes)
    return pl.pallas_call(
        functools.partial(body, plan),
        out_shape=shapes,
        in_specs=[pl.BlockSpec(memory_space=pltpu.HBM)] * kept
        + [pl.BlockSpec(memory_space=pltpu.VMEM)] * (len(args) - kept),
        out_specs=[pl.BlockSpec(memory_space=pltpu.VMEM)] * len(shapes),
        scratch_shapes=[
            pltpu.VMEM(*one) if isinstance(one, tuple) else one for one in scratch
        ],
        compiler_params=pltpu.CompilerParams(vmem_limit_bytes=mib * 2**20),
        cost_estimate=pl.CostEstimate(
            flops=micros * FLOPS_PER_MICRO, bytes_accessed=0, transcendentals=0
        ),
        name=name,
    )(*args)


FLOPS_PER_MICRO = 3_000_000_000
LATE = 4


def swap(value, axis, by):
    size = lax.axis_size(axis)
    return lax.ppermute(value, axis, [(i, i ^ by) for i in range(size)])


def after(value, *others):
    return lax.optimization_barrier((value, *others))[0]


def head_parallel(
    tokens, cotangent, segments, in_weight, out_weight, gain_in, conv_weight, conv_bias,
    dt_bias, a_log, d_skip, gain_out,
):
    rows = tokens.shape[1]
    plan = Plan(
        lax.axis_size("seq"), lax.axis_size("batch"), rows, in_weight.shape[0], out_weight.shape[0]
    )
    n, line, chan, heads = plan.seq, plan.line, plan.chan, plan.heads
    s = lax.axis_index("seq")
    tok, cot = tokens[0], cotangent[0]

    r = plan.in_rows
    own = call(
        pack_kernel, plan, [((r + 8, plan.cols + chan), bf16)] * n,
        [
            (in_weight.shape, bf16), (segments.shape, jnp.int32), pltpu.SemaphoreType.DMA((2,)),
            ((n, r, plan.cols + chan), bf16),
        ],
        in_weight, segments, name="pack", kept=2,
    )
    pieces = [own[0]] + [swap(own[m], "seq", m) for m in range(1, n)]
    toks = [tok] + [swap(after(tok, pieces[m]), "seq", m) for m in range(1, n)]
    main_shard, gate_shard = call(
        regroup_kernel, plan,
        [((n * r, plan.cols), bf16), ((n * r // 2 + plan.out_rows, WIDTH), bf16)], [],
        *pieces, out_weight, name="regroup",
    )

    def along(shard):
        return [shard] + [swap(shard, "batch", 2 * m) for m in range(1, line)]

    def both_cores(parts):
        return parts + [swap(one, "batch", 1) for one in parts]

    main_line = along(main_shard)
    main_parts = both_cores(main_line)
    gate_line = along(after(gate_shard, *main_line))
    cot_near = after(cot, *toks)
    conv, per_head, own_gain = call(
        own_params_kernel, plan,
        [((8, plan.mixed), f32), ((8, chan), f32), ((1, chan), f32)], [],
        conv_weight, conv_bias[None], dt_bias[None], a_log[None], d_skip[None], gain_out[None],
        name="own_params",
    )
    gain_row = gain_in[None]
    total = plan.total
    seg_rows = -(-plan.blocks // 8) * 8
    normed, w_main, x, dt_raw, segc, segr = call(
        project_kernel, plan,
        [
            ((total, WIDTH), bf16), ((WIDTH, plan.cols), bf16),
            ((total + LEAD, plan.mixed), f32), ((total, LANES), f32),
            ((total + 2 * LEAD, LANES), f32), ((seg_rows, GROUP), f32),
        ],
        [((WIDTH, plan.cols), f32)],
        *toks, *pieces, *main_parts, gain_row, mib=16, micros=5, name="project",
    )
    cot_far = after(cot, normed)
    cots = [cot] + [swap(cot_near if m < 3 else cot_far, "seq", m) for m in range(1, n)]
    half = plan.blocks // 2
    state_shape = (STATE, chan)
    scan_in = (x, dt_raw, segc, segr, conv, per_head)

    def scan_part(first, last, *early):
        count, size = last - first, (last - first) * GROUP
        return list(call(
            lambda p, *refs: scan_kernel(p, first, last, *refs), plan,
            [
                ((last * GROUP, chan), f32), (state_shape, f32), ((count,) + state_shape, f32),
                ((size, plan.mixed), f32), ((size, plan.mixed), f32), ((3, size, LANES), f32),
                ((size, GROUP), f32),
            ], [],
            *scan_in, *early, mib=16, micros=4, name="scan_forward",
        ))

    early_y, early_state, *early = scan_part(0, half)
    gate_line = [after(one, early_state) for one in gate_line]
    gate_parts = both_cores(gate_line)
    early_state = after(early_state, *gate_line, *cots[1:3])
    y, _, *late = scan_part(half, plan.blocks, early_y, early_state)
    piece_shape = (rows, WIDTH)
    w_gate, z, du, stats, *outs = call(
        gate_kernel, plan,
        [
            ((WIDTH, chan), bf16), ((total, chan), f32), ((total, chan), f32),
            ((2 * plan.blocks, GROUP), f32),
        ] + [(piece_shape, bf16)] * n,
        [((WIDTH, chan), f32), ((chan, WIDTH), bf16)],
        normed, y, *gate_parts, *cots, own_gain,
        mib=16, micros=6, name="gate_forward",
    )
    all_stats = [stats] + [swap(stats, "seq", m) for m in range(1, n)]
    dy, dz, scale, gain_out_grad, share, keep, send = call(
        regate_kernel, plan,
        [
            ((total, chan), f32), ((total, chan), bf16), ((total, LANES), f32), ((1, chan), f32),
            ((8, LANES), f32),
            ((line, n * r // 2 + plan.out_rows, WIDTH), bf16),
            ((line, n * r // 2 + plan.out_rows, WIDTH), bf16),
        ],
        [((total, chan), bf16), ((WIDTH, chan), f32), ((chan, WIDTH), f32)],
        *all_stats, normed, y, z, du, w_gate, *cots, own_gain,
        mib=16, micros=6, name="gate_backward",
    )

    def reduce_line(keep, send, body, name):
        got = swap(send, "batch", 1)
        parts = call(
            body, plan, [(keep.shape[1:], bf16)] * line, [], keep, got, name=name, micros=LATE,
        )
        return list(parts)

    def line_exchange(parts):
        return [parts[0]] + [swap(parts[m], "batch", 2 * m) for m in range(1, line)]

    gate_half = reduce_line(keep, send, gate_split_kernel, "gate_core_sum")
    dy = after(dy, *gate_half)
    back_in = (x, dt_raw, segc, segr, dy, conv, per_head)

    def scan_back_part(first, last, saved, *before):
        return call(
            lambda p, *refs: scan_back_kernel(p, first, last, *refs), plan,
            [
                ((total - first * GROUP, plan.cols), bf16), (state_shape, f32),
                ((LEAD, plan.mixed), f32), ((8, plan.mixed), f32), ((8, LANES), f32),
            ], [],
            *back_in, *saved, *before, mib=16, micros=7, name="scan_backward",
        )

    before = list(scan_back_part(half, plan.blocks, late))
    out_parts = [outs[0]] + [swap(outs[m], "seq", m) for m in range(1, n)]
    gate_half[-1] = after(gate_half[-1], before[1])
    gate_lines = line_exchange(gate_half)
    gate_rows, shard_out = call(
        gate_sum_kernel, plan,
        [((n * r // 2, WIDTH), bf16), ((plan.out_rows, WIDTH), f32)], [], *gate_lines,
        name="gate_sum", micros=LATE,
    )
    before[1] = after(before[1], *gate_lines[:-1])
    gp, _, _, acc, head_acc = scan_back_part(0, half, early, *before)
    (result,) = call(
        result_kernel, plan, [(piece_shape, bf16)], [], tok, scale, *out_parts, name="result", micros=LATE
    )

    grads = call(
        normed_grads_kernel, plan, [(piece_shape, bf16)] * n, [], gp, w_main, dz, w_gate,
        mib=12, micros=3 * LATE, name="normed_grads",
    )
    gp_late = after(gp, *out_parts, *gate_lines, *grads)
    keep, send = call(
        main_grads_kernel, plan, [((line, n * r + 16, plan.cols), bf16)] * 2,
        [((WIDTH, plan.cols), f32), ((8, plan.cols), f32)],
        normed, gp_late, w_main, gain_row, share, gain_out_grad, acc, head_acc,
        mib=12, micros=4 * LATE, name="main_grads",
    )
    main_half = reduce_line(keep, send, main_split_kernel, "main_core_sum")
    main_lines = line_exchange(main_half)
    grad_parts = [grads[0]] + [swap(grads[m], "seq", m) for m in range(1, n)]
    last = call(
        row_sum_kernel, plan, [((2 * r + 16, plan.cols), bf16)] * n, [], gate_rows, *main_lines,
        name="main_sum", micros=LATE,
    )
    last = [last[0]] + [swap(last[m], "seq", m) for m in range(1, n)]
    (grad_tokens,) = call(
        token_kernel, plan, [(piece_shape, bf16)], [], tok, cot, gain_row, *grad_parts,
        name="token_grad", micros=LATE,
    )
    shard_in, *smalls = call(
        columns_kernel, plan,
        [
            ((r, in_weight.shape[1]), f32),
            ((WIDTH,), f32), ((KERNEL, CONV), f32), ((CONV,), f32), ((1, HEADS), f32),
            ((1, HEADS), f32), ((1, HEADS), f32), ((INNER,), f32),
        ],
        [((n, r, chan), f32), ((n, r, plan.cols), f32), ((n, 8, plan.cols), f32)],
        *last, name="columns", micros=LATE,
    )
    return (
        result[None], grad_tokens[None], shard_in, shard_out, smalls[0], smalls[1],
        smalls[2], smalls[3][0], smalls[4][0], smalls[5][0], smalls[6],
    )


def shifted(value, axis, by):
    size = lax.axis_size(axis)
    pairs = [(i, i + by) for i in range(size) if 0 <= i + by < size]
    return lax.ppermute(value, axis, pairs)


def prefix(value, axis, join, neutral):
    place = lax.axis_index(axis)
    gathered = jax.tree.map(
        lambda a, kind: lax.all_gather(a.astype(kind), axis), value, (jnp.bfloat16, jnp.bfloat16)
    )
    state = jax.tree.map(lambda a, e: jnp.zeros_like(a) + jnp.asarray(e, a.dtype), value, neutral)

    def one(turn, state):
        return join(
            state,
            jax.tree.map(
                lambda a, own: lax.dynamic_index_in_dim(a, turn, 0, False).astype(own.dtype),
                gathered,
                value,
            ),
        )

    return lax.fori_loop(0, place, one, state)


def prefix_2(value, axis, join, neutral):
    count = lax.axis_size(axis)
    place = lax.axis_index(axis)
    ahead = count - 1 - place
    gathered = jax.tree.map(
        lambda a, kind: lax.all_gather(a.astype(kind), axis),
        value,
        jax.tree.map(lambda a: jnp.bfloat16 if a.dtype == jnp.float32 else a.dtype, value),
    )
    state = jax.tree.map(lambda a, e: jnp.zeros_like(a) + jnp.asarray(e, a.dtype), value, neutral)

    def one(turn, state):
        source = count - 1 - turn
        return join(
            state,
            jax.tree.map(
                lambda a, own: lax.dynamic_index_in_dim(a, source, 0, False).astype(own.dtype),
                gathered,
                value,
            ),
        )

    return lax.fori_loop(0, ahead, one, state)


def rms_scale(values, gain):
    mean_square = jnp.mean(values * values, axis=-1, keepdims=True)
    return values * lax.rsqrt(mean_square + norm_eps) * gain


def causal_conv(extended, ext_segs, conv_weight, conv_bias, row_count):
    target = ext_segs[KERNEL - 1 :]
    total = jnp.zeros((row_count, conv_weight.shape[1]), jnp.float32) + conv_bias[None, :]
    for offset in range(KERNEL):
        window = extended[offset : offset + row_count]
        same_doc = (ext_segs[offset : offset + row_count] == target).astype(jnp.float32)
        total = total + conv_weight[offset][None, :] * window * same_doc[:, None]
    return jax.nn.silu(total)


def prepare(xbc, dt_raw, edge_rows, ext_segs, conv_weight, conv_bias, dt_bias, a_log):
    row_count = xbc.shape[0]
    extended = jnp.concatenate([edge_rows, xbc], axis=0)
    mixed = causal_conv(extended, ext_segs, conv_weight, conv_bias, row_count)
    values = mixed[:, :INNER].reshape(row_count, HEADS, HEADDIM)
    key_vecs = mixed[:, INNER : INNER + STATE]
    queries = mixed[:, INNER + STATE :]
    step_sizes = jax.nn.softplus(dt_raw + dt_bias[None, :])
    log_decay = -step_sizes * jnp.exp(a_log)[None, :]
    return (values, key_vecs, queries, step_sizes, log_decay)


def group_block(carried, block_in):
    state_in, last_seg = carried
    values, key_vecs, queries, step_sizes, log_decay, seg_ids = block_in
    length_here = seg_ids.shape[0]
    cumulative = jnp.cumsum(log_decay, axis=0)
    positions = jnp.arange(length_here)
    allowed = (seg_ids[:, None] == seg_ids[None, :]) & (positions[:, None] >= positions[None, :])
    gap_logs = cumulative[:, None, :] - cumulative[None, :, :]
    decay_mask = jnp.where(allowed[:, :, None], jnp.exp(jnp.minimum(gap_logs, 0.0)), 0.0)
    scores = jnp.dot(queries, key_vecs.T, precision=highest)
    weights = decay_mask * scores[:, :, None] * step_sizes[None, :, :]
    inside = jnp.einsum("tsh,shp->thp", weights, values, precision=highest)
    keep_factor = jnp.where((seg_ids == last_seg)[:, None], jnp.exp(cumulative), 0.0)
    carried_out = (
        jnp.einsum("tn,hpn->thp", queries, state_in, precision=highest) * keep_factor[:, :, None]
    )
    to_end = (
        jnp.where(
            (seg_ids == seg_ids[-1])[:, None], jnp.exp(cumulative[-1][None, :] - cumulative), 0.0
        )
        * step_sizes
    )
    fresh_state = jnp.einsum("sh,shp,sn->hpn", to_end, values, key_vecs, precision=highest)
    new_state = state_in * keep_factor[-1][:, None, None] + fresh_state
    return ((new_state, seg_ids[-1]), inside + carried_out)


def grouped_ssd(
    values, key_vecs, queries, step_sizes, log_decay, seg_ids, d_skip, state_in, last_seg
):
    row_count = seg_ids.shape[0]
    block_count = row_count // GROUP

    def blocked(member):
        return member.reshape((block_count, GROUP) + member.shape[1:])

    inputs = (
        blocked(values),
        blocked(key_vecs),
        blocked(queries),
        blocked(step_sizes),
        blocked(log_decay),
        blocked(seg_ids),
    )
    (final_state, last_out), outputs = lax.scan(
        jax.checkpoint(group_block), (state_in, last_seg), inputs
    )
    outputs = outputs.reshape(row_count, HEADS, HEADDIM) + d_skip[None, :, None] * values
    return (outputs, final_state)


def gated_norm(mixed_out, gate_z, gain_out):
    return rms_scale(mixed_out * jax.nn.silu(gate_z), gain_out)


def chain_combine(earlier, later):
    decay_early, state_early = earlier
    decay_late, state_late = later
    return (decay_early * decay_late, decay_late[:, None, None] * state_early + state_late)


def cross_term(queries, log_decay, state_in, seg_ids, prev_seg):
    cumulative = jnp.cumsum(log_decay, axis=0)
    keep_factor = jnp.where((seg_ids == prev_seg)[:, None], jnp.exp(cumulative), 0.0)
    return jnp.einsum("tn,hpn->thp", queries, state_in, precision=highest) * keep_factor[:, :, None]


def device_decay(log_decay, seg_ids, prev_seg):
    total_log = jnp.sum(log_decay, axis=0)
    return jnp.where(seg_ids[-1] == prev_seg, jnp.exp(total_log), 0.0)


def on_device(
    tokens,
    cotangent,
    segments,
    in_weight,
    out_weight,
    gain_in,
    conv_weight,
    conv_bias,
    dt_bias,
    a_log,
    d_skip,
    gain_out,
):
    tokens_f = tokens[0].astype(jnp.float32)
    cot_low = cotangent[0]
    seg_ids = segments[0]
    row_count = seg_ids.shape[0]
    full_in, full_out = (
        lax.all_gather(in_weight, ("seq", "batch"), axis=0, tiled=True),
        lax.all_gather(out_weight, ("seq", "batch"), axis=0, tiled=True),
    )
    normed, norm_pull = jax.vjp(rms_scale, tokens_f, gain_in)
    normed_low = normed.astype(jnp.bfloat16)
    projected = jnp.dot(normed_low, full_in, preferred_element_type=jnp.float32)
    gate_z = projected[:, :INNER]
    xbc = projected[:, INNER : INNER + CONV]
    dt_raw = projected[:, INNER + CONV :]
    tail_start = row_count - KERNEL + 1
    edge_rows, edge_segs = shifted(
        (xbc[tail_start:], seg_ids[tail_start:].astype(jnp.float32)), "seq", 1
    )
    prev_segs = edge_segs.astype(jnp.int32)
    prev_seg = prev_segs[KERNEL - 2]
    ext_segs = jnp.concatenate([prev_segs, seg_ids])

    def prepare_local(xbc_in, dt_in, edge_in, weight_in, bias_in, shift_in, alog_in):
        return prepare(xbc_in, dt_in, edge_in, ext_segs, weight_in, bias_in, shift_in, alog_in)

    prepared, prepare_pull = jax.vjp(
        prepare_local, xbc, dt_raw, edge_rows, conv_weight, conv_bias, dt_bias, a_log
    )
    values, key_vecs, queries, step_sizes, log_decay = prepared
    zeros_state = jnp.zeros((HEADS, HEADDIM, STATE), jnp.float32)

    def local_ssd(values_in, keys_in, queries_in, sizes_in, logs_in, skip_in):
        return grouped_ssd(
            values_in,
            keys_in,
            queries_in,
            sizes_in,
            logs_in,
            seg_ids,
            skip_in,
            zeros_state,
            seg_ids[0],
        )

    (local_out, local_state), ssd_pull = jax.vjp(
        local_ssd, values, key_vecs, queries, step_sizes, log_decay, d_skip
    )

    def decay_local(logs_in):
        return device_decay(logs_in, seg_ids, prev_seg)

    decay_here, decay_pull = jax.vjp(decay_local, log_decay)
    identity = (jnp.ones((HEADS,), jnp.float32), zeros_state)
    decay_prefix, state_in = prefix((decay_here, local_state), "seq", chain_combine, identity)

    def cross_local(queries_in, logs_in, state_arg):
        return cross_term(queries_in, logs_in, state_arg, seg_ids, prev_seg)

    cross_out, cross_pull = jax.vjp(cross_local, queries, log_decay, state_in)
    mixed_out = (local_out + cross_out).reshape(row_count, INNER)
    gated, gated_pull = jax.vjp(gated_norm, mixed_out, gate_z, gain_out)
    gated_low = gated.astype(jnp.bfloat16)
    result = tokens_f + jnp.dot(gated_low, full_out, preferred_element_type=jnp.float32)
    back_in, back_out = (
        lax.all_gather(in_weight, ("seq", "batch"), axis=0, tiled=True),
        lax.all_gather(out_weight, ("seq", "batch"), axis=0, tiled=True),
    )
    contract_last = (((1,), (1,)), ((), ()))
    contract_first = (((0,), (0,)), ((), ()))
    grad_gated = lax.dot_general(
        cot_low, back_out, contract_last, preferred_element_type=jnp.float32
    )
    grad_mixed, grad_gate, grad_gain_out = gated_pull(grad_gated)
    grad_mixed = grad_mixed.reshape(row_count, HEADS, HEADDIM)
    grad_q_cross, grad_log_cross, grad_state_in = cross_pull(grad_mixed)
    decay_after, grad_exit = prefix_2((decay_here, grad_state_in), "seq", chain_combine, identity)
    grad_decay = jnp.sum(grad_exit * state_in, axis=(1, 2))
    grad_log_dev = decay_pull(grad_decay)[0]
    grad_values, grad_keys, grad_q_local, grad_sizes, grad_log_local, grad_skip = ssd_pull(
        (grad_mixed, grad_exit)
    )
    prep_grads = prepare_pull(
        (
            grad_values,
            grad_keys,
            grad_q_local + grad_q_cross,
            grad_sizes,
            grad_log_local + grad_log_cross + grad_log_dev,
        )
    )
    grad_xbc, grad_dt, grad_edge, grad_conv_w, grad_conv_b, grad_dt_bias, grad_a_log = prep_grads
    grad_next = shifted(grad_edge, "seq", -1)
    grad_xbc = grad_xbc.at[tail_start:].add(grad_next)
    grad_proj = jnp.concatenate([grad_gate, grad_xbc, grad_dt], axis=1).astype(jnp.bfloat16)
    grad_normed = lax.dot_general(
        grad_proj, back_in, contract_last, preferred_element_type=jnp.float32
    )
    grad_tokens_norm, grad_gain_in = norm_pull(grad_normed)
    grad_tokens = (cot_low.astype(jnp.float32) + grad_tokens_norm).astype(jnp.bfloat16)
    grad_in_w = lax.dot_general(
        normed_low, grad_proj, contract_first, preferred_element_type=jnp.float32
    )
    grad_out_w = lax.dot_general(
        gated_low, cot_low, contract_first, preferred_element_type=jnp.float32
    )
    shard_in, shard_out = (
        lax.psum_scatter(grad_in_w, ("seq", "batch"), scatter_dimension=0, tiled=True),
        lax.psum_scatter(grad_out_w, ("seq", "batch"), scatter_dimension=0, tiled=True),
    )
    summed = lax.psum(
        (
            grad_gain_in,
            grad_conv_w,
            grad_conv_b,
            grad_dt_bias,
            grad_a_log,
            grad_skip,
            grad_gain_out,
        ),
        ("seq", "batch"),
    )
    return (
        result.astype(jnp.bfloat16)[None],
        grad_tokens[None],
        shard_in,
        shard_out,
        summed[0],
        summed[1],
        summed[2],
        summed[3],
        summed[4],
        summed[5],
        summed[6],
    )


def solution(mesh):
    in_specs = (
        P("batch", "seq", None),
        P("batch", "seq", None),
        P("batch", "seq"),
        P(("seq", "batch"), None),
        P(("seq", "batch"), None),
        P(),
        P(),
        P(),
        P(),
        P(),
        P(),
        P(),
    )
    out_specs = (
        P("batch", "seq", None),
        P("batch", "seq", None),
        P(("seq", "batch"), None),
        P(("seq", "batch"), None),
        P(),
        P(),
        P(),
        P(),
        P(),
        P(),
        P(),
    )
    count = mesh.shape["seq"]
    even = HEADS % (2 * count) == 0 and count & (count - 1) == 0
    return jax.shard_map(
        head_parallel if even else on_device, mesh=mesh, in_specs=in_specs, out_specs=out_specs, check_vma=False
    )
```

```python
import functools

import jax
import jax.numpy as jnp
from jax import lax
from jax.experimental import pallas as pl
from jax.experimental.pallas import tpu as pltpu
from jax.sharding import PartitionSpec as P

HEADS = 24
HEADDIM = 64
STATE = 128
KERNEL = 4
GROUP = 128
INNER = 1536
CONV = 1792
WIDTH = 768
LANES = 128
LEAD = 8
TINY = 1e-37


highest = lax.Precision.HIGHEST
norm_eps = 1e-05
f32 = jnp.float32
bf16 = jnp.bfloat16
contract_last = (((1,), (1,)), ((), ()))
contract_first = (((0,), (0,)), ((), ()))


def mm(a, b):
    return jnp.dot(a.astype(bf16), b.astype(bf16), preferred_element_type=f32)


def mm_nt(a, b):
    return lax.dot_general(
        a.astype(bf16), b.astype(bf16), contract_last, preferred_element_type=f32
    )


def mm_tn(a, b):
    return lax.dot_general(
        a.astype(bf16), b.astype(bf16), contract_first, preferred_element_type=f32
    )


def two_parts(value):
    high = value.astype(bf16)
    return high, (value - high.astype(f32)).astype(bf16)


def mask_mm(mask, value):
    width = value.shape[1]
    out = mm(mask, jnp.concatenate(two_parts(value), axis=1))
    return out[:, :width] + out[:, width:]


def iota(shape, dim):
    return lax.broadcasted_iota(jnp.int32, shape, dim)


def aligned(value, unit):
    return pl.multiple_of(value, unit)


def wide(columns, chan):
    half = LANES // 2
    high, low = two_parts(columns)
    low = pltpu.roll(low.astype(f32), half, 1)
    both = jnp.where(iota(columns.shape, 1) < half, high.astype(f32), low)
    spread = iota((LANES, chan), 1) // HEADDIM == lax.rem(iota((LANES, chan), 0), half)
    return mm(both, spread.astype(f32))


def softplus(value):
    return jnp.maximum(value, 0.0) + jnp.log1p(jnp.exp(-jnp.abs(value)))


def sigmoid(value):
    return 0.5 + 0.5 * jnp.tanh(0.5 * value)


class Plan:
    def __init__(self, mesh_seq, mesh_batch, rows, in_rows, out_rows):
        self.seq = mesh_seq
        self.batch = mesh_batch
        self.line = mesh_batch // 2
        self.rows = rows
        self.total = rows * mesh_seq
        self.blocks = self.total // GROUP
        self.heads = HEADS // mesh_seq
        self.chan = self.heads * HEADDIM
        self.mixed = self.chan + 2 * STATE
        self.cols = self.mixed + LANES
        self.in_rows = in_rows
        self.out_rows = out_rows


def place():
    s = lax.axis_index("seq")
    b = lax.axis_index("batch")
    return s, lax.shift_right_logical(b, 1), lax.bitwise_and(b, 1)


def in_place(plan, ids, line_xor, core_xor, seq_xor):
    s, z, c = ids
    owner = (s ^ seq_xor) * plan.batch + (z ^ line_xor) * 2 + (c ^ core_xor)
    return aligned(owner * plan.in_rows, 8)


def exact_sigmoid(value):
    return 1.0 / (1.0 + jnp.exp(-value))


def convolved(plan, base, x_ref, segc_ref, convw, convb):
    win = x_ref[pl.ds(base, GROUP + LEAD), :]
    segw = segc_ref[pl.ds(base, GROUP + LEAD), :]
    seg = segw[LEAD:]
    pre = convb + convw[KERNEL - 1 : KERNEL] * win[LEAD:]
    for k in range(KERNEL - 1):
        start = LEAD - KERNEL + 1 + k
        same = (segw[start : start + GROUP] == seg).astype(f32)
        same = jnp.concatenate([same] * (plan.mixed // LANES), axis=1)
        pre = pre + convw[k : k + 1] * win[start : start + GROUP] * same
    sig = sigmoid(pre)
    mixed = pre * sig
    return mixed, sig + mixed * (1.0 - sig)


def decays(dt_in, heads_ref):
    steps = softplus(dt_in)
    row = iota((GROUP, GROUP), 0)
    col = iota((GROUP, GROUP), 1)
    decay = -steps * jnp.exp(heads_ref[1:2, :LANES])
    cum = mask_mm(row >= col, decay)
    half = LANES // 2
    turned = jnp.where(col < half, cum, pltpu.roll(steps, half, 1)).T
    return steps, cum, turned


def edges(segc_ref, base, cum):
    seg = segc_ref[pl.ds(aligned(base + LEAD, 8), GROUP), :]
    prev = segc_ref[pl.ds(base, LEAD), :][LEAD - 1 :]
    keep = jnp.where(seg == prev, jnp.exp(cum), 0.0)
    last = cum[GROUP - 1 :]
    to_last = jnp.where(seg == seg[GROUP - 1 :], jnp.exp(last - cum), 0.0)
    return seg, keep, to_last


def head_decay(cum, turned, h):
    return jnp.exp(jnp.minimum(cum[:, h : h + 1] - turned[h : h + 1, :], 0.0))


def split_pair(pair):
    low = iota(pair.shape, 1) < HEADDIM
    return jnp.concatenate([jnp.where(low, pair, 0.0), jnp.where(low, 0.0, pair)], axis=0)


def fetch(pairs, sems):
    copies = [
        pltpu.make_async_copy(src, dst, sems.at[i]) for i, (src, dst) in enumerate(pairs)
    ]
    for copy in copies:
        copy.start()
    for copy in copies:
        copy.wait()


def pack_kernel(plan, w_any, seg_any, *outs):
    n, heads, chan = plan.seq, plan.heads, plan.chan
    blocks, outs = outs[:n], outs[n:]
    w_ref, seg_ref, sems, all_ref = outs
    fetch([(w_any, w_ref), (seg_any, seg_ref)], sems)
    s = lax.axis_index("seq")
    lane = iota((plan.in_rows, LANES), 1)
    tail = w_ref[:, INNER + CONV :].astype(f32)
    tail = jnp.concatenate(
        [tail, jnp.zeros((plan.in_rows, LANES - HEADS), f32)], axis=1
    )
    for g in range(n):
        moved = tail if g == 0 else pltpu.roll(tail, LANES - g * heads, 1)
        all_ref[g] = jnp.concatenate(
            [
                w_ref[:, INNER + g * chan : INNER + (g + 1) * chan],
                w_ref[:, 2 * INNER : INNER + CONV],
                jnp.where(lane < heads, moved, 0.0).astype(bf16),
                w_ref[:, g * chan : (g + 1) * chan],
            ],
            axis=1,
        )
    seg = jnp.broadcast_to(seg_ref[...].astype(f32), (8, plan.rows)).astype(bf16)
    for m in range(n):
        blocks[m][0 : plan.in_rows, :] = all_ref[s ^ m]
        blocks[m][plan.in_rows : plan.in_rows + 8, :] = jnp.zeros((8, plan.cols + chan), bf16)
        blocks[m][plan.in_rows : plan.in_rows + 8, : plan.rows] = seg


def own_params_kernel(
    plan, convw_ref, convb_ref, dtb_ref, alog_ref, skip_ref, gain_ref, conv_ref, heads_ref,
    own_gain_ref,
):
    n, heads, chan = plan.seq, plan.heads, plan.chan
    s = lax.axis_index("seq")
    own = pl.ds(aligned(s * chan, LANES), chan)
    conv_ref[...] = jnp.zeros_like(conv_ref)
    conv_ref[0:KERNEL, :chan] = convw_ref[:, own]
    conv_ref[0:KERNEL, chan:] = convw_ref[:, INNER:]
    conv_ref[KERNEL : KERNEL + 1, :chan] = convb_ref[:, own]
    conv_ref[KERNEL : KERNEL + 1, chan:] = convb_ref[:, INNER:]
    own_gain_ref[...] = gain_ref[:, own]
    one_lane = iota((1, LANES), 1)

    def own_heads(ref):
        row = jnp.concatenate([ref[...], jnp.zeros((1, LANES - HEADS), f32)], axis=1)
        found = row
        for g in range(1, n):
            found = jnp.where(s == g, pltpu.roll(row, LANES - g * heads, 1), found)
        return jnp.where(one_lane < heads, found, 0.0)

    heads_ref[...] = jnp.zeros_like(heads_ref)
    heads_ref[0:1, :LANES] = own_heads(dtb_ref)
    heads_ref[1:2, :LANES] = own_heads(alog_ref)
    skip = jnp.broadcast_to(own_heads(skip_ref), (8, LANES))
    heads_ref[2:3, :] = wide(skip, chan)[0:1]


def regroup_kernel(plan, *refs):
    n, r = plan.seq, plan.in_rows
    pieces, out_w_ref = refs[:n], refs[n]
    main_ref, gate_ref = refs[n + 1 :]
    half = r * n // 2
    for m in range(n):
        main_ref[m * r : (m + 1) * r, :] = pieces[m][0:r, : plan.cols]
        top, left = (m // 2) * r, (m % 2) * plan.chan
        gate_ref[top : top + r, left : left + plan.chan] = pieces[m][0:r, plan.cols :]
    gate_ref[half : half + plan.out_rows, :] = out_w_ref[...]


def fill_segments(plan, s, pieces, segc_ref, segr_ref):
    per = plan.rows // GROUP
    segc_ref[...] = jnp.zeros_like(segc_ref)
    segr_ref[...] = jnp.zeros_like(segr_ref)
    for m in range(plan.seq):
        line = pieces[m][plan.in_rows : plan.in_rows + 1, : plan.rows].astype(f32)
        for j in range(per):
            b = (s ^ m) * per + j
            segr_ref[pl.ds(b, 1), :] = line[:, j * GROUP : (j + 1) * GROUP]
    every = segr_ref[...]
    turned = jnp.concatenate(
        [every, jnp.zeros((LANES - every.shape[0], GROUP), f32)], axis=0
    ).T
    for b in range(plan.blocks):
        segc_ref[LEAD + b * GROUP : LEAD + (b + 1) * GROUP, :] = jnp.broadcast_to(
            turned[:, b : b + 1], (GROUP, LANES)
        )


def project_kernel(plan, *refs):
    n = plan.seq
    toks, refs = refs[:n], refs[n:]
    pieces, refs = refs[:n], refs[n:]
    weights, refs = refs[: 2 * plan.line], refs[2 * plan.line :]
    gain_ref = refs[0]
    normed_ref, w_ref, x_ref, dt_ref, segc_ref, segr_ref, wf_ref = refs[1:]
    ids = place()
    s = ids[0]
    fill_segments(plan, s, pieces, segc_ref, segr_ref)
    for core_xor in range(2):
        for line_xor in range(plan.line):
            piece = weights[core_xor * plan.line + line_xor]
            for m in range(n):
                dest = pl.ds(in_place(plan, ids, line_xor, core_xor, m), plan.in_rows)
                wf_ref[dest, :] = piece[m * plan.in_rows : (m + 1) * plan.in_rows, :].astype(f32)
    w_ref[...] = wf_ref[...].astype(bf16)
    x_ref[0:LEAD, :] = jnp.zeros((LEAD, plan.mixed), f32)
    for m in range(n):
        tok = toks[m][...].astype(f32)
        scale = lax.rsqrt(jnp.mean(tok * tok, axis=1, keepdims=True) + norm_eps)
        low = (tok * scale * gain_ref[...]).astype(bf16)
        start = (s ^ m) * plan.rows
        normed_ref[pl.ds(aligned(start, plan.rows), plan.rows), :] = low
        out = jnp.dot(low, w_ref[...], preferred_element_type=f32)
        x_ref[pl.ds(aligned(start + LEAD, 8), plan.rows), :] = out[:, : plan.mixed]
        dt_ref[pl.ds(aligned(start, plan.rows), plan.rows), :] = out[:, plan.mixed :]


def scan_kernel(plan, first, last, *refs):
    x_ref, dt_ref, segc_ref, segr_ref, conv_ref, heads_ref = refs[:6]
    refs = refs[6:]
    if first:
        early_y_ref, early_ref = refs[:2]
        refs = refs[2:]
    y_ref, state_ref, states_ref, mixed_ref, slope_ref, table_ref, scores_ref = refs
    if first:
        y_ref[: first * GROUP, :] = early_y_ref[...]
        state_ref[...] = early_ref[...]
    else:
        state_ref[...] = jnp.zeros_like(state_ref)
    convw = conv_ref[0:KERNEL, :]
    convb = conv_ref[KERNEL : KERNEL + 1, :]
    chan, half = plan.chan, LANES // 2
    causal = iota((GROUP, GROUP), 0) >= iota((GROUP, GROUP), 1)

    def step(turn, carry):
        base = aligned((first + turn) * GROUP, GROUP)
        here = pl.ds(aligned(turn * GROUP, GROUP), GROUP)
        mixed, slope = convolved(plan, base, x_ref, segc_ref, convw, convb)
        mixed_ref[here, :] = mixed
        slope_ref[here, :] = slope
        values = mixed[:, :chan]
        keys = mixed[:, chan : chan + STATE]
        queries = mixed[:, chan + STATE :]
        dt_in = dt_ref[pl.ds(base, GROUP), :] + heads_ref[0:1, :LANES]
        steps, cum, turned = decays(dt_in, heads_ref)
        table_ref[0, here, :] = steps
        table_ref[1, here, :] = cum
        table_ref[2, here, :] = turned
        seg, keep, to_last = edges(segc_ref, base, cum)
        allowed = (seg == segr_ref[pl.ds(first + turn, 1), :]) & causal
        scores = jnp.where(allowed, mm_nt(queries, keys), 0.0)
        scores_ref[here, :] = scores
        state = state_ref[...]
        states_ref[turn] = state
        parts = []
        for pair in range(plan.heads // 2):
            lanes = slice(pair * LANES, (pair + 1) * LANES)
            weights_pair = []
            for h in (2 * pair, 2 * pair + 1):
                decay = head_decay(cum, turned, h)
                weights_pair.append(decay * scores * turned[half + h : half + h + 1, :])
            parts.append(mm(jnp.concatenate(weights_pair, axis=1), split_pair(values[:, lanes])))
        inside = jnp.concatenate(parts, axis=1)
        spread = wide(jnp.concatenate([keep, to_last * steps], axis=0), chan)
        keep, to_end = spread[:GROUP], spread[GROUP:]
        carried = mm(queries, state) * keep
        y_ref[pl.ds(base, GROUP), :] = inside + carried + heads_ref[2:3, :] * values
        state_ref[...] = state * keep[GROUP - 1 :] + mm_tn(keys, values * to_end)
        return carry

    lax.fori_loop(0, last - first, step, 0, unroll=True)


def gate_kernel(plan, *refs):
    n = plan.seq
    normed_ref, y_ref = refs[:2]
    weights = refs[2 : 2 + 2 * plan.line]
    cots = refs[2 + 2 * plan.line : 2 + 2 * plan.line + n]
    gain_ref = refs[2 + 2 * plan.line + n]
    outs = refs[3 + 2 * plan.line + n :]
    wz_ref, z_ref, du_ref, stats_ref, scaled_ref, wo_ref, wf_ref = outs
    ids = place()
    s, z, c = ids
    half = plan.in_rows * n // 2
    for core_xor in range(2):
        for line_xor in range(plan.line):
            piece = weights[core_xor * plan.line + line_xor]
            for m in range(n):
                dest = pl.ds(in_place(plan, ids, line_xor, core_xor, m), plan.in_rows)
                top = (m // 2) * plan.in_rows
                left = (m % 2) * plan.chan
                wf_ref[dest, :] = piece[
                    top : top + plan.in_rows, left : left + plan.chan
                ].astype(f32)
            start = ((z ^ line_xor) * 2 + (c ^ core_xor)) * plan.out_rows
            wo_ref[pl.ds(aligned(start, 16), plan.out_rows), :] = piece[
                half : half + plan.out_rows, :
            ]
    wz_ref[...] = wf_ref[...].astype(bf16)
    gain = gain_ref[...]
    lane = iota((plan.rows, LANES), 1)
    square = jnp.zeros((GROUP, LANES), f32)
    lane = iota((GROUP, LANES), 1)
    per = plan.rows // GROUP
    for m in range(n):
        start = aligned((s ^ m) * plan.rows, plan.rows)
        gate = jnp.dot(
            normed_ref[pl.ds(start, plan.rows), :], wz_ref[...], preferred_element_type=f32
        )
        z_ref[pl.ds(start, plan.rows), :] = gate
        gated = y_ref[pl.ds(start, plan.rows), :] * gate * sigmoid(gate)
        scaled = gated * gain
        scaled_ref[pl.ds(start, plan.rows), :] = scaled.astype(bf16)
        du = mm_nt(cots[m][...], wo_ref[...])
        du_ref[pl.ds(start, plan.rows), :] = du
        norm = jnp.sum(gated * gated, axis=1, keepdims=True)
        dots = jnp.sum(du * scaled, axis=1, keepdims=True)
        for j in range(per):
            b = (s ^ m) * per + j
            rows = slice(j * GROUP, (j + 1) * GROUP)
            square = square + jnp.where(lane == b, norm[rows], 0.0)
            square = square + jnp.where(lane == b + plan.blocks, dots[rows], 0.0)
    stats_ref[...] = square.T[: 2 * plan.blocks]


def out_kernel(plan, scaled_ref, wo_ref, *parts):
    s = lax.axis_index("seq")
    for m in range(plan.seq):
        rows = pl.ds(aligned((s ^ m) * plan.rows, plan.rows), plan.rows)
        parts[m][...] = mm(scaled_ref[rows, :], wo_ref[...]).astype(bf16)


def emit_rows(plan, ids, source_ref, put):
    for core_xor in range(2):
        for line_xor in range(plan.line):
            for m in range(plan.seq):
                rows = source_ref[
                    pl.ds(in_place(plan, ids, line_xor, core_xor, m), plan.in_rows), :
                ]
                put(core_xor, line_xor, m, rows)


def row_products(w_ref, grad_ref):
    lane = iota((LANES, LANES), 1)
    square = jnp.zeros((LANES, LANES), f32)
    for i in range(w_ref.shape[0] // LANES):
        rows = slice(i * LANES, (i + 1) * LANES)
        product = w_ref[rows, :].astype(f32) * grad_ref[rows, :]
        square = square + jnp.where(lane == i, jnp.sum(product, axis=1, keepdims=True), 0.0)
    return square.T[:8]


def regate_kernel(plan, *refs):
    n = plan.seq
    stats = refs[:n]
    normed_ref, y_ref, z_ref, du_ref, wz_ref = refs[n : n + 5]
    cots = refs[n + 5 : 2 * n + 5]
    gain_ref = refs[2 * n + 5]
    dy_ref, dz_ref, scale_ref, gain_out_ref, share_ref, keep_ref, send_ref = refs[
        2 * n + 6 : 2 * n + 13
    ]
    gated_ref, gz_ref, go_ref = refs[2 * n + 13 :]
    ids = place()
    s, z, c = ids
    total = stats[0][...]
    for m in range(1, n):
        total = total + stats[m][...]
    turned = jnp.concatenate(
        [total, jnp.zeros((LANES - total.shape[0], GROUP), f32)], axis=0
    ).T
    gain = gain_ref[...]
    sums = jnp.zeros((1, plan.chan), f32)
    for b in range(plan.blocks):
        rows = slice(b * GROUP, (b + 1) * GROUP)
        r = lax.rsqrt(turned[:, b : b + 1] / INNER + norm_eps)
        dot = turned[:, plan.blocks + b : plan.blocks + b + 1] / INNER
        scale_ref[rows, :] = jnp.broadcast_to(r, (GROUP, LANES))
        gate = z_ref[rows, :]
        sig = sigmoid(gate)
        silu = gate * sig
        y = y_ref[rows, :]
        gated = y * silu
        du = du_ref[rows, :]
        normal = gated * r
        grad_pre = r * (du * gain) - normal * (r * r * dot)
        dy_ref[rows, :] = grad_pre * silu
        dz_ref[rows, :] = (grad_pre * y * sig * (1.0 + gate * (1.0 - sig))).astype(bf16)
        gated_ref[rows, :] = (normal * gain).astype(bf16)
        sums = sums + jnp.sum(du * normal, axis=0, keepdims=True)
    gain_out_ref[...] = sums
    gz_ref[...] = mm_tn(normed_ref[...], dz_ref[...])
    share_ref[...] = row_products(wz_ref, gz_ref)
    out = None
    for m in range(n):
        start = aligned((s ^ m) * plan.rows, plan.rows)
        one = mm_tn(gated_ref[pl.ds(start, plan.rows), :], cots[m][...])
        out = one if out is None else out + one
    go_ref[...] = out
    half = plan.in_rows * n // 2
    both = (keep_ref, send_ref)

    def put(core_xor, line_xor, m, rows):
        top = (m // 2) * plan.in_rows
        left = (m % 2) * plan.chan
        both[core_xor][line_xor, top : top + plan.in_rows, left : left + plan.chan] = rows.astype(
            bf16
        )

    emit_rows(plan, ids, gz_ref, put)
    for core_xor in range(2):
        for line_xor in range(plan.line):
            start = ((z ^ line_xor) * 2 + (c ^ core_xor)) * plan.out_rows
            both[core_xor][line_xor, half : half + plan.out_rows, :] = go_ref[
                pl.ds(aligned(start, 16), plan.out_rows), :
            ].astype(bf16)


def scan_back_kernel(plan, first, last, *refs):
    x_ref, dt_ref, segc_ref, segr_ref, dy_ref, conv_ref, heads_ref = refs[:7]
    states_ref, mixed_ref, slope_ref, table_ref, scores_ref = refs[7:12]
    refs = refs[12:]
    later = last < plan.blocks
    if later:
        before, refs = refs[:5], refs[5:]
    gp_ref, adj_ref, edge_ref, acc_ref, head_ref = refs
    if later:
        gp_ref[(last - first) * GROUP :, :] = before[0][...]
        adj_ref[...] = before[1][...]
        edge_ref[...] = before[2][...]
        acc_ref[...] = before[3][...]
        head_ref[...] = before[4][...]
    else:
        adj_ref[...] = jnp.zeros_like(adj_ref)
        edge_ref[...] = jnp.zeros_like(edge_ref)
        acc_ref[...] = jnp.zeros_like(acc_ref)
        head_ref[...] = jnp.zeros_like(head_ref)
    convw = conv_ref[0:KERNEL, :]
    chan, half = plan.chan, LANES // 2
    repeat = plan.mixed // LANES
    pick = (iota((chan, LANES), 0) // HEADDIM == iota((chan, LANES), 1)).astype(f32)
    row = iota((GROUP, LANES), 0)
    lane = iota((GROUP, LANES), 1)

    def step(turn, carry):
        b = last - 1 - turn
        base = aligned(b * GROUP, GROUP)
        here = pl.ds(aligned((b - first) * GROUP, GROUP), GROUP)
        values = mixed_ref[here, :chan]
        keys = mixed_ref[here, chan : chan + STATE]
        queries = mixed_ref[here, chan + STATE :]
        steps = table_ref[0, here, :]
        cum = table_ref[1, here, :]
        turned = table_ref[2, here, :]
        scores = scores_ref[here, :]
        seg, keep_h, to_last = edges(segc_ref, base, cum)
        state = states_ref[b - first]
        adj = adj_ref[...]
        dy = dy_ref[pl.ds(base, GROUP), :]
        spread = wide(jnp.concatenate([keep_h, to_last * steps], axis=0), chan)
        keep, to_end = spread[:GROUP], spread[GROUP:]
        kept = dy * keep
        dq = mm_nt(kept, state)
        cross = kept * mm(queries, state)
        fed = mm(keys, adj)
        dk = mm_nt(values * to_end, adj)
        adj_ref[...] = adj * keep[GROUP - 1 :] + mm_tn(queries, kept)
        ended = jnp.sum(state * adj, axis=0, keepdims=True)
        pushed = fed * values
        skipped = jnp.sum(dy * values, axis=0, keepdims=True)
        few = jnp.concatenate([ended, skipped, jnp.zeros((6, chan), f32)], axis=0)
        high = few.astype(bf16).astype(f32)
        sums = mm(jnp.concatenate([cross, pushed, high, few - high], axis=0), pick)
        cross_h = sums[:GROUP]
        pushed_h = sums[GROUP : 2 * GROUP]
        few_h = sums[2 * GROUP : 2 * GROUP + 8] + sums[2 * GROUP + 8 :]
        ended_h = few_h[0:1]
        skipped_h = few_h[1:2]
        grad_steps = pushed_h * to_last
        pulled = grad_steps * steps
        dcum = cross_h - pulled
        at_end = jnp.sum(pulled, axis=0, keepdims=True) + keep_h[GROUP - 1 :] * ended_h
        dscores = None
        columns = []
        dvs = []
        for pair in range(plan.heads // 2):
            lanes = slice(pair * LANES, (pair + 1) * LANES)
            dy_pair = split_pair(dy[:, lanes])
            products = mm_nt(dy_pair, values[:, lanes])
            stacked = []
            for j, h in enumerate((2 * pair, 2 * pair + 1)):
                scaled = head_decay(cum, turned, h) * turned[half + h : half + h + 1, :]
                weighted = scaled * products[j * GROUP : (j + 1) * GROUP]
                both = weighted * scores
                dscores = weighted if dscores is None else dscores + weighted
                dcum = jnp.where(lane == h, dcum + jnp.sum(both, axis=1, keepdims=True), dcum)
                columns.append(jnp.sum(both, axis=0, keepdims=True))
                stacked.append(scaled * scores)
            dvs.append(mm_tn(jnp.concatenate(stacked, axis=0), dy_pair))
        allowed = (seg == segr_ref[pl.ds(b, 1), :]) & (row >= lane)
        dscores = jnp.where(allowed, dscores, 0.0)
        dv = jnp.concatenate(dvs, axis=1) + fed * to_end + heads_ref[2:3, :] * dy
        columns.append(jnp.zeros((LANES - plan.heads, GROUP), f32))
        down = jnp.concatenate(columns, axis=0).T
        grad_steps = grad_steps + down / jnp.maximum(steps, TINY)
        dcum = dcum - down
        dcum = dcum + jnp.where(row == GROUP - 1, at_end, 0.0)
        dk = dk + mm_tn(dscores, queries)
        dq = dq + mm(dscores, keys)
        ddecay = mask_mm(row <= lane, dcum)
        rate = jnp.exp(heads_ref[1:2, :LANES])
        grad_steps = grad_steps - ddecay * rate
        dt_in = dt_ref[pl.ds(base, GROUP), :] + heads_ref[0:1, :LANES]
        grad_dt = grad_steps * exact_sigmoid(dt_in)
        head_ref[0:1, :] += jnp.sum(grad_dt, axis=0, keepdims=True)
        head_ref[1:2, :] -= jnp.sum(ddecay * steps, axis=0, keepdims=True) * rate
        head_ref[2:3, :] += skipped_h
        dpre = jnp.concatenate([dv, dk, dq], axis=1) * slope_ref[here, :]
        longer = jnp.concatenate([dpre, edge_ref[...]], axis=0)
        edge_ref[...] = dpre[:LEAD]
        segn = segc_ref[pl.ds(aligned(base + LEAD, 8), GROUP + LEAD), :]
        x = x_ref[pl.ds(aligned(base + LEAD, 8), GROUP), :]
        acc_ref[KERNEL : KERNEL + 1, :] += jnp.sum(dpre, axis=0, keepdims=True)
        acc_ref[KERNEL - 1 : KERNEL, :] += jnp.sum(dpre * x, axis=0, keepdims=True)
        dx = convw[KERNEL - 1 : KERNEL] * dpre
        for k in range(KERNEL - 1):
            ahead = KERNEL - 1 - k
            same = (segn[ahead : ahead + GROUP] == seg).astype(f32)
            part = longer[ahead : ahead + GROUP] * jnp.concatenate([same] * repeat, axis=1)
            acc_ref[k : k + 1, :] += jnp.sum(part * x, axis=0, keepdims=True)
            dx = dx + convw[k : k + 1] * part
        live = jnp.where(lane < plan.heads, grad_dt, 0.0)
        gp_ref[here, :] = jnp.concatenate([dx, live], axis=1).astype(bf16)
        return carry

    lax.fori_loop(0, last - first, step, 0, unroll=True)


def main_grads_kernel(
    plan, normed_ref, gp_ref, w_ref, gain_ref, share_ref, gain_out_ref, acc_ref, head_ref,
    keep_ref, send_ref, gw_ref, small_ref,
):
    ids = place()
    gw_ref[...] = mm_tn(normed_ref[...], gp_ref[...])
    both = (keep_ref, send_ref)

    def put(core_xor, line_xor, m, rows):
        top = m * plan.in_rows
        both[core_xor][line_xor, top : top + plan.in_rows, :] = rows.astype(bf16)

    emit_rows(plan, ids, gw_ref, put)
    share = share_ref[...] + row_products(w_ref, gw_ref)
    small_ref[...] = jnp.zeros_like(small_ref)
    for i in range(WIDTH // LANES):
        lanes = slice(i * LANES, (i + 1) * LANES)
        small_ref[0:1, lanes] = share[i : i + 1] / gain_ref[:, lanes]
    small_ref[1:6, : plan.mixed] = acc_ref[0:5, :]
    small_ref[6:7, : plan.chan] = gain_out_ref[...]
    for j in range(3):
        small_ref[7:8, j * LANES : (j + 1) * LANES] = head_ref[j : j + 1, :]
    high, low = two_parts(small_ref[...])
    last = plan.seq * plan.in_rows
    for ref in both:
        for line_xor in range(plan.line):
            ref[line_xor, last : last + 8, :] = high
            ref[line_xor, last + 8 : last + 16, :] = low


def normed_grads_kernel(plan, gp_ref, w_ref, dz_ref, wz_ref, *grads):
    s = lax.axis_index("seq")
    for m in range(plan.seq):
        rows = pl.ds(aligned((s ^ m) * plan.rows, plan.rows), plan.rows)
        part = mm_nt(gp_ref[rows, :], w_ref[...]) + mm_nt(dz_ref[rows, :], wz_ref[...])
        grads[m][...] = part.astype(grads[m].dtype)


def joined(ref, top):
    return ref[top : top + 8, :].astype(f32) + ref[top + 8 : top + 16, :].astype(f32)


def main_split_kernel(plan, keep_ref, got_ref, *outs):
    last = plan.seq * plan.in_rows
    small = joined(keep_ref.at[0], last) + joined(got_ref.at[0], last)
    high, low = two_parts(small)
    for m in range(plan.line):
        total = keep_ref[m, :last, :].astype(f32) + got_ref[m, :last, :].astype(f32)
        outs[m][:last, :] = total.astype(bf16)
        outs[m][last : last + 8, :] = high
        outs[m][last + 8 :, :] = low


def gate_split_kernel(plan, keep_ref, got_ref, *outs):
    for m in range(plan.line):
        outs[m][...] = (keep_ref[m].astype(f32) + got_ref[m].astype(f32)).astype(bf16)


def gate_sum_kernel(plan, *refs):
    parts, (gate_ref, out_ref) = refs[: plan.line], refs[plan.line :]
    total = parts[0][...].astype(f32)
    for part in parts[1:]:
        total = total + part[...].astype(f32)
    half = plan.in_rows * plan.seq // 2
    gate_ref[...] = total[:half].astype(bf16)
    out_ref[...] = total[half : half + plan.out_rows]


def row_sum_kernel(plan, gate_ref, *refs):
    parts, outs = refs[: plan.line], refs[plan.line :]
    r, chan = plan.in_rows, plan.chan
    last = plan.seq * r
    small = joined(parts[0], last)
    for part in parts[1:]:
        small = small + joined(part, last)
    high, low = two_parts(small)
    for m in range(plan.seq):
        rows = slice(m * r, (m + 1) * r)
        total = parts[0][rows, :].astype(f32)
        for part in parts[1:]:
            total = total + part[rows, :].astype(f32)
        outs[m][:r, :] = total.astype(bf16)
        outs[m][r : r + 8, :] = high
        outs[m][r + 8 : r + 16, :] = low
        top, left = (m // 2) * r, (m % 2) * chan
        outs[m][r + 16 :, :chan] = gate_ref[top : top + r, left : left + chan]
        outs[m][r + 16 :, chan:] = jnp.zeros((r, plan.cols - chan), bf16)


def columns_kernel(plan, *refs):
    n, r, chan, heads = plan.seq, plan.in_rows, plan.chan, plan.heads
    parts, refs = refs[:n], refs[n:]
    out_ref, gain_in_ref, convw_ref, convb_ref, dtb_ref, alog_ref, skip_ref = refs[:7]
    gain_out_ref, gate_ref, main_ref, small_ref = refs[7:]
    s = lax.axis_index("seq")
    for m in range(n):
        main_ref[m] = parts[m][:r, :].astype(f32)
        small_ref[m] = joined(parts[m], r)
        gate_ref[m] = parts[m][r + 16 :, :chan].astype(f32)
    shared = jnp.zeros((r, 2 * STATE), f32)
    lane = iota((r, LANES), 1)
    dts = jnp.zeros((r, LANES), f32)
    gain_in = jnp.zeros((1, WIDTH), f32)
    small_shared = jnp.zeros((5, 2 * STATE), f32)
    one_lane = iota((1, LANES), 1)
    rows = [jnp.zeros((1, LANES), f32) for _ in range(3)]
    for g in range(n):
        cols = slice(g * chan, (g + 1) * chan)
        out_ref[:, cols] = gate_ref[s ^ g]
        main = main_ref[s ^ g]
        out_ref[:, INNER + g * chan : INNER + (g + 1) * chan] = main[:, :chan]
        shared = shared + main[:, chan : plan.mixed]
        one = main[:, plan.mixed :]
        moved = one if g == 0 else pltpu.roll(one, g * heads, 1)
        dts = jnp.where(lane // heads == g, moved, dts)
        part = small_ref[s ^ g]
        gain_in = gain_in + part[0:1, :WIDTH]
        convw_ref[:, cols] = part[1:5, :chan]
        convb_ref[cols] = part[5, :chan]
        gain_out_ref[cols] = part[6, :chan]
        small_shared = small_shared + part[1:6, chan : plan.mixed]
        for j in range(3):
            one = part[7:8, j * LANES : (j + 1) * LANES]
            moved = one if g == 0 else pltpu.roll(one, g * heads, 1)
            rows[j] = jnp.where(one_lane // heads == g, moved, rows[j])
    out_ref[:, 2 * INNER : INNER + CONV] = shared
    out_ref[:, INNER + CONV :] = dts[:, :HEADS]
    gain_in_ref[...] = gain_in[0]
    convw_ref[:, INNER:] = small_shared[:4]
    convb_ref[INNER:] = small_shared[4]
    dtb_ref[...] = rows[0][:, :HEADS]
    alog_ref[...] = rows[1][:, :HEADS]
    skip_ref[...] = rows[2][:, :HEADS]


def result_kernel(plan, tok_ref, scale_ref, *refs):
    parts, out_ref = refs[: plan.seq], refs[plan.seq]
    s = lax.axis_index("seq")
    total = parts[0][...].astype(f32)
    for part in parts[1:]:
        total = total + part[...].astype(f32)
    r = scale_ref[pl.ds(aligned(s * plan.rows, plan.rows), plan.rows), :]
    r = jnp.concatenate([r] * (WIDTH // LANES), axis=1)
    out_ref[...] = (tok_ref[...].astype(f32) + total * r).astype(bf16)


def token_kernel(plan, tok_ref, cot_ref, gain_ref, *refs):
    parts, out_ref = refs[: plan.seq], refs[plan.seq]
    total = parts[0][...].astype(f32)
    for part in parts[1:]:
        total = total + part[...].astype(f32)
    tok = tok_ref[...].astype(f32)
    q = lax.rsqrt(jnp.mean(tok * tok, axis=1, keepdims=True) + norm_eps)
    w = total * gain_ref[...]
    mean = jnp.mean(w * tok, axis=1, keepdims=True)
    grad = cot_ref[...].astype(f32) + q * w - tok * (q * q * q * mean)
    out_ref[...] = grad.astype(bf16)


def call(body, plan, outs, scratch, *args, mib=4, micros=1, name=None, kept=0):
    shapes = [jax.ShapeDtypeStruct(shape, kind) for shape, kind in outs]
    size = sum(a.size * a.dtype.itemsize for a in args)
    size += sum(a.size * a.dtype.itemsize for a in shapes)
    return pl.pallas_call(
        functools.partial(body, plan),
        out_shape=shapes,
        in_specs=[pl.BlockSpec(memory_space=pltpu.HBM)] * kept
        + [pl.BlockSpec(memory_space=pltpu.VMEM)] * (len(args) - kept),
        out_specs=[pl.BlockSpec(memory_space=pltpu.VMEM)] * len(shapes),
        scratch_shapes=[
            pltpu.VMEM(*one) if isinstance(one, tuple) else one for one in scratch
        ],
        compiler_params=pltpu.CompilerParams(vmem_limit_bytes=mib * 2**20),
        cost_estimate=pl.CostEstimate(
            flops=micros * FLOPS_PER_MICRO, bytes_accessed=0, transcendentals=0
        ),
        name=name,
    )(*args)


FLOPS_PER_MICRO = 3_000_000_000
LATE = 4


def swap(value, axis, by):
    size = lax.axis_size(axis)
    return lax.ppermute(value, axis, [(i, i ^ by) for i in range(size)])


def after(value, *others):
    return lax.optimization_barrier((value, *others))[0]


def head_parallel(
    tokens, cotangent, segments, in_weight, out_weight, gain_in, conv_weight, conv_bias,
    dt_bias, a_log, d_skip, gain_out,
):
    rows = tokens.shape[1]
    plan = Plan(
        lax.axis_size("seq"), lax.axis_size("batch"), rows, in_weight.shape[0], out_weight.shape[0]
    )
    n, line, chan, heads = plan.seq, plan.line, plan.chan, plan.heads
    s = lax.axis_index("seq")
    tok, cot = tokens[0], cotangent[0]

    r = plan.in_rows
    own = call(
        pack_kernel, plan, [((r + 8, plan.cols + chan), bf16)] * n,
        [
            (in_weight.shape, bf16), (segments.shape, jnp.int32), pltpu.SemaphoreType.DMA((2,)),
            ((n, r, plan.cols + chan), bf16),
        ],
        in_weight, segments, name="pack", kept=2,
    )
    pieces = [own[0]] + [swap(own[m], "seq", m) for m in range(1, n)]
    toks = [tok] + [swap(after(tok, pieces[m]), "seq", m) for m in range(1, n)]
    main_shard, gate_shard = call(
        regroup_kernel, plan,
        [((n * r, plan.cols), bf16), ((n * r // 2 + plan.out_rows, WIDTH), bf16)], [],
        *pieces, out_weight, name="regroup",
    )

    def along(shard):
        return [shard] + [swap(shard, "batch", 2 * m) for m in range(1, line)]

    def both_cores(parts):
        return parts + [swap(one, "batch", 1) for one in parts]

    main_line = along(main_shard)
    main_parts = both_cores(main_line)
    gate_line = along(after(gate_shard, *main_line))
    cot_near = after(cot, *toks)
    conv, per_head, own_gain = call(
        own_params_kernel, plan,
        [((8, plan.mixed), f32), ((8, chan), f32), ((1, chan), f32)], [],
        conv_weight, conv_bias[None], dt_bias[None], a_log[None], d_skip[None], gain_out[None],
        name="own_params",
    )
    gain_row = gain_in[None]
    total = plan.total
    seg_rows = -(-plan.blocks // 8) * 8
    normed, w_main, x, dt_raw, segc, segr = call(
        project_kernel, plan,
        [
            ((total, WIDTH), bf16), ((WIDTH, plan.cols), bf16),
            ((total + LEAD, plan.mixed), f32), ((total, LANES), f32),
            ((total + 2 * LEAD, LANES), f32), ((seg_rows, GROUP), f32),
        ],
        [((WIDTH, plan.cols), f32)],
        *toks, *pieces, *main_parts, gain_row, mib=16, micros=5, name="project",
    )
    cot_far = after(cot, normed)
    cots = [cot] + [swap(cot_near if m < 3 else cot_far, "seq", m) for m in range(1, n)]
    half = plan.blocks // 2
    state_shape = (STATE, chan)
    scan_in = (x, dt_raw, segc, segr, conv, per_head)

    def scan_part(first, last, *early):
        count, size = last - first, (last - first) * GROUP
        return list(call(
            lambda p, *refs: scan_kernel(p, first, last, *refs), plan,
            [
                ((last * GROUP, chan), f32), (state_shape, f32), ((count,) + state_shape, f32),
                ((size, plan.mixed), f32), ((size, plan.mixed), f32), ((3, size, LANES), f32),
                ((size, GROUP), f32),
            ], [],
            *scan_in, *early, mib=16, micros=4, name="scan_forward",
        ))

    early_y, early_state, *early = scan_part(0, half)
    gate_line = [after(one, early_state) for one in gate_line]
    gate_parts = both_cores(gate_line)
    early_state = after(early_state, *gate_line, *cots[1:3])
    y, _, *late = scan_part(half, plan.blocks, early_y, early_state)
    piece_shape = (rows, WIDTH)
    w_gate, z, du, stats, scaled, w_out = call(
        gate_kernel, plan,
        [
            ((WIDTH, chan), bf16), ((total, chan), f32), ((total, chan), f32),
            ((2 * plan.blocks, GROUP), f32), ((total, chan), bf16), ((chan, WIDTH), bf16),
        ],
        [((WIDTH, chan), f32)],
        normed, y, *gate_parts, *cots, own_gain,
        mib=16, micros=6, name="gate_forward",
    )
    outs = call(
        out_kernel, plan, [(piece_shape, bf16)] * n, [], scaled, w_out, mib=8, micros=2,
        name="out_partial",
    )
    all_stats = [stats] + [swap(stats, "seq", m) for m in range(1, n)]
    dy, dz, scale, gain_out_grad, share, keep, send = call(
        regate_kernel, plan,
        [
            ((total, chan), f32), ((total, chan), bf16), ((total, LANES), f32), ((1, chan), f32),
            ((8, LANES), f32),
            ((line, n * r // 2 + plan.out_rows, WIDTH), bf16),
            ((line, n * r // 2 + plan.out_rows, WIDTH), bf16),
        ],
        [((total, chan), bf16), ((WIDTH, chan), f32), ((chan, WIDTH), f32)],
        *all_stats, after(normed, *outs), y, z, du, w_gate, *cots, own_gain,
        mib=16, micros=6, name="gate_backward",
    )

    def reduce_line(keep, send, body, name):
        got = swap(send, "batch", 1)
        parts = call(
            body, plan, [(keep.shape[1:], bf16)] * line, [], keep, got, name=name, micros=LATE,
        )
        return list(parts)

    def line_exchange(parts):
        return [parts[0]] + [swap(parts[m], "batch", 2 * m) for m in range(1, line)]

    gate_half = reduce_line(keep, send, gate_split_kernel, "gate_core_sum")
    dy = after(dy, *gate_half)
    back_in = (x, dt_raw, segc, segr, dy, conv, per_head)

    def scan_back_part(first, last, saved, *before):
        return call(
            lambda p, *refs: scan_back_kernel(p, first, last, *refs), plan,
            [
                ((total - first * GROUP, plan.cols), bf16), (state_shape, f32),
                ((LEAD, plan.mixed), f32), ((8, plan.mixed), f32), ((8, LANES), f32),
            ], [],
            *back_in, *saved, *before, mib=16, micros=7, name="scan_backward",
        )

    before = list(scan_back_part(half, plan.blocks, late))
    out_parts = [outs[0]] + [swap(outs[m], "seq", m) for m in range(1, n)]
    gate_half[-1] = after(gate_half[-1], before[1])
    gate_lines = line_exchange(gate_half)
    gate_rows, shard_out = call(
        gate_sum_kernel, plan,
        [((n * r // 2, WIDTH), bf16), ((plan.out_rows, WIDTH), f32)], [], *gate_lines,
        name="gate_sum", micros=LATE,
    )
    before[1] = after(before[1], *gate_lines[:-1])
    gp, _, _, acc, head_acc = scan_back_part(0, half, early, *before)
    (result,) = call(
        result_kernel, plan, [(piece_shape, bf16)], [], tok, scale, *out_parts, name="result", micros=LATE
    )

    grads = call(
        normed_grads_kernel, plan, [(piece_shape, bf16)] * n, [], gp, w_main, dz, w_gate,
        mib=12, micros=3 * LATE, name="normed_grads",
    )
    gp_late = after(gp, *out_parts, *gate_lines, *grads)
    keep, send = call(
        main_grads_kernel, plan, [((line, n * r + 16, plan.cols), bf16)] * 2,
        [((WIDTH, plan.cols), f32), ((8, plan.cols), f32)],
        normed, gp_late, w_main, gain_row, share, gain_out_grad, acc, head_acc,
        mib=12, micros=4 * LATE, name="main_grads",
    )
    main_half = reduce_line(keep, send, main_split_kernel, "main_core_sum")
    main_lines = line_exchange(main_half)
    grad_parts = [grads[0]] + [swap(grads[m], "seq", m) for m in range(1, n)]
    last = call(
        row_sum_kernel, plan, [((2 * r + 16, plan.cols), bf16)] * n, [], gate_rows, *main_lines,
        name="main_sum", micros=LATE,
    )
    last = [last[0]] + [swap(last[m], "seq", m) for m in range(1, n)]
    (grad_tokens,) = call(
        token_kernel, plan, [(piece_shape, bf16)], [], tok, cot, gain_row, *grad_parts,
        name="token_grad", micros=LATE,
    )
    shard_in, *smalls = call(
        columns_kernel, plan,
        [
            ((r, in_weight.shape[1]), f32),
            ((WIDTH,), f32), ((KERNEL, CONV), f32), ((CONV,), f32), ((1, HEADS), f32),
            ((1, HEADS), f32), ((1, HEADS), f32), ((INNER,), f32),
        ],
        [((n, r, chan), f32), ((n, r, plan.cols), f32), ((n, 8, plan.cols), f32)],
        *last, name="columns", micros=LATE,
    )
    return (
        result[None], grad_tokens[None], shard_in, shard_out, smalls[0], smalls[1],
        smalls[2], smalls[3][0], smalls[4][0], smalls[5][0], smalls[6],
    )


def shifted(value, axis, by):
    size = lax.axis_size(axis)
    pairs = [(i, i + by) for i in range(size) if 0 <= i + by < size]
    return lax.ppermute(value, axis, pairs)


def prefix(value, axis, join, neutral):
    place = lax.axis_index(axis)
    gathered = jax.tree.map(
        lambda a, kind: lax.all_gather(a.astype(kind), axis), value, (jnp.bfloat16, jnp.bfloat16)
    )
    state = jax.tree.map(lambda a, e: jnp.zeros_like(a) + jnp.asarray(e, a.dtype), value, neutral)

    def one(turn, state):
        return join(
            state,
            jax.tree.map(
                lambda a, own: lax.dynamic_index_in_dim(a, turn, 0, False).astype(own.dtype),
                gathered,
                value,
            ),
        )

    return lax.fori_loop(0, place, one, state)


def prefix_2(value, axis, join, neutral):
    count = lax.axis_size(axis)
    place = lax.axis_index(axis)
    ahead = count - 1 - place
    gathered = jax.tree.map(
        lambda a, kind: lax.all_gather(a.astype(kind), axis),
        value,
        jax.tree.map(lambda a: jnp.bfloat16 if a.dtype == jnp.float32 else a.dtype, value),
    )
    state = jax.tree.map(lambda a, e: jnp.zeros_like(a) + jnp.asarray(e, a.dtype), value, neutral)

    def one(turn, state):
        source = count - 1 - turn
        return join(
            state,
            jax.tree.map(
                lambda a, own: lax.dynamic_index_in_dim(a, source, 0, False).astype(own.dtype),
                gathered,
                value,
            ),
        )

    return lax.fori_loop(0, ahead, one, state)


def rms_scale(values, gain):
    mean_square = jnp.mean(values * values, axis=-1, keepdims=True)
    return values * lax.rsqrt(mean_square + norm_eps) * gain


def causal_conv(extended, ext_segs, conv_weight, conv_bias, row_count):
    target = ext_segs[KERNEL - 1 :]
    total = jnp.zeros((row_count, conv_weight.shape[1]), jnp.float32) + conv_bias[None, :]
    for offset in range(KERNEL):
        window = extended[offset : offset + row_count]
        same_doc = (ext_segs[offset : offset + row_count] == target).astype(jnp.float32)
        total = total + conv_weight[offset][None, :] * window * same_doc[:, None]
    return jax.nn.silu(total)


def prepare(xbc, dt_raw, edge_rows, ext_segs, conv_weight, conv_bias, dt_bias, a_log):
    row_count = xbc.shape[0]
    extended = jnp.concatenate([edge_rows, xbc], axis=0)
    mixed = causal_conv(extended, ext_segs, conv_weight, conv_bias, row_count)
    values = mixed[:, :INNER].reshape(row_count, HEADS, HEADDIM)
    key_vecs = mixed[:, INNER : INNER + STATE]
    queries = mixed[:, INNER + STATE :]
    step_sizes = jax.nn.softplus(dt_raw + dt_bias[None, :])
    log_decay = -step_sizes * jnp.exp(a_log)[None, :]
    return (values, key_vecs, queries, step_sizes, log_decay)


def group_block(carried, block_in):
    state_in, last_seg = carried
    values, key_vecs, queries, step_sizes, log_decay, seg_ids = block_in
    length_here = seg_ids.shape[0]
    cumulative = jnp.cumsum(log_decay, axis=0)
    positions = jnp.arange(length_here)
    allowed = (seg_ids[:, None] == seg_ids[None, :]) & (positions[:, None] >= positions[None, :])
    gap_logs = cumulative[:, None, :] - cumulative[None, :, :]
    decay_mask = jnp.where(allowed[:, :, None], jnp.exp(jnp.minimum(gap_logs, 0.0)), 0.0)
    scores = jnp.dot(queries, key_vecs.T, precision=highest)
    weights = decay_mask * scores[:, :, None] * step_sizes[None, :, :]
    inside = jnp.einsum("tsh,shp->thp", weights, values, precision=highest)
    keep_factor = jnp.where((seg_ids == last_seg)[:, None], jnp.exp(cumulative), 0.0)
    carried_out = (
        jnp.einsum("tn,hpn->thp", queries, state_in, precision=highest) * keep_factor[:, :, None]
    )
    to_end = (
        jnp.where(
            (seg_ids == seg_ids[-1])[:, None], jnp.exp(cumulative[-1][None, :] - cumulative), 0.0
        )
        * step_sizes
    )
    fresh_state = jnp.einsum("sh,shp,sn->hpn", to_end, values, key_vecs, precision=highest)
    new_state = state_in * keep_factor[-1][:, None, None] + fresh_state
    return ((new_state, seg_ids[-1]), inside + carried_out)


def grouped_ssd(
    values, key_vecs, queries, step_sizes, log_decay, seg_ids, d_skip, state_in, last_seg
):
    row_count = seg_ids.shape[0]
    block_count = row_count // GROUP

    def blocked(member):
        return member.reshape((block_count, GROUP) + member.shape[1:])

    inputs = (
        blocked(values),
        blocked(key_vecs),
        blocked(queries),
        blocked(step_sizes),
        blocked(log_decay),
        blocked(seg_ids),
    )
    (final_state, last_out), outputs = lax.scan(
        jax.checkpoint(group_block), (state_in, last_seg), inputs
    )
    outputs = outputs.reshape(row_count, HEADS, HEADDIM) + d_skip[None, :, None] * values
    return (outputs, final_state)


def gated_norm(mixed_out, gate_z, gain_out):
    return rms_scale(mixed_out * jax.nn.silu(gate_z), gain_out)


def chain_combine(earlier, later):
    decay_early, state_early = earlier
    decay_late, state_late = later
    return (decay_early * decay_late, decay_late[:, None, None] * state_early + state_late)


def cross_term(queries, log_decay, state_in, seg_ids, prev_seg):
    cumulative = jnp.cumsum(log_decay, axis=0)
    keep_factor = jnp.where((seg_ids == prev_seg)[:, None], jnp.exp(cumulative), 0.0)
    return jnp.einsum("tn,hpn->thp", queries, state_in, precision=highest) * keep_factor[:, :, None]


def device_decay(log_decay, seg_ids, prev_seg):
    total_log = jnp.sum(log_decay, axis=0)
    return jnp.where(seg_ids[-1] == prev_seg, jnp.exp(total_log), 0.0)


def on_device(
    tokens,
    cotangent,
    segments,
    in_weight,
    out_weight,
    gain_in,
    conv_weight,
    conv_bias,
    dt_bias,
    a_log,
    d_skip,
    gain_out,
):
    tokens_f = tokens[0].astype(jnp.float32)
    cot_low = cotangent[0]
    seg_ids = segments[0]
    row_count = seg_ids.shape[0]
    full_in, full_out = (
        lax.all_gather(in_weight, ("seq", "batch"), axis=0, tiled=True),
        lax.all_gather(out_weight, ("seq", "batch"), axis=0, tiled=True),
    )
    normed, norm_pull = jax.vjp(rms_scale, tokens_f, gain_in)
    normed_low = normed.astype(jnp.bfloat16)
    projected = jnp.dot(normed_low, full_in, preferred_element_type=jnp.float32)
    gate_z = projected[:, :INNER]
    xbc = projected[:, INNER : INNER + CONV]
    dt_raw = projected[:, INNER + CONV :]
    tail_start = row_count - KERNEL + 1
    edge_rows, edge_segs = shifted(
        (xbc[tail_start:], seg_ids[tail_start:].astype(jnp.float32)), "seq", 1
    )
    prev_segs = edge_segs.astype(jnp.int32)
    prev_seg = prev_segs[KERNEL - 2]
    ext_segs = jnp.concatenate([prev_segs, seg_ids])

    def prepare_local(xbc_in, dt_in, edge_in, weight_in, bias_in, shift_in, alog_in):
        return prepare(xbc_in, dt_in, edge_in, ext_segs, weight_in, bias_in, shift_in, alog_in)

    prepared, prepare_pull = jax.vjp(
        prepare_local, xbc, dt_raw, edge_rows, conv_weight, conv_bias, dt_bias, a_log
    )
    values, key_vecs, queries, step_sizes, log_decay = prepared
    zeros_state = jnp.zeros((HEADS, HEADDIM, STATE), jnp.float32)

    def local_ssd(values_in, keys_in, queries_in, sizes_in, logs_in, skip_in):
        return grouped_ssd(
            values_in,
            keys_in,
            queries_in,
            sizes_in,
            logs_in,
            seg_ids,
            skip_in,
            zeros_state,
            seg_ids[0],
        )

    (local_out, local_state), ssd_pull = jax.vjp(
        local_ssd, values, key_vecs, queries, step_sizes, log_decay, d_skip
    )

    def decay_local(logs_in):
        return device_decay(logs_in, seg_ids, prev_seg)

    decay_here, decay_pull = jax.vjp(decay_local, log_decay)
    identity = (jnp.ones((HEADS,), jnp.float32), zeros_state)
    decay_prefix, state_in = prefix((decay_here, local_state), "seq", chain_combine, identity)

    def cross_local(queries_in, logs_in, state_arg):
        return cross_term(queries_in, logs_in, state_arg, seg_ids, prev_seg)

    cross_out, cross_pull = jax.vjp(cross_local, queries, log_decay, state_in)
    mixed_out = (local_out + cross_out).reshape(row_count, INNER)
    gated, gated_pull = jax.vjp(gated_norm, mixed_out, gate_z, gain_out)
    gated_low = gated.astype(jnp.bfloat16)
    result = tokens_f + jnp.dot(gated_low, full_out, preferred_element_type=jnp.float32)
    back_in, back_out = (
        lax.all_gather(in_weight, ("seq", "batch"), axis=0, tiled=True),
        lax.all_gather(out_weight, ("seq", "batch"), axis=0, tiled=True),
    )
    contract_last = (((1,), (1,)), ((), ()))
    contract_first = (((0,), (0,)), ((), ()))
    grad_gated = lax.dot_general(
        cot_low, back_out, contract_last, preferred_element_type=jnp.float32
    )
    grad_mixed, grad_gate, grad_gain_out = gated_pull(grad_gated)
    grad_mixed = grad_mixed.reshape(row_count, HEADS, HEADDIM)
    grad_q_cross, grad_log_cross, grad_state_in = cross_pull(grad_mixed)
    decay_after, grad_exit = prefix_2((decay_here, grad_state_in), "seq", chain_combine, identity)
    grad_decay = jnp.sum(grad_exit * state_in, axis=(1, 2))
    grad_log_dev = decay_pull(grad_decay)[0]
    grad_values, grad_keys, grad_q_local, grad_sizes, grad_log_local, grad_skip = ssd_pull(
        (grad_mixed, grad_exit)
    )
    prep_grads = prepare_pull(
        (
            grad_values,
            grad_keys,
            grad_q_local + grad_q_cross,
            grad_sizes,
            grad_log_local + grad_log_cross + grad_log_dev,
        )
    )
    grad_xbc, grad_dt, grad_edge, grad_conv_w, grad_conv_b, grad_dt_bias, grad_a_log = prep_grads
    grad_next = shifted(grad_edge, "seq", -1)
    grad_xbc = grad_xbc.at[tail_start:].add(grad_next)
    grad_proj = jnp.concatenate([grad_gate, grad_xbc, grad_dt], axis=1).astype(jnp.bfloat16)
    grad_normed = lax.dot_general(
        grad_proj, back_in, contract_last, preferred_element_type=jnp.float32
    )
    grad_tokens_norm, grad_gain_in = norm_pull(grad_normed)
    grad_tokens = (cot_low.astype(jnp.float32) + grad_tokens_norm).astype(jnp.bfloat16)
    grad_in_w = lax.dot_general(
        normed_low, grad_proj, contract_first, preferred_element_type=jnp.float32
    )
    grad_out_w = lax.dot_general(
        gated_low, cot_low, contract_first, preferred_element_type=jnp.float32
    )
    shard_in, shard_out = (
        lax.psum_scatter(grad_in_w, ("seq", "batch"), scatter_dimension=0, tiled=True),
        lax.psum_scatter(grad_out_w, ("seq", "batch"), scatter_dimension=0, tiled=True),
    )
    summed = lax.psum(
        (
            grad_gain_in,
            grad_conv_w,
            grad_conv_b,
            grad_dt_bias,
            grad_a_log,
            grad_skip,
            grad_gain_out,
        ),
        ("seq", "batch"),
    )
    return (
        result.astype(jnp.bfloat16)[None],
        grad_tokens[None],
        shard_in,
        shard_out,
        summed[0],
        summed[1],
        summed[2],
        summed[3],
        summed[4],
        summed[5],
        summed[6],
    )


def solution(mesh):
    in_specs = (
        P("batch", "seq", None),
        P("batch", "seq", None),
        P("batch", "seq"),
        P(("seq", "batch"), None),
        P(("seq", "batch"), None),
        P(),
        P(),
        P(),
        P(),
        P(),
        P(),
        P(),
    )
    out_specs = (
        P("batch", "seq", None),
        P("batch", "seq", None),
        P(("seq", "batch"), None),
        P(("seq", "batch"), None),
        P(),
        P(),
        P(),
        P(),
        P(),
        P(),
        P(),
    )
    count = mesh.shape["seq"]
    even = HEADS % (2 * count) == 0 and count & (count - 1) == 0
    return jax.shard_map(
        head_parallel if even else on_device, mesh=mesh, in_specs=in_specs, out_specs=out_specs, check_vma=False
    )
```

```python
import functools

import jax
import jax.numpy as jnp
from jax import lax
from jax.experimental import pallas as pl
from jax.experimental.pallas import tpu as pltpu
from jax.sharding import PartitionSpec as P

HEADS = 24
HEADDIM = 64
STATE = 128
KERNEL = 4
GROUP = 128
INNER = 1536
CONV = 1792
WIDTH = 768
LANES = 128
LEAD = 8
TINY = 1e-37


highest = lax.Precision.HIGHEST
norm_eps = 1e-05
f32 = jnp.float32
bf16 = jnp.bfloat16
contract_last = (((1,), (1,)), ((), ()))
contract_first = (((0,), (0,)), ((), ()))


def mm(a, b):
    return jnp.dot(a.astype(bf16), b.astype(bf16), preferred_element_type=f32)


def mm_nt(a, b):
    return lax.dot_general(
        a.astype(bf16), b.astype(bf16), contract_last, preferred_element_type=f32
    )


def mm_tn(a, b):
    return lax.dot_general(
        a.astype(bf16), b.astype(bf16), contract_first, preferred_element_type=f32
    )


def two_parts(value):
    high = value.astype(bf16)
    return high, (value - high.astype(f32)).astype(bf16)


def mask_mm(mask, value):
    width = value.shape[1]
    out = mm(mask, jnp.concatenate(two_parts(value), axis=1))
    return out[:, :width] + out[:, width:]


def iota(shape, dim):
    return lax.broadcasted_iota(jnp.int32, shape, dim)


def aligned(value, unit):
    return pl.multiple_of(value, unit)


def wide(columns, chan):
    half = LANES // 2
    high, low = two_parts(columns)
    low = pltpu.roll(low.astype(f32), half, 1)
    both = jnp.where(iota(columns.shape, 1) < half, high.astype(f32), low)
    spread = iota((LANES, chan), 1) // HEADDIM == lax.rem(iota((LANES, chan), 0), half)
    return mm(both, spread.astype(f32))


def softplus(value):
    return jnp.maximum(value, 0.0) + jnp.log1p(jnp.exp(-jnp.abs(value)))


def sigmoid(value):
    return 0.5 + 0.5 * jnp.tanh(0.5 * value)


class Plan:
    def __init__(self, mesh_seq, mesh_batch, rows, in_rows, out_rows):
        self.seq = mesh_seq
        self.batch = mesh_batch
        self.line = mesh_batch // 2
        self.rows = rows
        self.total = rows * mesh_seq
        self.blocks = self.total // GROUP
        self.heads = HEADS // mesh_seq
        self.chan = self.heads * HEADDIM
        self.mixed = self.chan + 2 * STATE
        self.cols = self.mixed + LANES
        self.in_rows = in_rows
        self.out_rows = out_rows


def place():
    s = lax.axis_index("seq")
    b = lax.axis_index("batch")
    return s, lax.shift_right_logical(b, 1), lax.bitwise_and(b, 1)


def in_place(plan, ids, line_xor, core_xor, seq_xor):
    s, z, c = ids
    owner = (s ^ seq_xor) * plan.batch + (z ^ line_xor) * 2 + (c ^ core_xor)
    return aligned(owner * plan.in_rows, 8)


def exact_sigmoid(value):
    return 1.0 / (1.0 + jnp.exp(-value))


def convolved(plan, base, x_ref, segc_ref, convw, convb):
    win = x_ref[pl.ds(base, GROUP + LEAD), :]
    segw = segc_ref[pl.ds(base, GROUP + LEAD), :]
    seg = segw[LEAD:]
    pre = convb + convw[KERNEL - 1 : KERNEL] * win[LEAD:]
    for k in range(KERNEL - 1):
        start = LEAD - KERNEL + 1 + k
        same = (segw[start : start + GROUP] == seg).astype(f32)
        same = jnp.concatenate([same] * (plan.mixed // LANES), axis=1)
        pre = pre + convw[k : k + 1] * win[start : start + GROUP] * same
    sig = sigmoid(pre)
    mixed = pre * sig
    return mixed, sig + mixed * (1.0 - sig)


def decays(dt_in, heads_ref):
    steps = softplus(dt_in)
    row = iota((GROUP, GROUP), 0)
    col = iota((GROUP, GROUP), 1)
    decay = -steps * jnp.exp(heads_ref[1:2, :LANES])
    cum = mask_mm(row >= col, decay)
    half = LANES // 2
    turned = jnp.where(col < half, cum, pltpu.roll(steps, half, 1)).T
    return steps, cum, turned


def edges(segc_ref, base, cum):
    seg = segc_ref[pl.ds(aligned(base + LEAD, 8), GROUP), :]
    prev = segc_ref[pl.ds(base, LEAD), :][LEAD - 1 :]
    keep = jnp.where(seg == prev, jnp.exp(cum), 0.0)
    last = cum[GROUP - 1 :]
    to_last = jnp.where(seg == seg[GROUP - 1 :], jnp.exp(last - cum), 0.0)
    return seg, keep, to_last


def head_decay(cum, turned, h):
    return jnp.exp(jnp.minimum(cum[:, h : h + 1] - turned[h : h + 1, :], 0.0))


def split_pair(pair):
    low = iota(pair.shape, 1) < HEADDIM
    return jnp.concatenate([jnp.where(low, pair, 0.0), jnp.where(low, 0.0, pair)], axis=0)


def fetch(pairs, sems):
    copies = [
        pltpu.make_async_copy(src, dst, sems.at[i]) for i, (src, dst) in enumerate(pairs)
    ]
    for copy in copies:
        copy.start()
    for copy in copies:
        copy.wait()


def pack_kernel(plan, w_any, seg_any, *outs):
    n, heads, chan = plan.seq, plan.heads, plan.chan
    blocks, outs = outs[:n], outs[n:]
    w_ref, seg_ref, sems, all_ref = outs
    fetch([(w_any, w_ref), (seg_any, seg_ref)], sems)
    s = lax.axis_index("seq")
    lane = iota((plan.in_rows, LANES), 1)
    tail = w_ref[:, INNER + CONV :].astype(f32)
    tail = jnp.concatenate(
        [tail, jnp.zeros((plan.in_rows, LANES - HEADS), f32)], axis=1
    )
    for g in range(n):
        moved = tail if g == 0 else pltpu.roll(tail, LANES - g * heads, 1)
        all_ref[g] = jnp.concatenate(
            [
                w_ref[:, INNER + g * chan : INNER + (g + 1) * chan],
                w_ref[:, 2 * INNER : INNER + CONV],
                jnp.where(lane < heads, moved, 0.0).astype(bf16),
                w_ref[:, g * chan : (g + 1) * chan],
            ],
            axis=1,
        )
    seg = jnp.broadcast_to(seg_ref[...].astype(f32), (8, plan.rows)).astype(bf16)
    for m in range(n):
        blocks[m][0 : plan.in_rows, :] = all_ref[s ^ m]
        blocks[m][plan.in_rows : plan.in_rows + 8, :] = jnp.zeros((8, plan.cols + chan), bf16)
        blocks[m][plan.in_rows : plan.in_rows + 8, : plan.rows] = seg


def own_params_kernel(
    plan, convw_ref, convb_ref, dtb_ref, alog_ref, skip_ref, gain_ref, conv_ref, heads_ref,
    own_gain_ref,
):
    n, heads, chan = plan.seq, plan.heads, plan.chan
    s = lax.axis_index("seq")
    own = pl.ds(aligned(s * chan, LANES), chan)
    conv_ref[...] = jnp.zeros_like(conv_ref)
    conv_ref[0:KERNEL, :chan] = convw_ref[:, own]
    conv_ref[0:KERNEL, chan:] = convw_ref[:, INNER:]
    conv_ref[KERNEL : KERNEL + 1, :chan] = convb_ref[:, own]
    conv_ref[KERNEL : KERNEL + 1, chan:] = convb_ref[:, INNER:]
    own_gain_ref[...] = gain_ref[:, own]
    one_lane = iota((1, LANES), 1)

    def own_heads(ref):
        row = jnp.concatenate([ref[...], jnp.zeros((1, LANES - HEADS), f32)], axis=1)
        found = row
        for g in range(1, n):
            found = jnp.where(s == g, pltpu.roll(row, LANES - g * heads, 1), found)
        return jnp.where(one_lane < heads, found, 0.0)

    heads_ref[...] = jnp.zeros_like(heads_ref)
    heads_ref[0:1, :LANES] = own_heads(dtb_ref)
    heads_ref[1:2, :LANES] = own_heads(alog_ref)
    skip = jnp.broadcast_to(own_heads(skip_ref), (8, LANES))
    heads_ref[2:3, :] = wide(skip, chan)[0:1]


def regroup_kernel(plan, *refs):
    n, r = plan.seq, plan.in_rows
    pieces, out_w_ref = refs[:n], refs[n]
    main_ref, gate_ref = refs[n + 1 :]
    half = r * n // 2
    for m in range(n):
        main_ref[m * r : (m + 1) * r, :] = pieces[m][0:r, : plan.cols]
        top, left = (m // 2) * r, (m % 2) * plan.chan
        gate_ref[top : top + r, left : left + plan.chan] = pieces[m][0:r, plan.cols :]
    gate_ref[half : half + plan.out_rows, :] = out_w_ref[...]


def fill_segments(plan, s, pieces, segc_ref, segr_ref):
    per = plan.rows // GROUP
    segc_ref[...] = jnp.zeros_like(segc_ref)
    segr_ref[...] = jnp.zeros_like(segr_ref)
    for m in range(plan.seq):
        line = pieces[m][plan.in_rows : plan.in_rows + 1, : plan.rows].astype(f32)
        for j in range(per):
            b = (s ^ m) * per + j
            segr_ref[pl.ds(b, 1), :] = line[:, j * GROUP : (j + 1) * GROUP]
    every = segr_ref[...]
    turned = jnp.concatenate(
        [every, jnp.zeros((LANES - every.shape[0], GROUP), f32)], axis=0
    ).T
    for b in range(plan.blocks):
        segc_ref[LEAD + b * GROUP : LEAD + (b + 1) * GROUP, :] = jnp.broadcast_to(
            turned[:, b : b + 1], (GROUP, LANES)
        )


def project_kernel(plan, *refs):
    n = plan.seq
    toks, refs = refs[:n], refs[n:]
    pieces, refs = refs[:n], refs[n:]
    weights, refs = refs[: 2 * plan.line], refs[2 * plan.line :]
    gain_ref = refs[0]
    normed_ref, w_ref, x_ref, dt_ref, segc_ref, segr_ref, wf_ref = refs[1:]
    ids = place()
    s = ids[0]
    fill_segments(plan, s, pieces, segc_ref, segr_ref)
    for core_xor in range(2):
        for line_xor in range(plan.line):
            piece = weights[core_xor * plan.line + line_xor]
            for m in range(n):
                dest = pl.ds(in_place(plan, ids, line_xor, core_xor, m), plan.in_rows)
                wf_ref[dest, :] = piece[m * plan.in_rows : (m + 1) * plan.in_rows, :].astype(f32)
    w_ref[...] = wf_ref[...].astype(bf16)
    x_ref[0:LEAD, :] = jnp.zeros((LEAD, plan.mixed), f32)
    for m in range(n):
        tok = toks[m][...].astype(f32)
        scale = lax.rsqrt(jnp.mean(tok * tok, axis=1, keepdims=True) + norm_eps)
        low = (tok * scale * gain_ref[...]).astype(bf16)
        start = (s ^ m) * plan.rows
        normed_ref[pl.ds(aligned(start, plan.rows), plan.rows), :] = low
        out = jnp.dot(low, w_ref[...], preferred_element_type=f32)
        x_ref[pl.ds(aligned(start + LEAD, 8), plan.rows), :] = out[:, : plan.mixed]
        dt_ref[pl.ds(aligned(start, plan.rows), plan.rows), :] = out[:, plan.mixed :]


def scan_kernel(plan, first, last, *refs):
    x_ref, dt_ref, segc_ref, segr_ref, conv_ref, heads_ref = refs[:6]
    refs = refs[6:]
    if first:
        early_y_ref, early_ref = refs[:2]
        refs = refs[2:]
    y_ref, state_ref, states_ref, mixed_ref, slope_ref, table_ref, scores_ref = refs
    if first:
        y_ref[: first * GROUP, :] = early_y_ref[...]
        state_ref[...] = early_ref[...]
    else:
        state_ref[...] = jnp.zeros_like(state_ref)
    convw = conv_ref[0:KERNEL, :]
    convb = conv_ref[KERNEL : KERNEL + 1, :]
    chan, half = plan.chan, LANES // 2
    causal = iota((GROUP, GROUP), 0) >= iota((GROUP, GROUP), 1)

    def step(turn, carry):
        base = aligned((first + turn) * GROUP, GROUP)
        here = pl.ds(aligned(turn * GROUP, GROUP), GROUP)
        mixed, slope = convolved(plan, base, x_ref, segc_ref, convw, convb)
        mixed_ref[here, :] = mixed
        slope_ref[here, :] = slope
        values = mixed[:, :chan]
        keys = mixed[:, chan : chan + STATE]
        queries = mixed[:, chan + STATE :]
        dt_in = dt_ref[pl.ds(base, GROUP), :] + heads_ref[0:1, :LANES]
        steps, cum, turned = decays(dt_in, heads_ref)
        table_ref[0, here, :] = steps
        table_ref[1, here, :] = cum
        table_ref[2, here, :] = turned
        seg, keep, to_last = edges(segc_ref, base, cum)
        allowed = (seg == segr_ref[pl.ds(first + turn, 1), :]) & causal
        scores = jnp.where(allowed, mm_nt(queries, keys), 0.0)
        scores_ref[here, :] = scores
        state = state_ref[...]
        states_ref[turn] = state
        parts = []
        for pair in range(plan.heads // 2):
            lanes = slice(pair * LANES, (pair + 1) * LANES)
            weights_pair = []
            for h in (2 * pair, 2 * pair + 1):
                decay = head_decay(cum, turned, h)
                weights_pair.append(decay * scores * turned[half + h : half + h + 1, :])
            parts.append(mm(jnp.concatenate(weights_pair, axis=1), split_pair(values[:, lanes])))
        inside = jnp.concatenate(parts, axis=1)
        spread = wide(jnp.concatenate([keep, to_last * steps], axis=0), chan)
        keep, to_end = spread[:GROUP], spread[GROUP:]
        carried = mm(queries, state) * keep
        y_ref[pl.ds(base, GROUP), :] = inside + carried + heads_ref[2:3, :] * values
        state_ref[...] = state * keep[GROUP - 1 :] + mm_tn(keys, values * to_end)
        return carry

    lax.fori_loop(0, last - first, step, 0, unroll=True)


def gate_kernel(plan, *refs):
    n = plan.seq
    normed_ref, y_ref = refs[:2]
    weights = refs[2 : 2 + 2 * plan.line]
    cots = refs[2 + 2 * plan.line : 2 + 2 * plan.line + n]
    gain_ref = refs[2 + 2 * plan.line + n]
    outs = refs[3 + 2 * plan.line + n :]
    wz_ref, z_ref, du_ref, stats_ref, scaled_ref, wo_ref, wf_ref = outs
    ids = place()
    s, z, c = ids
    half = plan.in_rows * n // 2
    for core_xor in range(2):
        for line_xor in range(plan.line):
            piece = weights[core_xor * plan.line + line_xor]
            for m in range(n):
                dest = pl.ds(in_place(plan, ids, line_xor, core_xor, m), plan.in_rows)
                top = (m // 2) * plan.in_rows
                left = (m % 2) * plan.chan
                wf_ref[dest, :] = piece[
                    top : top + plan.in_rows, left : left + plan.chan
                ].astype(f32)
            start = ((z ^ line_xor) * 2 + (c ^ core_xor)) * plan.out_rows
            wo_ref[pl.ds(aligned(start, 16), plan.out_rows), :] = piece[
                half : half + plan.out_rows, :
            ]
    wz_ref[...] = wf_ref[...].astype(bf16)
    gain = gain_ref[...]
    lane = iota((plan.rows, LANES), 1)
    square = jnp.zeros((GROUP, LANES), f32)
    lane = iota((GROUP, LANES), 1)
    per = plan.rows // GROUP
    for m in range(n):
        start = aligned((s ^ m) * plan.rows, plan.rows)
        gate = jnp.dot(
            normed_ref[pl.ds(start, plan.rows), :], wz_ref[...], preferred_element_type=f32
        )
        z_ref[pl.ds(start, plan.rows), :] = gate
        gated = y_ref[pl.ds(start, plan.rows), :] * gate * sigmoid(gate)
        scaled = gated * gain
        scaled_ref[pl.ds(start, plan.rows), :] = scaled.astype(bf16)
        du = mm_nt(cots[m][...], wo_ref[...])
        du_ref[pl.ds(start, plan.rows), :] = du
        norm = jnp.sum(gated * gated, axis=1, keepdims=True)
        dots = jnp.sum(du * scaled, axis=1, keepdims=True)
        for j in range(per):
            b = (s ^ m) * per + j
            rows = slice(j * GROUP, (j + 1) * GROUP)
            square = square + jnp.where(lane == b, norm[rows], 0.0)
            square = square + jnp.where(lane == b + plan.blocks, dots[rows], 0.0)
    stats_ref[...] = square.T[: 2 * plan.blocks]


def out_kernel(plan, scaled_ref, wo_ref, *parts):
    s = lax.axis_index("seq")
    for m in range(plan.seq):
        rows = pl.ds(aligned((s ^ m) * plan.rows, plan.rows), plan.rows)
        parts[m][...] = mm(scaled_ref[rows, :], wo_ref[...]).astype(bf16)


def emit_rows(plan, ids, source_ref, put):
    for core_xor in range(2):
        for line_xor in range(plan.line):
            for m in range(plan.seq):
                rows = source_ref[
                    pl.ds(in_place(plan, ids, line_xor, core_xor, m), plan.in_rows), :
                ]
                put(core_xor, line_xor, m, rows)


def row_products(w_ref, grad_ref):
    lane = iota((LANES, LANES), 1)
    square = jnp.zeros((LANES, LANES), f32)
    for i in range(w_ref.shape[0] // LANES):
        rows = slice(i * LANES, (i + 1) * LANES)
        product = w_ref[rows, :].astype(f32) * grad_ref[rows, :]
        square = square + jnp.where(lane == i, jnp.sum(product, axis=1, keepdims=True), 0.0)
    return square.T[:8]


def regate_kernel(plan, *refs):
    n = plan.seq
    stats = refs[:n]
    normed_ref, y_ref, z_ref, du_ref, wz_ref = refs[n : n + 5]
    cots = refs[n + 5 : 2 * n + 5]
    gain_ref = refs[2 * n + 5]
    dy_ref, dz_ref, scale_ref, gain_out_ref, share_ref, keep_ref, send_ref = refs[
        2 * n + 6 : 2 * n + 13
    ]
    gated_ref, gz_ref, go_ref = refs[2 * n + 13 :]
    ids = place()
    s, z, c = ids
    total = stats[0][...]
    for m in range(1, n):
        total = total + stats[m][...]
    turned = jnp.concatenate(
        [total, jnp.zeros((LANES - total.shape[0], GROUP), f32)], axis=0
    ).T
    gain = gain_ref[...]
    sums = jnp.zeros((1, plan.chan), f32)
    for b in range(plan.blocks):
        rows = slice(b * GROUP, (b + 1) * GROUP)
        r = lax.rsqrt(turned[:, b : b + 1] / INNER + norm_eps)
        dot = turned[:, plan.blocks + b : plan.blocks + b + 1] / INNER
        scale_ref[rows, :] = jnp.broadcast_to(r, (GROUP, LANES))
        gate = z_ref[rows, :]
        sig = sigmoid(gate)
        silu = gate * sig
        y = y_ref[rows, :]
        gated = y * silu
        du = du_ref[rows, :]
        normal = gated * r
        grad_pre = r * (du * gain) - normal * (r * r * dot)
        dy_ref[rows, :] = grad_pre * silu
        dz_ref[rows, :] = (grad_pre * y * sig * (1.0 + gate * (1.0 - sig))).astype(bf16)
        gated_ref[rows, :] = (normal * gain).astype(bf16)
        sums = sums + jnp.sum(du * normal, axis=0, keepdims=True)
    gain_out_ref[...] = sums
    gz_ref[...] = mm_tn(normed_ref[...], dz_ref[...])
    share_ref[...] = row_products(wz_ref, gz_ref)
    out = None
    for m in range(n):
        start = aligned((s ^ m) * plan.rows, plan.rows)
        one = mm_tn(gated_ref[pl.ds(start, plan.rows), :], cots[m][...])
        out = one if out is None else out + one
    go_ref[...] = out
    half = plan.in_rows * n // 2
    both = (keep_ref, send_ref)

    def put(core_xor, line_xor, m, rows):
        top = (m // 2) * plan.in_rows
        left = (m % 2) * plan.chan
        both[core_xor][line_xor, top : top + plan.in_rows, left : left + plan.chan] = rows.astype(
            bf16
        )

    emit_rows(plan, ids, gz_ref, put)
    for core_xor in range(2):
        for line_xor in range(plan.line):
            start = ((z ^ line_xor) * 2 + (c ^ core_xor)) * plan.out_rows
            both[core_xor][line_xor, half : half + plan.out_rows, :] = go_ref[
                pl.ds(aligned(start, 16), plan.out_rows), :
            ].astype(bf16)


def scan_back_kernel(plan, first, last, *refs):
    x_ref, dt_ref, segc_ref, segr_ref, dy_ref, conv_ref, heads_ref = refs[:7]
    states_ref, mixed_ref, slope_ref, table_ref, scores_ref = refs[7:12]
    refs = refs[12:]
    later = last < plan.blocks
    if later:
        before, refs = refs[:5], refs[5:]
    gp_ref, adj_ref, edge_ref, acc_ref, head_ref = refs
    if later:
        gp_ref[(last - first) * GROUP :, :] = before[0][...]
        adj_ref[...] = before[1][...]
        edge_ref[...] = before[2][...]
        acc_ref[...] = before[3][...]
        head_ref[...] = before[4][...]
    else:
        adj_ref[...] = jnp.zeros_like(adj_ref)
        edge_ref[...] = jnp.zeros_like(edge_ref)
        acc_ref[...] = jnp.zeros_like(acc_ref)
        head_ref[...] = jnp.zeros_like(head_ref)
    convw = conv_ref[0:KERNEL, :]
    chan, half = plan.chan, LANES // 2
    repeat = plan.mixed // LANES
    pick = (iota((chan, LANES), 0) // HEADDIM == iota((chan, LANES), 1)).astype(f32)
    row = iota((GROUP, LANES), 0)
    lane = iota((GROUP, LANES), 1)

    def step(turn, carry):
        b = last - 1 - turn
        base = aligned(b * GROUP, GROUP)
        here = pl.ds(aligned((b - first) * GROUP, GROUP), GROUP)
        values = mixed_ref[here, :chan]
        keys = mixed_ref[here, chan : chan + STATE]
        queries = mixed_ref[here, chan + STATE :]
        steps = table_ref[0, here, :]
        cum = table_ref[1, here, :]
        turned = table_ref[2, here, :]
        scores = scores_ref[here, :]
        seg, keep_h, to_last = edges(segc_ref, base, cum)
        state = states_ref[b - first]
        adj = adj_ref[...]
        dy = dy_ref[pl.ds(base, GROUP), :]
        spread = wide(jnp.concatenate([keep_h, to_last * steps], axis=0), chan)
        keep, to_end = spread[:GROUP], spread[GROUP:]
        kept = dy * keep
        dq = mm_nt(kept, state)
        cross = kept * mm(queries, state)
        fed = mm(keys, adj)
        dk = mm_nt(values * to_end, adj)
        adj_ref[...] = adj * keep[GROUP - 1 :] + mm_tn(queries, kept)
        ended = jnp.sum(state * adj, axis=0, keepdims=True)
        pushed = fed * values
        skipped = jnp.sum(dy * values, axis=0, keepdims=True)
        few = jnp.concatenate([ended, skipped, jnp.zeros((6, chan), f32)], axis=0)
        high = few.astype(bf16).astype(f32)
        sums = mm(jnp.concatenate([cross, pushed, high, few - high], axis=0), pick)
        cross_h = sums[:GROUP]
        pushed_h = sums[GROUP : 2 * GROUP]
        few_h = sums[2 * GROUP : 2 * GROUP + 8] + sums[2 * GROUP + 8 :]
        ended_h = few_h[0:1]
        skipped_h = few_h[1:2]
        grad_steps = pushed_h * to_last
        pulled = grad_steps * steps
        dcum = cross_h - pulled
        at_end = jnp.sum(pulled, axis=0, keepdims=True) + keep_h[GROUP - 1 :] * ended_h
        dscores = None
        columns = []
        dvs = []
        for pair in range(plan.heads // 2):
            lanes = slice(pair * LANES, (pair + 1) * LANES)
            dy_pair = split_pair(dy[:, lanes])
            products = mm_nt(dy_pair, values[:, lanes])
            stacked = []
            for j, h in enumerate((2 * pair, 2 * pair + 1)):
                scaled = head_decay(cum, turned, h) * turned[half + h : half + h + 1, :]
                weighted = scaled * products[j * GROUP : (j + 1) * GROUP]
                both = weighted * scores
                dscores = weighted if dscores is None else dscores + weighted
                dcum = jnp.where(lane == h, dcum + jnp.sum(both, axis=1, keepdims=True), dcum)
                columns.append(jnp.sum(both, axis=0, keepdims=True))
                stacked.append(scaled * scores)
            dvs.append(mm_tn(jnp.concatenate(stacked, axis=0), dy_pair))
        allowed = (seg == segr_ref[pl.ds(b, 1), :]) & (row >= lane)
        dscores = jnp.where(allowed, dscores, 0.0)
        dv = jnp.concatenate(dvs, axis=1) + fed * to_end + heads_ref[2:3, :] * dy
        columns.append(jnp.zeros((LANES - plan.heads, GROUP), f32))
        down = jnp.concatenate(columns, axis=0).T
        grad_steps = grad_steps + down / jnp.maximum(steps, TINY)
        dcum = dcum - down
        dcum = dcum + jnp.where(row == GROUP - 1, at_end, 0.0)
        dk = dk + mm_tn(dscores, queries)
        dq = dq + mm(dscores, keys)
        ddecay = mask_mm(row <= lane, dcum)
        rate = jnp.exp(heads_ref[1:2, :LANES])
        grad_steps = grad_steps - ddecay * rate
        dt_in = dt_ref[pl.ds(base, GROUP), :] + heads_ref[0:1, :LANES]
        grad_dt = grad_steps * exact_sigmoid(dt_in)
        head_ref[0:1, :] += jnp.sum(grad_dt, axis=0, keepdims=True)
        head_ref[1:2, :] -= jnp.sum(ddecay * steps, axis=0, keepdims=True) * rate
        head_ref[2:3, :] += skipped_h
        dpre = jnp.concatenate([dv, dk, dq], axis=1) * slope_ref[here, :]
        longer = jnp.concatenate([dpre, edge_ref[...]], axis=0)
        edge_ref[...] = dpre[:LEAD]
        segn = segc_ref[pl.ds(aligned(base + LEAD, 8), GROUP + LEAD), :]
        x = x_ref[pl.ds(aligned(base + LEAD, 8), GROUP), :]
        acc_ref[KERNEL : KERNEL + 1, :] += jnp.sum(dpre, axis=0, keepdims=True)
        acc_ref[KERNEL - 1 : KERNEL, :] += jnp.sum(dpre * x, axis=0, keepdims=True)
        dx = convw[KERNEL - 1 : KERNEL] * dpre
        for k in range(KERNEL - 1):
            ahead = KERNEL - 1 - k
            same = (segn[ahead : ahead + GROUP] == seg).astype(f32)
            part = longer[ahead : ahead + GROUP] * jnp.concatenate([same] * repeat, axis=1)
            acc_ref[k : k + 1, :] += jnp.sum(part * x, axis=0, keepdims=True)
            dx = dx + convw[k : k + 1] * part
        live = jnp.where(lane < plan.heads, grad_dt, 0.0)
        gp_ref[here, :] = jnp.concatenate([dx, live], axis=1).astype(bf16)
        return carry

    lax.fori_loop(0, last - first, step, 0, unroll=True)


def main_grads_kernel(
    plan, normed_ref, gp_ref, w_ref, gain_ref, share_ref, gain_out_ref, acc_ref, head_ref,
    keep_ref, send_ref, gw_ref, small_ref,
):
    ids = place()
    gw_ref[...] = mm_tn(normed_ref[...], gp_ref[...])
    both = (keep_ref, send_ref)

    def put(core_xor, line_xor, m, rows):
        top = m * plan.in_rows
        both[core_xor][line_xor, top : top + plan.in_rows, :] = rows.astype(bf16)

    emit_rows(plan, ids, gw_ref, put)
    share = share_ref[...] + row_products(w_ref, gw_ref)
    small_ref[...] = jnp.zeros_like(small_ref)
    for i in range(WIDTH // LANES):
        lanes = slice(i * LANES, (i + 1) * LANES)
        small_ref[0:1, lanes] = share[i : i + 1] / gain_ref[:, lanes]
    small_ref[1:6, : plan.mixed] = acc_ref[0:5, :]
    small_ref[6:7, : plan.chan] = gain_out_ref[...]
    for j in range(3):
        small_ref[7:8, j * LANES : (j + 1) * LANES] = head_ref[j : j + 1, :]
    high, low = two_parts(small_ref[...])
    last = plan.seq * plan.in_rows
    for ref in both:
        for line_xor in range(plan.line):
            ref[line_xor, last : last + 8, :] = high
            ref[line_xor, last + 8 : last + 16, :] = low


def normed_grads_kernel(plan, gp_ref, w_ref, dz_ref, wz_ref, *grads):
    s = lax.axis_index("seq")
    for m in range(plan.seq):
        rows = pl.ds(aligned((s ^ m) * plan.rows, plan.rows), plan.rows)
        part = mm_nt(gp_ref[rows, :], w_ref[...]) + mm_nt(dz_ref[rows, :], wz_ref[...])
        grads[m][...] = part.astype(grads[m].dtype)


def joined(ref, top):
    return ref[top : top + 8, :].astype(f32) + ref[top + 8 : top + 16, :].astype(f32)


def main_split_kernel(plan, keep_ref, got_ref, *outs):
    last = plan.seq * plan.in_rows
    small = joined(keep_ref.at[0], last) + joined(got_ref.at[0], last)
    high, low = two_parts(small)
    for m in range(plan.line):
        total = keep_ref[m, :last, :].astype(f32) + got_ref[m, :last, :].astype(f32)
        outs[m][:last, :] = total.astype(bf16)
        outs[m][last : last + 8, :] = high
        outs[m][last + 8 :, :] = low


def gate_split_kernel(plan, keep_ref, got_ref, *outs):
    for m in range(plan.line):
        outs[m][...] = (keep_ref[m].astype(f32) + got_ref[m].astype(f32)).astype(bf16)


def gate_sum_kernel(plan, *refs):
    parts, (gate_ref, out_ref) = refs[: plan.line], refs[plan.line :]
    total = parts[0][...].astype(f32)
    for part in parts[1:]:
        total = total + part[...].astype(f32)
    half = plan.in_rows * plan.seq // 2
    gate_ref[...] = total[:half].astype(bf16)
    out_ref[...] = total[half : half + plan.out_rows]


def row_sum_kernel(plan, gate_ref, *refs):
    parts, outs = refs[: plan.line], refs[plan.line :]
    r, chan = plan.in_rows, plan.chan
    last = plan.seq * r
    small = joined(parts[0], last)
    for part in parts[1:]:
        small = small + joined(part, last)
    high, low = two_parts(small)
    for m in range(plan.seq):
        rows = slice(m * r, (m + 1) * r)
        total = parts[0][rows, :].astype(f32)
        for part in parts[1:]:
            total = total + part[rows, :].astype(f32)
        outs[m][:r, :] = total.astype(bf16)
        outs[m][r : r + 8, :] = high
        outs[m][r + 8 : r + 16, :] = low
        top, left = (m // 2) * r, (m % 2) * chan
        outs[m][r + 16 :, :chan] = gate_ref[top : top + r, left : left + chan]
        outs[m][r + 16 :, chan:] = jnp.zeros((r, plan.cols - chan), bf16)


def columns_kernel(plan, *refs):
    n, r, chan, heads = plan.seq, plan.in_rows, plan.chan, plan.heads
    parts, refs = refs[:n], refs[n:]
    out_ref, gain_in_ref, convw_ref, convb_ref, dtb_ref, alog_ref, skip_ref = refs[:7]
    gain_out_ref, gate_ref, main_ref, small_ref = refs[7:]
    s = lax.axis_index("seq")
    for m in range(n):
        main_ref[m] = parts[m][:r, :].astype(f32)
        small_ref[m] = joined(parts[m], r)
        gate_ref[m] = parts[m][r + 16 :, :chan].astype(f32)
    shared = jnp.zeros((r, 2 * STATE), f32)
    lane = iota((r, LANES), 1)
    dts = jnp.zeros((r, LANES), f32)
    gain_in = jnp.zeros((1, WIDTH), f32)
    small_shared = jnp.zeros((5, 2 * STATE), f32)
    one_lane = iota((1, LANES), 1)
    rows = [jnp.zeros((1, LANES), f32) for _ in range(3)]
    for g in range(n):
        cols = slice(g * chan, (g + 1) * chan)
        out_ref[:, cols] = gate_ref[s ^ g]
        main = main_ref[s ^ g]
        out_ref[:, INNER + g * chan : INNER + (g + 1) * chan] = main[:, :chan]
        shared = shared + main[:, chan : plan.mixed]
        one = main[:, plan.mixed :]
        moved = one if g == 0 else pltpu.roll(one, g * heads, 1)
        dts = jnp.where(lane // heads == g, moved, dts)
        part = small_ref[s ^ g]
        gain_in = gain_in + part[0:1, :WIDTH]
        convw_ref[:, cols] = part[1:5, :chan]
        convb_ref[cols] = part[5, :chan]
        gain_out_ref[cols] = part[6, :chan]
        small_shared = small_shared + part[1:6, chan : plan.mixed]
        for j in range(3):
            one = part[7:8, j * LANES : (j + 1) * LANES]
            moved = one if g == 0 else pltpu.roll(one, g * heads, 1)
            rows[j] = jnp.where(one_lane // heads == g, moved, rows[j])
    out_ref[:, 2 * INNER : INNER + CONV] = shared
    out_ref[:, INNER + CONV :] = dts[:, :HEADS]
    gain_in_ref[...] = gain_in[0]
    convw_ref[:, INNER:] = small_shared[:4]
    convb_ref[INNER:] = small_shared[4]
    dtb_ref[...] = rows[0][:, :HEADS]
    alog_ref[...] = rows[1][:, :HEADS]
    skip_ref[...] = rows[2][:, :HEADS]


def result_kernel(plan, tok_ref, scale_ref, *refs):
    parts, out_ref = refs[: plan.seq], refs[plan.seq]
    s = lax.axis_index("seq")
    total = parts[0][...].astype(f32)
    for part in parts[1:]:
        total = total + part[...].astype(f32)
    r = scale_ref[pl.ds(aligned(s * plan.rows, plan.rows), plan.rows), :]
    r = jnp.concatenate([r] * (WIDTH // LANES), axis=1)
    out_ref[...] = (tok_ref[...].astype(f32) + total * r).astype(bf16)


def token_kernel(plan, tok_ref, cot_ref, gain_ref, *refs):
    parts, out_ref = refs[: plan.seq], refs[plan.seq]
    total = parts[0][...].astype(f32)
    for part in parts[1:]:
        total = total + part[...].astype(f32)
    tok = tok_ref[...].astype(f32)
    q = lax.rsqrt(jnp.mean(tok * tok, axis=1, keepdims=True) + norm_eps)
    w = total * gain_ref[...]
    mean = jnp.mean(w * tok, axis=1, keepdims=True)
    grad = cot_ref[...].astype(f32) + q * w - tok * (q * q * q * mean)
    out_ref[...] = grad.astype(bf16)


def call(body, plan, outs, scratch, *args, mib=4, micros=1, name=None, kept=0):
    shapes = [jax.ShapeDtypeStruct(shape, kind) for shape, kind in outs]
    size = sum(a.size * a.dtype.itemsize for a in args)
    size += sum(a.size * a.dtype.itemsize for a in shapes)
    return pl.pallas_call(
        functools.partial(body, plan),
        out_shape=shapes,
        in_specs=[pl.BlockSpec(memory_space=pltpu.HBM)] * kept
        + [pl.BlockSpec(memory_space=pltpu.VMEM)] * (len(args) - kept),
        out_specs=[pl.BlockSpec(memory_space=pltpu.VMEM)] * len(shapes),
        scratch_shapes=[
            pltpu.VMEM(*one) if isinstance(one, tuple) else one for one in scratch
        ],
        compiler_params=pltpu.CompilerParams(vmem_limit_bytes=mib * 2**20),
        cost_estimate=pl.CostEstimate(
            flops=micros * FLOPS_PER_MICRO, bytes_accessed=0, transcendentals=0
        ),
        name=name,
    )(*args)


FLOPS_PER_MICRO = 3_000_000_000
LATE = 4


def swap(value, axis, by):
    size = lax.axis_size(axis)
    return lax.ppermute(value, axis, [(i, i ^ by) for i in range(size)])


def after(value, *others):
    return lax.optimization_barrier((value, *others))[0]


def head_parallel(
    tokens, cotangent, segments, in_weight, out_weight, gain_in, conv_weight, conv_bias,
    dt_bias, a_log, d_skip, gain_out,
):
    rows = tokens.shape[1]
    plan = Plan(
        lax.axis_size("seq"), lax.axis_size("batch"), rows, in_weight.shape[0], out_weight.shape[0]
    )
    n, line, chan, heads = plan.seq, plan.line, plan.chan, plan.heads
    s = lax.axis_index("seq")
    tok, cot = tokens[0], cotangent[0]

    r = plan.in_rows
    own = call(
        pack_kernel, plan, [((r + 8, plan.cols + chan), bf16)] * n,
        [
            (in_weight.shape, bf16), (segments.shape, jnp.int32), pltpu.SemaphoreType.DMA((2,)),
            ((n, r, plan.cols + chan), bf16),
        ],
        in_weight, segments, name="pack", kept=2,
    )
    pieces = [own[0]] + [swap(own[m], "seq", m) for m in range(1, n)]
    toks = [tok] + [swap(after(tok, pieces[m]), "seq", m) for m in range(1, n)]
    main_shard, gate_shard = call(
        regroup_kernel, plan,
        [((n * r, plan.cols), bf16), ((n * r // 2 + plan.out_rows, WIDTH), bf16)], [],
        *pieces, out_weight, name="regroup",
    )

    def along(shard):
        return [shard] + [swap(shard, "batch", 2 * m) for m in range(1, line)]

    def both_cores(parts):
        return parts + [swap(one, "batch", 1) for one in parts]

    main_line = along(main_shard)
    main_parts = both_cores(main_line)
    gate_line = along(after(gate_shard, *main_line))
    cot_near = after(cot, *toks)
    conv, per_head, own_gain = call(
        own_params_kernel, plan,
        [((8, plan.mixed), f32), ((8, chan), f32), ((1, chan), f32)], [],
        conv_weight, conv_bias[None], dt_bias[None], a_log[None], d_skip[None], gain_out[None],
        name="own_params",
    )
    gain_row = gain_in[None]
    total = plan.total
    seg_rows = -(-plan.blocks // 8) * 8
    normed, w_main, x, dt_raw, segc, segr = call(
        project_kernel, plan,
        [
            ((total, WIDTH), bf16), ((WIDTH, plan.cols), bf16),
            ((total + LEAD, plan.mixed), f32), ((total, LANES), f32),
            ((total + 2 * LEAD, LANES), f32), ((seg_rows, GROUP), f32),
        ],
        [((WIDTH, plan.cols), f32)],
        *toks, *pieces, *main_parts, gain_row, mib=16, micros=5, name="project",
    )
    cot_far = after(cot, normed)
    cots = [cot] + [swap(cot_near if m < 3 else cot_far, "seq", m) for m in range(1, n)]
    half = plan.blocks // 2
    state_shape = (STATE, chan)
    scan_in = (x, dt_raw, segc, segr, conv, per_head)

    def scan_part(first, last, *early):
        count, size = last - first, (last - first) * GROUP
        return list(call(
            lambda p, *refs: scan_kernel(p, first, last, *refs), plan,
            [
                ((last * GROUP, chan), f32), (state_shape, f32), ((count,) + state_shape, f32),
                ((size, plan.mixed), f32), ((size, plan.mixed), f32), ((3, size, LANES), f32),
                ((size, GROUP), f32),
            ], [],
            *scan_in, *early, mib=16, micros=4, name="scan_forward",
        ))

    early_y, early_state, *early = scan_part(0, half)
    gate_line = [after(one, early_state) for one in gate_line]
    gate_parts = both_cores(gate_line)
    early_state = after(early_state, *gate_line, *cots[1:3])
    y, _, *late = scan_part(half, plan.blocks, early_y, early_state)
    piece_shape = (rows, WIDTH)
    w_gate, z, du, stats, scaled, w_out = call(
        gate_kernel, plan,
        [
            ((WIDTH, chan), bf16), ((total, chan), f32), ((total, chan), f32),
            ((2 * plan.blocks, GROUP), f32), ((total, chan), bf16), ((chan, WIDTH), bf16),
        ],
        [((WIDTH, chan), f32)],
        normed, y, *gate_parts, *cots, own_gain,
        mib=16, micros=6, name="gate_forward",
    )
    outs = call(
        out_kernel, plan, [(piece_shape, bf16)] * n, [], scaled, w_out, mib=8, micros=2,
        name="out_partial",
    )
    all_stats = [stats] + [swap(stats, "seq", m) for m in range(1, n)]
    dy, dz, scale, gain_out_grad, share, keep, send = call(
        regate_kernel, plan,
        [
            ((total, chan), f32), ((total, chan), bf16), ((total, LANES), f32), ((1, chan), f32),
            ((8, LANES), f32),
            ((line, n * r // 2 + plan.out_rows, WIDTH), bf16),
            ((line, n * r // 2 + plan.out_rows, WIDTH), bf16),
        ],
        [((total, chan), bf16), ((WIDTH, chan), f32), ((chan, WIDTH), f32)],
        *all_stats, after(normed, *outs), y, z, du, w_gate, *cots, own_gain,
        mib=16, micros=6, name="gate_backward",
    )

    def reduce_line(keep, send, body, name):
        got = swap(send, "batch", 1)
        parts = call(
            body, plan, [(keep.shape[1:], bf16)] * line, [], keep, got, name=name, micros=LATE,
        )
        return list(parts)

    def line_exchange(parts):
        return [parts[0]] + [swap(parts[m], "batch", 2 * m) for m in range(1, line)]

    gate_half = reduce_line(keep, send, gate_split_kernel, "gate_core_sum")
    dy = after(dy, *gate_half)
    back_in = (x, dt_raw, segc, segr, dy, conv, per_head)

    def scan_back_part(first, last, saved, *before):
        return call(
            lambda p, *refs: scan_back_kernel(p, first, last, *refs), plan,
            [
                ((total - first * GROUP, plan.cols), bf16), (state_shape, f32),
                ((LEAD, plan.mixed), f32), ((8, plan.mixed), f32), ((8, LANES), f32),
            ], [],
            *back_in, *saved, *before, mib=16, micros=7, name="scan_backward",
        )

    before = list(scan_back_part(half, plan.blocks, late))
    out_parts = [outs[0]] + [swap(outs[m], "seq", m) for m in range(1, n)]
    gate_half[-1] = after(gate_half[-1], before[1])
    gate_lines = line_exchange(gate_half)
    gate_rows, shard_out = call(
        gate_sum_kernel, plan,
        [((n * r // 2, WIDTH), bf16), ((plan.out_rows, WIDTH), f32)], [], *gate_lines,
        name="gate_sum", micros=LATE,
    )
    before[1] = after(before[1], *gate_lines[:-1])
    gp, _, _, acc, head_acc = scan_back_part(0, half, early, *before)
    (result,) = call(
        result_kernel, plan, [(piece_shape, bf16)], [], tok, scale, *out_parts, name="result"
    )

    grads = call(
        normed_grads_kernel, plan, [(piece_shape, bf16)] * n, [], gp, w_main, dz, w_gate,
        mib=12, micros=3 * LATE, name="normed_grads",
    )
    gp_late = after(gp, *out_parts, *gate_lines, *grads)
    keep, send = call(
        main_grads_kernel, plan, [((line, n * r + 16, plan.cols), bf16)] * 2,
        [((WIDTH, plan.cols), f32), ((8, plan.cols), f32)],
        normed, gp_late, w_main, gain_row, share, gain_out_grad, acc, head_acc,
        mib=12, micros=4 * LATE, name="main_grads",
    )
    main_half = reduce_line(keep, send, main_split_kernel, "main_core_sum")
    main_lines = line_exchange(main_half)
    grad_parts = [grads[0]] + [swap(grads[m], "seq", m) for m in range(1, n)]
    last = call(
        row_sum_kernel, plan, [((2 * r + 16, plan.cols), bf16)] * n, [], gate_rows, *main_lines,
        name="main_sum", micros=LATE,
    )
    last = [last[0]] + [swap(last[m], "seq", m) for m in range(1, n)]
    (grad_tokens,) = call(
        token_kernel, plan, [(piece_shape, bf16)], [], tok, cot, gain_row, *grad_parts,
        name="token_grad", micros=LATE,
    )
    shard_in, *smalls = call(
        columns_kernel, plan,
        [
            ((r, in_weight.shape[1]), f32),
            ((WIDTH,), f32), ((KERNEL, CONV), f32), ((CONV,), f32), ((1, HEADS), f32),
            ((1, HEADS), f32), ((1, HEADS), f32), ((INNER,), f32),
        ],
        [((n, r, chan), f32), ((n, r, plan.cols), f32), ((n, 8, plan.cols), f32)],
        *last, name="columns", micros=LATE,
    )
    return (
        result[None], grad_tokens[None], shard_in, shard_out, smalls[0], smalls[1],
        smalls[2], smalls[3][0], smalls[4][0], smalls[5][0], smalls[6],
    )


def shifted(value, axis, by):
    size = lax.axis_size(axis)
    pairs = [(i, i + by) for i in range(size) if 0 <= i + by < size]
    return lax.ppermute(value, axis, pairs)


def prefix(value, axis, join, neutral):
    place = lax.axis_index(axis)
    gathered = jax.tree.map(
        lambda a, kind: lax.all_gather(a.astype(kind), axis), value, (jnp.bfloat16, jnp.bfloat16)
    )
    state = jax.tree.map(lambda a, e: jnp.zeros_like(a) + jnp.asarray(e, a.dtype), value, neutral)

    def one(turn, state):
        return join(
            state,
            jax.tree.map(
                lambda a, own: lax.dynamic_index_in_dim(a, turn, 0, False).astype(own.dtype),
                gathered,
                value,
            ),
        )

    return lax.fori_loop(0, place, one, state)


def prefix_2(value, axis, join, neutral):
    count = lax.axis_size(axis)
    place = lax.axis_index(axis)
    ahead = count - 1 - place
    gathered = jax.tree.map(
        lambda a, kind: lax.all_gather(a.astype(kind), axis),
        value,
        jax.tree.map(lambda a: jnp.bfloat16 if a.dtype == jnp.float32 else a.dtype, value),
    )
    state = jax.tree.map(lambda a, e: jnp.zeros_like(a) + jnp.asarray(e, a.dtype), value, neutral)

    def one(turn, state):
        source = count - 1 - turn
        return join(
            state,
            jax.tree.map(
                lambda a, own: lax.dynamic_index_in_dim(a, source, 0, False).astype(own.dtype),
                gathered,
                value,
            ),
        )

    return lax.fori_loop(0, ahead, one, state)


def rms_scale(values, gain):
    mean_square = jnp.mean(values * values, axis=-1, keepdims=True)
    return values * lax.rsqrt(mean_square + norm_eps) * gain


def causal_conv(extended, ext_segs, conv_weight, conv_bias, row_count):
    target = ext_segs[KERNEL - 1 :]
    total = jnp.zeros((row_count, conv_weight.shape[1]), jnp.float32) + conv_bias[None, :]
    for offset in range(KERNEL):
        window = extended[offset : offset + row_count]
        same_doc = (ext_segs[offset : offset + row_count] == target).astype(jnp.float32)
        total = total + conv_weight[offset][None, :] * window * same_doc[:, None]
    return jax.nn.silu(total)


def prepare(xbc, dt_raw, edge_rows, ext_segs, conv_weight, conv_bias, dt_bias, a_log):
    row_count = xbc.shape[0]
    extended = jnp.concatenate([edge_rows, xbc], axis=0)
    mixed = causal_conv(extended, ext_segs, conv_weight, conv_bias, row_count)
    values = mixed[:, :INNER].reshape(row_count, HEADS, HEADDIM)
    key_vecs = mixed[:, INNER : INNER + STATE]
    queries = mixed[:, INNER + STATE :]
    step_sizes = jax.nn.softplus(dt_raw + dt_bias[None, :])
    log_decay = -step_sizes * jnp.exp(a_log)[None, :]
    return (values, key_vecs, queries, step_sizes, log_decay)


def group_block(carried, block_in):
    state_in, last_seg = carried
    values, key_vecs, queries, step_sizes, log_decay, seg_ids = block_in
    length_here = seg_ids.shape[0]
    cumulative = jnp.cumsum(log_decay, axis=0)
    positions = jnp.arange(length_here)
    allowed = (seg_ids[:, None] == seg_ids[None, :]) & (positions[:, None] >= positions[None, :])
    gap_logs = cumulative[:, None, :] - cumulative[None, :, :]
    decay_mask = jnp.where(allowed[:, :, None], jnp.exp(jnp.minimum(gap_logs, 0.0)), 0.0)
    scores = jnp.dot(queries, key_vecs.T, precision=highest)
    weights = decay_mask * scores[:, :, None] * step_sizes[None, :, :]
    inside = jnp.einsum("tsh,shp->thp", weights, values, precision=highest)
    keep_factor = jnp.where((seg_ids == last_seg)[:, None], jnp.exp(cumulative), 0.0)
    carried_out = (
        jnp.einsum("tn,hpn->thp", queries, state_in, precision=highest) * keep_factor[:, :, None]
    )
    to_end = (
        jnp.where(
            (seg_ids == seg_ids[-1])[:, None], jnp.exp(cumulative[-1][None, :] - cumulative), 0.0
        )
        * step_sizes
    )
    fresh_state = jnp.einsum("sh,shp,sn->hpn", to_end, values, key_vecs, precision=highest)
    new_state = state_in * keep_factor[-1][:, None, None] + fresh_state
    return ((new_state, seg_ids[-1]), inside + carried_out)


def grouped_ssd(
    values, key_vecs, queries, step_sizes, log_decay, seg_ids, d_skip, state_in, last_seg
):
    row_count = seg_ids.shape[0]
    block_count = row_count // GROUP

    def blocked(member):
        return member.reshape((block_count, GROUP) + member.shape[1:])

    inputs = (
        blocked(values),
        blocked(key_vecs),
        blocked(queries),
        blocked(step_sizes),
        blocked(log_decay),
        blocked(seg_ids),
    )
    (final_state, last_out), outputs = lax.scan(
        jax.checkpoint(group_block), (state_in, last_seg), inputs
    )
    outputs = outputs.reshape(row_count, HEADS, HEADDIM) + d_skip[None, :, None] * values
    return (outputs, final_state)


def gated_norm(mixed_out, gate_z, gain_out):
    return rms_scale(mixed_out * jax.nn.silu(gate_z), gain_out)


def chain_combine(earlier, later):
    decay_early, state_early = earlier
    decay_late, state_late = later
    return (decay_early * decay_late, decay_late[:, None, None] * state_early + state_late)


def cross_term(queries, log_decay, state_in, seg_ids, prev_seg):
    cumulative = jnp.cumsum(log_decay, axis=0)
    keep_factor = jnp.where((seg_ids == prev_seg)[:, None], jnp.exp(cumulative), 0.0)
    return jnp.einsum("tn,hpn->thp", queries, state_in, precision=highest) * keep_factor[:, :, None]


def device_decay(log_decay, seg_ids, prev_seg):
    total_log = jnp.sum(log_decay, axis=0)
    return jnp.where(seg_ids[-1] == prev_seg, jnp.exp(total_log), 0.0)


def on_device(
    tokens,
    cotangent,
    segments,
    in_weight,
    out_weight,
    gain_in,
    conv_weight,
    conv_bias,
    dt_bias,
    a_log,
    d_skip,
    gain_out,
):
    tokens_f = tokens[0].astype(jnp.float32)
    cot_low = cotangent[0]
    seg_ids = segments[0]
    row_count = seg_ids.shape[0]
    full_in, full_out = (
        lax.all_gather(in_weight, ("seq", "batch"), axis=0, tiled=True),
        lax.all_gather(out_weight, ("seq", "batch"), axis=0, tiled=True),
    )
    normed, norm_pull = jax.vjp(rms_scale, tokens_f, gain_in)
    normed_low = normed.astype(jnp.bfloat16)
    projected = jnp.dot(normed_low, full_in, preferred_element_type=jnp.float32)
    gate_z = projected[:, :INNER]
    xbc = projected[:, INNER : INNER + CONV]
    dt_raw = projected[:, INNER + CONV :]
    tail_start = row_count - KERNEL + 1
    edge_rows, edge_segs = shifted(
        (xbc[tail_start:], seg_ids[tail_start:].astype(jnp.float32)), "seq", 1
    )
    prev_segs = edge_segs.astype(jnp.int32)
    prev_seg = prev_segs[KERNEL - 2]
    ext_segs = jnp.concatenate([prev_segs, seg_ids])

    def prepare_local(xbc_in, dt_in, edge_in, weight_in, bias_in, shift_in, alog_in):
        return prepare(xbc_in, dt_in, edge_in, ext_segs, weight_in, bias_in, shift_in, alog_in)

    prepared, prepare_pull = jax.vjp(
        prepare_local, xbc, dt_raw, edge_rows, conv_weight, conv_bias, dt_bias, a_log
    )
    values, key_vecs, queries, step_sizes, log_decay = prepared
    zeros_state = jnp.zeros((HEADS, HEADDIM, STATE), jnp.float32)

    def local_ssd(values_in, keys_in, queries_in, sizes_in, logs_in, skip_in):
        return grouped_ssd(
            values_in,
            keys_in,
            queries_in,
            sizes_in,
            logs_in,
            seg_ids,
            skip_in,
            zeros_state,
            seg_ids[0],
        )

    (local_out, local_state), ssd_pull = jax.vjp(
        local_ssd, values, key_vecs, queries, step_sizes, log_decay, d_skip
    )

    def decay_local(logs_in):
        return device_decay(logs_in, seg_ids, prev_seg)

    decay_here, decay_pull = jax.vjp(decay_local, log_decay)
    identity = (jnp.ones((HEADS,), jnp.float32), zeros_state)
    decay_prefix, state_in = prefix((decay_here, local_state), "seq", chain_combine, identity)

    def cross_local(queries_in, logs_in, state_arg):
        return cross_term(queries_in, logs_in, state_arg, seg_ids, prev_seg)

    cross_out, cross_pull = jax.vjp(cross_local, queries, log_decay, state_in)
    mixed_out = (local_out + cross_out).reshape(row_count, INNER)
    gated, gated_pull = jax.vjp(gated_norm, mixed_out, gate_z, gain_out)
    gated_low = gated.astype(jnp.bfloat16)
    result = tokens_f + jnp.dot(gated_low, full_out, preferred_element_type=jnp.float32)
    back_in, back_out = (
        lax.all_gather(in_weight, ("seq", "batch"), axis=0, tiled=True),
        lax.all_gather(out_weight, ("seq", "batch"), axis=0, tiled=True),
    )
    contract_last = (((1,), (1,)), ((), ()))
    contract_first = (((0,), (0,)), ((), ()))
    grad_gated = lax.dot_general(
        cot_low, back_out, contract_last, preferred_element_type=jnp.float32
    )
    grad_mixed, grad_gate, grad_gain_out = gated_pull(grad_gated)
    grad_mixed = grad_mixed.reshape(row_count, HEADS, HEADDIM)
    grad_q_cross, grad_log_cross, grad_state_in = cross_pull(grad_mixed)
    decay_after, grad_exit = prefix_2((decay_here, grad_state_in), "seq", chain_combine, identity)
    grad_decay = jnp.sum(grad_exit * state_in, axis=(1, 2))
    grad_log_dev = decay_pull(grad_decay)[0]
    grad_values, grad_keys, grad_q_local, grad_sizes, grad_log_local, grad_skip = ssd_pull(
        (grad_mixed, grad_exit)
    )
    prep_grads = prepare_pull(
        (
            grad_values,
            grad_keys,
            grad_q_local + grad_q_cross,
            grad_sizes,
            grad_log_local + grad_log_cross + grad_log_dev,
        )
    )
    grad_xbc, grad_dt, grad_edge, grad_conv_w, grad_conv_b, grad_dt_bias, grad_a_log = prep_grads
    grad_next = shifted(grad_edge, "seq", -1)
    grad_xbc = grad_xbc.at[tail_start:].add(grad_next)
    grad_proj = jnp.concatenate([grad_gate, grad_xbc, grad_dt], axis=1).astype(jnp.bfloat16)
    grad_normed = lax.dot_general(
        grad_proj, back_in, contract_last, preferred_element_type=jnp.float32
    )
    grad_tokens_norm, grad_gain_in = norm_pull(grad_normed)
    grad_tokens = (cot_low.astype(jnp.float32) + grad_tokens_norm).astype(jnp.bfloat16)
    grad_in_w = lax.dot_general(
        normed_low, grad_proj, contract_first, preferred_element_type=jnp.float32
    )
    grad_out_w = lax.dot_general(
        gated_low, cot_low, contract_first, preferred_element_type=jnp.float32
    )
    shard_in, shard_out = (
        lax.psum_scatter(grad_in_w, ("seq", "batch"), scatter_dimension=0, tiled=True),
        lax.psum_scatter(grad_out_w, ("seq", "batch"), scatter_dimension=0, tiled=True),
    )
    summed = lax.psum(
        (
            grad_gain_in,
            grad_conv_w,
            grad_conv_b,
            grad_dt_bias,
            grad_a_log,
            grad_skip,
            grad_gain_out,
        ),
        ("seq", "batch"),
    )
    return (
        result.astype(jnp.bfloat16)[None],
        grad_tokens[None],
        shard_in,
        shard_out,
        summed[0],
        summed[1],
        summed[2],
        summed[3],
        summed[4],
        summed[5],
        summed[6],
    )


def solution(mesh):
    in_specs = (
        P("batch", "seq", None),
        P("batch", "seq", None),
        P("batch", "seq"),
        P(("seq", "batch"), None),
        P(("seq", "batch"), None),
        P(),
        P(),
        P(),
        P(),
        P(),
        P(),
        P(),
    )
    out_specs = (
        P("batch", "seq", None),
        P("batch", "seq", None),
        P(("seq", "batch"), None),
        P(("seq", "batch"), None),
        P(),
        P(),
        P(),
        P(),
        P(),
        P(),
        P(),
    )
    count = mesh.shape["seq"]
    even = HEADS % (2 * count) == 0 and count & (count - 1) == 0
    return jax.shard_map(
        head_parallel if even else on_device, mesh=mesh, in_specs=in_specs, out_specs=out_specs, check_vma=False
    )
```
